32 devices in a mesh: tile: 8 (over z, x), anc: 4 (over y, core).
Axes of the slice: x: 2, y: 2, z: 4, core: 2. Of those that a mesh axis runs over, the one named last changes fastest.
Arguments:
- points: bfloat16 [7, 35, 60416], P(None, None, ('tile', 'anc')), may hold values from -6 to 6
- npoints: int32 [60416], P(('tile', 'anc')), may hold values from 1 to 35
- coords: int32 [60416, 3], P(('tile', 'anc')), may hold values from 0 to 383, as said below
- labels: int32 [2, 384, 352], P(None, ('tile', 'anc')), may hold values from 0 to 2
- targets: float32 [2, 7, 384, 352], P(None, None, ('tile', 'anc')), may hold values from -6 to 6
- w_vfe1: bfloat16 [7, 32], replicated, may hold values from -2 to 2
- w_vfe2: bfloat16 [64, 128], replicated, may hold values from -0.75 to 0.75
- w_mid: bfloat16 [3, 3, 3, 128, 64], replicated, may hold values from -0.25 to 0.25
- w_rpn: bfloat16 [3, 3, 320, 128], P(None, None, 'anc'), may hold values from -0.15625 to 0.15625
- w_head: bfloat16 [128, 16], replicated, may hold values from -0.5 to 0.5
- bn_gain: bfloat16 [32], replicated, may hold values from 0.5 to 1.5
- biases: bfloat16 [368], replicated, may hold values from -0.59765625 to 0.59765625
- master: float32 [600688], P('anc'), may hold values from -0.18 to 0.18
- moment1: float32 [600688], P('anc'), may hold values from -4.3004195e-05 to 4.3004195e-05
- moment2: float32 [600688], P('anc'), may hold values from 4.1618944e-12 to 1.6647577e-11
Outputs:
- master_new: float32 [600688], P('anc')
- moment1_new: float32 [600688], P('anc')
- moment2_new: float32 [600688], P('anc')
- loss: float32 [], replicated
- grad_norm: float32 [], replicated
The draws below stay inside these ranges and needn't reach their ends.
Inputs may be any that keep to these rules, and one draw needn't show every extreme that they name: `coords`: every voxel occupies its own cell. The voxels of each block of 7552 consecutive voxels lie in the same 48 map rows, block t in rows t * 48 to (t+1) * 48 - 1.
All inputs are finite; a program needn't handle non-finite values.
Results may differ from the reference program's by a relative error of at most 0.0023.
Values may be sent and summed in bfloat16 or wider, within the bound.
No kernel may reach another device: no remote copies, remote signals or barrier semaphores. Data moves between devices by JAX's collectives and lax.ppermute only.
A program may use at most 256 MiB of HBM per device.

```python
import math
import jax
import jax.numpy as jnp
from jax import lax

C_VFE = 32
C_VOX = 128
C_MID = 64
C_RPN = 128
PTS = 35
DEPTH = 10
ANCH = 2
BOXD = 7
COLS = 352
SCENE_TILES = 4
TR = 48
C_BEV = 320
HEADS_OUT = 16
ROWS = 384
VOX = 60416
NBIAS = 368
PARAMS = 600688
N_ANC = 4


def draw_coords(key, part):
    tiles = ROWS // TR
    cells = DEPTH * TR * COLS
    per_tile = VOX // tiles

    def one_tile(tile_number):
        order = jax.random.permutation(jax.random.fold_in(key, tile_number), cells)[:per_tile]
        layer = order // (TR * COLS)
        remain = order % (TR * COLS)
        row_global = remain // COLS + tile_number * TR
        column = remain % COLS
        return jnp.stack([layer, row_global, column], axis=1)
    return jax.lax.map(one_tile, jnp.arange(tiles)).reshape(VOX, 3).astype(jnp.int32)


def place_ends(values, rng, least, top_value):
    dims = values.shape
    spot = [jax.random.randint(jax.random.fold_in(rng, axis), (), 0, dims[axis]) for axis in range(len(dims))]
    values = values.at[tuple(spot)].set(least)
    longest = dims.index(max(dims))
    spot[longest] = (spot[longest] + 1) % dims[longest]
    return values.at[tuple(spot)].set(top_value)


def steps_of(own_key, shape, cuts, smallest, top_value):
    factor_of, own = 1.0, jax.random.fold_in(own_key, 6)
    for axis_at, shards_of in cuts:
        steps = jnp.exp(jax.random.uniform(jax.random.fold_in(own, axis_at), (shards_of,), jnp.float32, smallest / len(cuts), top_value / len(cuts)))
        factor_of = factor_of * jnp.repeat(steps, shape[axis_at] // shards_of).reshape([-1 if axis == axis_at else 1 for axis in range(len(shape))])
    return factor_of


def gaussian(key, dims, deviation, limit, cuts=(), dtype=jnp.bfloat16):
    result = deviation * jax.random.normal(key, dims, jnp.float32)
    if cuts:
        result = result * steps_of(key, dims, cuts, -0.22, 0.18)
    return jnp.clip(result, -limit, limit).astype(dtype)


def setup_inputs(seed: int = 0) -> dict:
    streams_of = jax.random.split(jax.random.key(seed), 16)
    points = gaussian(streams_of[0], (7, PTS, VOX), 1.0, 6.0, ((2, 32),))
    npoints = place_ends(jax.random.randint(streams_of[1], (VOX,), 1, PTS + 1), jax.random.fold_in(streams_of[1], 1), 1, PTS).astype(jnp.int32)
    coords = draw_coords(jax.random.fold_in(streams_of[15], 71), 0)
    labels = place_ends(jax.random.randint(streams_of[3], (ANCH, ROWS, COLS), 0, 3), jax.random.fold_in(streams_of[3], 1), 0, 2).astype(jnp.int32)
    targets = gaussian(streams_of[4], (ANCH, BOXD, ROWS, COLS), 1.0, 6.0, ((2, 32),), jnp.float32)
    w_vfe1 = gaussian(streams_of[5], (7, C_VFE), 7 ** -0.5, 2.0)
    w_vfe2 = gaussian(streams_of[6], (2 * C_VFE, C_VOX), (2 * C_VFE) ** -0.5, 0.75)
    w_mid = gaussian(streams_of[7], (3, 3, 3, C_VOX, C_MID), (C_VOX * 4) ** -0.5, 0.25)
    w_rpn = gaussian(streams_of[8], (3, 3, C_BEV, C_RPN), (9 * C_BEV // 2) ** -0.5, 0.15625, ((2, 4),))
    w_head = gaussian(streams_of[9], (C_RPN, HEADS_OUT), C_RPN ** -0.5, 0.5)
    bn_gain = jnp.clip(1.0 + 0.1 * jax.random.normal(streams_of[10], (C_VFE,), jnp.float32), 0.5, 1.5).astype(jnp.bfloat16)
    biases = gaussian(streams_of[11], (NBIAS,), 0.1, 0.59765625)
    master = gaussian(streams_of[12], (PARAMS,), 0.03, 0.18, ((0, 4),), jnp.float32)
    moment1 = gaussian(streams_of[13], (PARAMS,), (0.1111 * 0.05 / PARAMS ** 0.5), 4.300419459468685e-05, ((0, 4),), jnp.float32)
    moment2 = jnp.clip(jnp.exp(math.log(1.6647577413819725e-11) - 1.3862944 * jax.random.uniform(streams_of[14], (PARAMS,), jnp.float32) ** steps_of(streams_of[14], (PARAMS,), ((0, 4),), -0.2, 0.2)), 4.161894353454931e-12, 1.6647577413819725e-11)
    return dict(points=points, npoints=npoints, coords=coords, labels=labels, targets=targets, w_vfe1=w_vfe1, w_vfe2=w_vfe2, w_mid=w_mid, w_rpn=w_rpn, w_head=w_head, bn_gain=bn_gain, biases=biases, master=master, moment1=moment1, moment2=moment2)


PRECISE = lax.Precision.HIGHEST
FOCAL_ALPHA = 0.25
BN_EPSILON = 0.001
CLIP_LIMIT = 0.05
LEARN_RATE = 0.03
BETA_FIRST = 0.9
BETA_SECOND = 0.999
WEIGHT_DECAY = 0.01
ADAM_EPSILON = 1e-08
STEP_NUMBER = 10

@jax.custom_vjp
def low(v):
    return lax.optimization_barrier(v.astype(jnp.bfloat16)).astype(jnp.float32)

@jax.custom_vjp
def low_back(v):
    return v

def low_keep(v):
    return (low(v), None)

def low_pass(kept, grad):
    return (grad,)

def back_keep(v):
    return (v, None)

def back_low(kept, grad):
    return (low(grad),)
low.defvjp(low_keep, low_pass)
low_back.defvjp(back_keep, back_low)

def detection(heads, labels, targets):
    logits = heads[:, 0]
    boxes = heads[:, 1:]
    probab = jax.nn.sigmoid(logits)
    positive = (labels == 1).astype(jnp.float32)
    negative = (labels == 0).astype(jnp.float32)
    focal = positive * FOCAL_ALPHA * (1.0 - probab) ** 2 * jax.nn.softplus(-logits)
    focal = focal + negative * (1.0 - FOCAL_ALPHA) * probab ** 2 * jax.nn.softplus(logits)
    offset = boxes - targets
    magnitude = jnp.abs(offset)
    smooth = jnp.where(magnitude < 1.0 / 9.0, 4.5 * offset * offset, magnitude - 1.0 / 18.0)
    return jnp.sum(focal) + 2.0 * jnp.sum(smooth * positive[:, None])

def middle_conv(features, coords, w_middle):
    depth_out = DEPTH // 2
    scene_rows = SCENE_TILES * TR
    half_rows = scene_rows // 2
    scenes = ROWS // scene_rows + 1
    flattened = jnp.zeros((depth_out * scenes * (scene_rows + 2) * (COLS + 2), C_MID), jnp.float32)
    moved_rows = coords[:, 1] + half_rows
    scene = moved_rows // scene_rows
    inner = moved_rows % scene_rows
    for depth_off in range(3):
        shifted = coords[:, 0] + 1 - depth_off
        usable = ((shifted % 2 == 0) & (shifted >= 0) & (shifted <= 2 * depth_out - 2)).astype(jnp.float32)
        out_depth = jnp.clip(shifted // 2, 0, depth_out - 1)
        for row_off in range(3):
            for col_off in range(3):
                target_index = ((out_depth * scenes + scene) * (scene_rows + 2) + inner - row_off + 2) * (COLS + 2) + coords[:, 2] - col_off + 2
                contrib = jnp.dot(features, w_middle[depth_off, row_off, col_off], precision=PRECISE) * usable[:, None]
                flattened = flattened.at[target_index].add(contrib)
    cube = flattened.reshape(depth_out, scenes, scene_rows + 2, COLS + 2, C_MID)[:, :, 1:-1, 1:-1]
    cube = cube.reshape(depth_out, scenes * scene_rows, COLS, C_MID)
    return cube[:, half_rows:half_rows + ROWS]

def forward(weights, points, npoints, coords, labels, targets):
    w_one, w_two, w_middle, w_region, w_output, gain, bias_all = weights
    shift = bias_all[:C_VFE]
    bias_two = bias_all[C_VFE:C_VFE + C_VOX]
    bias_mid = bias_all[C_VFE + C_VOX:C_VFE + C_VOX + C_MID]
    bias_rpn = bias_all[C_VFE + C_VOX + C_MID:C_VFE + C_VOX + C_MID + C_RPN]
    bias_head = bias_all[C_VFE + C_VOX + C_MID + C_RPN:]
    validity = (lax.broadcasted_iota(jnp.int32, (PTS, VOX), 0) < npoints[None, :]).astype(jnp.float32)
    hidden_one = low_back(jnp.einsum('kpv,kc->cpv', points, w_one, precision=PRECISE))
    count_all = jnp.sum(validity)
    average = lax.optimization_barrier(jnp.sum(hidden_one * validity, axis=(1, 2))) / count_all
    variance = lax.optimization_barrier(jnp.sum(hidden_one * hidden_one * validity, axis=(1, 2))) / count_all - average * average
    normed = (hidden_one - average[:, None, None]) * lax.rsqrt(variance + BN_EPSILON)[:, None, None]
    act_one = jax.nn.relu(gain[:, None, None] * normed + shift[:, None, None]) * validity
    pooled_one = lax.optimization_barrier(jnp.max(act_one, axis=1))
    joined = low(jnp.concatenate([act_one, jnp.broadcast_to(pooled_one[:, None, :], act_one.shape)], axis=0))
    pre_two = low_back(jnp.einsum('cpv,co->opv', joined, w_two, precision=PRECISE) + bias_two[:, None, None])
    act_two = jax.nn.relu(pre_two) * validity
    features = low(lax.optimization_barrier(jnp.max(act_two, axis=1))).T
    middle = middle_conv(features, coords, w_middle)
    pre_mid = low_back(middle + bias_mid)
    bev_cube = low(jax.nn.relu(pre_mid))
    bev = jnp.transpose(bev_cube, (1, 2, 3, 0)).reshape(ROWS, COLS, C_BEV)
    scene_rows = SCENE_TILES * TR
    half_rows = scene_rows // 2
    bev_full = jnp.pad(bev, ((half_rows, half_rows), (0, 0), (0, 0)))
    scene_maps = bev_full.reshape(ROWS // scene_rows + 1, scene_rows, COLS, C_BEV)
    region = lax.conv_general_dilated(scene_maps, w_region, (1, 1), ((1, 1), (1, 1)), dimension_numbers=('NHWC', 'HWIO', 'NHWC'), precision=PRECISE)
    region = region.reshape(-1, COLS, C_RPN)[half_rows:half_rows + ROWS]
    pre_rpn = low_back(region + bias_rpn)
    rpn_act = low(jax.nn.relu(pre_rpn))
    heads = jnp.einsum('rcx,xh->hrc', rpn_act, w_output, precision=PRECISE) + bias_head[:, None, None]
    heads = heads.reshape(ANCH, 1 + BOXD, ROWS, COLS)
    count_pos = jnp.sum((labels == 1).astype(jnp.float32))
    return detection(heads, labels, targets) / count_pos

def reference(points, npoints, coords, labels, targets, w_vfe1, w_vfe2, w_mid, w_rpn, w_head, bn_gain, biases, master, moment1, moment2):
    weights = tuple((item.astype(jnp.float32) for item in (w_vfe1, w_vfe2, w_mid, w_rpn, w_head, bn_gain, biases)))
    points_f = points.astype(jnp.float32)
    loss, pullback = jax.vjp(lambda wts: forward(wts, points_f, npoints, coords, labels, targets), weights)
    grads = pullback(jnp.ones((), jnp.float32))[0]
    g_one, g_two, g_mid, g_rpn, g_head, g_gain, g_bias = grads
    blocks = g_rpn.reshape(3, 3, N_ANC, C_BEV // N_ANC, C_RPN).transpose(2, 0, 1, 3, 4).reshape(-1)
    flattened = jnp.concatenate([blocks, g_one.reshape(-1), g_two.reshape(-1), g_mid.reshape(-1), g_head.reshape(-1), g_gain, g_bias])
    norm_value = jnp.sqrt(jnp.sum(flattened * flattened))
    clipped = flattened * jnp.minimum(1.0, CLIP_LIMIT / (norm_value + 1e-06))
    first = BETA_FIRST * moment1 + (1.0 - BETA_FIRST) * clipped
    second = BETA_SECOND * moment2 + (1.0 - BETA_SECOND) * clipped * clipped
    first_hat = first / (1.0 - BETA_FIRST ** STEP_NUMBER)
    second_hat = second / (1.0 - BETA_SECOND ** STEP_NUMBER)
    updated = master - LEARN_RATE * (first_hat / (jnp.sqrt(second_hat) + ADAM_EPSILON) + WEIGHT_DECAY * master)
    return (updated, first, second, loss, norm_value)
```

```python
import functools
import jax
import jax.numpy as jnp
from jax import lax
from jax.experimental import pallas as pl
from jax.experimental.pallas import tpu as pltpu
from jax.sharding import PartitionSpec as P

DEPTH = 10
PAIRS = DEPTH // 4 + 1
CROP_ROWS = 192
BLOCK_ROWS = 12
HALO = 2
LANES = 128
CHUNK = 384
CAP = 768
EDGE_CAP = 128
LARGE_ROWS = 2304
FOCAL_ALPHA = 0.25
BN_EPSILON = 0.001
CLIP_LIMIT = 0.05
LEARN_RATE = 0.03
BETA_FIRST = 0.9
BETA_SECOND = 0.999
WEIGHT_DECAY = 0.01
ADAM_EPSILON = 1e-08
STEP_NUMBER = 10
F32 = jnp.float32
BF16 = jnp.bfloat16
VMEM_LIMIT = 60 * 1024 * 1024


def vmem(count):
    return [pl.BlockSpec(memory_space=pltpu.VMEM)] * count


def smem(count):
    return [pl.BlockSpec(memory_space=pltpu.SMEM)] * count


def params(*semantics):
    return pltpu.CompilerParams(vmem_limit_bytes=VMEM_LIMIT, dimension_semantics=semantics or None)


def work(micros):
    return pl.CostEstimate(flops=micros, transcendentals=0, bytes_accessed=micros * 3_000_000)


def at_row(index, columns):
    return pl.ds(pl.multiple_of(index * columns, 32), columns)


def column_edges(columns, lanes):
    place = lax.broadcasted_iota(jnp.int32, (columns, lanes), 0)
    return place == 0, place == columns - 1


def from_left(values):
    columns, lanes = values.shape
    first, _ = column_edges(columns, lanes)
    return jnp.where(first, 0.0, pltpu.roll(values, 1, 0))


def from_right(values):
    columns, lanes = values.shape
    _, last = column_edges(columns, lanes)
    return jnp.where(last, 0.0, pltpu.roll(values, columns - 1, 0))


def low_lanes(columns):
    return lax.broadcasted_iota(jnp.int32, (columns, LANES), 1) < LANES // 2


def scatter_kernel(count, cells, fresh, *refs):
    if fresh:
        index_ref, feat_ref, out_ref, wide, rows = refs
    else:
        index_ref, feat_ref, old_ref, out_ref, wide, rows = refs
    step = 512

    def begin(i, carry):
        block = pl.ds(pl.multiple_of(i * step, step), step)
        if fresh:
            wide[block, :] = jnp.zeros((step, LANES), F32)
        else:
            wide[block, :] = old_ref[block, :].astype(F32)
        return carry

    lax.fori_loop(0, cells // step, begin, 0)
    rows[...] = feat_ref[...].astype(F32)

    def place(i, carry):
        for j in range(8):
            wide[pl.ds(index_ref[i * 8 + j], 1), :] = rows[pl.ds(i * 8 + j, 1), :]
        return carry

    lax.fori_loop(0, count // 8, place, 0)

    def finish(i, carry):
        block = pl.ds(pl.multiple_of(i * step, step), step)
        out_ref[block, :] = wide[block, :].astype(BF16)
        return carry

    lax.fori_loop(0, cells // step, finish, 0)


def scatter_rows(index, feats, old, columns):
    cells = DEPTH * (BLOCK_ROWS + 2 * HALO) * columns
    count = index.shape[0]
    fresh = old is None
    return pl.pallas_call(
        functools.partial(scatter_kernel, count, cells, fresh),
        out_shape=jax.ShapeDtypeStruct((cells, LANES), BF16),
        in_specs=smem(1) + vmem(1 if fresh else 2),
        out_specs=vmem(1)[0],
        scratch_shapes=[pltpu.VMEM((cells + 8, LANES), F32), pltpu.VMEM((count, LANES), F32)],
        compiler_params=params(),
        cost_estimate=work(15),
        name="grid_scatter",
    )(*((index, feats) if fresh else (index, feats, old)))


def middle_kernel(columns, edge_ref, grid_ref, weight_ref, bias_ref, out_ref):
    low = low_lanes(columns)
    grid_rows = BLOCK_ROWS + 2 * HALO
    depth_out = DEPTH // 2

    def row(m, carry):
        sums = []
        for o in range(depth_out):
            taps = (1, 2) if o == 0 else (0, 1, 2)
            left = jnp.concatenate(
                [
                    grid_ref[at_row((2 * o + a - 1) * grid_rows + m + b, columns), :]
                    for a in taps
                    for b in range(3)
                ],
                axis=1,
            )
            right = weight_ref[o % 2, 3 * LANES * (3 - len(taps)) :, :]
            sums.append(jnp.dot(left, right, preferred_element_type=F32))
        inside = (m > 0) & (m < BLOCK_ROWS + 1) | (m == 0) & (edge_ref[0] > 0)
        inside = inside | (m == BLOCK_ROWS + 1) & (edge_ref[1] > 0)
        keep = jnp.where(inside, 1.0, 0.0)
        for j in range(PAIRS):
            even = sums[2 * j]
            if 2 * j + 1 < depth_out:
                odd = sums[2 * j + 1]
                first = jnp.where(low, even[:, :LANES], odd[:, :LANES])
                middle = jnp.where(low, odd[:, :LANES], even[:, :LANES])
                last = even[:, LANES:] + odd[:, LANES:]
            else:
                first = even[:, :LANES]
                middle = first
                last = even[:, LANES:]
            total = from_left(first) + pltpu.roll(middle, LANES // 2, 1) + from_right(last)
            total = jnp.maximum(total + bias_ref[0:1, :], 0.0) * keep
            if 2 * j + 1 == depth_out:
                total = jnp.where(low, total, 0.0)
            out_ref[at_row(m, columns), j * LANES : (j + 1) * LANES] = total.astype(BF16)
        return carry

    lax.fori_loop(0, BLOCK_ROWS + 2, row, 0)


def middle_weights(w_mid):
    c_mid = w_mid.shape[4]
    kernel = w_mid.transpose(0, 1, 3, 2, 4).reshape(-1, 3, c_mid)
    none = jnp.zeros_like(kernel[:, 0])
    even = jnp.concatenate([kernel[:, 0], kernel[:, 1], kernel[:, 2], none], axis=1)
    odd = jnp.concatenate([kernel[:, 1], kernel[:, 0], none, kernel[:, 2]], axis=1)
    return jnp.stack([even, odd])


def middle_forward(edges, grid, weights, bias, columns):
    return pl.pallas_call(
        functools.partial(middle_kernel, columns),
        out_shape=jax.ShapeDtypeStruct(((BLOCK_ROWS + 2) * columns, PAIRS * LANES), BF16),
        in_specs=smem(1) + vmem(3),
        out_specs=vmem(1)[0],
        compiler_params=params(),
        cost_estimate=work(26),
        name="middle_forward",
    )(edges, grid, weights, jnp.tile(bias.reshape(1, -1), (8, 2)))


def column_taps(own, j):
    low = low_lanes(own.shape[0])
    other = pltpu.roll(own, LANES // 2, 1)
    both = [jnp.where(low, own, other)]
    if 2 * j + 1 < DEPTH // 2:
        both.append(jnp.where(low, other, own))
    return [(jnp.where(low, from_right(x), x), from_left(x)) for x in both]


def middle_data_kernel(
    count, columns, index_ref, edge_ref, d_ref, above_ref, below_ref, weight_ref, out_ref,
    near, far, wide, rows,
):
    padded = BLOCK_ROWS + 2
    half = LANES // 2
    cells = DEPTH * BLOCK_ROWS * columns

    def build(r, source, place, factor):
        for j in range(PAIRS):
            own = source[place, j * LANES : (j + 1) * LANES].astype(F32)
            if factor is not None:
                own = jnp.where(factor > 0, own, 0.0)
            for k, (pair, left) in enumerate(column_taps(own, j)):
                o = 2 * j + k
                near[o, at_row(r, columns), :] = pair.astype(BF16)
                far[o, at_row(r, columns), 0:half] = left[:, 0:half].astype(BF16)
                if not (isinstance(r, int) and r == 0):
                    far[o, at_row(r - 1, columns), half:LANES] = left[:, half:].astype(BF16)

    def build_own(r, carry):
        build(r + 1, d_ref, at_row(r, columns), None)
        return carry

    whole = slice(0, columns)
    build(0, above_ref, whole, edge_ref[0])
    lax.fori_loop(0, BLOCK_ROWS, build_own, 0)
    build(BLOCK_ROWS + 1, below_ref, whole, edge_ref[1])
    for o in range(DEPTH // 2):
        far[o, (padded - 1) * columns :, half:LANES] = jnp.zeros((columns, half), BF16)

    def row(r, carry):
        def pieces(o):
            return [near[o, at_row(r + i, columns), :] for i in range(3)] + [
                far[o, at_row(r + i, columns), :] for i in (0, 2)
            ]

        for o in range(DEPTH // 2):
            left = jnp.concatenate(pieces(o) + (pieces(o + 1) if o < DEPTH // 2 - 1 else []), axis=1)
            total = jnp.dot(left, weight_ref[0 : left.shape[1], :], preferred_element_type=F32)
            wide[at_row(2 * o * BLOCK_ROWS + r, columns), :] = total[:, :LANES]
            wide[at_row((2 * o + 1) * BLOCK_ROWS + r, columns), :] = total[:, LANES:]
        return carry

    lax.fori_loop(0, BLOCK_ROWS, row, 0)
    wide[cells:, :] = jnp.zeros((8, LANES), F32)

    def pick(i, carry):
        for j in range(8):
            rows[pl.ds(i * 8 + j, 1), :] = wide[pl.ds(index_ref[i * 8 + j], 1), :]
        return carry

    lax.fori_loop(0, count // 8, pick, 0)
    out_ref[...] = rows[...].astype(BF16)


def middle_data_weights(w_mid):
    three, _, _, c_in, c_out = w_mid.shape
    turned = w_mid.transpose(0, 1, 2, 4, 3)[:, ::-1]
    near = turned[:, :, :2].reshape(three, -1, c_in)
    far = turned[:, :, 2].reshape(three, -1, c_in)
    block = jnp.concatenate([near, far, jnp.zeros((three, c_out, c_in), w_mid.dtype)], axis=1)
    none = jnp.zeros_like(block[0])
    return jnp.concatenate(
        [
            jnp.concatenate([block[1], none], axis=0),
            jnp.concatenate([block[2], block[0]], axis=0),
        ],
        axis=1,
    )


def middle_data(index, edges, d_rows, above, below, weights, columns):
    count = index.shape[0]
    padded = (BLOCK_ROWS + 2) * columns
    return pl.pallas_call(
        functools.partial(middle_data_kernel, count, columns),
        out_shape=jax.ShapeDtypeStruct((count, LANES), BF16),
        in_specs=smem(2) + vmem(4),
        out_specs=vmem(1)[0],
        scratch_shapes=[
            pltpu.VMEM((DEPTH // 2, padded, LANES), BF16),
            pltpu.VMEM((DEPTH // 2, padded, LANES), BF16),
            pltpu.VMEM((DEPTH * BLOCK_ROWS * columns + 8, LANES), F32),
            pltpu.VMEM((count, LANES), F32),
        ],
        compiler_params=params(),
        cost_estimate=work(30),
        name="middle_data",
    )(index, edges, d_rows, above, below, weights)


def middle_weight_kernel(columns, grid_ref, d_ref, out_ref, total, taps_ref, turned):
    grid_rows = BLOCK_ROWS + 2 * HALO
    half = LANES // 2
    total[...] = jnp.zeros_like(total)

    def rows(i, carry):
        for k in range(2):
            for j in range(PAIRS):
                own = d_ref[at_row(i * 2 + k, columns), j * LANES : (j + 1) * LANES].astype(F32)
                for n, (pair, left) in enumerate(column_taps(own, j)):
                    place = slice(k * columns, (k + 1) * columns)
                    taps_ref[2 * j + n, place, 0:LANES] = pair.astype(BF16)
                    taps_ref[2 * j + n, place, LANES:] = left.astype(BF16)
        for o in range(DEPTH // 2):
            depth_taps = (1, 2) if o == 0 else (0, 1, 2)
            cells = jnp.concatenate(
                [
                    grid_ref[
                        pl.ds(
                            pl.multiple_of(
                                ((2 * o + a - 1) * grid_rows + i * 2 + 1 + b) * columns, 32
                            ),
                            2 * columns,
                        ),
                        :,
                    ]
                    for a in depth_taps
                    for b in range(3)
                ],
                axis=1,
            )
            part = lax.dot_general(
                taps_ref[o], cells, (((0,), (0,)), ((), ())), preferred_element_type=F32
            )
            if o == 0:
                total[:, 3 * LANES :] += part
            else:
                total[...] += part
        return carry

    lax.fori_loop(0, BLOCK_ROWS // 2, rows, 0)
    low = low_lanes(LANES // 2)
    used = 27 * half
    out_ref[used:, :] = jnp.zeros((out_ref.shape[0] - used, LANES), F32)
    for place in range(9):
        for side in range(2):
            turned[...] = total[
                side * LANES : (side + 1) * LANES, place * LANES : (place + 1) * LANES
            ].T
            even = turned[pl.ds(0, half, stride=2), :]
            odd = turned[pl.ds(1, half, stride=2), :]
            at = (place * 3 + side * 2) * half
            out_ref[at : at + half, :] = jnp.where(low, even, pltpu.roll(odd, half, 1))
            if side == 0:
                out_ref[at + half : at + 2 * half, :] = jnp.where(
                    low, pltpu.roll(even, half, 1), odd
                )


def middle_weight(grid, d_rows, columns, total_rows):
    return pl.pallas_call(
        functools.partial(middle_weight_kernel, columns),
        out_shape=jax.ShapeDtypeStruct((total_rows, LANES), F32),
        in_specs=vmem(2),
        out_specs=vmem(1)[0],
        scratch_shapes=[
            pltpu.VMEM((2 * LANES, 9 * LANES), F32),
            pltpu.VMEM((DEPTH // 2, 2 * columns, 2 * LANES), BF16),
            pltpu.VMEM((LANES, LANES), F32),
        ],
        compiler_params=params(),
        cost_estimate=work(26),
        name="middle_weight",
    )(grid, d_rows)


def region_kernel(
    columns,
    scale_ref,
    bev_ref,
    weight_ref,
    bias_ref,
    head_ref,
    head_bias_ref,
    labels_ref,
    targets_ref,
    d_ref,
    first_ref,
    last_ref,
    grad_head_ref,
    sums_ref,
    head_sum,
    loss_sum,
):
    width = PAIRS * LANES
    outs = head_ref.shape[0]
    scale = scale_ref[0, 0]
    head = head_ref[...]
    head_three = jnp.concatenate([head, head, head], axis=0)
    grad_head_ref[...] = jnp.zeros_like(grad_head_ref)
    sums_ref[...] = jnp.zeros_like(sums_ref)
    head_sum[...] = jnp.zeros_like(head_sum)
    loss_sum[...] = jnp.zeros_like(loss_sum)
    kind = lax.broadcasted_iota(jnp.int32, (outs, columns), 0) % 8 == 0

    def row(r, carry):
        left = jnp.concatenate([bev_ref[at_row(r + b, columns), :] for b in range(3)], axis=1)
        part = jnp.dot(left, weight_ref[...], preferred_element_type=F32)
        pre = from_left(part[:, :LANES]) + part[:, LANES : 2 * LANES]
        pre = pre + from_right(part[:, 2 * LANES :]) + bias_ref[0:1, :]
        act = jnp.maximum(pre, 0.0).astype(BF16)
        heads = lax.dot_general(head, act, (((1,), (1,)), ((), ())), preferred_element_type=F32)
        heads = heads + head_bias_ref[:, 0:1]
        label = labels_ref[r]
        positive = jnp.where(label == 1, 1.0, 0.0)
        negative = jnp.where(label == 0, 1.0, 0.0)
        tail = jnp.log1p(jnp.exp(-jnp.abs(heads)))
        soft_up = jnp.maximum(heads, 0.0) + tail
        soft_down = jnp.maximum(-heads, 0.0) + tail
        probab = jax.nn.sigmoid(heads)
        rest = 1.0 - probab
        focal = positive * FOCAL_ALPHA * rest * rest * soft_down
        focal = focal + negative * (1.0 - FOCAL_ALPHA) * probab * probab * soft_up
        d_focal = positive * FOCAL_ALPHA * rest * rest * (-2.0 * probab * soft_down - rest)
        d_focal = d_focal + negative * (1.0 - FOCAL_ALPHA) * probab * probab * (
            2.0 * rest * soft_up + probab
        )
        offset = heads - targets_ref[r]
        size = jnp.abs(offset)
        near = size < 1.0 / 9.0
        smooth = jnp.where(near, 4.5 * offset * offset, size - 1.0 / 18.0)
        d_smooth = jnp.where(near, 9.0 * offset, jnp.where(offset > 0.0, 1.0, -1.0))
        loss_sum[...] += jnp.where(kind, focal, 2.0 * positive * smooth)
        d_heads = jnp.where(kind, d_focal, 2.0 * positive * d_smooth) * scale
        head_sum[...] += d_heads
        high = d_heads.astype(BF16)
        rest_one = d_heads - high.astype(F32)
        mid = rest_one.astype(BF16)
        tiny = (rest_one - mid.astype(F32)).astype(BF16)
        three = jnp.concatenate([high, mid, tiny], axis=0)
        grad_head_ref[...] += jnp.dot(three, act, preferred_element_type=F32)
        d_act = lax.dot_general(
            three, head_three, (((0,), (0,)), ((), ())), preferred_element_type=F32
        )
        d_pre = jnp.where(pre > 0.0, d_act, 0.0).astype(BF16)
        d_ref[at_row(r, columns), :] = d_pre

        @pl.when(r == 0)
        def _():
            first_ref[...] = d_pre

        @pl.when(r == d_ref.shape[0] // columns - 1)
        def _():
            last_ref[...] = d_pre

        sums_ref[0:8, :] += jnp.sum(d_pre.astype(F32).reshape(columns // 8, 8, LANES), axis=0)
        return carry

    lax.fori_loop(0, d_ref.shape[0] // columns, row, 0)
    sums_ref[8:24, :] = jnp.broadcast_to(
        jnp.sum(head_sum[...], axis=1, keepdims=True), (outs, LANES)
    )
    sums_ref[24:32, :] = jnp.broadcast_to(
        jnp.sum(jnp.sum(loss_sum[...], axis=1, keepdims=True), axis=0, keepdims=True), (8, LANES)
    )


def region_forward(scale, bev, weights, bias, head, head_bias, labels, targets, columns):
    rows = labels.shape[0]
    outs = head.shape[0]
    return pl.pallas_call(
        functools.partial(region_kernel, columns),
        out_shape=(
            jax.ShapeDtypeStruct((rows * columns, LANES), BF16),
            jax.ShapeDtypeStruct((columns, LANES), BF16),
            jax.ShapeDtypeStruct((columns, LANES), BF16),
            jax.ShapeDtypeStruct((3 * outs, LANES), F32),
            jax.ShapeDtypeStruct((32, LANES), F32),
        ),
        in_specs=smem(1) + vmem(7),
        out_specs=vmem(5),
        scratch_shapes=[pltpu.VMEM((outs, columns), F32), pltpu.VMEM((outs, columns), F32)],
        compiler_params=params(),
        cost_estimate=work(16),
        name="region_forward",
    )(
        scale.reshape(1, 1),
        bev,
        weights,
        jnp.broadcast_to(bias.reshape(1, -1), (8, LANES)),
        head,
        jnp.broadcast_to(head_bias.reshape(-1, 1), (outs, LANES)),
        labels,
        targets,
    )


def region_order(w_all):
    three, _, channels, outs = w_all.shape
    depth_out = DEPTH // 2
    turned = w_all.reshape(three, three, channels // depth_out, depth_out, outs)
    turned = turned.transpose(0, 1, 3, 2, 4).reshape(three, three, channels, outs)
    return jnp.pad(turned, ((0, 0), (0, 0), (0, PAIRS * LANES - channels), (0, 0)))


def region_data_kernel(
    columns, edge_ref, d_ref, above_ref, below_ref, bev_ref, weight_ref,
    out_ref, first_ref, last_ref, sums_ref, taps_ref,
):
    rows = out_ref.shape[0] // columns
    width = PAIRS * LANES
    sums_ref[...] = jnp.zeros_like(sums_ref)

    def build(r, own):
        taps_ref[at_row(r, columns), 0:LANES] = from_right(own).astype(BF16)
        taps_ref[at_row(r, columns), LANES : 2 * LANES] = own.astype(BF16)
        taps_ref[at_row(r, columns), 2 * LANES :] = from_left(own).astype(BF16)

    def build_own(r, carry):
        build(r + 1, d_ref[at_row(r, columns), :].astype(F32))
        return carry

    build(0, jnp.where(edge_ref[0] > 0, above_ref[...].astype(F32), 0.0))
    lax.fori_loop(0, rows, build_own, 0)
    build(rows + 1, jnp.where(edge_ref[1] > 0, below_ref[...].astype(F32), 0.0))

    def row(r, carry):
        left = jnp.concatenate([taps_ref[at_row(r + 2 - b, columns), :] for b in range(3)], axis=1)
        total = jnp.dot(left, weight_ref[...], preferred_element_type=F32)
        alive = bev_ref[at_row(r + 1, columns), :].astype(F32) > 0.0
        kept = jnp.where(alive, total, 0.0).astype(BF16)
        out_ref[at_row(r, columns), :] = kept

        @pl.when(r == 0)
        def _():
            first_ref[...] = kept

        @pl.when(r == rows - 1)
        def _():
            last_ref[...] = kept

        sums_ref[...] += jnp.sum(kept.astype(F32).reshape(columns // 8, 8, width), axis=0)
        return carry

    lax.fori_loop(0, rows, row, 0)


def region_data(edges, d_rows, above, below, bev, weights, columns):
    width = PAIRS * LANES
    return pl.pallas_call(
        functools.partial(region_data_kernel, columns),
        out_shape=(
            jax.ShapeDtypeStruct((d_rows.shape[0], width), BF16),
            jax.ShapeDtypeStruct((columns, width), BF16),
            jax.ShapeDtypeStruct((columns, width), BF16),
            jax.ShapeDtypeStruct((8, width), F32),
        ),
        in_specs=smem(1) + vmem(5),
        out_specs=vmem(4),
        scratch_shapes=[pltpu.VMEM((d_rows.shape[0] + 2 * columns, 3 * LANES), BF16)],
        compiler_params=params(),
        cost_estimate=work(13),
        name="region_data",
    )(edges, d_rows, above, below, bev, weights)


def region_weight_kernel(columns, blocks, d_ref, bev_ref, out_ref, total, taps_ref):
    rows = d_ref.shape[0] // columns
    width = PAIRS * LANES
    depth_out = DEPTH // 2
    half = LANES // 2
    total[...] = jnp.zeros_like(total)

    def two(i, carry):
        for k in range(2):
            own = d_ref[at_row(i * 2 + k, columns), :].astype(F32)
            place = slice(k * columns, (k + 1) * columns)
            taps_ref[place, 0:LANES] = from_right(own).astype(BF16)
            taps_ref[place, LANES : 2 * LANES] = own.astype(BF16)
            taps_ref[place, 2 * LANES :] = from_left(own).astype(BF16)
        cells = jnp.concatenate(
            [
                bev_ref[pl.ds(pl.multiple_of((i * 2 + b) * columns, 32), 2 * columns), :]
                for b in range(3)
            ],
            axis=1,
        )
        total[...] += lax.dot_general(
            taps_ref[...], cells, (((0,), (0,)), ((), ())), preferred_element_type=F32
        )
        return carry

    lax.fori_loop(0, rows // 2, two, 0)
    share = half // blocks
    used = 9 * depth_out * half
    out_ref[used:, :] = jnp.zeros((out_ref.shape[0] - used, LANES), F32)
    for b in range(3):
        for e in range(3):
            for j in range(PAIRS):
                start = b * width + j * LANES
                turned = total[e * LANES : (e + 1) * LANES, start : start + LANES].T
                for k in range(min(2, depth_out - 2 * j)):
                    for q in range(blocks):
                        begin = k * half + q * share
                        base = ((q * 3 + b) * 3 + e) * share * depth_out
                        out_ref[pl.ds(base + 2 * j + k, share, stride=depth_out), :] = turned[
                            begin : begin + share, :
                        ]


def region_weight(d_own, bev, columns, blocks, total_rows):
    width = PAIRS * LANES
    return pl.pallas_call(
        functools.partial(region_weight_kernel, columns, blocks),
        out_shape=jax.ShapeDtypeStruct((total_rows, LANES), F32),
        in_specs=vmem(2),
        out_specs=vmem(1)[0],
        scratch_shapes=[
            pltpu.VMEM((3 * LANES, 3 * width), F32),
            pltpu.VMEM((2 * columns, 3 * LANES), BF16),
        ],
        compiler_params=params(),
        cost_estimate=work(10),
        name="region_weight",
    )(d_own, bev)


def prepare_kernel(
    slots, anc_count, device_rows, edge_ref, points_ref, count_ref, coord_ref, labels_ref,
    stats_ref, place_ref,
):
    voxels, width = points_ref.shape
    real = points_ref.shape[1] - 1
    features = 7
    lane = lax.broadcasted_iota(jnp.int32, (CHUNK, width), 1)
    ones_lane = features * slots
    total = jnp.zeros((width, width), F32)
    for i in range(voxels // CHUNK):
        block = points_ref[i * CHUNK : (i + 1) * CHUNK, :].astype(F32)
        valid = (lane % slots < count_ref[i * CHUNK : (i + 1) * CHUNK, :]) | (lane == ones_lane)
        block = jnp.where(valid, block, 0.0).astype(BF16)
        total = total + lax.dot_general(
            block, block, (((0,), (0,)), ((), ())), preferred_element_type=F32
        )
    row_at = lax.broadcasted_iota(jnp.int32, (width, width), 0)
    col_at = lax.broadcasted_iota(jnp.int32, (width, width), 1)
    same = (row_at % slots == col_at % slots) | (row_at == ones_lane)
    total = jnp.where(same & (row_at <= ones_lane) & (col_at < ones_lane), total, 0.0)
    rows = [
        jnp.sum(jnp.where(row_at // slots == k, total, 0.0), axis=0, keepdims=True)
        for k in range(features + 1)
    ]
    stacked = jnp.concatenate(rows, axis=0)
    col_eight = lax.broadcasted_iota(jnp.int32, (8, width), 1)
    lane_eight = lax.broadcasted_iota(jnp.int32, (8, LANES), 1)
    row_eight = lax.broadcasted_iota(jnp.int32, (8, LANES), 0)
    stats = jnp.zeros((8, LANES), F32)
    for k in range(features):
        picked = jnp.sum(jnp.where(col_eight // slots == k, stacked, 0.0), axis=1, keepdims=True)
        stats = stats + jnp.where(lane_eight == k, picked, 0.0)
    counted = jnp.sum(count_ref[...].astype(F32), axis=0, keepdims=True)
    found = jnp.zeros((1, 1), F32)
    for r in range(labels_ref.shape[0]):
        hits = jnp.where(labels_ref[r] == 1, 1.0, 0.0)
        found = found + jnp.sum(jnp.sum(hits, axis=1, keepdims=True), axis=0, keepdims=True)
    row = coord_ref[1:2, :]
    exists = coord_ref[3:4, :] > 0
    lists = []
    for q in range(anc_count):
        begin = q * device_rows - HALO
        lists.append(exists & (row >= begin) & (row < begin + device_rows + 2 * HALO))
    lists.append(exists & (row < HALO) & (edge_ref[0] > 0))
    lists.append(exists & (row >= anc_count * device_rows - HALO) & (edge_ref[1] > 0))
    lists += [exists & (row < 0)] * (8 - len(lists))
    member = jnp.concatenate([jnp.where(x, 1.0, 0.0) for x in lists], axis=0)
    before = (
        lax.broadcasted_iota(jnp.int32, (LANES, LANES), 0)
        < lax.broadcasted_iota(jnp.int32, (LANES, LANES), 1)
    )
    before = jnp.where(before, 1.0, 0.0).astype(BF16)
    carry = jnp.zeros((8, 1), F32)
    for i in range(voxels // LANES):
        part = member[:, i * LANES : (i + 1) * LANES]
        ahead = jnp.dot(part.astype(BF16), before, preferred_element_type=F32) + carry
        place_ref[:, i * LANES : (i + 1) * LANES] = jnp.where(part > 0.0, ahead, -1.0).astype(
            jnp.int32
        )
        carry = carry + jnp.sum(part, axis=1, keepdims=True)
    is_edge = lax.broadcasted_iota(jnp.int32, (8, 1), 0) >= anc_count
    need = carry / jnp.where(is_edge, float(EDGE_CAP), float(CAP))
    need = jnp.max(need, axis=0, keepdims=True)
    for k, value in enumerate((counted, found, need)):
        stats = stats + jnp.where((lane_eight == 8) & (row_eight == k), value, 0.0)
    stats_ref[...] = stats


def prepare(edges, points, counts, coords, labels, anc_count, device_rows, slots):
    voxels = points.shape[0]
    return pl.pallas_call(
        functools.partial(prepare_kernel, slots, anc_count, device_rows),
        out_shape=(
            jax.ShapeDtypeStruct((8, LANES), F32),
            jax.ShapeDtypeStruct((8, voxels), jnp.int32),
        ),
        in_specs=smem(1) + vmem(4),
        out_specs=vmem(2),
        compiler_params=params(),
        cost_estimate=work(4),
        name="prepare",
    )(edges, points, counts, coords, labels)


def exact_dot(left, right):
    return jnp.dot(left, right, preferred_element_type=F32, precision=lax.Precision.HIGHEST)


def batch_norm(stats, kernel, gain, shift):
    lanes = kernel.shape[1]
    moments = stats[:, 0:8]
    count = stats[0:1, 8:9]
    mixed = jnp.zeros((8, lanes), F32)
    for k in range(7):
        mixed = mixed + moments[:, k : k + 1] * kernel[k : k + 1, :]
    mean = mixed[7:8, :] / count
    second = jnp.sum(mixed * kernel, axis=0, keepdims=True) / count
    inv_std = lax.rsqrt(second - mean * mean + BN_EPSILON)
    return mixed, mean, inv_std, count


def first_layer(points, first_ref, scale, offset, valid):
    hidden = jnp.dot(points, first_ref[...], preferred_element_type=F32)
    act = jnp.where(valid, jnp.maximum(hidden * scale + offset, 0.0), 0.0)
    return act


def group_fold(values, combine):
    groups = values.shape[1] // LANES
    out = values[:, :LANES]
    for g in range(1, groups):
        out = combine(out, values[:, g * LANES : (g + 1) * LANES])
    out = combine(out, pltpu.roll(out, 32, 1))
    return combine(out, pltpu.roll(out, 64, 1))


def second_tail(pooled):
    lane = lax.broadcasted_iota(jnp.int32, pooled.shape, 1)
    return jnp.where(lane < 32, pooled, jnp.where(lane == 32, 1.0, 0.0)).astype(BF16)


def encode_kernel(
    slots, points_ref, count_ref, stats_ref, kernel_ref, gain_ref, first_ref, second_ref,
    feat_ref, share_ref, held,
):
    lanes = first_ref.shape[1]
    _, mean, inv_std, _ = batch_norm(stats_ref[...], kernel_ref[...], None, None)
    scale = gain_ref[0:1, :] * inv_std
    offset = gain_ref[1:2, :] - mean * scale
    count = count_ref[...]
    slot = lax.broadcasted_iota(jnp.int32, (CHUNK, lanes), 1) // 32
    act = first_layer(points_ref[...], first_ref, scale, offset, slot < count)
    tail = second_tail(group_fold(act, jnp.maximum))
    low = act.astype(BF16)
    top = jnp.full((CHUNK, LANES), -jnp.inf, F32)
    for g in range(lanes // LANES):
        left = jnp.concatenate([low[:, g * LANES : (g + 1) * LANES], tail], axis=1)
        part = jnp.dot(left, second_ref[...], preferred_element_type=F32)
        for s in range(min(4, slots - 4 * g)):
            p = 4 * g + s
            one = jnp.where(p < count, part[:, s * LANES : (s + 1) * LANES], -jnp.inf)
            held[p] = one
            top = jnp.maximum(top, one)
    ties = jnp.zeros((CHUNK, LANES), F32)
    for p in range(slots):
        ties = ties + jnp.where(held[p] == top, 1.0, 0.0)
    feat_ref[...] = jnp.maximum(top, 0.0)
    share_ref[...] = jnp.where(top > 0.0, 1.0 / ties, 0.0)


def encode(points, counts, stats, kernel, gain, first, second, slots):
    voxels, width = points.shape
    lanes = first.shape[1]
    whole = lambda *shape: pl.BlockSpec(shape, lambda i: (0,) * len(shape))
    block = lambda size: pl.BlockSpec((CHUNK, size), lambda i: (i, 0))
    return pl.pallas_call(
        functools.partial(encode_kernel, slots),
        grid=(voxels // CHUNK,),
        out_shape=(
            jax.ShapeDtypeStruct((voxels, LANES), F32),
            jax.ShapeDtypeStruct((voxels, LANES), F32),
        ),
        in_specs=[
            block(width),
            block(1),
            whole(8, LANES),
            whole(8, lanes),
            whole(8, lanes),
            whole(width, lanes),
            whole(2 * LANES, 4 * LANES),
        ],
        out_specs=[block(LANES), block(LANES)],
        scratch_shapes=[pltpu.VMEM((slots, CHUNK, LANES), F32)],
        compiler_params=params("arbitrary"),
        cost_estimate=work(19),
        name="encode",
    )(points, counts, stats, kernel, gain, first, second)


def decode_kernel(
    slots, points_ref, count_ref, stats_ref, kernel_ref, gain_ref, first_ref, second_ref,
    feat_ref, share_ref, d_feat_ref, first_out_ref, second_out_ref,
    first_sum, second_sum, joined,
):
    lanes = first_ref.shape[1]
    width = points_ref.shape[1]
    step = pl.program_id(0)

    @pl.when(step == 0)
    def _():
        first_sum[...] = jnp.zeros_like(first_sum)
        second_sum[...] = jnp.zeros_like(second_sum)

    _, mean, inv_std, _ = batch_norm(stats_ref[...], kernel_ref[...], None, None)
    scale = gain_ref[0:1, :] * inv_std
    offset = gain_ref[1:2, :] - mean * scale
    count = count_ref[...]
    points = points_ref[...]
    slot = lax.broadcasted_iota(jnp.int32, (CHUNK, lanes), 1) // 32
    act = first_layer(points, first_ref, scale, offset, slot < count)
    pooled = group_fold(act, jnp.maximum)
    tail = second_tail(pooled)
    low = act.astype(BF16)
    top = feat_ref[...]
    d_feat = d_feat_ref[...] * share_ref[...]
    d_tail = jnp.zeros((CHUNK, LANES), F32)
    for g in range(lanes // LANES):
        left = jnp.concatenate([low[:, g * LANES : (g + 1) * LANES], tail], axis=1)
        part = jnp.dot(left, second_ref[...], preferred_element_type=F32)
        pieces = []
        for s in range(4):
            p = 4 * g + s
            if p < slots:
                hit = (part[:, s * LANES : (s + 1) * LANES] == top) & (p < count)
                pieces.append(jnp.where(hit, d_feat, 0.0).astype(BF16))
            else:
                pieces.append(jnp.zeros((CHUNK, LANES), BF16))
        d_part = jnp.concatenate(pieces, axis=1)
        second_sum[...] += lax.dot_general(
            left, d_part, (((0,), (0,)), ((), ())), preferred_element_type=F32
        )
        d_left = lax.dot_general(
            d_part, second_ref[...], (((1,), (1,)), ((), ())), preferred_element_type=F32
        )
        joined[:, g * LANES : (g + 1) * LANES] = d_left[:, :LANES]
        d_tail = d_tail + d_left[:, LANES:]
    ties = group_fold(
        jnp.where(act == jnp.concatenate([pooled] * (lanes // LANES), axis=1), 1.0, 0.0), jnp.add
    )
    lane = lax.broadcasted_iota(jnp.int32, (CHUNK, LANES), 1)
    spread = jnp.where(lane < 32, d_tail, 0.0)
    spread = spread + pltpu.roll(spread, 32, 1)
    spread = (spread + pltpu.roll(spread, 64, 1)) / ties
    spread = jnp.concatenate([spread] * (lanes // LANES), axis=1)
    wide = jnp.concatenate([pooled] * (lanes // LANES), axis=1)
    d_act = joined[...] + jnp.where(act == wide, spread, 0.0)
    d_act = jnp.where(act > 0.0, d_act, 0.0)
    high = d_act.astype(BF16)
    rest = (d_act - high.astype(F32)).astype(BF16)
    for piece in (high, rest):
        first_sum[...] += lax.dot_general(
            points, piece, (((0,), (0,)), ((), ())), preferred_element_type=F32
        )

    @pl.when(step == pl.num_programs(0) - 1)
    def _():
        row_at = lax.broadcasted_iota(jnp.int32, (width, lanes), 0)
        col_at = lax.broadcasted_iota(jnp.int32, (width, lanes), 1)
        same = (row_at % slots == col_at // 32) | (row_at == 7 * slots)
        total = jnp.where(same & (col_at // 32 < slots), first_sum[...], 0.0)
        rows = [
            jnp.sum(jnp.where(row_at // slots == k, total, 0.0), axis=0, keepdims=True)
            for k in range(8)
        ]
        first_out_ref[...] = group_fold(jnp.concatenate(rows, axis=0), jnp.add)
        for s in range(4):
            cols = slice(s * LANES, (s + 1) * LANES)
            upper = second_sum[s * 32 : (s + 1) * 32, cols]
            lower = second_sum[LANES : LANES + 40, cols]
            if s == 0:
                second_out_ref[0:32, :] = upper
                second_out_ref[32:72, :] = lower
            else:
                second_out_ref[0:32, :] += upper
                second_out_ref[32:72, :] += lower


def decode(points, counts, stats, kernel, gain, first, second, feat, share, d_feat, slots):
    voxels, width = points.shape
    lanes = first.shape[1]
    whole = lambda *shape: pl.BlockSpec(shape, lambda i: (0,) * len(shape))
    block = lambda size: pl.BlockSpec((CHUNK, size), lambda i: (i, 0))
    return pl.pallas_call(
        functools.partial(decode_kernel, slots),
        grid=(voxels // CHUNK,),
        out_shape=(
            jax.ShapeDtypeStruct((8, LANES), F32),
            jax.ShapeDtypeStruct((72, LANES), F32),
        ),
        in_specs=[
            block(width),
            block(1),
            whole(8, LANES),
            whole(8, lanes),
            whole(8, lanes),
            whole(width, lanes),
            whole(2 * LANES, 4 * LANES),
            block(LANES),
            block(LANES),
            block(LANES),
        ],
        out_specs=[whole(8, LANES), whole(72, LANES)],
        scratch_shapes=[
            pltpu.VMEM((width, lanes), F32),
            pltpu.VMEM((2 * LANES, 4 * LANES), F32),
            pltpu.VMEM((CHUNK, lanes), F32),
        ],
        compiler_params=params("arbitrary"),
        cost_estimate=work(35),
        name="decode",
    )(points, counts, stats, kernel, gain, first, second, feat, share, d_feat)


def encoder_weights(w_one, w_two, bias_two, gain, shift, slots):
    features, c_one = w_one.shape
    groups = -(-slots // 4)
    lanes = groups * LANES
    width = -(-(features * slots + 1) // LANES) * LANES
    row_at = lax.broadcasted_iota(jnp.int32, (width, lanes), 0)
    col_at = lax.broadcasted_iota(jnp.int32, (width, lanes), 1)
    tall = jnp.pad(
        jnp.repeat(w_one, slots, axis=0), ((0, width - features * slots), (0, 0))
    )
    same = (row_at % slots == col_at // c_one) & (row_at < features * slots)
    first = jnp.where(same, jnp.tile(tall, (1, lanes // c_one)), jnp.zeros((), BF16))
    c_two = w_two.shape[1]
    row_two = lax.broadcasted_iota(jnp.int32, (LANES, 4 * c_two), 0)
    col_two = lax.broadcasted_iota(jnp.int32, (LANES, 4 * c_two), 1)
    upper = jnp.where(
        row_two // c_one == col_two // c_two, jnp.tile(w_two[:c_one], (4, 4)), jnp.zeros((), BF16)
    )
    lower = jnp.concatenate([w_two[c_one:], bias_two.reshape(1, -1)], axis=0)
    lower = jnp.pad(lower, ((0, LANES - lower.shape[0]), (0, 0)))
    second = jnp.concatenate([upper, jnp.tile(lower, (1, 4))], axis=0)
    kernel = jnp.pad(w_one.astype(F32), ((0, 1), (0, 0)))
    kernel = jnp.tile(kernel, (1, lanes // c_one))
    rows = jnp.pad(jnp.stack([gain, shift]).astype(F32), ((0, 6), (0, 0)))
    return first, second, kernel, jnp.tile(rows, (1, lanes // c_one))


def gather_lists_kernel(anc_count, offset_ref, feat_ref, digit_ref, place_ref, main_ref, up_ref, down_ref):
    source = jnp.concatenate([feat_ref[...].astype(BF16), digit_ref[...]], axis=1)
    voxels = source.shape[0]

    def pick(line, capacity, offset):
        want = place_ref[line : line + 1, :] - offset
        row_at = lax.broadcasted_iota(jnp.int32, (capacity, voxels), 0)
        chosen = jnp.where(want == row_at, 1.0, 0.0).astype(BF16)
        found = jnp.dot(chosen, source, preferred_element_type=F32)
        return found[:, :LANES].astype(BF16), found[:, LANES:].T

    for q in range(anc_count):
        rows, digits = pick(q, CAP, offset_ref[0])
        main_ref[q, 0:CAP, :] = rows
        lines = [
            digits[k : k + 1, i * LANES : (i + 1) * LANES]
            for k in range(3)
            for i in range(CAP // LANES)
        ]
        lines.append(jnp.zeros((32 - len(lines), LANES), F32))
        main_ref[q, CAP : CAP + 32, :] = jnp.concatenate(lines, axis=0).astype(BF16)
        main_ref[q, CAP + 32 :, :] = jnp.zeros((EDGE_CAP + 16, LANES), BF16)
    for side, edge_ref in enumerate((up_ref, down_ref)):
        rows, digits = pick(anc_count + side, EDGE_CAP, offset_ref[1])
        edge_ref[0:EDGE_CAP, :] = rows
        digits = jnp.concatenate([digits[0:8, :], jnp.zeros((8, LANES), F32)], axis=0)
        edge_ref[EDGE_CAP : EDGE_CAP + 16, :] = digits.astype(BF16)


def gather_lists(offsets, feat, digits, place, anc_count):
    return pl.pallas_call(
        functools.partial(gather_lists_kernel, anc_count),
        out_shape=(
            jax.ShapeDtypeStruct((anc_count, CAP + EDGE_CAP + 48, LANES), BF16),
            jax.ShapeDtypeStruct((EDGE_CAP + 16, LANES), BF16),
            jax.ShapeDtypeStruct((EDGE_CAP + 16, LANES), BF16),
        ),
        in_specs=smem(1) + vmem(3),
        out_specs=vmem(3),
        compiler_params=params(),
        cost_estimate=work(5),
        name="gather_lists",
    )(offsets, feat, digits, place)


def spread_lists_kernel(received_ref, where_ref, out_ref):
    total = received_ref.shape[0]
    lane = lax.broadcasted_iota(jnp.int32, (CHUNK, total), 1)
    chosen = jnp.where(where_ref[...] == lane, 1.0, 0.0).astype(BF16)
    out_ref[...] = jnp.dot(chosen, received_ref[...], preferred_element_type=F32)


def spread_lists(received, where):
    voxels = where.shape[0]
    total = received.shape[0]
    return pl.pallas_call(
        spread_lists_kernel,
        grid=(voxels // CHUNK,),
        out_shape=jax.ShapeDtypeStruct((voxels, LANES), F32),
        in_specs=[
            pl.BlockSpec((total, LANES), lambda i: (0, 0)),
            pl.BlockSpec((CHUNK, 1), lambda i: (i, 0)),
        ],
        out_specs=pl.BlockSpec((CHUNK, LANES), lambda i: (i, 0)),
        compiler_params=params("arbitrary"),
        cost_estimate=work(6),
        name="spread_lists",
    )(received, where)


def finish_kernel(stats_ref, kernel_ref, gain_ref, sums_ref, out_ref):
    kernel = kernel_ref[:, :LANES]
    mixed, mean, inv_std, count = batch_norm(stats_ref[...], kernel, None, None)
    sums = sums_ref[...]
    total_shift = sums[7:8, :]
    total_gain = inv_std * (jnp.sum(kernel * sums, axis=0, keepdims=True) - mean * total_shift)
    slope = gain_ref[0:1, :LANES] * inv_std
    for k in range(7):
        first = stats_ref[7:8, k : k + 1]
        pull = total_shift * first + total_gain * inv_std * (mixed[k : k + 1, :] - mean * first)
        out_ref[k : k + 1, :] = slope * (sums[k : k + 1, :] - pull / count)
    out_ref[7:8, :] = total_gain
    out_ref[8:16, :] = jnp.broadcast_to(total_shift, (8, LANES))


def finish_encoder(stats, kernel, gain, sums):
    return pl.pallas_call(
        finish_kernel,
        out_shape=jax.ShapeDtypeStruct((16, LANES), F32),
        in_specs=vmem(4),
        out_specs=vmem(1)[0],
        compiler_params=params(),
        cost_estimate=work(1),
        name="finish_encoder",
    )(stats, kernel, gain, sums)


def everyone(values, axes):
    count = 1
    for axis in axes:
        count *= lax.axis_size(axis)
    copies = jnp.broadcast_to(values[None], (count,) + values.shape)
    return lax.all_to_all(copies, axes, 0, 0)


def neighbour_rows(first, last):
    axes = ("tile", "anc")
    count = lax.axis_size("tile") * lax.axis_size("anc")
    down = [(i, i + 1) for i in range(count - 1)]
    return lax.ppermute(last, axes, down), lax.ppermute(first, axes, [(j, i) for i, j in down])


def sum_chunk(rows, axes):
    devices = 1
    for axis in axes:
        devices *= lax.axis_size(axis)
    parts = rows.reshape(devices, -1, rows.shape[1])
    return jnp.sum(lax.all_to_all(parts, axes, 0, 0), axis=0)


def shard_windows(segments, shard, count):
    windows = []
    for a in range(count):
        begin, end = a * shard, (a + 1) * shard
        at = 0
        pieces = []
        for name, size in segments:
            low, high = max(begin, at), min(end, at + size)
            if low < high:
                pieces.append((name, low - at, high - at))
            at += size
        windows.append(pieces)
    return windows


def on_device(
    points,
    npoints,
    coords,
    labels,
    targets,
    w_vfe1,
    w_vfe2,
    w_mid,
    w_rpn,
    w_head,
    bn_gain,
    biases,
    master,
    moment1,
    moment2,
):
    both = ("tile", "anc")
    anc_count = lax.axis_size("anc")
    tile_count = lax.axis_size("tile")
    anc = lax.axis_index("anc")
    tile = lax.axis_index("tile")
    device_rows = labels.shape[1]
    columns = labels.shape[2]
    blocks = device_rows // BLOCK_ROWS
    tile_rows = device_rows * anc_count
    all_rows = tile_rows * tile_count
    slots = points.shape[1]
    voxels = points.shape[2]
    c_vfe = w_vfe1.shape[1]
    c_vox = w_vfe2.shape[1]
    c_mid = w_mid.shape[4]
    c_rpn = w_rpn.shape[3]
    outs = w_head.shape[1]
    shift = biases[:c_vfe]
    bias_two = biases[c_vfe : c_vfe + c_vox]
    bias_mid, bias_rpn, bias_head = jnp.split(
        biases[c_vfe + c_vox :].astype(F32), [c_mid, c_mid + c_rpn]
    )

    def joined(row):
        return (row % CROP_ROWS != CROP_ROWS // 2) & (row > 0) & (row < all_rows)

    padded = -(-voxels // CHUNK) * CHUNK
    width = -(-(points.shape[0] * slots + 1) // LANES) * LANES
    flat_points = points.reshape(-1, voxels).T
    flat_points = jnp.pad(
        flat_points, ((0, padded - voxels), (0, width - flat_points.shape[1]))
    )
    lane = lax.broadcasted_iota(jnp.int32, flat_points.shape, 1)
    flat_points = jnp.where(lane == points.shape[0] * slots, jnp.ones((), BF16), flat_points)
    counts = jnp.pad(npoints, (0, padded - voxels)).reshape(padded, 1)
    layer = jnp.pad(coords[:, 0], (0, padded - voxels))
    row = jnp.pad(coords[:, 1] - tile * tile_rows, (0, padded - voxels))
    column = jnp.pad(coords[:, 2], (0, padded - voxels))
    exists = (jnp.arange(padded) < voxels).astype(jnp.int32)
    lines = jnp.pad(jnp.stack([layer, row, column, exists]), ((0, 4), (0, 0)))
    tile_edges = jnp.stack([joined(tile * tile_rows), joined((tile + 1) * tile_rows)])
    stats, place = prepare(
        tile_edges.astype(jnp.int32),
        flat_points,
        counts,
        lines,
        labels.transpose(1, 0, 2),
        anc_count,
        device_rows,
        slots,
    )
    sent, w_mid, w_rpn = lax.optimization_barrier((stats, w_mid, w_rpn))
    gathered = everyone(sent, both)
    weights = middle_weights(w_mid)
    data_weights = middle_data_weights(w_mid)
    region = everyone(w_rpn, ("anc",)).transpose(1, 2, 0, 3, 4)
    region = region_order(region.reshape(w_rpn.shape[:2] + (-1, c_rpn)))
    stats = jnp.sum(gathered, axis=0)
    count_pos = stats[1, 8]
    rounds = jnp.ceil(jnp.max(gathered[:, 2, 8])).astype(jnp.int32)

    first, second, kernel, gain_rows = encoder_weights(
        w_vfe1, w_vfe2, bias_two, bn_gain, shift, slots
    )
    feat, share = encode(flat_points, counts, stats, kernel, gain_rows, first, second, slots)

    digits = jnp.stack(
        [(layer + 1) * exists, column // 2 * exists, (row * 2 + column % 2) * exists], axis=1
    )
    digits = jnp.pad(digits, ((0, 0), (0, LANES - 3))).astype(BF16)
    slot_own = sum(
        jnp.where(row // device_rows == q, place[q], 0) for q in range(anc_count)
    )
    owner = jnp.clip(row // device_rows, 0, anc_count - 1)
    in_tile = lax.axis_size("tile")
    upward = [(i + 1, i) for i in range(in_tile - 1)]
    downward = [(i, i + 1) for i in range(in_tile - 1)]

    def exchange(number):
        offsets = jnp.stack([number * CAP, number * EDGE_CAP]).astype(jnp.int32)
        main, up, down = gather_lists(offsets, feat, digits, place, anc_count)
        from_below = lax.ppermute(up, "tile", upward)
        from_above = lax.ppermute(down, "tile", downward)
        main = lax.dynamic_update_slice(main, from_above[None], (0, CAP + 32, 0))
        main = lax.dynamic_update_slice(main, from_below[None], (anc_count - 1, CAP + 32, 0))
        got = lax.all_to_all(main, "anc", 0, 0)
        words = got[:, CAP : CAP + 32].reshape(anc_count, -1).astype(jnp.int32)
        start = CAP + 32 + EDGE_CAP
        edge_words = got[:, start : start + 16].astype(jnp.int32)

        def word(k):
            gap = jnp.zeros((anc_count, 32), jnp.int32)
            parts = [words[:, k * CAP : (k + 1) * CAP], gap, edge_words[:, k], gap[:, :16]]
            return jnp.concatenate(parts, axis=1)

        high, half, mixed = word(0), word(1), word(2)
        local = mixed // 2 - anc * device_rows
        is_edge = lax.broadcasted_iota(jnp.int32, local.shape, 1) >= CAP
        local = local + jnp.where(is_edge, jnp.where(anc == 0, -tile_rows, tile_rows), 0)
        cross = half * 2 + mixed % 2
        scatter_at, own_at = [], []
        for k in range(blocks):
            line = local - k * BLOCK_ROWS
            tall = BLOCK_ROWS + 2 * HALO
            inside = (high > 0) & (line >= -HALO) & (line < BLOCK_ROWS + HALO)
            spot = ((high - 1) * tall + line + HALO) * columns + cross
            scatter_at.append(jnp.where(inside, spot, DEPTH * tall * columns).reshape(-1))
            inside = (high > 0) & (line >= 0) & (line < BLOCK_ROWS)
            spot = ((high - 1) * BLOCK_ROWS + line) * columns + cross
            spot = jnp.where(inside, spot, DEPTH * BLOCK_ROWS * columns)
            own_at.append(spot[:, :CAP].reshape(-1))
        return got.reshape(-1, LANES), scatter_at, own_at

    feats, scatter_at, own_at = exchange(0)
    grids = [scatter_rows(index, feats, None, columns) for index in scatter_at]

    def more(state):
        return state[0] < rounds

    def another(state):
        number, held = state
        rows, index, _ = exchange(number)
        held = [scatter_rows(at, rows, old, columns) for at, old in zip(index, held)]
        return number + 1, held

    _, grids = lax.while_loop(more, another, (jnp.int32(1), grids))

    first_row = tile * tile_rows + anc * device_rows
    bevs, edges = [], []
    for k in range(blocks):
        top = first_row + k * BLOCK_ROWS
        edges.append(jnp.stack([joined(top), joined(top + BLOCK_ROWS)]).astype(jnp.int32))
        bevs.append(middle_forward(edges[k], grids[k], weights, bias_mid, columns))

    lanes = region.shape[2]
    region_in = region.transpose(0, 2, 1, 3).reshape(3 * lanes, 3 * c_rpn)
    region_back = region.transpose(0, 1, 3, 2).reshape(9 * c_rpn, lanes)
    wide_labels = jnp.repeat(labels.transpose(1, 0, 2), outs // 2, axis=1)
    wide_targets = jnp.pad(targets.transpose(2, 0, 1, 3), ((0, 0), (0, 0), (1, 0), (0, 0)))
    wide_targets = wide_targets.reshape(device_rows, outs, columns)
    scale = 1.0 / count_pos
    d_rows, head_sums, row_sums = [], 0.0, 0.0
    d_first, d_last = [], []
    for k in range(blocks):
        here = slice(k * BLOCK_ROWS, (k + 1) * BLOCK_ROWS)
        d_block, top_row, end_row, heads, sums = region_forward(
            scale,
            bevs[k],
            region_in,
            bias_rpn,
            w_head.T,
            bias_head,
            wide_labels[here],
            wide_targets[here],
            columns,
        )
        d_rows.append(d_block)
        d_first.append(top_row)
        d_last.append(end_row)
        head_sums = head_sums + heads
        row_sums = row_sums + sums

    def beside(firsts, lasts):
        above, below = neighbour_rows(firsts[0], lasts[-1])
        return [above] + lasts[:-1], firsts[1:] + [below]

    devices = anc_count * tile_count
    unit = devices * 8
    above, below = beside(d_first, d_last)
    region_rows = -(-(9 * w_rpn.shape[2] * anc_count) // unit) * unit
    grad_region = sum(
        region_weight(d_rows[k], bevs[k], columns, anc_count, region_rows) for k in range(blocks)
    )
    d_rows, grad_region = lax.optimization_barrier((d_rows, grad_region))
    region_chunk = sum_chunk(grad_region, both)
    d_mids, mid_sums = [], 0.0
    mid_first, mid_last = [], []
    for k in range(blocks):
        d_block, top_row, end_row, sums = region_data(
            edges[k], d_rows[k], above[k], below[k], bevs[k], region_back, columns
        )
        d_mids.append(d_block)
        mid_first.append(top_row)
        mid_last.append(end_row)
        mid_sums = mid_sums + sums
    above, below = beside(mid_first, mid_last)
    middle_size = w_mid.size
    tail_size = c_rpn * outs + bn_gain.shape[0] + biases.shape[0]
    used = middle_size // LANES
    middle_rows = -(-max(used - (-tail_size // LANES), LARGE_ROWS) // unit) * unit
    grad_mid = sum(
        middle_weight(grids[k], d_mids[k], columns, middle_rows) for k in range(blocks)
    )

    head_three = head_sums.reshape(3, outs, c_rpn)
    grad_head = (head_three[0] + head_three[1] + head_three[2]).T
    grad_bias_mid = jnp.sum(mid_sums, axis=0)[: c_mid * DEPTH // 2].reshape(-1, c_mid).sum(axis=0)
    grad_bias_rpn = jnp.sum(row_sums[:8], axis=0)
    tail = jnp.concatenate(
        [
            grad_head.reshape(-1),
            jnp.zeros((c_vfe + c_vfe + c_vox,), F32),
            grad_bias_mid,
            grad_bias_rpn,
            row_sums[8 : 8 + outs, 0],
        ]
    )
    tail_rows = jnp.pad(tail, (0, -tail.shape[0] % LANES)).reshape(-1, LANES)
    grad_mid = lax.dynamic_update_slice(grad_mid, tail_rows, (used, 0))
    own_at, grad_mid, region_chunk = lax.optimization_barrier((own_at, grad_mid, region_chunk))
    middle_chunk = sum_chunk(grad_mid, both)
    region_full = lax.all_gather(region_chunk, both, axis=0, tiled=True)

    def collect(number, own_index, chunk):
        lists = sum(
            middle_data(
                own_index[k], edges[k], d_mids[k], above[k], below[k], data_weights, columns
            )
            for k in range(blocks)
        )
        lists, chunk = lax.optimization_barrier((lists, chunk))
        back = lax.all_to_all(lists.reshape(anc_count, CAP, LANES), "anc", 0, 0)
        mine = slot_own - number * CAP
        known = (exists > 0) & (mine >= 0) & (mine < CAP)
        where = jnp.where(known, owner * CAP + mine, -1).reshape(padded, 1)
        return spread_lists(back.reshape(-1, LANES), where), chunk

    d_feat, middle_chunk = collect(0, own_at, middle_chunk)
    middle_full = lax.all_gather(middle_chunk, both, axis=0, tiled=True)

    def collect_more(state):
        number, held = state
        _, _, index = exchange(number)
        return number + 1, held + collect(number, index, ())[0]

    _, d_feat = lax.while_loop(more, collect_more, (jnp.int32(1), d_feat))
    d_feat, region_full = lax.optimization_barrier((d_feat, region_full))
    first_sums, second_sums = decode(
        flat_points, counts, stats, kernel, gain_rows, first, second, feat, share, d_feat, slots
    )

    late = jnp.concatenate([first_sums, second_sums, row_sums[24:32]], axis=0)
    rows = late.shape[0]
    late = late.reshape(devices, -1)
    late = jnp.sum(lax.all_to_all(late[:, None], both, 0, 0), axis=0)
    late = everyone(late, both).reshape(rows, LANES)
    encoder = finish_encoder(stats, kernel, gain_rows, late[:8])
    second_total = late[8 : 8 + second_sums.shape[0]]
    loss = late[rows - 1, 0] / count_pos
    encoder_flat = jnp.concatenate(
        [encoder[:7, :c_vfe].reshape(-1), second_total[: 2 * c_vfe].reshape(-1)]
    )
    tail_late = jnp.concatenate(
        [
            jnp.zeros((c_rpn * outs,), F32),
            encoder[7, :c_vfe],
            encoder[8, :c_vfe],
            second_total[2 * c_vfe],
            jnp.zeros((c_mid + c_rpn + outs,), F32),
        ]
    )
    shard = master.shape[0]
    segments = (
        ("region", w_rpn.size * anc_count),
        ("encoder", encoder_flat.shape[0]),
        ("middle", middle_size),
        ("tail", tail_size),
    )
    region_flat = region_full.reshape(-1)
    middle_flat = middle_full.reshape(-1)

    def assemble(pieces):
        parts = []
        for name, low, high in pieces:
            if name == "encoder":
                parts.append(encoder_flat[low:high])
            elif name == "region":
                parts.append(region_flat[low:high])
            elif name == "middle":
                parts.append(middle_flat[low:high])
            else:
                early = middle_flat[middle_size + low : middle_size + high]
                parts.append(early + tail_late[low:high])
        return jnp.concatenate(parts) if len(parts) > 1 else parts[0]

    reduced = None
    for a, pieces in enumerate(shard_windows(segments, shard, anc_count)):
        one = assemble(pieces)
        reduced = one if a == 0 else jnp.where(anc == a, one, reduced)
    square_sum = jnp.sum(region_full * region_full) + jnp.sum(middle_full * middle_full)
    square_sum = square_sum + jnp.sum(encoder_flat * encoder_flat) + jnp.sum(tail_late * tail_late)
    norm_value = jnp.sqrt(square_sum)
    clipped = reduced * jnp.minimum(1.0, CLIP_LIMIT / (norm_value + 1e-06))
    first_new = BETA_FIRST * moment1 + (1.0 - BETA_FIRST) * clipped
    second_new = BETA_SECOND * moment2 + (1.0 - BETA_SECOND) * clipped * clipped
    first_hat = first_new / (1.0 - BETA_FIRST**STEP_NUMBER)
    second_hat = second_new / (1.0 - BETA_SECOND**STEP_NUMBER)
    updated = master - LEARN_RATE * (
        first_hat / (jnp.sqrt(second_hat) + ADAM_EPSILON) + WEIGHT_DECAY * master
    )
    return (updated, first_new, second_new, loss, norm_value)


def solution(mesh):
    placed = (
        P(None, None, ("tile", "anc")),
        P(("tile", "anc")),
        P(("tile", "anc"), None),
        P(None, ("tile", "anc"), None),
        P(None, None, ("tile", "anc"), None),
        P(),
        P(),
        P(),
        P(None, None, "anc", None),
        P(),
        P(),
        P(),
        P("anc"),
        P("anc"),
        P("anc"),
    )
    return jax.shard_map(
        on_device,
        mesh=mesh,
        in_specs=placed,
        out_specs=(P("anc"), P("anc"), P("anc"), P(), P()),
        check_vma=False,
    )
```

```python
import functools
import jax
import jax.numpy as jnp
from jax import lax
from jax.experimental import pallas as pl
from jax.experimental.pallas import tpu as pltpu
from jax.sharding import PartitionSpec as P

DEPTH = 10
PAIRS = DEPTH // 4 + 1
CROP_ROWS = 192
BLOCK_ROWS = 12
HALO = 2
LANES = 128
CHUNK = 384
CAP = 768
EDGE_CAP = 128
EMPTY = -1e30
FOCAL_ALPHA = 0.25
BN_EPSILON = 0.001
CLIP_LIMIT = 0.05
LEARN_RATE = 0.03
BETA_FIRST = 0.9
BETA_SECOND = 0.999
WEIGHT_DECAY = 0.01
ADAM_EPSILON = 1e-08
STEP_NUMBER = 10
F32 = jnp.float32
BF16 = jnp.bfloat16
VMEM_LIMIT = 60 * 1024 * 1024


def vmem(count):
    return [pl.BlockSpec(memory_space=pltpu.VMEM)] * count


def smem(count):
    return [pl.BlockSpec(memory_space=pltpu.SMEM)] * count


def params(*semantics):
    return pltpu.CompilerParams(vmem_limit_bytes=VMEM_LIMIT, dimension_semantics=semantics or None)


def work(micros):
    return pl.CostEstimate(flops=micros, transcendentals=0, bytes_accessed=micros * 3_000_000)


def at_row(index, columns):
    return pl.ds(pl.multiple_of(index * columns, 32), columns)


def column_edges(columns, lanes):
    place = lax.broadcasted_iota(jnp.int32, (columns, lanes), 0)
    return place == 0, place == columns - 1


def from_left(values):
    columns, lanes = values.shape
    first, _ = column_edges(columns, lanes)
    return jnp.where(first, 0.0, pltpu.roll(values, 1, 0))


def from_right(values):
    columns, lanes = values.shape
    _, last = column_edges(columns, lanes)
    return jnp.where(last, 0.0, pltpu.roll(values, columns - 1, 0))


def low_lanes(columns):
    return lax.broadcasted_iota(jnp.int32, (columns, LANES), 1) < LANES // 2


def scatter_kernel(count, cells, fresh, *refs):
    if fresh:
        index_ref, feat_ref, out_ref, wide, rows = refs
    else:
        index_ref, feat_ref, old_ref, out_ref, wide, rows = refs
    step = 512

    def begin(i, carry):
        block = pl.ds(pl.multiple_of(i * step, step), step)
        if fresh:
            wide[block, :] = jnp.zeros((step, LANES), F32)
        else:
            wide[block, :] = old_ref[block, :].astype(F32)
        return carry

    lax.fori_loop(0, cells // step, begin, 0)
    rows[...] = feat_ref[...].astype(F32)

    def place(i, carry):
        for j in range(8):
            wide[pl.ds(index_ref[i * 8 + j], 1), :] = rows[pl.ds(i * 8 + j, 1), :]
        return carry

    lax.fori_loop(0, count // 8, place, 0)

    def finish(i, carry):
        block = pl.ds(pl.multiple_of(i * step, step), step)
        out_ref[block, :] = wide[block, :].astype(BF16)
        return carry

    lax.fori_loop(0, cells // step, finish, 0)


def scatter_rows(index, feats, old, columns):
    cells = DEPTH * (BLOCK_ROWS + 2 * HALO) * columns
    count = index.shape[0]
    fresh = old is None
    return pl.pallas_call(
        functools.partial(scatter_kernel, count, cells, fresh),
        out_shape=jax.ShapeDtypeStruct((cells, LANES), BF16),
        in_specs=smem(1) + vmem(1 if fresh else 2),
        out_specs=vmem(1)[0],
        scratch_shapes=[pltpu.VMEM((cells + 8, LANES), F32), pltpu.VMEM((count, LANES), F32)],
        compiler_params=params(),
        cost_estimate=work(15),
        name="grid_scatter",
    )(*((index, feats) if fresh else (index, feats, old)))


def middle_kernel(columns, edge_ref, grid_ref, kernel_ref, bias_ref, out_ref, weight_ref):
    low = low_lanes(columns)
    none = jnp.zeros((LANES, LANES // 2), BF16)
    for place in range(9):
        one, two, three = (kernel_ref[place * 3 + e] for e in range(3))
        rows = slice(place * LANES, (place + 1) * LANES)
        weight_ref[0, rows, :] = jnp.concatenate([one, two, three, none], axis=1)
        weight_ref[1, rows, :] = jnp.concatenate([two, one, none, three], axis=1)
    grid_rows = BLOCK_ROWS + 2 * HALO
    depth_out = DEPTH // 2

    def row(m, carry):
        sums = []
        for o in range(depth_out):
            taps = (1, 2) if o == 0 else (0, 1, 2)
            left = jnp.concatenate(
                [
                    grid_ref[at_row((2 * o + a - 1) * grid_rows + m + b, columns), :]
                    for a in taps
                    for b in range(3)
                ],
                axis=1,
            )
            right = weight_ref[o % 2, 3 * LANES * (3 - len(taps)) :, :]
            sums.append(jnp.dot(left, right, preferred_element_type=F32))
        inside = (m > 0) & (m < BLOCK_ROWS + 1) | (m == 0) & (edge_ref[0] > 0)
        inside = inside | (m == BLOCK_ROWS + 1) & (edge_ref[1] > 0)
        keep = jnp.where(inside, 1.0, 0.0)
        for j in range(PAIRS):
            even = sums[2 * j]
            if 2 * j + 1 < depth_out:
                odd = sums[2 * j + 1]
                first = jnp.where(low, even[:, :LANES], odd[:, :LANES])
                middle = jnp.where(low, odd[:, :LANES], even[:, :LANES])
                last = even[:, LANES:] + odd[:, LANES:]
            else:
                first = even[:, :LANES]
                middle = first
                last = even[:, LANES:]
            total = from_left(first) + pltpu.roll(middle, LANES // 2, 1) + from_right(last)
            total = jnp.maximum(total + bias_ref[0:1, :], 0.0) * keep
            if 2 * j + 1 == depth_out:
                total = jnp.where(low, total, 0.0)
            out_ref[at_row(m, columns), j * LANES : (j + 1) * LANES] = total.astype(BF16)
        return carry

    lax.fori_loop(0, BLOCK_ROWS + 2, row, 0)


def middle_forward(edges, grid, w_mid, bias, columns):
    return pl.pallas_call(
        functools.partial(middle_kernel, columns),
        out_shape=jax.ShapeDtypeStruct(((BLOCK_ROWS + 2) * columns, PAIRS * LANES), BF16),
        in_specs=smem(1) + vmem(3),
        out_specs=vmem(1)[0],
        scratch_shapes=[pltpu.VMEM((2, 9 * LANES, 2 * LANES), BF16)],
        compiler_params=params(),
        cost_estimate=work(26),
        name="middle_forward",
    )(edges, grid, w_mid, jnp.tile(bias.reshape(1, -1), (8, 2)))


def column_taps(own, j):
    low = low_lanes(own.shape[0])
    other = pltpu.roll(own, LANES // 2, 1)
    both = [jnp.where(low, own, other)]
    if 2 * j + 1 < DEPTH // 2:
        both.append(jnp.where(low, other, own))
    return [(jnp.where(low, from_right(x), x), from_left(x)) for x in both]


def middle_data_kernel(
    count, columns, index_ref, edge_ref, d_ref, above_ref, below_ref, kernel_ref, out_ref,
    near, far, wide, rows, weight_ref,
):
    padded = BLOCK_ROWS + 2
    half = LANES // 2
    cells = DEPTH * BLOCK_ROWS * columns
    span = 10 * half
    for a, first, side in ((1, 0, 0), (2, 0, 1), (0, span, 1)):
        lanes = slice(side * LANES, (side + 1) * LANES)
        for b in range(3):
            for e in range(3):
                block = (2 - b) * 2 + e if e < 2 else 6 + 2 - b
                turned = kernel_ref[(a * 3 + b) * 3 + e].astype(F32).T.astype(BF16)
                weight_ref[first + block * half : first + (block + 1) * half, lanes] = turned
        weight_ref[first + span - half : first + span, lanes] = jnp.zeros((half, LANES), BF16)
    weight_ref[span:, :LANES] = jnp.zeros((span, LANES), BF16)

    def build(r, source, place, factor):
        for j in range(PAIRS):
            own = source[place, j * LANES : (j + 1) * LANES].astype(F32)
            if factor is not None:
                own = jnp.where(factor > 0, own, 0.0)
            for k, (pair, left) in enumerate(column_taps(own, j)):
                o = 2 * j + k
                near[o, at_row(r, columns), :] = pair.astype(BF16)
                far[o, at_row(r, columns), 0:half] = left[:, 0:half].astype(BF16)
                if not (isinstance(r, int) and r == 0):
                    far[o, at_row(r - 1, columns), half:LANES] = left[:, half:].astype(BF16)

    def build_own(r, carry):
        build(r + 1, d_ref, at_row(r, columns), None)
        return carry

    whole = slice(0, columns)
    build(0, above_ref, whole, edge_ref[0])
    lax.fori_loop(0, BLOCK_ROWS, build_own, 0)
    build(BLOCK_ROWS + 1, below_ref, whole, edge_ref[1])
    for o in range(DEPTH // 2):
        far[o, (padded - 1) * columns :, half:LANES] = jnp.zeros((columns, half), BF16)

    def row(r, carry):
        def pieces(o):
            return [near[o, at_row(r + i, columns), :] for i in range(3)] + [
                far[o, at_row(r + i, columns), :] for i in (0, 2)
            ]

        for o in range(DEPTH // 2):
            left = jnp.concatenate(pieces(o) + (pieces(o + 1) if o < DEPTH // 2 - 1 else []), axis=1)
            total = jnp.dot(left, weight_ref[0 : left.shape[1], :], preferred_element_type=F32)
            wide[at_row(2 * o * BLOCK_ROWS + r, columns), :] = total[:, :LANES]
            wide[at_row((2 * o + 1) * BLOCK_ROWS + r, columns), :] = total[:, LANES:]
        return carry

    lax.fori_loop(0, BLOCK_ROWS, row, 0)
    wide[cells:, :] = jnp.zeros((8, LANES), F32)

    def pick(i, carry):
        for j in range(8):
            rows[pl.ds(i * 8 + j, 1), :] = wide[pl.ds(index_ref[i * 8 + j], 1), :]
        return carry

    lax.fori_loop(0, count // 8, pick, 0)
    out_ref[...] = rows[...].astype(BF16)


def middle_data(index, edges, d_rows, above, below, w_mid, columns):
    count = index.shape[0]
    padded = (BLOCK_ROWS + 2) * columns
    return pl.pallas_call(
        functools.partial(middle_data_kernel, count, columns),
        out_shape=jax.ShapeDtypeStruct((count, LANES), BF16),
        in_specs=smem(2) + vmem(4),
        out_specs=vmem(1)[0],
        scratch_shapes=[
            pltpu.VMEM((DEPTH // 2, padded, LANES), BF16),
            pltpu.VMEM((DEPTH // 2, padded, LANES), BF16),
            pltpu.VMEM((DEPTH * BLOCK_ROWS * columns + 8, LANES), F32),
            pltpu.VMEM((count, LANES), F32),
            pltpu.VMEM((10 * LANES, 2 * LANES), BF16),
        ],
        compiler_params=params(),
        cost_estimate=work(30),
        name="middle_data",
    )(index, edges, d_rows, above, below, w_mid)


def middle_weight_kernel(columns, grid_ref, d_ref, out_ref, total, taps_ref, turned):
    grid_rows = BLOCK_ROWS + 2 * HALO
    half = LANES // 2
    total[...] = jnp.zeros_like(total)

    def rows(i, carry):
        for k in range(2):
            for j in range(PAIRS):
                own = d_ref[at_row(i * 2 + k, columns), j * LANES : (j + 1) * LANES].astype(F32)
                for n, (pair, left) in enumerate(column_taps(own, j)):
                    place = slice(k * columns, (k + 1) * columns)
                    taps_ref[2 * j + n, place, 0:LANES] = pair.astype(BF16)
                    taps_ref[2 * j + n, place, LANES:] = left.astype(BF16)
        for o in range(DEPTH // 2):
            depth_taps = (1, 2) if o == 0 else (0, 1, 2)
            cells = jnp.concatenate(
                [
                    grid_ref[
                        pl.ds(
                            pl.multiple_of(
                                ((2 * o + a - 1) * grid_rows + i * 2 + 1 + b) * columns, 32
                            ),
                            2 * columns,
                        ),
                        :,
                    ]
                    for a in depth_taps
                    for b in range(3)
                ],
                axis=1,
            )
            part = lax.dot_general(
                taps_ref[o], cells, (((0,), (0,)), ((), ())), preferred_element_type=F32
            )
            if o == 0:
                total[:, 3 * LANES :] += part
            else:
                total[...] += part
        return carry

    lax.fori_loop(0, BLOCK_ROWS // 2, rows, 0)
    low = low_lanes(LANES // 2)
    for place in range(9):
        for side in range(2):
            turned[...] = total[
                side * LANES : (side + 1) * LANES, place * LANES : (place + 1) * LANES
            ].T
            even = turned[pl.ds(0, half, stride=2), :]
            odd = turned[pl.ds(1, half, stride=2), :]
            at = (place * 3 + side * 2) * half
            out_ref[at : at + half, :] = jnp.where(low, even, pltpu.roll(odd, half, 1))
            if side == 0:
                out_ref[at + half : at + 2 * half, :] = jnp.where(
                    low, pltpu.roll(even, half, 1), odd
                )


def middle_weight(grid, d_rows, columns):
    return pl.pallas_call(
        functools.partial(middle_weight_kernel, columns),
        out_shape=jax.ShapeDtypeStruct((27 * LANES // 2, LANES), F32),
        in_specs=vmem(2),
        out_specs=vmem(1)[0],
        scratch_shapes=[
            pltpu.VMEM((2 * LANES, 9 * LANES), F32),
            pltpu.VMEM((DEPTH // 2, 2 * columns, 2 * LANES), BF16),
            pltpu.VMEM((LANES, LANES), F32),
        ],
        compiler_params=params(),
        cost_estimate=work(26),
        name="middle_weight",
    )(grid, d_rows)


def region_kernel(
    columns,
    scale_ref,
    bev_ref,
    weight_ref,
    bias_ref,
    head_ref,
    head_bias_ref,
    labels_ref,
    targets_ref,
    d_ref,
    first_ref,
    last_ref,
    grad_head_ref,
    sums_ref,
    head_sum,
    loss_sum,
):
    width = PAIRS * LANES
    outs = head_ref.shape[0]
    scale = scale_ref[0, 0]
    head = head_ref[...]
    head_three = jnp.concatenate([head, head, head], axis=0)
    grad_head_ref[...] = jnp.zeros_like(grad_head_ref)
    sums_ref[...] = jnp.zeros_like(sums_ref)
    head_sum[...] = jnp.zeros_like(head_sum)
    loss_sum[...] = jnp.zeros_like(loss_sum)
    kind = lax.broadcasted_iota(jnp.int32, (outs, columns), 0) % 8 == 0

    def row(r, carry):
        left = jnp.concatenate([bev_ref[at_row(r + b, columns), :] for b in range(3)], axis=1)
        part = jnp.dot(left, weight_ref[...], preferred_element_type=F32)
        pre = from_left(part[:, :LANES]) + part[:, LANES : 2 * LANES]
        pre = pre + from_right(part[:, 2 * LANES :]) + bias_ref[0:1, :]
        act = jnp.maximum(pre, 0.0).astype(BF16)
        heads = lax.dot_general(head, act, (((1,), (1,)), ((), ())), preferred_element_type=F32)
        heads = heads + head_bias_ref[:, 0:1]
        label = labels_ref[r]
        positive = jnp.where(label == 1, 1.0, 0.0)
        negative = jnp.where(label == 0, 1.0, 0.0)
        tail = jnp.log1p(jnp.exp(-jnp.abs(heads)))
        soft_up = jnp.maximum(heads, 0.0) + tail
        soft_down = jnp.maximum(-heads, 0.0) + tail
        probab = jax.nn.sigmoid(heads)
        rest = 1.0 - probab
        focal = positive * FOCAL_ALPHA * rest * rest * soft_down
        focal = focal + negative * (1.0 - FOCAL_ALPHA) * probab * probab * soft_up
        d_focal = positive * FOCAL_ALPHA * rest * rest * (-2.0 * probab * soft_down - rest)
        d_focal = d_focal + negative * (1.0 - FOCAL_ALPHA) * probab * probab * (
            2.0 * rest * soft_up + probab
        )
        offset = heads - targets_ref[r]
        size = jnp.abs(offset)
        near = size < 1.0 / 9.0
        smooth = jnp.where(near, 4.5 * offset * offset, size - 1.0 / 18.0)
        d_smooth = jnp.where(near, 9.0 * offset, jnp.where(offset > 0.0, 1.0, -1.0))
        loss_sum[...] += jnp.where(kind, focal, 2.0 * positive * smooth)
        d_heads = jnp.where(kind, d_focal, 2.0 * positive * d_smooth) * scale
        head_sum[...] += d_heads
        high = d_heads.astype(BF16)
        rest_one = d_heads - high.astype(F32)
        mid = rest_one.astype(BF16)
        tiny = (rest_one - mid.astype(F32)).astype(BF16)
        three = jnp.concatenate([high, mid, tiny], axis=0)
        grad_head_ref[...] += jnp.dot(three, act, preferred_element_type=F32)
        d_act = lax.dot_general(
            three, head_three, (((0,), (0,)), ((), ())), preferred_element_type=F32
        )
        d_pre = jnp.where(pre > 0.0, d_act, 0.0).astype(BF16)
        d_ref[at_row(r, columns), :] = d_pre

        @pl.when(r == 0)
        def _():
            first_ref[...] = d_pre

        @pl.when(r == d_ref.shape[0] // columns - 1)
        def _():
            last_ref[...] = d_pre

        sums_ref[0:8, :] += jnp.sum(d_pre.astype(F32).reshape(columns // 8, 8, LANES), axis=0)
        return carry

    lax.fori_loop(0, d_ref.shape[0] // columns, row, 0)
    sums_ref[8:24, :] = jnp.broadcast_to(
        jnp.sum(head_sum[...], axis=1, keepdims=True), (outs, LANES)
    )
    sums_ref[24:32, :] = jnp.broadcast_to(
        jnp.sum(jnp.sum(loss_sum[...], axis=1, keepdims=True), axis=0, keepdims=True), (8, LANES)
    )


def region_forward(scale, bev, weights, bias, head, head_bias, labels, targets, columns):
    rows = labels.shape[0]
    outs = head.shape[0]
    return pl.pallas_call(
        functools.partial(region_kernel, columns),
        out_shape=(
            jax.ShapeDtypeStruct((rows * columns, LANES), BF16),
            jax.ShapeDtypeStruct((columns, LANES), BF16),
            jax.ShapeDtypeStruct((columns, LANES), BF16),
            jax.ShapeDtypeStruct((3 * outs, LANES), F32),
            jax.ShapeDtypeStruct((32, LANES), F32),
        ),
        in_specs=smem(1) + vmem(7),
        out_specs=vmem(5),
        scratch_shapes=[pltpu.VMEM((outs, columns), F32), pltpu.VMEM((outs, columns), F32)],
        compiler_params=params(),
        cost_estimate=work(16),
        name="region_forward",
    )(
        scale.reshape(1, 1),
        bev,
        weights,
        jnp.broadcast_to(bias.reshape(1, -1), (8, LANES)),
        head,
        jnp.broadcast_to(head_bias.reshape(-1, 1), (outs, LANES)),
        labels,
        targets,
    )


def region_order(w_all):
    three, _, channels, outs = w_all.shape
    depth_out = DEPTH // 2
    turned = w_all.reshape(three, three, channels // depth_out, depth_out, outs)
    turned = turned.transpose(0, 1, 3, 2, 4).reshape(three, three, channels, outs)
    return jnp.pad(turned, ((0, 0), (0, 0), (0, PAIRS * LANES - channels), (0, 0)))


def region_data_kernel(
    columns, edge_ref, d_ref, above_ref, below_ref, bev_ref, weight_ref,
    out_ref, first_ref, last_ref, sums_ref, taps_ref,
):
    rows = out_ref.shape[0] // columns
    width = PAIRS * LANES
    sums_ref[...] = jnp.zeros_like(sums_ref)

    def build(r, own):
        taps_ref[at_row(r, columns), 0:LANES] = from_right(own).astype(BF16)
        taps_ref[at_row(r, columns), LANES : 2 * LANES] = own.astype(BF16)
        taps_ref[at_row(r, columns), 2 * LANES :] = from_left(own).astype(BF16)

    def build_own(r, carry):
        build(r + 1, d_ref[at_row(r, columns), :].astype(F32))
        return carry

    build(0, jnp.where(edge_ref[0] > 0, above_ref[...].astype(F32), 0.0))
    lax.fori_loop(0, rows, build_own, 0)
    build(rows + 1, jnp.where(edge_ref[1] > 0, below_ref[...].astype(F32), 0.0))

    def row(r, carry):
        left = jnp.concatenate([taps_ref[at_row(r + 2 - b, columns), :] for b in range(3)], axis=1)
        total = jnp.dot(left, weight_ref[...], preferred_element_type=F32)
        alive = bev_ref[at_row(r + 1, columns), :].astype(F32) > 0.0
        kept = jnp.where(alive, total, 0.0).astype(BF16)
        out_ref[at_row(r, columns), :] = kept

        @pl.when(r == 0)
        def _():
            first_ref[...] = kept

        @pl.when(r == rows - 1)
        def _():
            last_ref[...] = kept

        sums_ref[...] += jnp.sum(kept.astype(F32).reshape(columns // 8, 8, width), axis=0)
        return carry

    lax.fori_loop(0, rows, row, 0)


def region_data(edges, d_rows, above, below, bev, weights, columns):
    width = PAIRS * LANES
    return pl.pallas_call(
        functools.partial(region_data_kernel, columns),
        out_shape=(
            jax.ShapeDtypeStruct((d_rows.shape[0], width), BF16),
            jax.ShapeDtypeStruct((columns, width), BF16),
            jax.ShapeDtypeStruct((columns, width), BF16),
            jax.ShapeDtypeStruct((8, width), F32),
        ),
        in_specs=smem(1) + vmem(5),
        out_specs=vmem(4),
        scratch_shapes=[pltpu.VMEM((d_rows.shape[0] + 2 * columns, 3 * LANES), BF16)],
        compiler_params=params(),
        cost_estimate=work(13),
        name="region_data",
    )(edges, d_rows, above, below, bev, weights)


def region_weight_kernel(columns, blocks, d_ref, bev_ref, out_ref, total, taps_ref):
    rows = d_ref.shape[0] // columns
    width = PAIRS * LANES
    depth_out = DEPTH // 2
    half = LANES // 2
    total[...] = jnp.zeros_like(total)

    def two(i, carry):
        for k in range(2):
            own = d_ref[at_row(i * 2 + k, columns), :].astype(F32)
            place = slice(k * columns, (k + 1) * columns)
            taps_ref[place, 0:LANES] = from_right(own).astype(BF16)
            taps_ref[place, LANES : 2 * LANES] = own.astype(BF16)
            taps_ref[place, 2 * LANES :] = from_left(own).astype(BF16)
        cells = jnp.concatenate(
            [
                bev_ref[pl.ds(pl.multiple_of((i * 2 + b) * columns, 32), 2 * columns), :]
                for b in range(3)
            ],
            axis=1,
        )
        total[...] += lax.dot_general(
            taps_ref[...], cells, (((0,), (0,)), ((), ())), preferred_element_type=F32
        )
        return carry

    lax.fori_loop(0, rows // 2, two, 0)
    share = half // blocks
    for b in range(3):
        for e in range(3):
            for j in range(PAIRS):
                start = b * width + j * LANES
                turned = total[e * LANES : (e + 1) * LANES, start : start + LANES].T
                for k in range(min(2, depth_out - 2 * j)):
                    for q in range(blocks):
                        begin = k * half + q * share
                        base = ((q * 3 + b) * 3 + e) * share * depth_out
                        out_ref[pl.ds(base + 2 * j + k, share, stride=depth_out), :] = turned[
                            begin : begin + share, :
                        ]


def region_weight(d_own, bev, columns, blocks):
    width = PAIRS * LANES
    return pl.pallas_call(
        functools.partial(region_weight_kernel, columns, blocks),
        out_shape=jax.ShapeDtypeStruct((9 * (DEPTH // 2) * (LANES // 2), LANES), F32),
        in_specs=vmem(2),
        out_specs=vmem(1)[0],
        scratch_shapes=[
            pltpu.VMEM((3 * LANES, 3 * width), F32),
            pltpu.VMEM((2 * columns, 3 * LANES), BF16),
        ],
        compiler_params=params(),
        cost_estimate=work(10),
        name="region_weight",
    )(d_own, bev)


def prepare_kernel(
    slots, anc_count, device_rows, edge_ref, points_ref, count_ref, coord_ref, labels_ref,
    stats_ref, place_ref,
):
    voxels, width = points_ref.shape
    real = points_ref.shape[1] - 1
    features = 7
    lane = lax.broadcasted_iota(jnp.int32, (CHUNK, width), 1)
    ones_lane = features * slots
    total = jnp.zeros((width, width), F32)
    for i in range(voxels // CHUNK):
        block = points_ref[i * CHUNK : (i + 1) * CHUNK, :].astype(F32)
        valid = (lane % slots < count_ref[i * CHUNK : (i + 1) * CHUNK, :]) | (lane == ones_lane)
        block = jnp.where(valid, block, 0.0).astype(BF16)
        total = total + lax.dot_general(
            block, block, (((0,), (0,)), ((), ())), preferred_element_type=F32
        )
    row_at = lax.broadcasted_iota(jnp.int32, (width, width), 0)
    col_at = lax.broadcasted_iota(jnp.int32, (width, width), 1)
    same = (row_at % slots == col_at % slots) | (row_at == ones_lane)
    total = jnp.where(same & (row_at <= ones_lane) & (col_at < ones_lane), total, 0.0)
    rows = [
        jnp.sum(jnp.where(row_at // slots == k, total, 0.0), axis=0, keepdims=True)
        for k in range(features + 1)
    ]
    stacked = jnp.concatenate(rows, axis=0)
    col_eight = lax.broadcasted_iota(jnp.int32, (8, width), 1)
    lane_eight = lax.broadcasted_iota(jnp.int32, (8, LANES), 1)
    row_eight = lax.broadcasted_iota(jnp.int32, (8, LANES), 0)
    stats = jnp.zeros((8, LANES), F32)
    for k in range(features):
        picked = jnp.sum(jnp.where(col_eight // slots == k, stacked, 0.0), axis=1, keepdims=True)
        stats = stats + jnp.where(lane_eight == k, picked, 0.0)
    counted = jnp.sum(count_ref[...].astype(F32), axis=0, keepdims=True)
    found = jnp.zeros((1, 1), F32)
    for r in range(labels_ref.shape[0]):
        hits = jnp.where(labels_ref[r] == 1, 1.0, 0.0)
        found = found + jnp.sum(jnp.sum(hits, axis=1, keepdims=True), axis=0, keepdims=True)
    row = coord_ref[1:2, :]
    exists = coord_ref[3:4, :] > 0
    lists = []
    for q in range(anc_count):
        begin = q * device_rows - HALO
        lists.append(exists & (row >= begin) & (row < begin + device_rows + 2 * HALO))
    lists.append(exists & (row < HALO) & (edge_ref[0] > 0))
    lists.append(exists & (row >= anc_count * device_rows - HALO) & (edge_ref[1] > 0))
    lists += [exists & (row < 0)] * (8 - len(lists))
    member = jnp.concatenate([jnp.where(x, 1.0, 0.0) for x in lists], axis=0)
    before = (
        lax.broadcasted_iota(jnp.int32, (LANES, LANES), 0)
        < lax.broadcasted_iota(jnp.int32, (LANES, LANES), 1)
    )
    before = jnp.where(before, 1.0, 0.0).astype(BF16)
    carry = jnp.zeros((8, 1), F32)
    for i in range(voxels // LANES):
        part = member[:, i * LANES : (i + 1) * LANES]
        ahead = jnp.dot(part.astype(BF16), before, preferred_element_type=F32) + carry
        place_ref[:, i * LANES : (i + 1) * LANES] = jnp.where(part > 0.0, ahead, -1.0).astype(
            jnp.int32
        )
        carry = carry + jnp.sum(part, axis=1, keepdims=True)
    is_edge = lax.broadcasted_iota(jnp.int32, (8, 1), 0) >= anc_count
    need = carry / jnp.where(is_edge, float(EDGE_CAP), float(CAP))
    need = jnp.max(need, axis=0, keepdims=True)
    for k, value in enumerate((counted, found, need)):
        stats = stats + jnp.where((lane_eight == 8) & (row_eight == k), value, 0.0)
    stats_ref[...] = stats


def prepare(edges, points, counts, coords, labels, anc_count, device_rows, slots):
    voxels = points.shape[0]
    return pl.pallas_call(
        functools.partial(prepare_kernel, slots, anc_count, device_rows),
        out_shape=(
            jax.ShapeDtypeStruct((8, LANES), F32),
            jax.ShapeDtypeStruct((8, voxels), jnp.int32),
        ),
        in_specs=smem(1) + vmem(4),
        out_specs=vmem(2),
        compiler_params=params(),
        cost_estimate=work(4),
        name="prepare",
    )(edges, points, counts, coords, labels)


def exact_dot(left, right):
    return jnp.dot(left, right, preferred_element_type=F32, precision=lax.Precision.HIGHEST)


def batch_norm(stats, kernel, gain, shift):
    lanes = kernel.shape[1]
    moments = stats[:, 0:8]
    count = stats[0:1, 8:9]
    mixed = jnp.zeros((8, lanes), F32)
    for k in range(7):
        mixed = mixed + moments[:, k : k + 1] * kernel[k : k + 1, :]
    mean = mixed[7:8, :] / count
    second = jnp.sum(mixed * kernel, axis=0, keepdims=True) / count
    inv_std = lax.rsqrt(second - mean * mean + BN_EPSILON)
    return mixed, mean, inv_std, count


def first_layer(points, first_ref, scale, offset, valid):
    hidden = jnp.dot(points, first_ref[...], preferred_element_type=F32)
    act = jnp.where(valid, jnp.maximum(hidden * scale + offset, 0.0), 0.0)
    return act


def group_fold(values, combine):
    groups = values.shape[1] // LANES
    out = values[:, :LANES]
    for g in range(1, groups):
        out = combine(out, values[:, g * LANES : (g + 1) * LANES])
    out = combine(out, pltpu.roll(out, 32, 1))
    return combine(out, pltpu.roll(out, 64, 1))


def second_tail(pooled):
    lane = lax.broadcasted_iota(jnp.int32, pooled.shape, 1)
    return jnp.where(lane < 32, pooled, jnp.where(lane == 32, 1.0, 0.0))


def group_left(low, tail, count, g):
    lane = lax.broadcasted_iota(jnp.int32, tail.shape, 1)
    marked = (lane > 32) & (lane < 37) & (lane - (33 - 4 * g) >= count)
    side = jnp.where(marked, 1.0, tail).astype(BF16)
    return jnp.concatenate([low[:, g * LANES : (g + 1) * LANES], side], axis=1)


def encode_kernel(
    slots, points_ref, count_ref, stats_ref, kernel_ref, gain_ref, first_ref, second_ref,
    feat_ref, share_ref, held,
):
    lanes = first_ref.shape[1]
    _, mean, inv_std, _ = batch_norm(stats_ref[...], kernel_ref[...], None, None)
    scale = gain_ref[0:1, :] * inv_std
    offset = gain_ref[1:2, :] - mean * scale
    count = count_ref[...]
    slot = lax.broadcasted_iota(jnp.int32, (CHUNK, lanes), 1) // 32
    act = first_layer(points_ref[...], first_ref, scale, offset, slot < count)
    tail = second_tail(group_fold(act, jnp.maximum))
    low = act.astype(BF16)
    top = jnp.full((CHUNK, LANES), -jnp.inf, F32)
    for g in range(lanes // LANES):
        left = group_left(low, tail, count, g)
        part = jnp.dot(left, second_ref[...], preferred_element_type=F32)
        for s in range(min(4, slots - 4 * g)):
            p = 4 * g + s
            one = part[:, s * LANES : (s + 1) * LANES]
            held[p] = one
            top = jnp.maximum(top, one)
    ties = jnp.zeros((CHUNK, LANES), F32)
    for p in range(slots):
        ties = ties + jnp.where(held[p] == top, 1.0, 0.0)
    feat_ref[...] = jnp.maximum(top, 0.0)
    share_ref[...] = jnp.where(top > 0.0, 1.0 / ties, 0.0)


def encode(points, counts, stats, kernel, gain, first, second, slots):
    voxels, width = points.shape
    lanes = first.shape[1]
    whole = lambda *shape: pl.BlockSpec(shape, lambda i: (0,) * len(shape))
    block = lambda size: pl.BlockSpec((CHUNK, size), lambda i: (i, 0))
    return pl.pallas_call(
        functools.partial(encode_kernel, slots),
        grid=(voxels // CHUNK,),
        out_shape=(
            jax.ShapeDtypeStruct((voxels, LANES), F32),
            jax.ShapeDtypeStruct((voxels, LANES), F32),
        ),
        in_specs=[
            block(width),
            block(1),
            whole(8, LANES),
            whole(8, lanes),
            whole(8, lanes),
            whole(width, lanes),
            whole(2 * LANES, 4 * LANES),
        ],
        out_specs=[block(LANES), block(LANES)],
        scratch_shapes=[pltpu.VMEM((slots, CHUNK, LANES), F32)],
        compiler_params=params("arbitrary"),
        cost_estimate=work(19),
        name="encode",
    )(points, counts, stats, kernel, gain, first, second)


def decode_kernel(
    slots, points_ref, count_ref, stats_ref, kernel_ref, gain_ref, first_ref, second_ref,
    feat_ref, share_ref, d_feat_ref, first_out_ref, second_out_ref,
    first_sum, second_sum, joined,
):
    lanes = first_ref.shape[1]
    width = points_ref.shape[1]
    step = pl.program_id(0)

    @pl.when(step == 0)
    def _():
        first_sum[...] = jnp.zeros_like(first_sum)
        second_sum[...] = jnp.zeros_like(second_sum)

    _, mean, inv_std, _ = batch_norm(stats_ref[...], kernel_ref[...], None, None)
    scale = gain_ref[0:1, :] * inv_std
    offset = gain_ref[1:2, :] - mean * scale
    count = count_ref[...]
    points = points_ref[...]
    slot = lax.broadcasted_iota(jnp.int32, (CHUNK, lanes), 1) // 32
    act = first_layer(points, first_ref, scale, offset, slot < count)
    pooled = group_fold(act, jnp.maximum)
    tail = second_tail(pooled)
    low = act.astype(BF16)
    top = feat_ref[...]
    d_feat = d_feat_ref[...] * share_ref[...]
    d_tail = jnp.zeros((CHUNK, LANES), F32)
    for g in range(lanes // LANES):
        left = group_left(low, tail, count, g)
        part = jnp.dot(left, second_ref[...], preferred_element_type=F32)
        pieces = []
        for s in range(4):
            p = 4 * g + s
            if p < slots:
                hit = part[:, s * LANES : (s + 1) * LANES] == top
                pieces.append(jnp.where(hit, d_feat, 0.0).astype(BF16))
            else:
                pieces.append(jnp.zeros((CHUNK, LANES), BF16))
        d_part = jnp.concatenate(pieces, axis=1)
        second_sum[...] += lax.dot_general(
            left, d_part, (((0,), (0,)), ((), ())), preferred_element_type=F32
        )
        d_left = lax.dot_general(
            d_part, second_ref[...], (((1,), (1,)), ((), ())), preferred_element_type=F32
        )
        joined[:, g * LANES : (g + 1) * LANES] = d_left[:, :LANES]
        d_tail = d_tail + d_left[:, LANES:]
    ties = group_fold(
        jnp.where(act == jnp.concatenate([pooled] * (lanes // LANES), axis=1), 1.0, 0.0), jnp.add
    )
    lane = lax.broadcasted_iota(jnp.int32, (CHUNK, LANES), 1)
    spread = jnp.where(lane < 32, d_tail, 0.0)
    spread = spread + pltpu.roll(spread, 32, 1)
    spread = (spread + pltpu.roll(spread, 64, 1)) / ties
    spread = jnp.concatenate([spread] * (lanes // LANES), axis=1)
    wide = jnp.concatenate([pooled] * (lanes // LANES), axis=1)
    d_act = joined[...] + jnp.where(act == wide, spread, 0.0)
    d_act = jnp.where(act > 0.0, d_act, 0.0)
    high = d_act.astype(BF16)
    rest = (d_act - high.astype(F32)).astype(BF16)
    for piece in (high, rest):
        first_sum[...] += lax.dot_general(
            points, piece, (((0,), (0,)), ((), ())), preferred_element_type=F32
        )

    @pl.when(step == pl.num_programs(0) - 1)
    def _():
        row_at = lax.broadcasted_iota(jnp.int32, (width, lanes), 0)
        col_at = lax.broadcasted_iota(jnp.int32, (width, lanes), 1)
        same = (row_at % slots == col_at // 32) | (row_at == 7 * slots)
        total = jnp.where(same & (col_at // 32 < slots), first_sum[...], 0.0)
        rows = [
            jnp.sum(jnp.where(row_at // slots == k, total, 0.0), axis=0, keepdims=True)
            for k in range(8)
        ]
        first_out_ref[...] = group_fold(jnp.concatenate(rows, axis=0), jnp.add)
        for s in range(4):
            cols = slice(s * LANES, (s + 1) * LANES)
            upper = second_sum[s * 32 : (s + 1) * 32, cols]
            lower = second_sum[LANES : LANES + 40, cols]
            if s == 0:
                second_out_ref[0:32, :] = upper
                second_out_ref[32:72, :] = lower
            else:
                second_out_ref[0:32, :] += upper
                second_out_ref[32:72, :] += lower


def decode(points, counts, stats, kernel, gain, first, second, feat, share, d_feat, slots):
    voxels, width = points.shape
    lanes = first.shape[1]
    whole = lambda *shape: pl.BlockSpec(shape, lambda i: (0,) * len(shape))
    block = lambda size: pl.BlockSpec((CHUNK, size), lambda i: (i, 0))
    return pl.pallas_call(
        functools.partial(decode_kernel, slots),
        grid=(voxels // CHUNK,),
        out_shape=(
            jax.ShapeDtypeStruct((8, LANES), F32),
            jax.ShapeDtypeStruct((72, LANES), F32),
        ),
        in_specs=[
            block(width),
            block(1),
            whole(8, LANES),
            whole(8, lanes),
            whole(8, lanes),
            whole(width, lanes),
            whole(2 * LANES, 4 * LANES),
            block(LANES),
            block(LANES),
            block(LANES),
        ],
        out_specs=[whole(8, LANES), whole(72, LANES)],
        scratch_shapes=[
            pltpu.VMEM((width, lanes), F32),
            pltpu.VMEM((2 * LANES, 4 * LANES), F32),
            pltpu.VMEM((CHUNK, lanes), F32),
        ],
        compiler_params=params("arbitrary"),
        cost_estimate=work(35),
        name="decode",
    )(points, counts, stats, kernel, gain, first, second, feat, share, d_feat)


def encoder_weights(w_one, w_two, bias_two, gain, shift, slots):
    features, c_one = w_one.shape
    groups = -(-slots // 4)
    lanes = groups * LANES
    width = -(-(features * slots + 1) // LANES) * LANES
    row_at = lax.broadcasted_iota(jnp.int32, (width, lanes), 0)
    col_at = lax.broadcasted_iota(jnp.int32, (width, lanes), 1)
    tall = jnp.pad(
        jnp.repeat(w_one, slots, axis=0), ((0, width - features * slots), (0, 0))
    )
    same = (row_at % slots == col_at // c_one) & (row_at < features * slots)
    first = jnp.where(same, jnp.tile(tall, (1, lanes // c_one)), jnp.zeros((), BF16))
    c_two = w_two.shape[1]
    row_two = lax.broadcasted_iota(jnp.int32, (LANES, 4 * c_two), 0)
    col_two = lax.broadcasted_iota(jnp.int32, (LANES, 4 * c_two), 1)
    upper = jnp.where(
        row_two // c_one == col_two // c_two, jnp.tile(w_two[:c_one], (4, 4)), jnp.zeros((), BF16)
    )
    lower = jnp.concatenate([w_two[c_one:], bias_two.reshape(1, -1)], axis=0)
    lower = jnp.tile(jnp.pad(lower, ((0, LANES - lower.shape[0]), (0, 0))), (1, 4))
    lower = jnp.where(row_two == c_one + 1 + col_two // c_two, jnp.asarray(EMPTY, BF16), lower)
    second = jnp.concatenate([upper, lower], axis=0)
    kernel = jnp.pad(w_one.astype(F32), ((0, 1), (0, 0)))
    kernel = jnp.tile(kernel, (1, lanes // c_one))
    rows = jnp.pad(jnp.stack([gain, shift]).astype(F32), ((0, 6), (0, 0)))
    return first, second, kernel, jnp.tile(rows, (1, lanes // c_one))


def gather_lists_kernel(anc_count, offset_ref, feat_ref, digit_ref, place_ref, main_ref, up_ref, down_ref):
    source = jnp.concatenate([feat_ref[...].astype(BF16), digit_ref[...]], axis=1)
    voxels = source.shape[0]

    def pick(line, capacity, offset):
        want = place_ref[line : line + 1, :] - offset
        row_at = lax.broadcasted_iota(jnp.int32, (capacity, voxels), 0)
        chosen = jnp.where(want == row_at, 1.0, 0.0).astype(BF16)
        found = jnp.dot(chosen, source, preferred_element_type=F32)
        return found[:, :LANES].astype(BF16), found[:, LANES:].T

    for q in range(anc_count):
        rows, digits = pick(q, CAP, offset_ref[0])
        main_ref[q, 0:CAP, :] = rows
        lines = [
            digits[k : k + 1, i * LANES : (i + 1) * LANES]
            for k in range(3)
            for i in range(CAP // LANES)
        ]
        lines.append(jnp.zeros((32 - len(lines), LANES), F32))
        main_ref[q, CAP : CAP + 32, :] = jnp.concatenate(lines, axis=0).astype(BF16)
        main_ref[q, CAP + 32 :, :] = jnp.zeros((EDGE_CAP + 16, LANES), BF16)
    for side, edge_ref in enumerate((up_ref, down_ref)):
        rows, digits = pick(anc_count + side, EDGE_CAP, offset_ref[1])
        edge_ref[0:EDGE_CAP, :] = rows
        digits = jnp.concatenate([digits[0:8, :], jnp.zeros((8, LANES), F32)], axis=0)
        edge_ref[EDGE_CAP : EDGE_CAP + 16, :] = digits.astype(BF16)


def gather_lists(offsets, feat, digits, place, anc_count):
    return pl.pallas_call(
        functools.partial(gather_lists_kernel, anc_count),
        out_shape=(
            jax.ShapeDtypeStruct((anc_count, CAP + EDGE_CAP + 48, LANES), BF16),
            jax.ShapeDtypeStruct((EDGE_CAP + 16, LANES), BF16),
            jax.ShapeDtypeStruct((EDGE_CAP + 16, LANES), BF16),
        ),
        in_specs=smem(1) + vmem(3),
        out_specs=vmem(3),
        compiler_params=params(),
        cost_estimate=work(5),
        name="gather_lists",
    )(offsets, feat, digits, place)


def spread_lists_kernel(received_ref, where_ref, out_ref):
    total = received_ref.shape[0]
    lane = lax.broadcasted_iota(jnp.int32, (CHUNK, total), 1)
    chosen = jnp.where(where_ref[...] == lane, 1.0, 0.0).astype(BF16)
    out_ref[...] = jnp.dot(chosen, received_ref[...], preferred_element_type=F32)


def spread_lists(received, where):
    voxels = where.shape[0]
    total = received.shape[0]
    return pl.pallas_call(
        spread_lists_kernel,
        grid=(voxels // CHUNK,),
        out_shape=jax.ShapeDtypeStruct((voxels, LANES), F32),
        in_specs=[
            pl.BlockSpec((total, LANES), lambda i: (0, 0)),
            pl.BlockSpec((CHUNK, 1), lambda i: (i, 0)),
        ],
        out_specs=pl.BlockSpec((CHUNK, LANES), lambda i: (i, 0)),
        compiler_params=params("arbitrary"),
        cost_estimate=work(6),
        name="spread_lists",
    )(received, where)


def finish_kernel(stats_ref, kernel_ref, gain_ref, sums_ref, out_ref):
    kernel = kernel_ref[:, :LANES]
    mixed, mean, inv_std, count = batch_norm(stats_ref[...], kernel, None, None)
    sums = sums_ref[...]
    total_shift = sums[7:8, :]
    total_gain = inv_std * (jnp.sum(kernel * sums, axis=0, keepdims=True) - mean * total_shift)
    slope = gain_ref[0:1, :LANES] * inv_std
    for k in range(7):
        first = stats_ref[7:8, k : k + 1]
        pull = total_shift * first + total_gain * inv_std * (mixed[k : k + 1, :] - mean * first)
        out_ref[k : k + 1, :] = slope * (sums[k : k + 1, :] - pull / count)
    out_ref[7:8, :] = total_gain
    out_ref[8:16, :] = jnp.broadcast_to(total_shift, (8, LANES))


def finish_encoder(stats, kernel, gain, sums):
    return pl.pallas_call(
        finish_kernel,
        out_shape=jax.ShapeDtypeStruct((16, LANES), F32),
        in_specs=vmem(4),
        out_specs=vmem(1)[0],
        compiler_params=params(),
        cost_estimate=work(1),
        name="finish_encoder",
    )(stats, kernel, gain, sums)


def pack_kernel(plan, tiles, chunk, region_ref, middle_ref, tail_ref, out_ref, held):
    sources = {"region": region_ref, "middle": middle_ref, "tail": tail_ref}
    lane = lax.broadcasted_iota(jnp.int32, (1, LANES), 1)
    for a, pieces in enumerate(plan):
        at = 0
        for name, low, high in pieces:
            begin, end = low // LANES, -(-high // LANES)
            held[at : at + end - begin, :] = sources[name][begin:end, :]
            if low % LANES:
                held[at : at + 1, :] = jnp.where(lane < low % LANES, 0.0, held[at : at + 1, :])
            at += end - begin
            if high % LANES:
                held[at - 1 : at, :] = jnp.where(lane < high % LANES, held[at - 1 : at, :], 0.0)
        held[at:, :] = jnp.zeros((held.shape[0] - at, LANES), F32)
        for t in range(tiles):
            out_ref[t * len(plan) + a] = held[t * chunk : (t + 1) * chunk, :].astype(BF16)


def pack(plan, tiles, chunk, region, middle, tail):
    return pl.pallas_call(
        functools.partial(pack_kernel, plan, tiles, chunk),
        out_shape=jax.ShapeDtypeStruct((tiles * len(plan), chunk, LANES), BF16),
        in_specs=vmem(3),
        out_specs=vmem(1)[0],
        scratch_shapes=[pltpu.VMEM((tiles * chunk, LANES), F32)],
        compiler_params=params(),
        cost_estimate=work(3),
        name="pack",
    )(region, middle, tail)


def everyone(values, axes):
    count = 1
    for axis in axes:
        count *= lax.axis_size(axis)
    copies = jnp.broadcast_to(values[None], (count,) + values.shape)
    return lax.all_to_all(copies, axes, 0, 0)


def neighbour_rows(first, last):
    axes = ("tile", "anc")
    count = lax.axis_size("tile") * lax.axis_size("anc")
    down = [(i, i + 1) for i in range(count - 1)]
    return lax.ppermute(last, axes, down), lax.ppermute(first, axes, [(j, i) for i, j in down])


def shard_windows(segments, shard, count):
    windows = []
    for a in range(count):
        begin, end = a * shard, (a + 1) * shard
        at = 0
        pieces = []
        for name, size in segments:
            low, high = max(begin, at), min(end, at + size)
            if low < high:
                pieces.append((name, low - at, high - at))
            at += size
        windows.append(pieces)
    return windows


def on_device(
    points,
    npoints,
    coords,
    labels,
    targets,
    w_vfe1,
    w_vfe2,
    w_mid,
    w_rpn,
    w_head,
    bn_gain,
    biases,
    master,
    moment1,
    moment2,
):
    both = ("tile", "anc")
    anc_count = lax.axis_size("anc")
    tile_count = lax.axis_size("tile")
    anc = lax.axis_index("anc")
    tile = lax.axis_index("tile")
    device_rows = labels.shape[1]
    columns = labels.shape[2]
    blocks = device_rows // BLOCK_ROWS
    tile_rows = device_rows * anc_count
    all_rows = tile_rows * tile_count
    slots = points.shape[1]
    voxels = points.shape[2]
    c_vfe = w_vfe1.shape[1]
    c_vox = w_vfe2.shape[1]
    c_mid = w_mid.shape[4]
    c_rpn = w_rpn.shape[3]
    outs = w_head.shape[1]
    shift = biases[:c_vfe]
    bias_two = biases[c_vfe : c_vfe + c_vox]
    bias_mid, bias_rpn, bias_head = jnp.split(
        biases[c_vfe + c_vox :].astype(F32), [c_mid, c_mid + c_rpn]
    )

    def joined(row):
        return (row % CROP_ROWS != CROP_ROWS // 2) & (row > 0) & (row < all_rows)

    padded = -(-voxels // CHUNK) * CHUNK
    width = -(-(points.shape[0] * slots + 1) // LANES) * LANES
    flat_points = points.reshape(-1, voxels).T
    flat_points = jnp.pad(
        flat_points, ((0, padded - voxels), (0, width - flat_points.shape[1]))
    )
    lane = lax.broadcasted_iota(jnp.int32, flat_points.shape, 1)
    flat_points = jnp.where(lane == points.shape[0] * slots, jnp.ones((), BF16), flat_points)
    counts = jnp.pad(npoints, (0, padded - voxels)).reshape(padded, 1)
    layer = jnp.pad(coords[:, 0], (0, padded - voxels))
    row = jnp.pad(coords[:, 1] - tile * tile_rows, (0, padded - voxels))
    column = jnp.pad(coords[:, 2], (0, padded - voxels))
    exists = (jnp.arange(padded) < voxels).astype(jnp.int32)
    lines = jnp.pad(jnp.stack([layer, row, column, exists]), ((0, 4), (0, 0)))
    tile_edges = jnp.stack([joined(tile * tile_rows), joined((tile + 1) * tile_rows)])
    parts = everyone(w_rpn, ("anc",))
    stats, place = prepare(
        tile_edges.astype(jnp.int32),
        flat_points,
        counts,
        lines,
        labels.transpose(1, 0, 2),
        anc_count,
        device_rows,
        slots,
    )
    sent, parts = lax.optimization_barrier((stats, parts))
    gathered = everyone(sent, both)
    middle_kernel_all = w_mid.reshape(-1, c_vox, c_mid)
    region = parts.transpose(1, 2, 0, 3, 4)
    region = region_order(region.reshape(w_rpn.shape[:2] + (-1, c_rpn)))
    stats = jnp.sum(gathered, axis=0)
    count_pos = stats[1, 8]
    rounds = jnp.ceil(jnp.max(gathered[:, 2, 8])).astype(jnp.int32)

    first, second, kernel, gain_rows = encoder_weights(
        w_vfe1, w_vfe2, bias_two, bn_gain, shift, slots
    )
    feat, share = encode(flat_points, counts, stats, kernel, gain_rows, first, second, slots)

    digits = jnp.stack(
        [(layer + 1) * exists, column // 2 * exists, (row * 2 + column % 2) * exists], axis=1
    )
    digits = jnp.pad(digits, ((0, 0), (0, LANES - 3))).astype(BF16)
    slot_own = sum(
        jnp.where(row // device_rows == q, place[q], 0) for q in range(anc_count)
    )
    owner = jnp.clip(row // device_rows, 0, anc_count - 1)
    in_tile = lax.axis_size("tile")
    upward = [(i + 1, i) for i in range(in_tile - 1)]
    downward = [(i, i + 1) for i in range(in_tile - 1)]

    def exchange(number):
        offsets = jnp.stack([number * CAP, number * EDGE_CAP]).astype(jnp.int32)
        main, up, down = gather_lists(offsets, feat, digits, place, anc_count)
        from_below = lax.ppermute(up, "tile", upward)
        from_above = lax.ppermute(down, "tile", downward)
        main = lax.dynamic_update_slice(main, from_above[None], (0, CAP + 32, 0))
        main = lax.dynamic_update_slice(main, from_below[None], (anc_count - 1, CAP + 32, 0))
        got = lax.all_to_all(main, "anc", 0, 0)
        words = got[:, CAP : CAP + 32].reshape(anc_count, -1).astype(jnp.int32)
        start = CAP + 32 + EDGE_CAP
        edge_words = got[:, start : start + 16].astype(jnp.int32)

        def word(k):
            gap = jnp.zeros((anc_count, 32), jnp.int32)
            parts = [words[:, k * CAP : (k + 1) * CAP], gap, edge_words[:, k], gap[:, :16]]
            return jnp.concatenate(parts, axis=1)

        high, half, mixed = word(0), word(1), word(2)
        local = mixed // 2 - anc * device_rows
        is_edge = lax.broadcasted_iota(jnp.int32, local.shape, 1) >= CAP
        local = local + jnp.where(is_edge, jnp.where(anc == 0, -tile_rows, tile_rows), 0)
        cross = half * 2 + mixed % 2
        scatter_at, own_at = [], []
        for k in range(blocks):
            line = local - k * BLOCK_ROWS
            tall = BLOCK_ROWS + 2 * HALO
            inside = (high > 0) & (line >= -HALO) & (line < BLOCK_ROWS + HALO)
            spot = ((high - 1) * tall + line + HALO) * columns + cross
            scatter_at.append(jnp.where(inside, spot, DEPTH * tall * columns).reshape(-1))
            inside = (high > 0) & (line >= 0) & (line < BLOCK_ROWS)
            spot = ((high - 1) * BLOCK_ROWS + line) * columns + cross
            spot = jnp.where(inside, spot, DEPTH * BLOCK_ROWS * columns)
            own_at.append(spot[:, :CAP].reshape(-1))
        return got.reshape(-1, LANES), scatter_at, own_at

    feats, scatter_at, own_at = exchange(0)
    grids = [scatter_rows(index, feats, None, columns) for index in scatter_at]

    def more(state):
        return state[0] < rounds

    def another(state):
        number, held = state
        rows, index, _ = exchange(number)
        held = [scatter_rows(at, rows, old, columns) for at, old in zip(index, held)]
        return number + 1, held

    _, grids = lax.while_loop(more, another, (jnp.int32(1), grids))

    first_row = tile * tile_rows + anc * device_rows
    bevs, edges = [], []
    for k in range(blocks):
        top = first_row + k * BLOCK_ROWS
        edges.append(jnp.stack([joined(top), joined(top + BLOCK_ROWS)]).astype(jnp.int32))
        bevs.append(middle_forward(edges[k], grids[k], middle_kernel_all, bias_mid, columns))

    lanes = region.shape[2]
    region_in = region.transpose(0, 2, 1, 3).reshape(3 * lanes, 3 * c_rpn)
    region_back = region.transpose(0, 1, 3, 2).reshape(9 * c_rpn, lanes)
    wide_labels = jnp.repeat(labels.transpose(1, 0, 2), outs // 2, axis=1)
    wide_targets = jnp.pad(targets.transpose(2, 0, 1, 3), ((0, 0), (0, 0), (1, 0), (0, 0)))
    wide_targets = wide_targets.reshape(device_rows, outs, columns)
    scale = 1.0 / count_pos
    d_rows, head_sums, row_sums = [], 0.0, 0.0
    d_first, d_last = [], []
    for k in range(blocks):
        here = slice(k * BLOCK_ROWS, (k + 1) * BLOCK_ROWS)
        d_block, top_row, end_row, heads, sums = region_forward(
            scale,
            bevs[k],
            region_in,
            bias_rpn,
            w_head.T,
            bias_head,
            wide_labels[here],
            wide_targets[here],
            columns,
        )
        d_rows.append(d_block)
        d_first.append(top_row)
        d_last.append(end_row)
        head_sums = head_sums + heads
        row_sums = row_sums + sums

    def beside(firsts, lasts):
        above, below = neighbour_rows(firsts[0], lasts[-1])
        return [above] + lasts[:-1], firsts[1:] + [below]

    above, below = beside(d_first, d_last)
    grad_region = sum(
        region_weight(d_rows[k], bevs[k], columns, anc_count) for k in range(blocks)
    )
    d_rows, grad_region, above, below = lax.optimization_barrier(
        (d_rows, grad_region, above, below)
    )
    d_mids, mid_sums = [], 0.0
    mid_first, mid_last = [], []
    for k in range(blocks):
        d_block, top_row, end_row, sums = region_data(
            edges[k], d_rows[k], above[k], below[k], bevs[k], region_back, columns
        )
        d_mids.append(d_block)
        mid_first.append(top_row)
        mid_last.append(end_row)
        mid_sums = mid_sums + sums
    above, below = beside(mid_first, mid_last)
    grad_mid = sum(middle_weight(grids[k], d_mids[k], columns) for k in range(blocks))
    grad_mid, above, below = lax.optimization_barrier((grad_mid, above, below))

    head_three = head_sums.reshape(3, outs, c_rpn)
    grad_head = (head_three[0] + head_three[1] + head_three[2]).T
    grad_bias_mid = jnp.sum(mid_sums, axis=0)[: c_mid * DEPTH // 2].reshape(-1, c_mid).sum(axis=0)
    grad_bias_rpn = jnp.sum(row_sums[:8], axis=0)
    tail = jnp.concatenate(
        [
            grad_head.reshape(-1),
            jnp.zeros((c_vfe + c_vfe + c_vox,), F32),
            grad_bias_mid,
            grad_bias_rpn,
            row_sums[8 : 8 + outs, 0],
        ]
    )
    tail_rows = jnp.pad(tail, (0, -tail.shape[0] % LANES)).reshape(-1, LANES)
    shard = master.shape[0]
    segments = (
        ("region", grad_region.size),
        ("encoder", w_vfe1.size + w_vfe2.size),
        ("middle", grad_mid.size),
        ("tail", tail.shape[0]),
    )
    windows = shard_windows(segments, shard, anc_count)
    plan = tuple(tuple(p for p in pieces if p[0] != "encoder") for pieces in windows)
    tallest = max(sum(-(-high // LANES) - low // LANES for _, low, high in p) for p in plan)
    chunk_rows = -(-tallest // (16 * tile_count)) * 16
    packed = pack(plan, tile_count, chunk_rows, grad_region, grad_mid, tail_rows)
    own_at, packed = lax.optimization_barrier((own_at, packed))
    chunk = jnp.sum(lax.all_to_all(packed, both, 0, 0).astype(F32), axis=0)

    def collect(number, own_index, chunk):
        lists = sum(
            middle_data(
                own_index[k], edges[k], d_mids[k], above[k], below[k], middle_kernel_all, columns
            )
            for k in range(blocks)
        )
        lists, chunk = lax.optimization_barrier((lists, chunk))
        back = lax.all_to_all(lists.reshape(anc_count, CAP, LANES), "anc", 0, 0)
        mine = slot_own - number * CAP
        known = (exists > 0) & (mine >= 0) & (mine < CAP)
        where = jnp.where(known, owner * CAP + mine, -1).reshape(padded, 1)
        return spread_lists(back.reshape(-1, LANES), where), chunk

    d_feat, chunk = collect(0, own_at, chunk)
    chunk_square = jnp.sum(chunk * chunk)
    early = everyone(chunk, ("tile",)).reshape(-1)

    def collect_more(state):
        number, held = state
        _, _, index = exchange(number)
        return number + 1, held + collect(number, index, ())[0]

    d_feat = lax.cond(
        rounds > 1,
        lambda held: lax.while_loop(more, collect_more, (jnp.int32(1), held))[1],
        lambda held: held,
        d_feat,
    )
    first_sums, second_sums = decode(
        flat_points, counts, stats, kernel, gain_rows, first, second, feat, share, d_feat, slots
    )

    late = jnp.concatenate([first_sums, second_sums, row_sums[24:32]], axis=0)
    rows = late.shape[0]
    late, early = lax.optimization_barrier((late, early))
    late = late.reshape(anc_count * tile_count, 1, -1)
    late = jnp.sum(lax.all_to_all(late, both, 0, 0), axis=0)
    size = late.shape[1]
    late = jnp.concatenate([late, chunk_square.reshape(1, 1)], axis=1)
    late = everyone(late, both)
    square_sum = jnp.sum(late[:, 0, size])
    late = late[:, 0, :size].reshape(rows, LANES)
    encoder = finish_encoder(stats, kernel, gain_rows, late[:8])
    second_total = late[8 : 8 + second_sums.shape[0]]
    loss = late[rows - 1, 0] / count_pos
    encoder_flat = jnp.concatenate(
        [encoder[:7, :c_vfe].reshape(-1), second_total[: 2 * c_vfe].reshape(-1)]
    )
    tail_late = jnp.concatenate(
        [
            jnp.zeros((c_rpn * outs,), F32),
            encoder[7, :c_vfe],
            encoder[8, :c_vfe],
            second_total[2 * c_vfe],
            jnp.zeros((c_mid + c_rpn + outs,), F32),
        ]
    )

    def assemble(pieces):
        parts, at = [], 0
        for name, low, high in pieces:
            if name == "encoder":
                parts.append(encoder_flat[low:high])
                continue
            start = at + low % LANES
            part = early[start : start + high - low]
            at += (-(-high // LANES) - low // LANES) * LANES
            parts.append(part + tail_late[low:high] if name == "tail" else part)
        return jnp.concatenate(parts) if len(parts) > 1 else parts[0]

    reduced = None
    for a, pieces in enumerate(windows):
        one = assemble(pieces)
        reduced = one if a == 0 else jnp.where(anc == a, one, reduced)
    square_sum = square_sum + jnp.sum(encoder_flat * encoder_flat)
    square_sum = square_sum + jnp.sum(tail_late * tail_late)
    norm_value = jnp.sqrt(square_sum)
    clipped = reduced * jnp.minimum(1.0, CLIP_LIMIT / (norm_value + 1e-06))
    first_new = BETA_FIRST * moment1 + (1.0 - BETA_FIRST) * clipped
    second_new = BETA_SECOND * moment2 + (1.0 - BETA_SECOND) * clipped * clipped
    first_hat = first_new / (1.0 - BETA_FIRST**STEP_NUMBER)
    second_hat = second_new / (1.0 - BETA_SECOND**STEP_NUMBER)
    updated = master - LEARN_RATE * (
        first_hat / (jnp.sqrt(second_hat) + ADAM_EPSILON) + WEIGHT_DECAY * master
    )
    return (updated, first_new, second_new, loss, norm_value)


def solution(mesh):
    placed = (
        P(None, None, ("tile", "anc")),
        P(("tile", "anc")),
        P(("tile", "anc"), None),
        P(None, ("tile", "anc"), None),
        P(None, None, ("tile", "anc"), None),
        P(),
        P(),
        P(),
        P(None, None, "anc", None),
        P(),
        P(),
        P(),
        P("anc"),
        P("anc"),
        P("anc"),
    )
    return jax.shard_map(
        on_device,
        mesh=mesh,
        in_specs=placed,
        out_specs=(P("anc"), P("anc"), P("anc"), P(), P()),
        check_vma=False,
    )
```

```python
import functools
import jax
import jax.numpy as jnp
from jax import lax
from jax.experimental import pallas as pl
from jax.experimental.pallas import tpu as pltpu
from jax.sharding import PartitionSpec as P

DEPTH = 10
PAIRS = DEPTH // 4 + 1
CROP_ROWS = 192
BLOCK_ROWS = 12
HALO = 2
LANES = 128
CHUNK = 384
CAP = 768
EDGE_CAP = 128
EMPTY = -1e30
FOCAL_ALPHA = 0.25
BN_EPSILON = 0.001
CLIP_LIMIT = 0.05
LEARN_RATE = 0.03
BETA_FIRST = 0.9
BETA_SECOND = 0.999
WEIGHT_DECAY = 0.01
ADAM_EPSILON = 1e-08
STEP_NUMBER = 10
F32 = jnp.float32
BF16 = jnp.bfloat16


def vmem(count):
    return [pl.BlockSpec(memory_space=pltpu.VMEM)] * count


def smem(count):
    return [pl.BlockSpec(memory_space=pltpu.SMEM)] * count


def params(*semantics, limit=60):
    return pltpu.CompilerParams(
        vmem_limit_bytes=limit * 1024 * 1024, dimension_semantics=semantics or None
    )


def work(micros):
    return pl.CostEstimate(flops=micros, transcendentals=0, bytes_accessed=micros * 3_000_000)


def at_row(index, columns):
    return pl.ds(pl.multiple_of(index * columns, 32), columns)


def column_edges(columns, lanes):
    place = lax.broadcasted_iota(jnp.int32, (columns, lanes), 0)
    return place == 0, place == columns - 1


def from_left(values):
    columns, lanes = values.shape
    first, _ = column_edges(columns, lanes)
    return jnp.where(first, 0.0, pltpu.roll(values, 1, 0))


def from_right(values):
    columns, lanes = values.shape
    _, last = column_edges(columns, lanes)
    return jnp.where(last, 0.0, pltpu.roll(values, columns - 1, 0))


def low_lanes(columns):
    return lax.broadcasted_iota(jnp.int32, (columns, LANES), 1) < LANES // 2


def place_rows(count, cells, index_ref, feat_ref, old_ref, out_ref, wide, rows):
    step = 512

    def begin(i, carry):
        block = pl.ds(pl.multiple_of(i * step, step), step)
        if old_ref is None:
            wide[block, :] = jnp.zeros((step, LANES), F32)
        else:
            wide[block, :] = old_ref[block, :].astype(F32)
        return carry

    lax.fori_loop(0, cells // step, begin, 0)
    rows[...] = feat_ref[...].astype(F32)

    def place(i, carry):
        for j in range(8):
            wide[pl.ds(index_ref[i * 8 + j], 1), :] = rows[pl.ds(i * 8 + j, 1), :]
        return carry

    lax.fori_loop(0, count // 8, place, 0)

    def finish(i, carry):
        block = pl.ds(pl.multiple_of(i * step, step), step)
        out_ref[block, :] = wide[block, :].astype(BF16)
        return carry

    lax.fori_loop(0, cells // step, finish, 0)


def scatter_kernel(count, cells, fresh, *refs):
    if fresh:
        index_ref, feat_ref, out_ref, wide, rows = refs
        place_rows(count, cells, index_ref, feat_ref, None, out_ref, wide, rows)
    else:
        place_rows(count, cells, *refs)


def scatter_rows(index, feats, old, columns):
    cells = DEPTH * (BLOCK_ROWS + 2 * HALO) * columns
    count = index.shape[0]
    fresh = old is None
    return pl.pallas_call(
        functools.partial(scatter_kernel, count, cells, fresh),
        out_shape=jax.ShapeDtypeStruct((cells, LANES), BF16),
        in_specs=smem(1) + vmem(1 if fresh else 2),
        out_specs=vmem(1)[0],
        scratch_shapes=[pltpu.VMEM((cells + 8, LANES), F32), pltpu.VMEM((count, LANES), F32)],
        compiler_params=params(),
        cost_estimate=work(15),
        name="grid_scatter",
    )(*((index, feats) if fresh else (index, feats, old)))


def scatter_middle_kernel(
    count, columns, index_ref, edge_ref, feat_ref, kernel_ref, bias_ref, grid_ref, out_ref,
    wide, rows, held, weight_ref, done,
):
    place_rows(count, held.shape[0], index_ref, feat_ref, None, held, wide, rows)
    copy = pltpu.make_async_copy(held, grid_ref, done)
    copy.start()
    middle_kernel(columns, edge_ref, held, kernel_ref, bias_ref, out_ref, weight_ref)
    copy.wait()


def scatter_middle(index, edges, feats, w_mid, bias, columns):
    cells = DEPTH * (BLOCK_ROWS + 2 * HALO) * columns
    count = index.shape[0]
    return pl.pallas_call(
        functools.partial(scatter_middle_kernel, count, columns),
        out_shape=(
            jax.ShapeDtypeStruct((cells, LANES), BF16),
            jax.ShapeDtypeStruct(((BLOCK_ROWS + 2) * columns, PAIRS * LANES), BF16),
        ),
        in_specs=smem(2) + vmem(3),
        out_specs=[pl.BlockSpec(memory_space=pl.ANY), vmem(1)[0]],
        scratch_shapes=[
            pltpu.VMEM((cells + 8, LANES), F32),
            pltpu.VMEM((count, LANES), F32),
            pltpu.VMEM((cells, LANES), BF16),
            pltpu.VMEM((2, 9 * LANES, 2 * LANES), BF16),
            pltpu.SemaphoreType.DMA,
        ],
        compiler_params=params(),
        cost_estimate=work(36),
        name="scatter_middle",
    )(index, edges, feats, w_mid, jnp.tile(bias.reshape(1, -1), (8, 2)))


def middle_kernel(columns, edge_ref, grid_ref, kernel_ref, bias_ref, out_ref, weight_ref):
    low = low_lanes(columns)
    none = jnp.zeros((LANES, LANES // 2), BF16)
    for place in range(9):
        one, two, three = (kernel_ref[place * 3 + e] for e in range(3))
        rows = slice(place * LANES, (place + 1) * LANES)
        weight_ref[0, rows, :] = jnp.concatenate([one, two, three, none], axis=1)
        weight_ref[1, rows, :] = jnp.concatenate([two, one, none, three], axis=1)
    grid_rows = BLOCK_ROWS + 2 * HALO
    depth_out = DEPTH // 2

    def row(m, carry):
        sums = []
        for o in range(depth_out):
            taps = (1, 2) if o == 0 else (0, 1, 2)
            left = jnp.concatenate(
                [
                    grid_ref[at_row((2 * o + a - 1) * grid_rows + m + b, columns), :]
                    for a in taps
                    for b in range(3)
                ],
                axis=1,
            )
            right = weight_ref[o % 2, 3 * LANES * (3 - len(taps)) :, :]
            sums.append(jnp.dot(left, right, preferred_element_type=F32))
        inside = (m > 0) & (m < BLOCK_ROWS + 1) | (m == 0) & (edge_ref[0] > 0)
        inside = inside | (m == BLOCK_ROWS + 1) & (edge_ref[1] > 0)
        keep = jnp.where(inside, 1.0, 0.0)
        for j in range(PAIRS):
            even = sums[2 * j]
            if 2 * j + 1 < depth_out:
                odd = sums[2 * j + 1]
                first = jnp.where(low, even[:, :LANES], odd[:, :LANES])
                middle = jnp.where(low, odd[:, :LANES], even[:, :LANES])
                last = even[:, LANES:] + odd[:, LANES:]
            else:
                first = even[:, :LANES]
                middle = first
                last = even[:, LANES:]
            total = from_left(first) + pltpu.roll(middle, LANES // 2, 1) + from_right(last)
            total = jnp.maximum(total + bias_ref[0:1, :], 0.0) * keep
            if 2 * j + 1 == depth_out:
                total = jnp.where(low, total, 0.0)
            out_ref[at_row(m, columns), j * LANES : (j + 1) * LANES] = total.astype(BF16)
        return carry

    lax.fori_loop(0, BLOCK_ROWS + 2, row, 0, unroll=2)


def middle_forward(edges, grid, w_mid, bias, columns):
    return pl.pallas_call(
        functools.partial(middle_kernel, columns),
        out_shape=jax.ShapeDtypeStruct(((BLOCK_ROWS + 2) * columns, PAIRS * LANES), BF16),
        in_specs=smem(1) + vmem(3),
        out_specs=vmem(1)[0],
        scratch_shapes=[pltpu.VMEM((2, 9 * LANES, 2 * LANES), BF16)],
        compiler_params=params(),
        cost_estimate=work(26),
        name="middle_forward",
    )(edges, grid, w_mid, jnp.tile(bias.reshape(1, -1), (8, 2)))


def column_taps(own, j):
    low = low_lanes(own.shape[0])
    other = pltpu.roll(own, LANES // 2, 1)
    both = [jnp.where(low, own, other)]
    if 2 * j + 1 < DEPTH // 2:
        both.append(jnp.where(low, other, own))
    return [(jnp.where(low, from_right(x), x), from_left(x)) for x in both]


def middle_data_kernel(
    count, columns, index_ref, edge_ref, d_ref, above_ref, below_ref, kernel_ref, out_ref,
    near, far, wide, rows, weight_ref,
):
    padded = BLOCK_ROWS + 2
    half = LANES // 2
    cells = DEPTH * BLOCK_ROWS * columns
    span = 10 * half
    for a, first, side in ((1, 0, 0), (2, 0, 1), (0, span, 1)):
        lanes = slice(side * LANES, (side + 1) * LANES)
        for b in range(3):
            for e in range(3):
                block = (2 - b) * 2 + e if e < 2 else 6 + 2 - b
                turned = kernel_ref[(a * 3 + b) * 3 + e].astype(F32).T.astype(BF16)
                weight_ref[first + block * half : first + (block + 1) * half, lanes] = turned
        weight_ref[first + span - half : first + span, lanes] = jnp.zeros((half, LANES), BF16)
    weight_ref[span:, :LANES] = jnp.zeros((span, LANES), BF16)

    def build(r, source, place, factor):
        for j in range(PAIRS):
            own = source[place, j * LANES : (j + 1) * LANES].astype(F32)
            if factor is not None:
                own = jnp.where(factor > 0, own, 0.0)
            for k, (pair, left) in enumerate(column_taps(own, j)):
                o = 2 * j + k
                near[o, at_row(r, columns), :] = pair.astype(BF16)
                far[o, at_row(r, columns), 0:half] = left[:, 0:half].astype(BF16)
                if not (isinstance(r, int) and r == 0):
                    far[o, at_row(r - 1, columns), half:LANES] = left[:, half:].astype(BF16)

    def build_own(r, carry):
        build(r + 1, d_ref, at_row(r, columns), None)
        return carry

    whole = slice(0, columns)
    build(0, above_ref, whole, edge_ref[0])
    lax.fori_loop(0, BLOCK_ROWS, build_own, 0)
    build(BLOCK_ROWS + 1, below_ref, whole, edge_ref[1])
    for o in range(DEPTH // 2):
        far[o, (padded - 1) * columns :, half:LANES] = jnp.zeros((columns, half), BF16)

    def row(r, carry):
        def pieces(o):
            return [near[o, at_row(r + i, columns), :] for i in range(3)] + [
                far[o, at_row(r + i, columns), :] for i in (0, 2)
            ]

        for o in range(DEPTH // 2):
            left = jnp.concatenate(pieces(o) + (pieces(o + 1) if o < DEPTH // 2 - 1 else []), axis=1)
            total = jnp.dot(left, weight_ref[0 : left.shape[1], :], preferred_element_type=F32)
            wide[at_row(2 * o * BLOCK_ROWS + r, columns), :] = total[:, :LANES]
            wide[at_row((2 * o + 1) * BLOCK_ROWS + r, columns), :] = total[:, LANES:]
        return carry

    lax.fori_loop(0, BLOCK_ROWS, row, 0, unroll=2)
    wide[cells:, :] = jnp.zeros((8, LANES), F32)

    def pick(i, carry):
        for j in range(8):
            rows[pl.ds(i * 8 + j, 1), :] = wide[pl.ds(index_ref[i * 8 + j], 1), :]
        return carry

    lax.fori_loop(0, count // 8, pick, 0)
    out_ref[...] = rows[...].astype(BF16)


def middle_data(index, edges, d_rows, above, below, w_mid, columns):
    count = index.shape[0]
    padded = (BLOCK_ROWS + 2) * columns
    return pl.pallas_call(
        functools.partial(middle_data_kernel, count, columns),
        out_shape=jax.ShapeDtypeStruct((count, LANES), BF16),
        in_specs=smem(2) + vmem(4),
        out_specs=vmem(1)[0],
        scratch_shapes=[
            pltpu.VMEM((DEPTH // 2, padded, LANES), BF16),
            pltpu.VMEM((DEPTH // 2, padded, LANES), BF16),
            pltpu.VMEM((DEPTH * BLOCK_ROWS * columns + 8, LANES), F32),
            pltpu.VMEM((count, LANES), F32),
            pltpu.VMEM((10 * LANES, 2 * LANES), BF16),
        ],
        compiler_params=params(),
        cost_estimate=work(30),
        name="middle_data",
    )(index, edges, d_rows, above, below, w_mid)


def middle_weight_kernel(columns, grid_ref, d_ref, out_ref, total, taps_ref, turned):
    grid_rows = BLOCK_ROWS + 2 * HALO
    half = LANES // 2
    total[...] = jnp.zeros_like(total)

    def rows(i, carry):
        for k in range(2):
            for j in range(PAIRS):
                own = d_ref[at_row(i * 2 + k, columns), j * LANES : (j + 1) * LANES].astype(F32)
                for n, (pair, left) in enumerate(column_taps(own, j)):
                    place = slice(k * columns, (k + 1) * columns)
                    taps_ref[2 * j + n, place, 0:LANES] = pair.astype(BF16)
                    taps_ref[2 * j + n, place, LANES:] = left.astype(BF16)
        for o in range(DEPTH // 2):
            depth_taps = (1, 2) if o == 0 else (0, 1, 2)
            cells = jnp.concatenate(
                [
                    grid_ref[
                        pl.ds(
                            pl.multiple_of(
                                ((2 * o + a - 1) * grid_rows + i * 2 + 1 + b) * columns, 32
                            ),
                            2 * columns,
                        ),
                        :,
                    ]
                    for a in depth_taps
                    for b in range(3)
                ],
                axis=1,
            )
            part = lax.dot_general(
                taps_ref[o], cells, (((0,), (0,)), ((), ())), preferred_element_type=F32
            )
            if o == 0:
                total[:, 3 * LANES :] += part
            else:
                total[...] += part
        return carry

    lax.fori_loop(0, BLOCK_ROWS // 2, rows, 0, unroll=2)
    low = low_lanes(LANES // 2)
    for place in range(9):
        for side in range(2):
            turned[...] = total[
                side * LANES : (side + 1) * LANES, place * LANES : (place + 1) * LANES
            ].T
            even = turned[pl.ds(0, half, stride=2), :]
            odd = turned[pl.ds(1, half, stride=2), :]
            at = (place * 3 + side * 2) * half
            out_ref[at : at + half, :] = jnp.where(low, even, pltpu.roll(odd, half, 1))
            if side == 0:
                out_ref[at + half : at + 2 * half, :] = jnp.where(
                    low, pltpu.roll(even, half, 1), odd
                )


def middle_weight(grid, d_rows, columns):
    return pl.pallas_call(
        functools.partial(middle_weight_kernel, columns),
        out_shape=jax.ShapeDtypeStruct((27 * LANES // 2, LANES), F32),
        in_specs=vmem(2),
        out_specs=vmem(1)[0],
        scratch_shapes=[
            pltpu.VMEM((2 * LANES, 9 * LANES), F32),
            pltpu.VMEM((DEPTH // 2, 2 * columns, 2 * LANES), BF16),
            pltpu.VMEM((LANES, LANES), F32),
        ],
        compiler_params=params(limit=40),
        cost_estimate=work(26),
        name="middle_weight",
    )(grid, d_rows)


def region_kernel(
    columns,
    scale_ref,
    bev_ref,
    weight_ref,
    bias_ref,
    head_ref,
    head_bias_ref,
    labels_ref,
    targets_ref,
    d_ref,
    first_ref,
    last_ref,
    grad_head_ref,
    sums_ref,
    held,
):
    outs = head_ref.shape[0]
    cells = d_ref.shape[0]
    span = cells // 3
    scale = scale_ref[0, 0]
    head = head_ref[...]
    head_three = jnp.concatenate([head, head, head], axis=0)

    def row(r, carry):
        left = jnp.concatenate([bev_ref[at_row(r + b, columns), :] for b in range(3)], axis=1)
        part = jnp.dot(left, weight_ref[...], preferred_element_type=F32)
        pre = from_left(part[:, :LANES]) + part[:, LANES : 2 * LANES]
        held[at_row(r, columns), :] = pre + from_right(part[:, 2 * LANES :]) + bias_ref[0:1, :]
        return carry

    lax.fori_loop(0, cells // columns, row, 0, unroll=2)
    kind = lax.broadcasted_iota(jnp.int32, (outs, span), 0) % 8 == 0
    grad_head = jnp.zeros((3 * outs, LANES), F32)
    head_sum = jnp.zeros((outs, 1), F32)
    loss_sum = jnp.zeros((outs, 1), F32)
    row_sum = jnp.zeros((8, LANES), F32)
    for i in range(3):
        place = slice(i * span, (i + 1) * span)
        pre = held[place, :]
        act = jnp.maximum(pre, 0.0).astype(BF16)
        heads = lax.dot_general(head, act, (((1,), (1,)), ((), ())), preferred_element_type=F32)
        heads = heads + head_bias_ref[:, 0:1]
        label = labels_ref[:, place]
        positive = jnp.where(label == 1, 1.0, 0.0)
        negative = jnp.where(label == 0, 1.0, 0.0)
        tail = jnp.log1p(jnp.exp(-jnp.abs(heads)))
        soft_up = jnp.maximum(heads, 0.0) + tail
        soft_down = jnp.maximum(-heads, 0.0) + tail
        probab = jax.nn.sigmoid(heads)
        rest = 1.0 - probab
        focal = positive * FOCAL_ALPHA * rest * rest * soft_down
        focal = focal + negative * (1.0 - FOCAL_ALPHA) * probab * probab * soft_up
        d_focal = positive * FOCAL_ALPHA * rest * rest * (-2.0 * probab * soft_down - rest)
        d_focal = d_focal + negative * (1.0 - FOCAL_ALPHA) * probab * probab * (
            2.0 * rest * soft_up + probab
        )
        offset = heads - targets_ref[:, place]
        size = jnp.abs(offset)
        near = size < 1.0 / 9.0
        smooth = jnp.where(near, 4.5 * offset * offset, size - 1.0 / 18.0)
        d_smooth = jnp.where(near, 9.0 * offset, jnp.where(offset > 0.0, 1.0, -1.0))
        losses = jnp.where(kind, focal, 2.0 * positive * smooth)
        loss_sum = loss_sum + jnp.sum(losses, axis=1, keepdims=True)
        d_heads = jnp.where(kind, d_focal, 2.0 * positive * d_smooth) * scale
        head_sum = head_sum + jnp.sum(d_heads, axis=1, keepdims=True)
        high = d_heads.astype(BF16)
        rest_one = d_heads - high.astype(F32)
        mid = rest_one.astype(BF16)
        tiny = (rest_one - mid.astype(F32)).astype(BF16)
        three = jnp.concatenate([high, mid, tiny], axis=0)
        grad_head = grad_head + jnp.dot(three, act, preferred_element_type=F32)
        d_act = lax.dot_general(
            three, head_three, (((0,), (0,)), ((), ())), preferred_element_type=F32
        )
        d_pre = jnp.where(pre > 0.0, d_act, 0.0).astype(BF16)
        d_ref[place, :] = d_pre
        row_sum = row_sum + jnp.sum(d_pre.astype(F32).reshape(span // 8, 8, LANES), axis=0)
        if i == 0:
            first_ref[...] = d_pre[:columns, :]
        if i == 2:
            last_ref[...] = d_pre[span - columns :, :]
    grad_head_ref[...] = grad_head
    sums_ref[0:8, :] = row_sum
    sums_ref[8:24, :] = jnp.broadcast_to(head_sum, (outs, LANES))
    sums_ref[24:32, :] = jnp.broadcast_to(jnp.sum(loss_sum, axis=0, keepdims=True), (8, LANES))


def region_forward(scale, bev, weights, bias, head, head_bias, labels, targets, columns):
    cells = labels.shape[1]
    outs = head.shape[0]
    return pl.pallas_call(
        functools.partial(region_kernel, columns),
        out_shape=(
            jax.ShapeDtypeStruct((cells, LANES), BF16),
            jax.ShapeDtypeStruct((columns, LANES), BF16),
            jax.ShapeDtypeStruct((columns, LANES), BF16),
            jax.ShapeDtypeStruct((3 * outs, LANES), F32),
            jax.ShapeDtypeStruct((32, LANES), F32),
        ),
        in_specs=smem(1) + vmem(7),
        out_specs=vmem(5),
        scratch_shapes=[pltpu.VMEM((cells, LANES), F32)],
        compiler_params=params(limit=28),
        cost_estimate=work(16),
        name="region_forward",
    )(
        scale.reshape(1, 1),
        bev,
        weights,
        jnp.broadcast_to(bias.reshape(1, -1), (8, LANES)),
        head,
        jnp.broadcast_to(head_bias.reshape(-1, 1), (outs, LANES)),
        labels,
        targets,
    )


def region_order(w_all):
    three, _, channels, outs = w_all.shape
    depth_out = DEPTH // 2
    turned = w_all.reshape(three, three, channels // depth_out, depth_out, outs)
    turned = turned.transpose(0, 1, 3, 2, 4).reshape(three, three, channels, outs)
    return jnp.pad(turned, ((0, 0), (0, 0), (0, PAIRS * LANES - channels), (0, 0)))


def region_data_kernel(
    columns, edge_ref, d_ref, above_ref, below_ref, bev_ref, weight_ref,
    out_ref, first_ref, last_ref, sums_ref, taps_ref,
):
    rows = out_ref.shape[0] // columns
    width = PAIRS * LANES
    sums_ref[...] = jnp.zeros_like(sums_ref)

    def build(r, own):
        taps_ref[at_row(r, columns), 0:LANES] = from_right(own).astype(BF16)
        taps_ref[at_row(r, columns), LANES : 2 * LANES] = own.astype(BF16)
        taps_ref[at_row(r, columns), 2 * LANES :] = from_left(own).astype(BF16)

    def build_own(r, carry):
        build(r + 1, d_ref[at_row(r, columns), :].astype(F32))
        return carry

    build(0, jnp.where(edge_ref[0] > 0, above_ref[...].astype(F32), 0.0))
    lax.fori_loop(0, rows, build_own, 0)
    build(rows + 1, jnp.where(edge_ref[1] > 0, below_ref[...].astype(F32), 0.0))

    def row(r, carry):
        left = jnp.concatenate([taps_ref[at_row(r + 2 - b, columns), :] for b in range(3)], axis=1)
        total = jnp.dot(left, weight_ref[...], preferred_element_type=F32)
        alive = bev_ref[at_row(r + 1, columns), :].astype(F32) > 0.0
        kept = jnp.where(alive, total, 0.0).astype(BF16)
        out_ref[at_row(r, columns), :] = kept

        @pl.when(r == 0)
        def _():
            first_ref[...] = kept

        @pl.when(r == rows - 1)
        def _():
            last_ref[...] = kept

        sums_ref[...] += jnp.sum(kept.astype(F32).reshape(columns // 8, 8, width), axis=0)
        return carry

    lax.fori_loop(0, rows, row, 0, unroll=2)


def region_data(edges, d_rows, above, below, bev, weights, columns):
    width = PAIRS * LANES
    return pl.pallas_call(
        functools.partial(region_data_kernel, columns),
        out_shape=(
            jax.ShapeDtypeStruct((d_rows.shape[0], width), BF16),
            jax.ShapeDtypeStruct((columns, width), BF16),
            jax.ShapeDtypeStruct((columns, width), BF16),
            jax.ShapeDtypeStruct((8, width), F32),
        ),
        in_specs=smem(1) + vmem(5),
        out_specs=vmem(4),
        scratch_shapes=[pltpu.VMEM((d_rows.shape[0] + 2 * columns, 3 * LANES), BF16)],
        compiler_params=params(limit=28),
        cost_estimate=work(13),
        name="region_data",
    )(edges, d_rows, above, below, bev, weights)


def region_weight_kernel(columns, blocks, d_ref, bev_ref, out_ref, total, taps_ref):
    rows = d_ref.shape[0] // columns
    width = PAIRS * LANES
    depth_out = DEPTH // 2
    half = LANES // 2
    total[...] = jnp.zeros_like(total)

    def two(i, carry):
        for k in range(2):
            own = d_ref[at_row(i * 2 + k, columns), :].astype(F32)
            place = slice(k * columns, (k + 1) * columns)
            taps_ref[place, 0:LANES] = from_right(own).astype(BF16)
            taps_ref[place, LANES : 2 * LANES] = own.astype(BF16)
            taps_ref[place, 2 * LANES :] = from_left(own).astype(BF16)
        cells = jnp.concatenate(
            [
                bev_ref[pl.ds(pl.multiple_of((i * 2 + b) * columns, 32), 2 * columns), :]
                for b in range(3)
            ],
            axis=1,
        )
        total[...] += lax.dot_general(
            taps_ref[...], cells, (((0,), (0,)), ((), ())), preferred_element_type=F32
        )
        return carry

    lax.fori_loop(0, rows // 2, two, 0, unroll=2)
    share = half // blocks
    for b in range(3):
        for e in range(3):
            for j in range(PAIRS):
                start = b * width + j * LANES
                turned = total[e * LANES : (e + 1) * LANES, start : start + LANES].T
                for k in range(min(2, depth_out - 2 * j)):
                    for q in range(blocks):
                        begin = k * half + q * share
                        base = ((q * 3 + b) * 3 + e) * share * depth_out
                        out_ref[pl.ds(base + 2 * j + k, share, stride=depth_out), :] = turned[
                            begin : begin + share, :
                        ]


def region_weight(d_own, bev, columns, blocks):
    width = PAIRS * LANES
    return pl.pallas_call(
        functools.partial(region_weight_kernel, columns, blocks),
        out_shape=jax.ShapeDtypeStruct((9 * (DEPTH // 2) * (LANES // 2), LANES), F32),
        in_specs=vmem(2),
        out_specs=vmem(1)[0],
        scratch_shapes=[
            pltpu.VMEM((3 * LANES, 3 * width), F32),
            pltpu.VMEM((2 * columns, 3 * LANES), BF16),
        ],
        compiler_params=params(limit=28),
        cost_estimate=work(10),
        name="region_weight",
    )(d_own, bev)


def prepare_kernel(
    slots, anc_count, device_rows, edge_ref, points_ref, count_ref, coord_ref, labels_ref,
    stats_ref, place_ref,
):
    voxels, width = points_ref.shape
    real = points_ref.shape[1] - 1
    features = 7
    lane = lax.broadcasted_iota(jnp.int32, (CHUNK, width), 1)
    ones_lane = features * slots
    total = jnp.zeros((width, width), F32)
    for i in range(voxels // CHUNK):
        block = points_ref[i * CHUNK : (i + 1) * CHUNK, :].astype(F32)
        valid = (lane % slots < count_ref[i * CHUNK : (i + 1) * CHUNK, :]) | (lane == ones_lane)
        block = jnp.where(valid, block, 0.0).astype(BF16)
        total = total + lax.dot_general(
            block, block, (((0,), (0,)), ((), ())), preferred_element_type=F32
        )
    row_at = lax.broadcasted_iota(jnp.int32, (width, width), 0)
    col_at = lax.broadcasted_iota(jnp.int32, (width, width), 1)
    same = (row_at % slots == col_at % slots) | (row_at == ones_lane)
    total = jnp.where(same & (row_at <= ones_lane) & (col_at < ones_lane), total, 0.0)
    rows = [
        jnp.sum(jnp.where(row_at // slots == k, total, 0.0), axis=0, keepdims=True)
        for k in range(features + 1)
    ]
    stacked = jnp.concatenate(rows, axis=0)
    col_eight = lax.broadcasted_iota(jnp.int32, (8, width), 1)
    lane_eight = lax.broadcasted_iota(jnp.int32, (8, LANES), 1)
    row_eight = lax.broadcasted_iota(jnp.int32, (8, LANES), 0)
    stats = jnp.zeros((8, LANES), F32)
    for k in range(features):
        picked = jnp.sum(jnp.where(col_eight // slots == k, stacked, 0.0), axis=1, keepdims=True)
        stats = stats + jnp.where(lane_eight == k, picked, 0.0)
    counted = jnp.sum(count_ref[...].astype(F32), axis=0, keepdims=True)
    found = jnp.zeros((1, 1), F32)
    for r in range(labels_ref.shape[0]):
        hits = jnp.where(labels_ref[r] == 1, 1.0, 0.0)
        found = found + jnp.sum(jnp.sum(hits, axis=1, keepdims=True), axis=0, keepdims=True)
    row = coord_ref[1:2, :]
    exists = coord_ref[3:4, :] > 0
    lists = []
    for q in range(anc_count):
        begin = q * device_rows - HALO
        lists.append(exists & (row >= begin) & (row < begin + device_rows + 2 * HALO))
    lists.append(exists & (row < HALO) & (edge_ref[0] > 0))
    lists.append(exists & (row >= anc_count * device_rows - HALO) & (edge_ref[1] > 0))
    lists += [exists & (row < 0)] * (8 - len(lists))
    member = jnp.concatenate([jnp.where(x, 1.0, 0.0) for x in lists], axis=0)
    before = (
        lax.broadcasted_iota(jnp.int32, (LANES, LANES), 0)
        < lax.broadcasted_iota(jnp.int32, (LANES, LANES), 1)
    )
    before = jnp.where(before, 1.0, 0.0).astype(BF16)
    carry = jnp.zeros((8, 1), F32)
    for i in range(voxels // LANES):
        part = member[:, i * LANES : (i + 1) * LANES]
        ahead = jnp.dot(part.astype(BF16), before, preferred_element_type=F32) + carry
        place_ref[:, i * LANES : (i + 1) * LANES] = jnp.where(part > 0.0, ahead, -1.0).astype(
            jnp.int32
        )
        carry = carry + jnp.sum(part, axis=1, keepdims=True)
    is_edge = lax.broadcasted_iota(jnp.int32, (8, 1), 0) >= anc_count
    need = carry / jnp.where(is_edge, float(EDGE_CAP), float(CAP))
    need = jnp.max(need, axis=0, keepdims=True)
    for k, value in enumerate((counted, found, need)):
        stats = stats + jnp.where((lane_eight == 8) & (row_eight == k), value, 0.0)
    stats_ref[...] = stats


def prepare(edges, points, counts, coords, labels, anc_count, device_rows, slots):
    voxels = points.shape[0]
    return pl.pallas_call(
        functools.partial(prepare_kernel, slots, anc_count, device_rows),
        out_shape=(
            jax.ShapeDtypeStruct((8, LANES), F32),
            jax.ShapeDtypeStruct((8, voxels), jnp.int32),
        ),
        in_specs=smem(1) + vmem(4),
        out_specs=vmem(2),
        compiler_params=params(),
        cost_estimate=work(4),
        name="prepare",
    )(edges, points, counts, coords, labels)


def exact_dot(left, right):
    return jnp.dot(left, right, preferred_element_type=F32, precision=lax.Precision.HIGHEST)


def batch_norm(stats, kernel, gain, shift):
    lanes = kernel.shape[1]
    moments = stats[:, 0:8]
    count = stats[0:1, 8:9]
    mixed = jnp.zeros((8, lanes), F32)
    for k in range(7):
        mixed = mixed + moments[:, k : k + 1] * kernel[k : k + 1, :]
    mean = mixed[7:8, :] / count
    second = jnp.sum(mixed * kernel, axis=0, keepdims=True) / count
    inv_std = lax.rsqrt(second - mean * mean + BN_EPSILON)
    return mixed, mean, inv_std, count


def first_layer(points, first_ref, scale, offset, valid):
    hidden = jnp.dot(points, first_ref[...], preferred_element_type=F32)
    act = jnp.where(valid, jnp.maximum(hidden * scale + offset, 0.0), 0.0)
    return act


def group_fold(values, combine):
    groups = values.shape[1] // LANES
    out = values[:, :LANES]
    for g in range(1, groups):
        out = combine(out, values[:, g * LANES : (g + 1) * LANES])
    out = combine(out, pltpu.roll(out, 32, 1))
    return combine(out, pltpu.roll(out, 64, 1))


def second_tail(pooled):
    lane = lax.broadcasted_iota(jnp.int32, pooled.shape, 1)
    return jnp.where(lane < 32, pooled, jnp.where(lane == 32, 1.0, 0.0))


def group_left(low, tail, count, g):
    lane = lax.broadcasted_iota(jnp.int32, tail.shape, 1)
    marked = (lane > 32) & (lane < 37) & (lane - (33 - 4 * g) >= count)
    side = jnp.where(marked, 1.0, tail).astype(BF16)
    return jnp.concatenate([low[:, g * LANES : (g + 1) * LANES], side], axis=1)


def encode_kernel(
    slots, points_ref, count_ref, stats_ref, kernel_ref, gain_ref, first_ref, second_ref,
    feat_ref, share_ref, slot_ref, held,
):
    lanes = first_ref.shape[1]
    _, mean, inv_std, _ = batch_norm(stats_ref[...], kernel_ref[...], None, None)
    scale = gain_ref[0:1, :] * inv_std
    offset = gain_ref[1:2, :] - mean * scale
    count = count_ref[...]
    slot = lax.broadcasted_iota(jnp.int32, (CHUNK, lanes), 1) // 32
    act = first_layer(points_ref[...], first_ref, scale, offset, slot < count)
    tail = second_tail(group_fold(act, jnp.maximum))
    low = act.astype(BF16)
    top = jnp.full((CHUNK, LANES), -jnp.inf, F32)
    for g in range(lanes // LANES):
        left = group_left(low, tail, count, g)
        part = jnp.dot(left, second_ref[...], preferred_element_type=F32)
        for s in range(min(4, slots - 4 * g)):
            p = 4 * g + s
            one = part[:, s * LANES : (s + 1) * LANES]
            held[p] = one
            top = jnp.maximum(top, one)
    code = jnp.zeros((CHUNK, LANES), F32)
    for p in range(slots):
        code = code + jnp.where(held[p] == top, 2048.0 + p, 0.0)
    ties = jnp.floor(code / 2048.0)
    feat_ref[...] = jnp.maximum(top, 0.0)
    share_ref[...] = jnp.where(top > 0.0, 1.0 / ties, 0.0)
    slot_ref[...] = jnp.minimum(code - 2048.0 * ties, 127.0).astype(BF16)


def encode(points, counts, stats, kernel, gain, first, second, slots):
    voxels, width = points.shape
    lanes = first.shape[1]
    whole = lambda *shape: pl.BlockSpec(shape, lambda i: (0,) * len(shape))
    block = lambda size: pl.BlockSpec((CHUNK, size), lambda i: (i, 0))
    return pl.pallas_call(
        functools.partial(encode_kernel, slots),
        grid=(voxels // CHUNK,),
        out_shape=(
            jax.ShapeDtypeStruct((voxels, LANES), F32),
            jax.ShapeDtypeStruct((voxels, LANES), F32),
            jax.ShapeDtypeStruct((voxels, LANES), BF16),
        ),
        in_specs=[
            block(width),
            block(1),
            whole(8, LANES),
            whole(8, lanes),
            whole(8, lanes),
            whole(width, lanes),
            whole(2 * LANES, 4 * LANES),
        ],
        out_specs=[block(LANES), block(LANES), block(LANES)],
        scratch_shapes=[pltpu.VMEM((slots, CHUNK, LANES), F32)],
        compiler_params=params("arbitrary", limit=40),
        cost_estimate=work(14),
        name="encode",
    )(points, counts, stats, kernel, gain, first, second)


def decode_kernel(
    slots, points_ref, count_ref, stats_ref, kernel_ref, gain_ref, first_ref, second_ref,
    feat_ref, share_ref, slot_ref, d_feat_ref, loss_ref, out_ref,
    first_sum, second_sum, joined, tail_sum,
):
    lanes = first_ref.shape[1]
    width = points_ref.shape[1]
    step = pl.program_id(0)

    @pl.when(step == 0)
    def _():
        first_sum[...] = jnp.zeros_like(first_sum)
        second_sum[...] = jnp.zeros_like(second_sum)

    _, mean, inv_std, _ = batch_norm(stats_ref[...], kernel_ref[...], None, None)
    scale = gain_ref[0:1, :] * inv_std
    offset = gain_ref[1:2, :] - mean * scale
    count = count_ref[...]
    points = points_ref[...]
    slot = lax.broadcasted_iota(jnp.int32, (CHUNK, lanes), 1) // 32
    act = first_layer(points, first_ref, scale, offset, slot < count)
    pooled = group_fold(act, jnp.maximum)
    tail = second_tail(pooled)
    low = act.astype(BF16)
    share = share_ref[...]
    d_feat = d_feat_ref[...] * share
    d_low = d_feat.astype(BF16)
    shared = jnp.where((share > 0.0) & (share < 1.0), 1.0, 0.0)
    shared = jnp.max(jnp.max(shared, axis=1, keepdims=True)) > 0.0

    def group_back(g, left, pieces):
        d_part = jnp.concatenate(pieces, axis=1)
        second_sum[...] += lax.dot_general(
            left, d_part, (((0,), (0,)), ((), ())), preferred_element_type=F32
        )
        d_left = lax.dot_general(
            d_part, second_ref[...], (((1,), (1,)), ((), ())), preferred_element_type=F32
        )
        joined[:, g * LANES : (g + 1) * LANES] = d_left[:, :LANES]
        return d_left[:, LANES:]

    none = jnp.zeros((CHUNK, LANES), BF16)

    @pl.when(jnp.logical_not(shared))
    def _():
        found = slot_ref[...]
        d_tail = jnp.zeros((CHUNK, LANES), F32)
        for g in range(lanes // LANES):
            left = group_left(low, tail, count, g)
            pieces = [
                jnp.where(found == jnp.asarray(4 * g + s, BF16), d_low, none)
                if 4 * g + s < slots
                else none
                for s in range(4)
            ]
            d_tail = d_tail + group_back(g, left, pieces)
        tail_sum[...] = d_tail

    @pl.when(shared)
    def _():
        top = feat_ref[...]
        d_tail = jnp.zeros((CHUNK, LANES), F32)
        for g in range(lanes // LANES):
            left = group_left(low, tail, count, g)
            part = jnp.dot(left, second_ref[...], preferred_element_type=F32)
            pieces = []
            for s in range(4):
                if 4 * g + s < slots:
                    hit = part[:, s * LANES : (s + 1) * LANES] == top
                    pieces.append(jnp.where(hit, d_feat, 0.0).astype(BF16))
                else:
                    pieces.append(none)
            d_tail = d_tail + group_back(g, left, pieces)
        tail_sum[...] = d_tail

    wide = jnp.concatenate([pooled] * (lanes // LANES), axis=1)
    reached = act == wide
    ties = group_fold(jnp.where(reached, 1.0, 0.0), jnp.add)
    lane = lax.broadcasted_iota(jnp.int32, (CHUNK, LANES), 1)
    spread = jnp.where(lane < 32, tail_sum[...], 0.0)
    spread = spread + pltpu.roll(spread, 32, 1)
    spread = (spread + pltpu.roll(spread, 64, 1)) / ties
    spread = jnp.concatenate([spread] * (lanes // LANES), axis=1)
    d_act = joined[...] + jnp.where(reached, spread, 0.0)
    d_act = jnp.where(act > 0.0, d_act, 0.0).astype(BF16)
    first_sum[...] += lax.dot_general(
        points, d_act, (((0,), (0,)), ((), ())), preferred_element_type=F32
    )

    @pl.when(step == pl.num_programs(0) - 1)
    def _():
        row_at = lax.broadcasted_iota(jnp.int32, (width, lanes), 0)
        col_at = lax.broadcasted_iota(jnp.int32, (width, lanes), 1)
        same = (row_at % slots == col_at // 32) | (row_at == 7 * slots)
        total = jnp.where(same & (col_at // 32 < slots), first_sum[...], 0.0)
        rows = [
            jnp.sum(jnp.where(row_at // slots == k, total, 0.0), axis=0, keepdims=True)
            for k in range(8)
        ]
        out_ref[0:8, :] = group_fold(jnp.concatenate(rows, axis=0), jnp.add)
        upper = second_sum[0:32, 0:LANES]
        lower = second_sum[LANES : LANES + 40, 0:LANES]
        for s in range(1, 4):
            cols = slice(s * LANES, (s + 1) * LANES)
            upper = upper + second_sum[s * 32 : (s + 1) * 32, cols]
            lower = lower + second_sum[LANES : LANES + 40, cols]
        out_ref[8:40, :] = upper
        out_ref[40:80, :] = lower
        out_ref[80:88, :] = loss_ref[...]
        out_ref[88:, :] = jnp.zeros((out_ref.shape[0] - 88, LANES), F32)


def decode(
    points, counts, stats, kernel, gain, first, second, feat, share, slot, d_feat, loss, rows, slots
):
    voxels, width = points.shape
    lanes = first.shape[1]
    whole = lambda *shape: pl.BlockSpec(shape, lambda i: (0,) * len(shape))
    block = lambda size: pl.BlockSpec((CHUNK, size), lambda i: (i, 0))
    return pl.pallas_call(
        functools.partial(decode_kernel, slots),
        grid=(voxels // CHUNK,),
        out_shape=jax.ShapeDtypeStruct((rows, LANES), F32),
        in_specs=[
            block(width),
            block(1),
            whole(8, LANES),
            whole(8, lanes),
            whole(8, lanes),
            whole(width, lanes),
            whole(2 * LANES, 4 * LANES),
            block(LANES),
            block(LANES),
            block(LANES),
            block(LANES),
            whole(8, LANES),
        ],
        out_specs=whole(rows, LANES),
        scratch_shapes=[
            pltpu.VMEM((width, lanes), F32),
            pltpu.VMEM((2 * LANES, 4 * LANES), F32),
            pltpu.VMEM((CHUNK, lanes), F32),
            pltpu.VMEM((CHUNK, LANES), F32),
        ],
        compiler_params=params("arbitrary", limit=40),
        cost_estimate=work(28),
        name="decode",
    )(points, counts, stats, kernel, gain, first, second, feat, share, slot, d_feat, loss)


def encoder_weights(w_one, w_two, bias_two, gain, shift, slots):
    features, c_one = w_one.shape
    groups = -(-slots // 4)
    lanes = groups * LANES
    width = -(-(features * slots + 1) // LANES) * LANES
    row_at = lax.broadcasted_iota(jnp.int32, (width, lanes), 0)
    col_at = lax.broadcasted_iota(jnp.int32, (width, lanes), 1)
    tall = jnp.pad(
        jnp.repeat(w_one, slots, axis=0), ((0, width - features * slots), (0, 0))
    )
    same = (row_at % slots == col_at // c_one) & (row_at < features * slots)
    first = jnp.where(same, jnp.tile(tall, (1, lanes // c_one)), jnp.zeros((), BF16))
    c_two = w_two.shape[1]
    row_two = lax.broadcasted_iota(jnp.int32, (LANES, 4 * c_two), 0)
    col_two = lax.broadcasted_iota(jnp.int32, (LANES, 4 * c_two), 1)
    upper = jnp.where(
        row_two // c_one == col_two // c_two, jnp.tile(w_two[:c_one], (4, 4)), jnp.zeros((), BF16)
    )
    lower = jnp.concatenate([w_two[c_one:], bias_two.reshape(1, -1)], axis=0)
    lower = jnp.tile(jnp.pad(lower, ((0, LANES - lower.shape[0]), (0, 0))), (1, 4))
    lower = jnp.where(row_two == c_one + 1 + col_two // c_two, jnp.asarray(EMPTY, BF16), lower)
    second = jnp.concatenate([upper, lower], axis=0)
    kernel = jnp.pad(w_one.astype(F32), ((0, 1), (0, 0)))
    kernel = jnp.tile(kernel, (1, lanes // c_one))
    rows = jnp.pad(jnp.stack([gain, shift]).astype(F32), ((0, 6), (0, 0)))
    return first, second, kernel, jnp.tile(rows, (1, lanes // c_one))


def pick_rows(source, place_ref, line, capacity, offset):
    want = place_ref[line : line + 1, :] - offset
    row_at = lax.broadcasted_iota(jnp.int32, (capacity, source.shape[0]), 0)
    chosen = jnp.where(want == row_at, 1.0, 0.0).astype(BF16)
    found = jnp.dot(chosen, source, preferred_element_type=F32)
    return found[:, :LANES].astype(BF16), found[:, LANES:].T


def edge_lists_kernel(anc_count, offset_ref, feat_ref, digit_ref, place_ref, up_ref, down_ref):
    source = jnp.concatenate([feat_ref[...].astype(BF16), digit_ref[...]], axis=1)
    for side, edge_ref in enumerate((up_ref, down_ref)):
        rows, digits = pick_rows(source, place_ref, anc_count + side, EDGE_CAP, offset_ref[1])
        edge_ref[0:EDGE_CAP, :] = rows
        digits = jnp.concatenate([digits[0:8, :], jnp.zeros((8, LANES), F32)], axis=0)
        edge_ref[EDGE_CAP : EDGE_CAP + 16, :] = digits.astype(BF16)


def edge_lists(offsets, feat, digits, place, anc_count):
    return pl.pallas_call(
        functools.partial(edge_lists_kernel, anc_count),
        out_shape=(
            jax.ShapeDtypeStruct((EDGE_CAP + 16, LANES), BF16),
            jax.ShapeDtypeStruct((EDGE_CAP + 16, LANES), BF16),
        ),
        in_specs=smem(1) + vmem(3),
        out_specs=vmem(2),
        compiler_params=params(limit=24),
        cost_estimate=work(1),
        name="edge_lists",
    )(offsets, feat, digits, place)


def gather_lists_kernel(anc_count, offset_ref, feat_ref, digit_ref, place_ref, main_ref):
    source = jnp.concatenate([feat_ref[...].astype(BF16), digit_ref[...]], axis=1)
    for q in range(anc_count):
        rows, digits = pick_rows(source, place_ref, q, CAP, offset_ref[0])
        main_ref[q, 0:CAP, :] = rows
        lines = [
            digits[k : k + 1, i * LANES : (i + 1) * LANES]
            for k in range(3)
            for i in range(CAP // LANES)
        ]
        lines.append(jnp.zeros((32 - len(lines), LANES), F32))
        main_ref[q, CAP : CAP + 32, :] = jnp.concatenate(lines, axis=0).astype(BF16)
        main_ref[q, CAP + 32 :, :] = jnp.zeros((EDGE_CAP + 16, LANES), BF16)


def gather_lists(offsets, feat, digits, place, anc_count):
    return pl.pallas_call(
        functools.partial(gather_lists_kernel, anc_count),
        out_shape=jax.ShapeDtypeStruct((anc_count, CAP + EDGE_CAP + 48, LANES), BF16),
        in_specs=smem(1) + vmem(3),
        out_specs=vmem(1)[0],
        compiler_params=params(limit=40),
        cost_estimate=work(5),
        name="gather_lists",
    )(offsets, feat, digits, place)


def spread_lists_kernel(index_ref, received_ref, out_ref, held):
    total = received_ref.shape[0]
    held[0:total, :] = received_ref[...].astype(F32)
    held[total:, :] = jnp.zeros((8, LANES), F32)

    def pick(i, carry):
        for j in range(8):
            out_ref[pl.ds(i * 8 + j, 1), :] = held[pl.ds(index_ref[i * 8 + j], 1), :]
        return carry

    lax.fori_loop(0, out_ref.shape[0] // 8, pick, 0)


def spread_lists(index, received):
    voxels = index.shape[0]
    total = received.shape[0]
    return pl.pallas_call(
        spread_lists_kernel,
        out_shape=jax.ShapeDtypeStruct((voxels, LANES), F32),
        in_specs=smem(1) + vmem(1),
        out_specs=vmem(1)[0],
        scratch_shapes=[pltpu.VMEM((total + 8, LANES), F32)],
        compiler_params=params(limit=24),
        cost_estimate=work(4),
        name="spread_lists",
    )(index, received)


def add_piece(held, source, low, high, start):
    lane = lax.broadcasted_iota(jnp.int32, (1, LANES), 1)
    begin, end = low // LANES, -(-high // LANES)
    gap = start - low
    turn = gap % LANES
    at = begin + gap // LANES
    rows = source[begin:end, :]
    count = end - begin
    place = lax.broadcasted_iota(jnp.int32, (count, LANES), 0) * LANES
    place = place + lax.broadcasted_iota(jnp.int32, (count, LANES), 1) + begin * LANES
    if low % LANES or high % LANES:
        rows = jnp.where((place >= low) & (place < high), rows, 0.0)
    if turn == 0:
        held[at : at + count, :] += rows
        return
    rows = pltpu.roll(rows, turn, 1)
    here = jnp.where(lane >= turn, rows, 0.0)
    after = jnp.where(lane < turn, rows, 0.0)
    skip = max(-at, 0)
    if count > skip:
        held[at + skip : at + count, :] += here[skip:, :]
    held[at + 1 : at + 1 + count, :] += after


def pack_kernel(plan, tiles, chunk, region_ref, middle_ref, head_ref, rest_ref, out_ref, held):
    sources = {"region": region_ref, "middle": middle_ref, "head": head_ref, "rest": rest_ref}
    for a, pieces in enumerate(plan):
        held[...] = jnp.zeros_like(held)
        for name, low, high, start in pieces:
            if name in sources:
                add_piece(held, sources[name], low, high, start)
        for t in range(tiles):
            out_ref[t * len(plan) + a] = held[t * chunk : (t + 1) * chunk, :].astype(BF16)


def pack(plan, tiles, chunk, region, middle, head, rest):
    return pl.pallas_call(
        functools.partial(pack_kernel, plan, tiles, chunk),
        out_shape=jax.ShapeDtypeStruct((tiles * len(plan), chunk, LANES), BF16),
        in_specs=vmem(4),
        out_specs=vmem(1)[0],
        scratch_shapes=[pltpu.VMEM((tiles * chunk, LANES), F32)],
        compiler_params=params(limit=28),
        cost_estimate=work(3),
        name="pack",
    )(region, middle, head, rest)


def finish_kernel(
    plan, anc_ref, early_ref, late_ref, stats_ref, kernel_ref, gain_ref,
    out_ref, scalar_ref, one, norm,
):
    stats = stats_ref[...]
    kernel = kernel_ref[:, :LANES]
    mixed, mean, inv_std, count = batch_norm(stats, kernel, None, None)
    layers = late_ref.shape[1] - 1
    late = jnp.concatenate([late_ref[:, k, :] for k in range(layers)], axis=0)
    sums = late[0:8, :]
    total_shift = sums[7:8, :]
    total_gain = inv_std * (jnp.sum(kernel * sums, axis=0, keepdims=True) - mean * total_shift)
    slope = gain_ref[0:1, :LANES] * inv_std
    lane = lax.broadcasted_iota(jnp.int32, (1, LANES), 1)
    one[...] = jnp.zeros_like(one)
    norm[...] = jnp.zeros_like(norm)
    for k in range(7):
        first = stats[7:8, k : k + 1]
        pull = total_shift * first + total_gain * inv_std * (mixed[k : k + 1, :] - mean * first)
        grad = jnp.where(lane < 32, slope * (sums[k : k + 1, :] - pull / count), 0.0)
        if k % 4:
            grad = pltpu.roll(grad, 32 * (k % 4), 1)
        one[k // 4 : k // 4 + 1, :] += grad
    bias = late[72:73, :]
    top = jnp.where(lane < 32, total_gain, 0.0)
    top = top + pltpu.roll(jnp.where(lane < 32, total_shift, 0.0), 32, 1)
    norm[0:1, :] = top + jnp.where(lane < 64, 0.0, pltpu.roll(bias, 64, 1))
    norm[1:2, :] = jnp.where(lane < 64, pltpu.roll(bias, 64, 1), 0.0)
    two = late[8:72, :]
    square = jnp.sum(late_ref[:, layers, :]) / LANES
    square = square + jnp.sum(two * two) + jnp.sum(one[...] * one[...])
    square = square + jnp.sum(norm[...] * norm[...])
    size = jnp.sqrt(jnp.broadcast_to(square, (1, LANES)))
    scalar_ref[0:1, :] = late[80:81, :] / stats[1:2, 8:9]
    scalar_ref[1:2, :] = size
    scalar_ref[2:8, :] = jnp.broadcast_to(jnp.minimum(1.0, CLIP_LIMIT / (size + 1e-06)), (6, LANES))
    out_ref[...] = early_ref[...]
    sources = {"one": one, "two": two, "norm": norm}
    for a, pieces in enumerate(plan):

        @pl.when(anc_ref[0] == a)
        def _():
            for name, low, high, start in pieces:
                if name in sources:
                    add_piece(out_ref, sources[name], low, high, start)


def finish(plan, anc, early, late, stats, kernel, gain):
    return pl.pallas_call(
        functools.partial(finish_kernel, plan),
        out_shape=(
            jax.ShapeDtypeStruct(early.shape, F32),
            jax.ShapeDtypeStruct((8, LANES), F32),
        ),
        in_specs=smem(1) + vmem(5),
        out_specs=vmem(2),
        scratch_shapes=[pltpu.VMEM((8, LANES), F32), pltpu.VMEM((8, LANES), F32)],
        compiler_params=params(limit=24),
        cost_estimate=work(3),
        name="finish",
    )(anc, early, late, stats, kernel, gain)


def everyone(values, axes):
    count = 1
    for axis in axes:
        count *= lax.axis_size(axis)
    copies = jnp.broadcast_to(values[None], (count,) + values.shape)
    return lax.all_to_all(copies, axes, 0, 0)


def neighbour_rows(first, last):
    axes = ("tile", "anc")
    count = lax.axis_size("tile") * lax.axis_size("anc")
    down = [(i, i + 1) for i in range(count - 1)]
    return lax.ppermute(last, axes, down), lax.ppermute(first, axes, [(j, i) for i, j in down])


def shard_windows(segments, shard, count):
    windows = []
    for a in range(count):
        begin, end = a * shard, (a + 1) * shard
        at = 0
        pieces = []
        for name, size in segments:
            low, high = max(begin, at), min(end, at + size)
            if low < high:
                pieces.append((name, low - at, high - at, low - begin))
            at += size
        windows.append(tuple(pieces))
    return tuple(windows)


def on_device(
    points,
    npoints,
    coords,
    labels,
    targets,
    w_vfe1,
    w_vfe2,
    w_mid,
    w_rpn,
    w_head,
    bn_gain,
    biases,
    master,
    moment1,
    moment2,
):
    both = ("tile", "anc")
    anc_count = lax.axis_size("anc")
    tile_count = lax.axis_size("tile")
    anc = lax.axis_index("anc")
    tile = lax.axis_index("tile")
    device_rows = labels.shape[1]
    columns = labels.shape[2]
    blocks = device_rows // BLOCK_ROWS
    tile_rows = device_rows * anc_count
    all_rows = tile_rows * tile_count
    slots = points.shape[1]
    voxels = points.shape[2]
    c_vfe = w_vfe1.shape[1]
    c_vox = w_vfe2.shape[1]
    c_mid = w_mid.shape[4]
    c_rpn = w_rpn.shape[3]
    outs = w_head.shape[1]
    shift = biases[:c_vfe]
    bias_two = biases[c_vfe : c_vfe + c_vox]
    bias_mid, bias_rpn, bias_head = jnp.split(
        biases[c_vfe + c_vox :].astype(F32), [c_mid, c_mid + c_rpn]
    )

    def joined(row):
        return (row % CROP_ROWS != CROP_ROWS // 2) & (row > 0) & (row < all_rows)

    padded = -(-voxels // CHUNK) * CHUNK
    width = -(-(points.shape[0] * slots + 1) // LANES) * LANES
    flat_points = points.reshape(-1, voxels).T
    flat_points = jnp.pad(
        flat_points, ((0, padded - voxels), (0, width - flat_points.shape[1]))
    )
    lane = lax.broadcasted_iota(jnp.int32, flat_points.shape, 1)
    flat_points = jnp.where(lane == points.shape[0] * slots, jnp.ones((), BF16), flat_points)
    counts = jnp.pad(npoints, (0, padded - voxels)).reshape(padded, 1)
    layer = jnp.pad(coords[:, 0], (0, padded - voxels))
    row = jnp.pad(coords[:, 1] - tile * tile_rows, (0, padded - voxels))
    column = jnp.pad(coords[:, 2], (0, padded - voxels))
    exists = (jnp.arange(padded) < voxels).astype(jnp.int32)
    lines = jnp.pad(jnp.stack([layer, row, column, exists]), ((0, 4), (0, 0)))
    tile_edges = jnp.stack([joined(tile * tile_rows), joined((tile + 1) * tile_rows)])
    stats, place = prepare(
        tile_edges.astype(jnp.int32),
        flat_points,
        counts,
        lines,
        labels.transpose(1, 0, 2),
        anc_count,
        device_rows,
        slots,
    )
    gathered, w_rpn = lax.optimization_barrier((everyone(stats, both), w_rpn))
    parts = everyone(w_rpn, ("anc",))
    middle_kernel_all = w_mid.reshape(-1, c_vox, c_mid)
    stats = jnp.sum(gathered, axis=0)
    count_pos = stats[1, 8]
    rounds = jnp.ceil(jnp.max(gathered[:, 2, 8])).astype(jnp.int32)

    first, second, kernel, gain_rows = encoder_weights(
        w_vfe1, w_vfe2, bias_two, bn_gain, shift, slots
    )
    feat, share, found = encode(
        flat_points, counts, stats, kernel, gain_rows, first, second, slots
    )
    feat, parts = lax.optimization_barrier((feat, parts))

    region = parts.transpose(1, 2, 0, 3, 4)
    region = region_order(region.reshape(w_rpn.shape[:2] + (-1, c_rpn)))
    digits = jnp.stack(
        [(layer + 1) * exists, column // 2 * exists, (row * 2 + column % 2) * exists], axis=1
    )
    digits = jnp.pad(digits, ((0, 0), (0, LANES - 3))).astype(BF16)
    slot_own = sum(
        jnp.where(row // device_rows == q, place[q], 0) for q in range(anc_count)
    )
    owner = jnp.clip(row // device_rows, 0, anc_count - 1)
    in_tile = lax.axis_size("tile")
    upward = [(i + 1, i) for i in range(in_tile - 1)]
    downward = [(i, i + 1) for i in range(in_tile - 1)]

    def exchange(number):
        offsets = jnp.stack([number * CAP, number * EDGE_CAP]).astype(jnp.int32)
        up, down = edge_lists(offsets, feat, digits, place, anc_count)
        from_below = lax.ppermute(up, "tile", upward)
        from_above = lax.ppermute(down, "tile", downward)
        main = gather_lists(offsets, feat, digits, place, anc_count)
        main, from_below, from_above = lax.optimization_barrier((main, from_below, from_above))
        main = lax.dynamic_update_slice(main, from_above[None], (0, CAP + 32, 0))
        main = lax.dynamic_update_slice(main, from_below[None], (anc_count - 1, CAP + 32, 0))
        got = lax.all_to_all(main, "anc", 0, 0)
        words = got[:, CAP : CAP + 32].reshape(anc_count, -1).astype(jnp.int32)
        start = CAP + 32 + EDGE_CAP
        edge_words = got[:, start : start + 16].astype(jnp.int32)

        def word(k):
            gap = jnp.zeros((anc_count, 32), jnp.int32)
            parts = [words[:, k * CAP : (k + 1) * CAP], gap, edge_words[:, k], gap[:, :16]]
            return jnp.concatenate(parts, axis=1)

        high, half, mixed = word(0), word(1), word(2)
        local = mixed // 2 - anc * device_rows
        is_edge = lax.broadcasted_iota(jnp.int32, local.shape, 1) >= CAP
        local = local + jnp.where(is_edge, jnp.where(anc == 0, -tile_rows, tile_rows), 0)
        cross = half * 2 + mixed % 2
        scatter_at, own_at = [], []
        for k in range(blocks):
            line = local - k * BLOCK_ROWS
            tall = BLOCK_ROWS + 2 * HALO
            inside = (high > 0) & (line >= -HALO) & (line < BLOCK_ROWS + HALO)
            spot = ((high - 1) * tall + line + HALO) * columns + cross
            scatter_at.append(jnp.where(inside, spot, DEPTH * tall * columns).reshape(-1))
            inside = (high > 0) & (line >= 0) & (line < BLOCK_ROWS)
            spot = ((high - 1) * BLOCK_ROWS + line) * columns + cross
            spot = jnp.where(inside, spot, DEPTH * BLOCK_ROWS * columns)
            own_at.append(spot[:, :CAP].reshape(-1))
        return got.reshape(-1, LANES), scatter_at, own_at

    feats, scatter_at, own_at = exchange(0)
    first_row = tile * tile_rows + anc * device_rows
    edges = []
    for k in range(blocks):
        top = first_row + k * BLOCK_ROWS
        edges.append(jnp.stack([joined(top), joined(top + BLOCK_ROWS)]).astype(jnp.int32))

    def more(state):
        return state[0] < rounds

    def another(state):
        number, held = state
        rows, index, _ = exchange(number)
        held = [scatter_rows(at, rows, old, columns) for at, old in zip(index, held)]
        return number + 1, held

    def one_round():
        made = [
            scatter_middle(scatter_at[k], edges[k], feats, middle_kernel_all, bias_mid, columns)
            for k in range(blocks)
        ]
        return [grid for grid, _ in made], [bev for _, bev in made]

    def many_rounds():
        held = [scatter_rows(index, feats, None, columns) for index in scatter_at]
        _, held = lax.while_loop(more, another, (jnp.int32(1), held))
        return held, [
            middle_forward(edges[k], held[k], middle_kernel_all, bias_mid, columns)
            for k in range(blocks)
        ]

    grids, bevs = lax.cond(rounds > 1, many_rounds, one_round)

    lanes = region.shape[2]
    region_in = region.transpose(0, 2, 1, 3).reshape(3 * lanes, 3 * c_rpn)
    region_back = region.transpose(0, 1, 3, 2).reshape(9 * c_rpn, lanes)
    wide_labels = jnp.repeat(labels.reshape(2, -1), outs // 2, axis=0)
    wide_targets = jnp.pad(targets, ((0, 0), (1, 0), (0, 0), (0, 0))).reshape(outs, -1)
    step = BLOCK_ROWS * columns
    scale = 1.0 / count_pos
    d_rows, head_sums, row_sums = [], 0.0, 0.0
    d_first, d_last = [], []
    for k in range(blocks):
        here = slice(k * step, (k + 1) * step)
        d_block, top_row, end_row, heads, sums = region_forward(
            scale,
            bevs[k],
            region_in,
            bias_rpn,
            w_head.T,
            bias_head,
            wide_labels[:, here],
            wide_targets[:, here],
            columns,
        )
        d_rows.append(d_block)
        d_first.append(top_row)
        d_last.append(end_row)
        head_sums = head_sums + heads
        row_sums = row_sums + sums

    def beside(firsts, lasts):
        above, below = neighbour_rows(firsts[0], lasts[-1])
        return [above] + lasts[:-1], firsts[1:] + [below]

    above, below = beside(d_first, d_last)
    grad_region = sum(
        region_weight(d_rows[k], bevs[k], columns, anc_count) for k in range(blocks)
    )
    d_rows, grad_region, above, below = lax.optimization_barrier(
        (d_rows, grad_region, above, below)
    )
    d_mids, mid_sums = [], 0.0
    mid_first, mid_last = [], []
    for k in range(blocks):
        d_block, top_row, end_row, sums = region_data(
            edges[k], d_rows[k], above[k], below[k], bevs[k], region_back, columns
        )
        d_mids.append(d_block)
        mid_first.append(top_row)
        mid_last.append(end_row)
        mid_sums = mid_sums + sums
    above, below = beside(mid_first, mid_last)
    grad_mid = sum(middle_weight(grids[k], d_mids[k], columns) for k in range(blocks))
    grad_mid, above, below = lax.optimization_barrier((grad_mid, above, below))

    head_three = head_sums.reshape(3, outs, c_rpn)
    grad_head = (head_three[0] + head_three[1] + head_three[2]).T
    grad_bias_mid = jnp.sum(mid_sums, axis=0)[: c_mid * DEPTH // 2].reshape(-1, c_mid).sum(axis=0)
    grad_bias_rpn = jnp.sum(row_sums[:8], axis=0)
    head_rows = grad_head.reshape(-1, LANES)
    rest = jnp.concatenate([grad_bias_mid, grad_bias_rpn, row_sums[8 : 8 + outs, 0]])
    segments = (
        ("region", grad_region.size),
        ("one", w_vfe1.size),
        ("two", w_vfe2.size),
        ("middle", grad_mid.size),
        ("head", w_head.size),
        ("norm", c_vfe + c_vfe + c_vox),
        ("rest", rest.shape[0]),
    )
    rest_rows = jnp.pad(rest, (0, -rest.shape[0] % LANES)).reshape(-1, LANES)
    shard = master.shape[0]
    plan = shard_windows(segments, shard, anc_count)
    chunk_rows = -(-(shard // LANES + 2) // (16 * tile_count)) * 16
    packed = pack(
        plan, tile_count, chunk_rows, grad_region, grad_mid, head_rows, rest_rows
    )
    own_at, packed = lax.optimization_barrier((own_at, packed))
    chunk = jnp.sum(lax.all_to_all(packed, both, 0, 0).astype(F32), axis=0)

    def collect(number, own_index, chunk):
        lists = sum(
            middle_data(
                own_index[k], edges[k], d_mids[k], above[k], below[k], middle_kernel_all, columns
            )
            for k in range(blocks)
        )
        lists, chunk = lax.optimization_barrier((lists, chunk))
        back = lax.all_to_all(lists.reshape(anc_count, CAP, LANES), "anc", 0, 0)
        mine = slot_own - number * CAP
        known = (exists > 0) & (mine >= 0) & (mine < CAP)
        index = jnp.where(known, owner * CAP + mine, anc_count * CAP)
        return spread_lists(index, back.reshape(-1, LANES)), chunk

    d_feat, chunk = collect(0, own_at, chunk)
    early = everyone(chunk, ("tile",)).reshape(-1, LANES)

    def collect_more(state):
        number, held = state
        _, _, index = exchange(number)
        return number + 1, held + collect(number, index, ())[0]

    d_feat = lax.cond(
        rounds > 1,
        lambda held: lax.while_loop(more, collect_more, (jnp.int32(1), held))[1],
        lambda held: held,
        d_feat,
    )
    devices = anc_count * tile_count
    layers = -(-88 // devices)
    late = decode(
        flat_points,
        counts,
        stats,
        kernel,
        gain_rows,
        first,
        second,
        feat,
        share,
        found,
        d_feat,
        row_sums[24:32],
        layers * devices,
        slots,
    )
    late, early = lax.optimization_barrier((late, early))
    late = late.reshape(layers, devices, LANES).transpose(1, 0, 2)
    late = jnp.sum(lax.all_to_all(late, both, 0, 0), axis=0)
    chunk_square = jnp.broadcast_to(jnp.sum(chunk * chunk), (1, LANES))
    late = everyone(jnp.concatenate([late, chunk_square], axis=0), both)
    reduced, scalars = finish(plan, anc.reshape(1), early, late, stats, kernel, gain_rows)
    loss = scalars[0, 0]
    norm_value = scalars[1, 0]
    reduced = reduced.reshape(-1)[:shard]
    clipped = reduced * scalars[2, 0]
    first_new = BETA_FIRST * moment1 + (1.0 - BETA_FIRST) * clipped
    second_new = BETA_SECOND * moment2 + (1.0 - BETA_SECOND) * clipped * clipped
    first_hat = first_new / (1.0 - BETA_FIRST**STEP_NUMBER)
    second_hat = second_new / (1.0 - BETA_SECOND**STEP_NUMBER)
    updated = master - LEARN_RATE * (
        first_hat / (jnp.sqrt(second_hat) + ADAM_EPSILON) + WEIGHT_DECAY * master
    )
    return (updated, first_new, second_new, loss, norm_value)


def solution(mesh):
    placed = (
        P(None, None, ("tile", "anc")),
        P(("tile", "anc")),
        P(("tile", "anc"), None),
        P(None, ("tile", "anc"), None),
        P(None, None, ("tile", "anc"), None),
        P(),
        P(),
        P(),
        P(None, None, "anc", None),
        P(),
        P(),
        P(),
        P("anc"),
        P("anc"),
        P("anc"),
    )
    return jax.shard_map(
        on_device,
        mesh=mesh,
        in_specs=placed,
        out_specs=(P("anc"), P("anc"), P("anc"), P(), P()),
        check_vma=False,
    )
```

```python
import functools
import jax
import jax.numpy as jnp
from jax import lax
from jax.experimental import pallas as pl
from jax.experimental.pallas import tpu as pltpu
from jax.sharding import PartitionSpec as P

DEPTH = 10
PAIRS = DEPTH // 4 + 1
CROP_ROWS = 192
BLOCK_ROWS = 12
HALO = 2
LANES = 128
CHUNK = 384
CAP = 768
EDGE_CAP = 128
EMPTY = -1e30
FOCAL_ALPHA = 0.25
BN_EPSILON = 0.001
CLIP_LIMIT = 0.05
LEARN_RATE = 0.03
BETA_FIRST = 0.9
BETA_SECOND = 0.999
WEIGHT_DECAY = 0.01
ADAM_EPSILON = 1e-08
STEP_NUMBER = 10
F32 = jnp.float32
BF16 = jnp.bfloat16


def vmem(count):
    return [pl.BlockSpec(memory_space=pltpu.VMEM)] * count


def smem(count):
    return [pl.BlockSpec(memory_space=pltpu.SMEM)] * count


def params(*semantics, limit=60):
    return pltpu.CompilerParams(
        vmem_limit_bytes=limit * 1024 * 1024, dimension_semantics=semantics or None
    )


def work(micros):
    return pl.CostEstimate(flops=micros, transcendentals=0, bytes_accessed=micros * 3_000_000)


def at_row(index, columns):
    return pl.ds(pl.multiple_of(index * columns, 32), columns)


def column_edges(columns, lanes):
    place = lax.broadcasted_iota(jnp.int32, (columns, lanes), 0)
    return place == 0, place == columns - 1


def from_left(values):
    columns, lanes = values.shape
    first, _ = column_edges(columns, lanes)
    return jnp.where(first, 0.0, pltpu.roll(values, 1, 0))


def from_right(values):
    columns, lanes = values.shape
    _, last = column_edges(columns, lanes)
    return jnp.where(last, 0.0, pltpu.roll(values, columns - 1, 0))


def low_lanes(columns):
    return lax.broadcasted_iota(jnp.int32, (columns, LANES), 1) < LANES // 2


def clear(wide, cells):
    step = 512

    def begin(i, carry):
        wide[pl.ds(pl.multiple_of(i * step, step), step), :] = jnp.zeros((step, LANES), F32)
        return carry

    lax.fori_loop(0, cells // step, begin, 0)


def narrow(wide, out_ref):
    step = 512

    def finish(i, carry):
        block = pl.ds(pl.multiple_of(i * step, step), step)
        out_ref[block, :] = wide[block, :].astype(BF16)
        return carry

    lax.fori_loop(0, out_ref.shape[0] // step, finish, 0)


def place_rows(count, cells, index_ref, feat_ref, old_ref, out_ref, wide, rows):
    if old_ref is None:
        clear(wide, cells)
    else:
        wide[0:cells, :] = old_ref[...].astype(F32)
    rows[...] = feat_ref[...].astype(F32)

    def place(i, carry):
        for j in range(8):
            wide[pl.ds(index_ref[i * 8 + j], 1), :] = rows[pl.ds(i * 8 + j, 1), :]
        return carry

    lax.fori_loop(0, count // 8, place, 0)
    narrow(wide, out_ref)


def scatter_kernel(count, cells, fresh, *refs):
    if fresh:
        index_ref, feat_ref, out_ref, wide, rows = refs
        place_rows(count, cells, index_ref, feat_ref, None, out_ref, wide, rows)
    else:
        place_rows(count, cells, *refs)


def scatter_rows(index, feats, old, columns):
    cells = DEPTH * (BLOCK_ROWS + 2 * HALO) * columns
    count = index.shape[0]
    fresh = old is None
    return pl.pallas_call(
        functools.partial(scatter_kernel, count, cells, fresh),
        out_shape=jax.ShapeDtypeStruct((cells, LANES), BF16),
        in_specs=smem(1) + vmem(1 if fresh else 2),
        out_specs=vmem(1)[0],
        scratch_shapes=[pltpu.VMEM((cells + 8, LANES), F32), pltpu.VMEM((count, LANES), F32)],
        compiler_params=params(),
        cost_estimate=work(15),
        name="grid_scatter",
    )(*((index, feats) if fresh else (index, feats, old)))


TOP, BOTTOM, EVEN, FIRST_ROW, EDGE_SHIFT = range(5)


def list_cells(columns, edge_ref, feat_ref, spots, owns):
    sources = feat_ref.shape[0] // (CAP + EDGE_CAP + 48)
    main = CAP // LANES
    tall = BLOCK_ROWS + 2 * HALO
    for a in range(sources):
        base = a * (CAP + EDGE_CAP + 48)
        words = feat_ref[base + CAP : base + CAP + 32, :].astype(F32).astype(jnp.int32)
        start = base + CAP + 32 + EDGE_CAP
        edges = feat_ref[start : start + 16, :].astype(F32).astype(jnp.int32)
        for side, (high, half, mixed) in enumerate(
            (
                (words[0:main], words[main : 2 * main], words[2 * main : 3 * main]),
                (edges[0:1], edges[1:2], edges[2:3]),
            )
        ):
            line = (mixed >> 1) - edge_ref[FIRST_ROW]
            if side:
                line = line + edge_ref[EDGE_SHIFT]
            cross = half * 2 + (mixed & 1)
            inside = (high > 0) & (line >= -HALO) & (line < BLOCK_ROWS + HALO)
            spot = ((high - 1) * tall + line + HALO) * columns + cross
            spot = jnp.where(inside, spot, DEPTH * tall * columns)
            if side:
                spots[a * (main + 1) + main : (a + 1) * (main + 1), :] = spot
                continue
            spots[a * (main + 1) : a * (main + 1) + main, :] = spot
            inside = (high > 0) & (line >= 0) & (line < BLOCK_ROWS)
            spot = ((high - 1) * BLOCK_ROWS + line) * columns + cross
            owns[a * main : (a + 1) * main, :] = jnp.where(
                inside, spot, DEPTH * BLOCK_ROWS * columns
            )


def scatter_middle_kernel(
    columns, edge_ref, feat_ref, kernel_ref, bias_ref, grid_ref, out_ref, own_ref,
    wide, rows, held, weight_ref, spots, index, copied, done,
):
    list_cells(columns, edge_ref, feat_ref, spots, own_ref)
    to_scalar = pltpu.make_async_copy(spots, index, copied)
    to_scalar.start()
    clear(wide, held.shape[0])
    rows[...] = feat_ref[...].astype(F32)
    to_scalar.wait()
    blocks = CAP // LANES + 1
    length = CAP + EDGE_CAP + 48

    def place(part, carry):
        block = part % blocks
        base = part // blocks * length + block * LANES + jnp.where(block == blocks - 1, 32, 0)

        def eight(i, inner):
            for j in range(8):
                at = i * 8 + j
                wide[pl.ds(index[part, at], 1), :] = rows[pl.ds(base + at, 1), :]
            return inner

        return lax.fori_loop(0, LANES // 8, eight, carry)

    lax.fori_loop(0, index.shape[0], place, 0)
    narrow(wide, held)
    copy = pltpu.make_async_copy(held, grid_ref, done)
    copy.start()
    middle_kernel(columns, edge_ref, held, kernel_ref, bias_ref, out_ref, weight_ref)
    copy.wait()


def scatter_middle(edges, feats, w_mid, bias, columns):
    cells = DEPTH * (BLOCK_ROWS + 2 * HALO) * columns
    count = feats.shape[0]
    sources = count // (CAP + EDGE_CAP + 48)
    parts = sources * (CAP // LANES + 1)
    return pl.pallas_call(
        functools.partial(scatter_middle_kernel, columns),
        out_shape=(
            jax.ShapeDtypeStruct((cells, LANES), BF16),
            jax.ShapeDtypeStruct(((BLOCK_ROWS + 2) * columns, PAIRS * LANES), BF16),
            jax.ShapeDtypeStruct((sources * CAP // LANES, LANES), jnp.int32),
        ),
        in_specs=smem(1) + vmem(3),
        out_specs=[pl.BlockSpec(memory_space=pl.ANY)] + vmem(2),
        scratch_shapes=[
            pltpu.VMEM((cells + 8, LANES), F32),
            pltpu.VMEM((count, LANES), F32),
            pltpu.VMEM((cells, LANES), BF16),
            pltpu.VMEM((2, 9 * LANES, 2 * LANES), BF16),
            pltpu.VMEM((parts, LANES), jnp.int32),
            pltpu.SMEM((parts, LANES), jnp.int32),
            pltpu.SemaphoreType.DMA,
            pltpu.SemaphoreType.DMA,
        ],
        compiler_params=params(),
        cost_estimate=work(36),
        name="scatter_middle",
    )(edges, feats, w_mid, jnp.tile(bias.reshape(1, -1), (8, 2)))


def middle_kernel(columns, edge_ref, grid_ref, kernel_ref, bias_ref, out_ref, weight_ref):
    low = low_lanes(columns)
    none = jnp.zeros((LANES, LANES // 2), BF16)
    for place in range(9):
        one, two, three = (
            kernel_ref[place * 3 + e].astype(F32).T.astype(BF16) for e in range(3)
        )
        rows = slice(place * LANES, (place + 1) * LANES)
        weight_ref[0, rows, :] = jnp.concatenate([one, two, three, none], axis=1)
        weight_ref[1, rows, :] = jnp.concatenate([two, one, none, three], axis=1)
    grid_rows = BLOCK_ROWS + 2 * HALO
    depth_out = DEPTH // 2

    def row(m, carry):
        sums = []
        for o in range(depth_out):
            taps = (1, 2) if o == 0 else (0, 1, 2)
            left = jnp.concatenate(
                [
                    grid_ref[at_row((2 * o + a - 1) * grid_rows + m + b, columns), :]
                    for a in taps
                    for b in range(3)
                ],
                axis=1,
            )
            right = weight_ref[o % 2, 3 * LANES * (3 - len(taps)) :, :]
            sums.append(jnp.dot(left, right, preferred_element_type=F32))
        inside = (m > 0) & (m < BLOCK_ROWS + 1) | (m == 0) & (edge_ref[0] > 0)
        inside = inside | (m == BLOCK_ROWS + 1) & (edge_ref[1] > 0)
        keep = jnp.where(inside, 1.0, 0.0)
        for j in range(PAIRS):
            even = sums[2 * j]
            if 2 * j + 1 < depth_out:
                odd = sums[2 * j + 1]
                first = jnp.where(low, even[:, :LANES], odd[:, :LANES])
                middle = jnp.where(low, odd[:, :LANES], even[:, :LANES])
                last = even[:, LANES:] + odd[:, LANES:]
            else:
                first = even[:, :LANES]
                middle = first
                last = even[:, LANES:]
            total = from_left(first) + pltpu.roll(middle, LANES // 2, 1) + from_right(last)
            total = jnp.maximum(total + bias_ref[0:1, :], 0.0) * keep
            if 2 * j + 1 == depth_out:
                total = jnp.where(low, total, 0.0)
            out_ref[at_row(m, columns), j * LANES : (j + 1) * LANES] = total.astype(BF16)
        return carry

    lax.fori_loop(0, BLOCK_ROWS + 2, row, 0, unroll=2)


def middle_forward(edges, grid, w_mid, bias, columns):
    return pl.pallas_call(
        functools.partial(middle_kernel, columns),
        out_shape=jax.ShapeDtypeStruct(((BLOCK_ROWS + 2) * columns, PAIRS * LANES), BF16),
        in_specs=smem(1) + vmem(3),
        out_specs=vmem(1)[0],
        scratch_shapes=[pltpu.VMEM((2, 9 * LANES, 2 * LANES), BF16)],
        compiler_params=params(),
        cost_estimate=work(26),
        name="middle_forward",
    )(edges, grid, w_mid, jnp.tile(bias.reshape(1, -1), (8, 2)))


def row_above(edge_ref, beside_ref, across_ref, lanes):
    found = jnp.where(
        edge_ref[EVEN] > 0, across_ref[:, lanes].astype(F32), beside_ref[:, lanes].astype(F32)
    )
    return jnp.where(edge_ref[TOP] > 0, found, 0.0)


def row_below(edge_ref, beside_ref, across_ref, lanes):
    found = jnp.where(
        edge_ref[EVEN] > 0, beside_ref[:, lanes].astype(F32), across_ref[:, lanes].astype(F32)
    )
    return jnp.where(edge_ref[BOTTOM] > 0, found, 0.0)


def put_edges(edge_ref, beside_ref, across_ref, first, last):
    if first is not None:

        @pl.when(edge_ref[EVEN] > 0)
        def _():
            across_ref[...] = first

        @pl.when(edge_ref[EVEN] == 0)
        def _():
            beside_ref[...] = first

    if last is not None:

        @pl.when(edge_ref[EVEN] > 0)
        def _():
            beside_ref[...] = last

        @pl.when(edge_ref[EVEN] == 0)
        def _():
            across_ref[...] = last


def column_taps(own, j):
    low = low_lanes(own.shape[0])
    other = pltpu.roll(own, LANES // 2, 1)
    both = [jnp.where(low, own, other)]
    if 2 * j + 1 < DEPTH // 2:
        both.append(jnp.where(low, other, own))
    return [(jnp.where(low, from_right(x), x), from_left(x)) for x in both]


def middle_data_kernel(
    count, columns, index_ref, edge_ref, d_ref, beside_ref, across_ref, kernel_ref, out_ref,
    near, far, wide, rows, weight_ref,
):
    padded = BLOCK_ROWS + 2
    half = LANES // 2
    cells = DEPTH * BLOCK_ROWS * columns
    span = 10 * half
    for a, first, side in ((1, 0, 0), (2, 0, 1), (0, span, 1)):
        lanes = slice(side * LANES, (side + 1) * LANES)
        for b in range(3):
            for e in range(3):
                block = (2 - b) * 2 + e if e < 2 else 6 + 2 - b
                own = kernel_ref[(a * 3 + b) * 3 + e]
                weight_ref[first + block * half : first + (block + 1) * half, lanes] = own
        weight_ref[first + span - half : first + span, lanes] = jnp.zeros((half, LANES), BF16)
    weight_ref[span:, :LANES] = jnp.zeros((span, LANES), BF16)

    def build(r, load):
        for j in range(PAIRS):
            own = load(slice(j * LANES, (j + 1) * LANES))
            for k, (pair, left) in enumerate(column_taps(own, j)):
                o = 2 * j + k
                near[o, at_row(r, columns), :] = pair.astype(BF16)
                far[o, at_row(r, columns), 0:half] = left[:, 0:half].astype(BF16)
                if not (isinstance(r, int) and r == 0):
                    far[o, at_row(r - 1, columns), half:LANES] = left[:, half:].astype(BF16)

    def build_own(r, carry):
        build(r + 1, lambda lanes: d_ref[at_row(r, columns), lanes].astype(F32))
        return carry

    build(0, lambda lanes: row_above(edge_ref, beside_ref, across_ref, lanes))
    lax.fori_loop(0, BLOCK_ROWS, build_own, 0)
    build(BLOCK_ROWS + 1, lambda lanes: row_below(edge_ref, beside_ref, across_ref, lanes))
    for o in range(DEPTH // 2):
        far[o, (padded - 1) * columns :, half:LANES] = jnp.zeros((columns, half), BF16)

    def row(r, carry):
        def pieces(o):
            return [near[o, at_row(r + i, columns), :] for i in range(3)] + [
                far[o, at_row(r + i, columns), :] for i in (0, 2)
            ]

        for o in range(DEPTH // 2):
            left = jnp.concatenate(pieces(o) + (pieces(o + 1) if o < DEPTH // 2 - 1 else []), axis=1)
            total = jnp.dot(left, weight_ref[0 : left.shape[1], :], preferred_element_type=F32)
            wide[at_row(2 * o * BLOCK_ROWS + r, columns), :] = total[:, :LANES]
            wide[at_row((2 * o + 1) * BLOCK_ROWS + r, columns), :] = total[:, LANES:]
        return carry

    lax.fori_loop(0, BLOCK_ROWS, row, 0, unroll=2)
    wide[cells:, :] = jnp.zeros((8, LANES), F32)

    def pick(part, carry):
        def eight(i, inner):
            for j in range(8):
                at = i * 8 + j
                rows[pl.ds(part * LANES + at, 1), :] = wide[pl.ds(index_ref[part, at], 1), :]
            return inner

        return lax.fori_loop(0, LANES // 8, eight, carry)

    lax.fori_loop(0, count // LANES, pick, 0)
    out_ref[...] = rows[...].astype(BF16)


def middle_data(index, edges, d_rows, beside, across, w_mid, columns):
    count = index.size
    padded = (BLOCK_ROWS + 2) * columns
    return pl.pallas_call(
        functools.partial(middle_data_kernel, count, columns),
        out_shape=jax.ShapeDtypeStruct((count, LANES), BF16),
        in_specs=smem(2) + vmem(4),
        out_specs=vmem(1)[0],
        scratch_shapes=[
            pltpu.VMEM((DEPTH // 2, padded, LANES), BF16),
            pltpu.VMEM((DEPTH // 2, padded, LANES), BF16),
            pltpu.VMEM((DEPTH * BLOCK_ROWS * columns + 8, LANES), F32),
            pltpu.VMEM((count, LANES), F32),
            pltpu.VMEM((10 * LANES, 2 * LANES), BF16),
        ],
        compiler_params=params(),
        cost_estimate=work(30),
        name="middle_data",
    )(index, edges, d_rows, beside, across, w_mid)


def middle_weight_kernel(
    columns, grid_hbm, d_ref, out_ref, total, taps_ref, turned, grid_ref, arrived
):
    grid_rows = BLOCK_ROWS + 2 * HALO
    half = LANES // 2

    def copy(i):
        ahead = 2 if isinstance(i, int) and i == 0 else 0
        parts = []
        for d in range(DEPTH):
            begin = (d * grid_rows + 2 * i + 3 - ahead) * columns
            rows = pl.ds(begin if isinstance(i, int) else pl.multiple_of(begin, 32), (2 + ahead) * columns)
            parts.append(
                pltpu.make_async_copy(grid_hbm.at[rows, :], grid_ref.at[rows, :], arrived.at[i, d])
            )
        return parts

    for i in range(BLOCK_ROWS // 2):
        for part in copy(i):
            part.start()
    total[...] = jnp.zeros_like(total)
    for part in copy(0):
        part.wait()

    def rows(i, carry):
        @pl.when(i > 0)
        def _():
            for part in copy(i):
                part.wait()

        for k in range(2):
            for j in range(PAIRS):
                own = d_ref[at_row(i * 2 + k, columns), j * LANES : (j + 1) * LANES].astype(F32)
                for n, (pair, left) in enumerate(column_taps(own, j)):
                    place = slice(k * columns, (k + 1) * columns)
                    taps_ref[2 * j + n, place, 0:LANES] = pair.astype(BF16)
                    taps_ref[2 * j + n, place, LANES:] = left.astype(BF16)
        for o in range(DEPTH // 2):
            depth_taps = (1, 2) if o == 0 else (0, 1, 2)
            cells = jnp.concatenate(
                [
                    grid_ref[
                        pl.ds(
                            pl.multiple_of(
                                ((2 * o + a - 1) * grid_rows + i * 2 + 1 + b) * columns, 32
                            ),
                            2 * columns,
                        ),
                        :,
                    ]
                    for a in depth_taps
                    for b in range(3)
                ],
                axis=1,
            )
            part = lax.dot_general(
                taps_ref[o], cells, (((0,), (0,)), ((), ())), preferred_element_type=F32
            )
            if o == 0:
                total[:, 3 * LANES :] += part
            else:
                total[...] += part
        return carry

    lax.fori_loop(0, BLOCK_ROWS // 2, rows, 0, unroll=2)
    low = low_lanes(LANES // 2)
    for place in range(9):
        for side in range(2):
            turned[...] = total[
                side * LANES : (side + 1) * LANES, place * LANES : (place + 1) * LANES
            ].T
            even = turned[pl.ds(0, half, stride=2), :]
            odd = turned[pl.ds(1, half, stride=2), :]
            at = (place * 3 + side * 2) * half
            out_ref[at : at + half, :] = jnp.where(low, even, pltpu.roll(odd, half, 1))
            if side == 0:
                out_ref[at + half : at + 2 * half, :] = jnp.where(
                    low, pltpu.roll(even, half, 1), odd
                )


def middle_weight(grid, d_rows, columns):
    return pl.pallas_call(
        functools.partial(middle_weight_kernel, columns),
        out_shape=jax.ShapeDtypeStruct((27 * LANES // 2, LANES), F32),
        in_specs=[pl.BlockSpec(memory_space=pl.ANY)] + vmem(1),
        out_specs=vmem(1)[0],
        scratch_shapes=[
            pltpu.VMEM((2 * LANES, 9 * LANES), F32),
            pltpu.VMEM((DEPTH // 2, 2 * columns, 2 * LANES), BF16),
            pltpu.VMEM((LANES, LANES), F32),
            pltpu.VMEM(grid.shape, BF16),
            pltpu.SemaphoreType.DMA((BLOCK_ROWS // 2, DEPTH)),
        ],
        compiler_params=params(limit=40),
        cost_estimate=work(26),
        name="middle_weight",
    )(grid, d_rows)


def region_kernel(
    columns,
    scale_ref,
    edge_ref,
    bev_ref,
    weight_ref,
    bias_ref,
    head_ref,
    head_bias_ref,
    labels_ref,
    targets_ref,
    d_ref,
    beside_ref,
    across_ref,
    grad_head_ref,
    sums_ref,
    held,
):
    outs = head_ref.shape[0]
    cells = d_ref.shape[0]
    span = cells // 3
    scale = scale_ref[0, 0]
    head = head_ref[...]
    head_three = jnp.concatenate([head, head, head], axis=0)

    def row(r, carry):
        left = jnp.concatenate([bev_ref[at_row(r + b, columns), :] for b in range(3)], axis=1)
        part = jnp.dot(left, weight_ref[...], preferred_element_type=F32)
        pre = from_left(part[:, :LANES]) + part[:, LANES : 2 * LANES]
        held[at_row(r, columns), :] = pre + from_right(part[:, 2 * LANES :]) + bias_ref[0:1, :]
        return carry

    lax.fori_loop(0, cells // columns, row, 0, unroll=2)
    kind = lax.broadcasted_iota(jnp.int32, (outs, span), 0) % 8 == 0
    grad_head = jnp.zeros((3 * outs, LANES), F32)
    head_sum = jnp.zeros((outs, 1), F32)
    loss_sum = jnp.zeros((outs, 1), F32)
    row_sum = jnp.zeros((8, LANES), F32)
    for i in range(3):
        place = slice(i * span, (i + 1) * span)
        pre = held[place, :]
        act = jnp.maximum(pre, 0.0).astype(BF16)
        heads = lax.dot_general(head, act, (((1,), (1,)), ((), ())), preferred_element_type=F32)
        heads = heads + head_bias_ref[:, 0:1]
        label = labels_ref[:, place]
        positive = jnp.where(label == 1, 1.0, 0.0)
        negative = jnp.where(label == 0, 1.0, 0.0)
        tail = jnp.log1p(jnp.exp(-jnp.abs(heads)))
        soft_up = jnp.maximum(heads, 0.0) + tail
        soft_down = jnp.maximum(-heads, 0.0) + tail
        probab = jax.nn.sigmoid(heads)
        rest = 1.0 - probab
        focal = positive * FOCAL_ALPHA * rest * rest * soft_down
        focal = focal + negative * (1.0 - FOCAL_ALPHA) * probab * probab * soft_up
        d_focal = positive * FOCAL_ALPHA * rest * rest * (-2.0 * probab * soft_down - rest)
        d_focal = d_focal + negative * (1.0 - FOCAL_ALPHA) * probab * probab * (
            2.0 * rest * soft_up + probab
        )
        offset = heads - targets_ref[:, place]
        size = jnp.abs(offset)
        near = size < 1.0 / 9.0
        smooth = jnp.where(near, 4.5 * offset * offset, size - 1.0 / 18.0)
        d_smooth = jnp.where(near, 9.0 * offset, jnp.where(offset > 0.0, 1.0, -1.0))
        losses = jnp.where(kind, focal, 2.0 * positive * smooth)
        loss_sum = loss_sum + jnp.sum(losses, axis=1, keepdims=True)
        d_heads = jnp.where(kind, d_focal, 2.0 * positive * d_smooth) * scale
        head_sum = head_sum + jnp.sum(d_heads, axis=1, keepdims=True)
        high = d_heads.astype(BF16)
        rest_one = d_heads - high.astype(F32)
        mid = rest_one.astype(BF16)
        tiny = (rest_one - mid.astype(F32)).astype(BF16)
        three = jnp.concatenate([high, mid, tiny], axis=0)
        grad_head = grad_head + jnp.dot(three, act, preferred_element_type=F32)
        d_act = lax.dot_general(
            three, head_three, (((0,), (0,)), ((), ())), preferred_element_type=F32
        )
        d_pre = jnp.where(pre > 0.0, d_act, 0.0).astype(BF16)
        d_ref[place, :] = d_pre
        row_sum = row_sum + jnp.sum(d_pre.astype(F32).reshape(span // 8, 8, LANES), axis=0)
        if i == 0:
            put_edges(edge_ref, beside_ref, across_ref, d_pre[:columns, :], None)
        if i == 2:
            put_edges(edge_ref, beside_ref, across_ref, None, d_pre[span - columns :, :])
    grad_head_ref[...] = grad_head
    sums_ref[0:8, :] = row_sum
    sums_ref[8:24, :] = jnp.broadcast_to(head_sum, (outs, LANES))
    sums_ref[24:32, :] = jnp.broadcast_to(jnp.sum(loss_sum, axis=0, keepdims=True), (8, LANES))


def region_forward(scale, edges, bev, weights, bias, head, head_bias, labels, targets, columns):
    cells = labels.shape[1]
    outs = head.shape[0]
    return pl.pallas_call(
        functools.partial(region_kernel, columns),
        out_shape=(
            jax.ShapeDtypeStruct((cells, LANES), BF16),
            jax.ShapeDtypeStruct((columns, LANES), BF16),
            jax.ShapeDtypeStruct((columns, LANES), BF16),
            jax.ShapeDtypeStruct((3 * outs, LANES), F32),
            jax.ShapeDtypeStruct((32, LANES), F32),
        ),
        in_specs=smem(2) + vmem(7),
        out_specs=vmem(5),
        scratch_shapes=[pltpu.VMEM((cells, LANES), F32)],
        compiler_params=params(limit=28),
        cost_estimate=work(16),
        name="region_forward",
    )(
        scale.reshape(1, 1),
        edges,
        bev,
        weights,
        jnp.broadcast_to(bias.reshape(1, -1), (8, LANES)),
        head,
        jnp.broadcast_to(head_bias.reshape(-1, 1), (outs, LANES)),
        labels,
        targets,
    )


def region_order_kernel(part_ref, in_ref, back_ref, wide, lined):
    depth_out = DEPTH // 2
    half = LANES // 2
    width = PAIRS * LANES
    blocks = part_ref.shape[0]
    share = half // blocks
    used = depth_out * half
    for b in range(3):
        for e in range(3):
            for q in range(blocks):
                wide[...] = part_ref[q, b, e].astype(F32)
                for h in range(depth_out):
                    at = h * half + q * share
                    lined[at : at + share, :] = wide[pl.ds(h, share, stride=depth_out), :]
            lined[used:, :] = jnp.zeros((width - used, LANES), F32)
            in_ref[b * width : (b + 1) * width, e * LANES : (e + 1) * LANES] = lined[...].astype(
                BF16
            )
            at = (b * 3 + e) * LANES
            back_ref[at : at + LANES, :] = lined[...].T.astype(BF16)


def region_order(parts):
    width = PAIRS * LANES
    return pl.pallas_call(
        region_order_kernel,
        out_shape=(
            jax.ShapeDtypeStruct((3 * width, 3 * LANES), BF16),
            jax.ShapeDtypeStruct((9 * LANES, width), BF16),
        ),
        in_specs=vmem(1),
        out_specs=vmem(2),
        scratch_shapes=[
            pltpu.VMEM((parts.shape[3], LANES), F32),
            pltpu.VMEM((width, LANES), F32),
        ],
        compiler_params=params(limit=24),
        cost_estimate=work(4),
        name="region_order",
    )(parts)


def region_data_kernel(
    columns, edge_ref, d_ref, beside_in, across_in, bev_ref, weight_ref,
    out_ref, beside_ref, across_ref, sums_ref, taps_ref,
):
    rows = out_ref.shape[0] // columns
    width = PAIRS * LANES
    sums_ref[...] = jnp.zeros_like(sums_ref)

    def build(r, own):
        taps_ref[at_row(r, columns), 0:LANES] = from_right(own).astype(BF16)
        taps_ref[at_row(r, columns), LANES : 2 * LANES] = own.astype(BF16)
        taps_ref[at_row(r, columns), 2 * LANES :] = from_left(own).astype(BF16)

    def build_own(r, carry):
        build(r + 1, d_ref[at_row(r, columns), :].astype(F32))
        return carry

    build(0, row_above(edge_ref, beside_in, across_in, slice(None)))
    lax.fori_loop(0, rows, build_own, 0)
    build(rows + 1, row_below(edge_ref, beside_in, across_in, slice(None)))

    def row(r, carry):
        left = jnp.concatenate([taps_ref[at_row(r + 2 - b, columns), :] for b in range(3)], axis=1)
        total = jnp.dot(left, weight_ref[...], preferred_element_type=F32)
        alive = bev_ref[at_row(r + 1, columns), :].astype(F32) > 0.0
        kept = jnp.where(alive, total, 0.0).astype(BF16)
        out_ref[at_row(r, columns), :] = kept

        @pl.when(r == 0)
        def _():
            put_edges(edge_ref, beside_ref, across_ref, kept, None)

        @pl.when(r == rows - 1)
        def _():
            put_edges(edge_ref, beside_ref, across_ref, None, kept)

        sums_ref[...] += jnp.sum(kept.astype(F32).reshape(columns // 8, 8, width), axis=0)
        return carry

    lax.fori_loop(0, rows, row, 0, unroll=2)


def region_data(edges, d_rows, beside, across, bev, weights, columns):
    width = PAIRS * LANES
    return pl.pallas_call(
        functools.partial(region_data_kernel, columns),
        out_shape=(
            jax.ShapeDtypeStruct((d_rows.shape[0], width), BF16),
            jax.ShapeDtypeStruct((columns, width), BF16),
            jax.ShapeDtypeStruct((columns, width), BF16),
            jax.ShapeDtypeStruct((8, width), F32),
        ),
        in_specs=smem(1) + vmem(5),
        out_specs=vmem(4),
        scratch_shapes=[pltpu.VMEM((d_rows.shape[0] + 2 * columns, 3 * LANES), BF16)],
        compiler_params=params(limit=28),
        cost_estimate=work(13),
        name="region_data",
    )(edges, d_rows, beside, across, bev, weights)


def region_weight_kernel(columns, blocks, d_ref, bev_ref, out_ref, total, taps_ref):
    rows = d_ref.shape[0] // columns
    width = PAIRS * LANES
    depth_out = DEPTH // 2
    half = LANES // 2
    total[...] = jnp.zeros_like(total)

    def two(i, carry):
        for k in range(2):
            own = d_ref[at_row(i * 2 + k, columns), :].astype(F32)
            place = slice(k * columns, (k + 1) * columns)
            taps_ref[place, 0:LANES] = from_right(own).astype(BF16)
            taps_ref[place, LANES : 2 * LANES] = own.astype(BF16)
            taps_ref[place, 2 * LANES :] = from_left(own).astype(BF16)
        cells = jnp.concatenate(
            [
                bev_ref[pl.ds(pl.multiple_of((i * 2 + b) * columns, 32), 2 * columns), :]
                for b in range(3)
            ],
            axis=1,
        )
        total[...] += lax.dot_general(
            taps_ref[...], cells, (((0,), (0,)), ((), ())), preferred_element_type=F32
        )
        return carry

    lax.fori_loop(0, rows // 2, two, 0, unroll=2)
    share = half // blocks
    for b in range(3):
        for e in range(3):
            for j in range(PAIRS):
                start = b * width + j * LANES
                turned = total[e * LANES : (e + 1) * LANES, start : start + LANES].T
                for k in range(min(2, depth_out - 2 * j)):
                    for q in range(blocks):
                        begin = k * half + q * share
                        base = ((q * 3 + b) * 3 + e) * share * depth_out
                        out_ref[pl.ds(base + 2 * j + k, share, stride=depth_out), :] = turned[
                            begin : begin + share, :
                        ]


def region_weight(d_own, bev, columns, blocks):
    width = PAIRS * LANES
    return pl.pallas_call(
        functools.partial(region_weight_kernel, columns, blocks),
        out_shape=jax.ShapeDtypeStruct((9 * (DEPTH // 2) * (LANES // 2), LANES), F32),
        in_specs=vmem(2),
        out_specs=vmem(1)[0],
        scratch_shapes=[
            pltpu.VMEM((3 * LANES, 3 * width), F32),
            pltpu.VMEM((2 * columns, 3 * LANES), BF16),
        ],
        compiler_params=params(limit=28),
        cost_estimate=work(10),
        name="region_weight",
    )(d_own, bev)


def prepare_kernel(
    slots, anc_count, device_rows, edge_ref, points_ref, line_ref, labels_ref,
    stats_ref, place_ref, digit_ref,
):
    voxels, width = points_ref.shape
    features = 7
    row = line_ref[1:2, :]
    exists = line_ref[3:4, :]
    column = line_ref[2:3, :]
    digits = jnp.concatenate(
        [
            (line_ref[0:1, :] + 1) * exists,
            (column >> 1) * exists,
            (row * 2 + (column & 1)) * exists,
            line_ref[4:5, :],
        ],
        axis=0,
    ).astype(F32)
    none = jnp.zeros((LANES - 4, LANES), F32)
    for i in range(voxels // LANES):
        here = slice(i * LANES, (i + 1) * LANES)
        digit_ref[here, :] = jnp.concatenate([digits[:, here], none], axis=0).T.astype(BF16)
    lane = lax.broadcasted_iota(jnp.int32, (CHUNK, width), 1)
    ones_lane = features * slots
    slot = jnp.where(lane == ones_lane, -1, lane % slots)
    total = jnp.zeros((width, width), F32)
    for i in range(voxels // CHUNK):
        here = slice(i * CHUNK, (i + 1) * CHUNK)
        count = digit_ref[here, 3:4].astype(F32).astype(jnp.int32)
        block = jnp.where(slot < count, points_ref[here, :].astype(F32), 0.0).astype(BF16)
        total = total + lax.dot_general(
            block, block, (((0,), (0,)), ((), ())), preferred_element_type=F32
        )
    row_at = lax.broadcasted_iota(jnp.int32, (width, width), 0)
    col_at = lax.broadcasted_iota(jnp.int32, (width, width), 1)
    same = (row_at % slots == col_at % slots) | (row_at == ones_lane)
    total = jnp.where(same & (row_at <= ones_lane) & (col_at < ones_lane), total, 0.0)
    rows = [
        jnp.sum(jnp.where(row_at // slots == k, total, 0.0), axis=0, keepdims=True)
        for k in range(features + 1)
    ]
    stacked = jnp.concatenate(rows, axis=0)
    col_eight = lax.broadcasted_iota(jnp.int32, (8, width), 1)
    lane_eight = lax.broadcasted_iota(jnp.int32, (8, LANES), 1)
    row_eight = lax.broadcasted_iota(jnp.int32, (8, LANES), 0)
    stats = jnp.zeros((8, LANES), F32)
    for k in range(features):
        picked = jnp.sum(jnp.where(col_eight // slots == k, stacked, 0.0), axis=1, keepdims=True)
        stats = stats + jnp.where(lane_eight == k, picked, 0.0)
    counted = jnp.sum(digits[3:4, :], axis=1, keepdims=True)
    hits = jnp.zeros(labels_ref.shape[1:], F32)
    for r in range(labels_ref.shape[0]):
        hits = hits + jnp.where(labels_ref[r] == 1, 1.0, 0.0)
    found = jnp.sum(jnp.sum(hits, axis=1, keepdims=True), axis=0, keepdims=True)
    real = exists > 0
    lists = []
    for q in range(anc_count):
        begin = q * device_rows - HALO
        lists.append(real & (row >= begin) & (row < begin + device_rows + 2 * HALO))
    lists.append(real & (row < HALO) & (edge_ref[0] > 0))
    lists.append(real & (row >= anc_count * device_rows - HALO) & (edge_ref[1] > 0))
    lists += [real & (row < 0)] * (8 - len(lists))
    member = jnp.concatenate([jnp.where(x, 1.0, 0.0) for x in lists], axis=0)
    before = (
        lax.broadcasted_iota(jnp.int32, (LANES, LANES), 0)
        < lax.broadcasted_iota(jnp.int32, (LANES, LANES), 1)
    )
    before = jnp.where(before, 1.0, 0.0).astype(BF16)
    carry = jnp.zeros((8, 1), F32)
    eight = lax.broadcasted_iota(jnp.int32, (8, LANES), 0)
    for i in range(voxels // LANES):
        here = slice(i * LANES, (i + 1) * LANES)
        part = member[:, here]
        ahead = jnp.dot(part.astype(BF16), before, preferred_element_type=F32) + carry
        places = jnp.where(part > 0.0, ahead, -1.0).astype(jnp.int32)
        owner = jnp.zeros((1, LANES), jnp.int32)
        own = jnp.full((1, LANES), -1, jnp.int32)
        for q in range(anc_count):
            mine = (row[:, here] >= q * device_rows) & (row[:, here] < (q + 1) * device_rows)
            mine = mine & real[:, here]
            owner = jnp.where(mine, q, owner)
            own = jnp.where(mine, places[q : q + 1, :], own)
        places = jnp.where(eight == 6, owner, jnp.where(eight == 7, own, places))
        place_ref[:, here] = places
        carry = carry + jnp.sum(part, axis=1, keepdims=True)
    is_edge = lax.broadcasted_iota(jnp.int32, (8, 1), 0) >= anc_count
    need = carry / jnp.where(is_edge, float(EDGE_CAP), float(CAP))
    need = jnp.max(need, axis=0, keepdims=True)
    for k, value in enumerate((counted, found, need)):
        stats = stats + jnp.where((lane_eight == 8) & (row_eight == k), value, 0.0)
    for i in range(stats_ref.shape[0]):
        stats_ref[i] = stats


def prepare(edges, points, lines, labels, anc_count, device_rows, slots, devices):
    voxels = points.shape[0]
    return pl.pallas_call(
        functools.partial(prepare_kernel, slots, anc_count, device_rows),
        out_shape=(
            jax.ShapeDtypeStruct((devices, 8, LANES), F32),
            jax.ShapeDtypeStruct((8, voxels), jnp.int32),
            jax.ShapeDtypeStruct((voxels, LANES), BF16),
        ),
        in_specs=smem(1) + vmem(3),
        out_specs=vmem(3),
        compiler_params=params(limit=24),
        cost_estimate=work(4),
        name="prepare",
    )(edges, points, lines, labels)


def batch_norm(stats, kernel):
    lanes = kernel.shape[1]
    moments = stats[:, 0:8]
    count = stats[0:1, 8:9]
    mixed = jnp.zeros((8, lanes), F32)
    for k in range(7):
        mixed = mixed + moments[:, k : k + 1] * kernel[k : k + 1, :]
    mean = mixed[7:8, :] / count
    second = jnp.sum(mixed * kernel, axis=0, keepdims=True) / count
    inv_std = lax.rsqrt(second - mean * mean + BN_EPSILON)
    return mixed, mean, inv_std, count


def first_layer(points, first_ref, scale, offset, valid):
    hidden = jnp.dot(points, first_ref[...], preferred_element_type=F32)
    act = jnp.where(valid, jnp.maximum(hidden * scale + offset, 0.0), 0.0)
    return act


def group_fold(values, combine):
    groups = values.shape[1] // LANES
    out = values[:, :LANES]
    for g in range(1, groups):
        out = combine(out, values[:, g * LANES : (g + 1) * LANES])
    out = combine(out, pltpu.roll(out, 32, 1))
    return combine(out, pltpu.roll(out, 64, 1))


def second_tail(pooled):
    lane = lax.broadcasted_iota(jnp.int32, pooled.shape, 1)
    return jnp.where(lane < 32, pooled, jnp.where(lane == 32, 1.0, 0.0))


def group_left(low, tail, count, g):
    lane = lax.broadcasted_iota(jnp.int32, tail.shape, 1)
    marked = (lane > 32) & (lane < 37) & (lane - (33 - 4 * g) >= count)
    side = jnp.where(marked, 1.0, tail).astype(BF16)
    return jnp.concatenate([low[:, g * LANES : (g + 1) * LANES], side], axis=1)


def encode_kernel(
    slots, points_ref, count_ref, stats_ref, kernel_ref, gain_ref, first_ref, second_ref,
    feat_ref, share_ref, slot_ref, held,
):
    lanes = first_ref.shape[1]
    _, mean, inv_std, _ = batch_norm(jnp.sum(stats_ref[...], axis=0), kernel_ref[...])
    scale = gain_ref[0:1, :] * inv_std
    offset = gain_ref[1:2, :] - mean * scale
    count = count_ref[:, 3:4].astype(F32).astype(jnp.int32)
    slot = lax.broadcasted_iota(jnp.int32, (CHUNK, lanes), 1) // 32
    act = first_layer(points_ref[...], first_ref, scale, offset, slot < count)
    tail = second_tail(group_fold(act, jnp.maximum))
    low = act.astype(BF16)
    top = jnp.full((CHUNK, LANES), -jnp.inf, F32)
    for g in range(lanes // LANES):
        left = group_left(low, tail, count, g)
        part = jnp.dot(left, second_ref[...], preferred_element_type=F32)
        for s in range(min(4, slots - 4 * g)):
            p = 4 * g + s
            one = part[:, s * LANES : (s + 1) * LANES]
            held[p] = one
            top = jnp.maximum(top, one)
    code = jnp.zeros((CHUNK, LANES), F32)
    for p in range(slots):
        code = code + jnp.where(held[p] == top, 2048.0 + p, 0.0)
    ties = jnp.floor(code / 2048.0)
    feat_ref[...] = jnp.maximum(top, 0.0)
    share_ref[...] = jnp.where(top > 0.0, 1.0 / ties, 0.0)
    slot_ref[...] = jnp.minimum(code - 2048.0 * ties, 127.0).astype(BF16)


def encode(points, counts, stats, kernel, gain, first, second, slots):
    voxels, width = points.shape
    lanes = first.shape[1]
    whole = lambda *shape: pl.BlockSpec(shape, lambda i: (0,) * len(shape))
    block = lambda size: pl.BlockSpec((CHUNK, size), lambda i: (i, 0))
    return pl.pallas_call(
        functools.partial(encode_kernel, slots),
        grid=(voxels // CHUNK,),
        out_shape=(
            jax.ShapeDtypeStruct((voxels, LANES), F32),
            jax.ShapeDtypeStruct((voxels, LANES), F32),
            jax.ShapeDtypeStruct((voxels, LANES), BF16),
        ),
        in_specs=[
            block(width),
            block(LANES),
            whole(*stats.shape),
            whole(8, lanes),
            whole(8, lanes),
            whole(width, lanes),
            whole(2 * LANES, 4 * LANES),
        ],
        out_specs=[block(LANES), block(LANES), block(LANES)],
        scratch_shapes=[pltpu.VMEM((slots, CHUNK, LANES), F32)],
        compiler_params=params("arbitrary", limit=40),
        cost_estimate=work(14),
        name="encode",
    )(points, counts, stats, kernel, gain, first, second)


def decode_kernel(
    slots, points_ref, count_ref, stats_ref, kernel_ref, gain_ref, first_ref, second_ref,
    feat_ref, share_ref, slot_ref, d_feat_ref, loss_ref, out_ref,
    first_sum, second_sum, joined, tail_sum,
):
    lanes = first_ref.shape[1]
    width = points_ref.shape[1]
    step = pl.program_id(0)

    @pl.when(step == 0)
    def _():
        first_sum[...] = jnp.zeros_like(first_sum)
        second_sum[...] = jnp.zeros_like(second_sum)

    _, mean, inv_std, _ = batch_norm(jnp.sum(stats_ref[...], axis=0), kernel_ref[...])
    scale = gain_ref[0:1, :] * inv_std
    offset = gain_ref[1:2, :] - mean * scale
    count = count_ref[:, 3:4].astype(F32).astype(jnp.int32)
    points = points_ref[...]
    slot = lax.broadcasted_iota(jnp.int32, (CHUNK, lanes), 1) // 32
    act = first_layer(points, first_ref, scale, offset, slot < count)
    pooled = group_fold(act, jnp.maximum)
    tail = second_tail(pooled)
    low = act.astype(BF16)
    share = share_ref[...]
    d_feat = d_feat_ref[...] * share
    d_low = d_feat.astype(BF16)
    shared = jnp.where((share > 0.0) & (share < 1.0), 1.0, 0.0)
    shared = jnp.max(jnp.max(shared, axis=1, keepdims=True)) > 0.0

    def group_back(g, left, pieces):
        d_part = jnp.concatenate(pieces, axis=1)
        second_sum[...] += lax.dot_general(
            left, d_part, (((0,), (0,)), ((), ())), preferred_element_type=F32
        )
        d_left = lax.dot_general(
            d_part, second_ref[...], (((1,), (1,)), ((), ())), preferred_element_type=F32
        )
        joined[:, g * LANES : (g + 1) * LANES] = d_left[:, :LANES]
        return d_left[:, LANES:]

    none = jnp.zeros((CHUNK, LANES), BF16)

    @pl.when(jnp.logical_not(shared))
    def _():
        found = slot_ref[...]
        d_tail = jnp.zeros((CHUNK, LANES), F32)
        for g in range(lanes // LANES):
            left = group_left(low, tail, count, g)
            pieces = [
                jnp.where(found == jnp.asarray(4 * g + s, BF16), d_low, none)
                if 4 * g + s < slots
                else none
                for s in range(4)
            ]
            d_tail = d_tail + group_back(g, left, pieces)
        tail_sum[...] = d_tail

    @pl.when(shared)
    def _():
        top = feat_ref[...]
        d_tail = jnp.zeros((CHUNK, LANES), F32)
        for g in range(lanes // LANES):
            left = group_left(low, tail, count, g)
            part = jnp.dot(left, second_ref[...], preferred_element_type=F32)
            pieces = []
            for s in range(4):
                if 4 * g + s < slots:
                    hit = part[:, s * LANES : (s + 1) * LANES] == top
                    pieces.append(jnp.where(hit, d_feat, 0.0).astype(BF16))
                else:
                    pieces.append(none)
            d_tail = d_tail + group_back(g, left, pieces)
        tail_sum[...] = d_tail

    wide = jnp.concatenate([pooled] * (lanes // LANES), axis=1)
    reached = act == wide
    ties = group_fold(jnp.where(reached, 1.0, 0.0), jnp.add)
    lane = lax.broadcasted_iota(jnp.int32, (CHUNK, LANES), 1)
    spread = jnp.where(lane < 32, tail_sum[...], 0.0)
    spread = spread + pltpu.roll(spread, 32, 1)
    spread = (spread + pltpu.roll(spread, 64, 1)) / ties
    spread = jnp.concatenate([spread] * (lanes // LANES), axis=1)
    d_act = joined[...] + jnp.where(reached, spread, 0.0)
    d_act = jnp.where(act > 0.0, d_act, 0.0).astype(BF16)
    first_sum[...] += lax.dot_general(
        points, d_act, (((0,), (0,)), ((), ())), preferred_element_type=F32
    )

    @pl.when(step == pl.num_programs(0) - 1)
    def _():
        row_at = lax.broadcasted_iota(jnp.int32, (width, lanes), 0)
        col_at = lax.broadcasted_iota(jnp.int32, (width, lanes), 1)
        same = (row_at % slots == col_at // 32) | (row_at == 7 * slots)
        total = jnp.where(same & (col_at // 32 < slots), first_sum[...], 0.0)
        rows = [
            jnp.sum(jnp.where(row_at // slots == k, total, 0.0), axis=0, keepdims=True)
            for k in range(8)
        ]
        first = group_fold(jnp.concatenate(rows, axis=0), jnp.add)
        upper = second_sum[0:32, 0:LANES]
        lower = second_sum[LANES : LANES + 40, 0:LANES]
        for s in range(1, 4):
            cols = slice(s * LANES, (s + 1) * LANES)
            upper = upper + second_sum[s * 32 : (s + 1) * 32, cols]
            lower = lower + second_sum[LANES : LANES + 40, cols]
        devices, layers = out_ref.shape[:2]
        none = jnp.zeros((devices * layers - 88, LANES), F32)
        rows = jnp.concatenate([first, upper, lower, loss_ref[...], none], axis=0)
        for k in range(layers):
            out_ref[:, k, :] = rows[k * devices : (k + 1) * devices, :]


def decode(
    points, counts, stats, kernel, gain, first, second, feat, share, slot, d_feat, loss, shape, slots
):
    voxels, width = points.shape
    lanes = first.shape[1]
    whole = lambda *shape: pl.BlockSpec(shape, lambda i: (0,) * len(shape))
    block = lambda size: pl.BlockSpec((CHUNK, size), lambda i: (i, 0))
    return pl.pallas_call(
        functools.partial(decode_kernel, slots),
        grid=(voxels // CHUNK,),
        out_shape=jax.ShapeDtypeStruct(shape + (LANES,), F32),
        in_specs=[
            block(width),
            block(LANES),
            whole(*stats.shape),
            whole(8, lanes),
            whole(8, lanes),
            whole(width, lanes),
            whole(2 * LANES, 4 * LANES),
            block(LANES),
            block(LANES),
            block(LANES),
            block(LANES),
            whole(8, LANES),
        ],
        out_specs=whole(*shape, LANES),
        scratch_shapes=[
            pltpu.VMEM((width, lanes), F32),
            pltpu.VMEM((2 * LANES, 4 * LANES), F32),
            pltpu.VMEM((CHUNK, lanes), F32),
            pltpu.VMEM((CHUNK, LANES), F32),
        ],
        compiler_params=params("arbitrary", limit=40),
        cost_estimate=work(28),
        name="decode",
    )(points, counts, stats, kernel, gain, first, second, feat, share, slot, d_feat, loss)


def encoder_weights(w_one, w_two, bias_two, gain, shift, slots):
    features, c_one = w_one.shape
    groups = -(-slots // 4)
    lanes = groups * LANES
    width = -(-(features * slots + 1) // LANES) * LANES
    row_at = lax.broadcasted_iota(jnp.int32, (width, lanes), 0)
    col_at = lax.broadcasted_iota(jnp.int32, (width, lanes), 1)
    tall = jnp.pad(
        jnp.repeat(w_one, slots, axis=0), ((0, width - features * slots), (0, 0))
    )
    same = (row_at % slots == col_at // c_one) & (row_at < features * slots)
    first = jnp.where(same, jnp.tile(tall, (1, lanes // c_one)), jnp.zeros((), BF16))
    c_two = w_two.shape[1]
    row_two = lax.broadcasted_iota(jnp.int32, (LANES, 4 * c_two), 0)
    col_two = lax.broadcasted_iota(jnp.int32, (LANES, 4 * c_two), 1)
    upper = jnp.where(
        row_two // c_one == col_two // c_two, jnp.tile(w_two[:c_one], (4, 4)), jnp.zeros((), BF16)
    )
    lower = jnp.concatenate([w_two[c_one:], bias_two.reshape(1, -1)], axis=0)
    lower = jnp.tile(jnp.pad(lower, ((0, LANES - lower.shape[0]), (0, 0))), (1, 4))
    lower = jnp.where(row_two == c_one + 1 + col_two // c_two, jnp.asarray(EMPTY, BF16), lower)
    second = jnp.concatenate([upper, lower], axis=0)
    kernel = jnp.pad(w_one.astype(F32), ((0, 1), (0, 0)))
    kernel = jnp.tile(kernel, (1, lanes // c_one))
    rows = jnp.pad(jnp.stack([gain, shift]).astype(F32), ((0, 6), (0, 0)))
    return first, second, kernel, jnp.tile(rows, (1, lanes // c_one))


def pick_rows(source, place_ref, line, capacity, offset):
    want = place_ref[line : line + 1, :] - offset
    row_at = lax.broadcasted_iota(jnp.int32, (capacity, source.shape[0]), 0)
    chosen = jnp.where(want == row_at, 1.0, 0.0).astype(BF16)
    found = jnp.dot(chosen, source, preferred_element_type=F32)
    return found[:, :LANES].astype(BF16), found[:, LANES:].T


def edge_lists_kernel(anc_count, offset_ref, feat_ref, digit_ref, place_ref, up_ref, down_ref):
    source = jnp.concatenate([feat_ref[...].astype(BF16), digit_ref[...]], axis=1)
    for side, edge_ref in enumerate((up_ref, down_ref)):
        rows, digits = pick_rows(source, place_ref, anc_count + side, EDGE_CAP, offset_ref[1])
        edge_ref[0:EDGE_CAP, :] = rows
        digits = jnp.concatenate([digits[0:8, :], jnp.zeros((8, LANES), F32)], axis=0)
        edge_ref[EDGE_CAP : EDGE_CAP + 16, :] = digits.astype(BF16)


def edge_lists(offsets, feat, digits, place, anc_count):
    return pl.pallas_call(
        functools.partial(edge_lists_kernel, anc_count),
        out_shape=(
            jax.ShapeDtypeStruct((EDGE_CAP + 16, LANES), BF16),
            jax.ShapeDtypeStruct((EDGE_CAP + 16, LANES), BF16),
        ),
        in_specs=smem(1) + vmem(3),
        out_specs=vmem(2),
        compiler_params=params(limit=24),
        cost_estimate=work(1),
        name="edge_lists",
    )(offsets, feat, digits, place)


def gather_lists_kernel(anc_count, offset_ref, feat_ref, digit_ref, place_ref, main_ref):
    source = jnp.concatenate([feat_ref[...].astype(BF16), digit_ref[...]], axis=1)
    for q in range(anc_count):
        rows, digits = pick_rows(source, place_ref, q, CAP, offset_ref[0])
        main_ref[q, 0:CAP, :] = rows
        lines = [
            digits[k : k + 1, i * LANES : (i + 1) * LANES]
            for k in range(3)
            for i in range(CAP // LANES)
        ]
        lines.append(jnp.zeros((32 - len(lines), LANES), F32))
        main_ref[q, CAP : CAP + 32, :] = jnp.concatenate(lines, axis=0).astype(BF16)
        main_ref[q, CAP + 32 :, :] = jnp.zeros((EDGE_CAP + 16, LANES), BF16)


def gather_lists(offsets, feat, digits, place, anc_count):
    return pl.pallas_call(
        functools.partial(gather_lists_kernel, anc_count),
        out_shape=jax.ShapeDtypeStruct((anc_count, CAP + EDGE_CAP + 48, LANES), BF16),
        in_specs=smem(1) + vmem(3),
        out_specs=vmem(1)[0],
        compiler_params=params(limit=40),
        cost_estimate=work(5),
        name="gather_lists",
    )(offsets, feat, digits, place)


def spread_lists_kernel(index_ref, received_ref, out_ref, held):
    total = received_ref.shape[0]
    held[0:total, :] = received_ref[...].astype(F32)
    held[total:, :] = jnp.zeros((8, LANES), F32)

    def pick(i, carry):
        for j in range(8):
            out_ref[pl.ds(i * 8 + j, 1), :] = held[pl.ds(index_ref[i * 8 + j], 1), :]
        return carry

    lax.fori_loop(0, out_ref.shape[0] // 8, pick, 0)


def spread_lists(index, received):
    voxels = index.shape[0]
    total = received.shape[0]
    return pl.pallas_call(
        spread_lists_kernel,
        out_shape=jax.ShapeDtypeStruct((voxels, LANES), F32),
        in_specs=smem(1) + vmem(1),
        out_specs=vmem(1)[0],
        scratch_shapes=[pltpu.VMEM((total + 8, LANES), F32)],
        compiler_params=params(limit=24),
        cost_estimate=work(4),
        name="spread_lists",
    )(index, received)


def add_piece(held, source, low, high, start):
    lane = lax.broadcasted_iota(jnp.int32, (1, LANES), 1)
    begin, end = low // LANES, -(-high // LANES)
    gap = start - low
    turn = gap % LANES
    at = begin + gap // LANES
    rows = source[begin:end, :]
    count = end - begin
    place = lax.broadcasted_iota(jnp.int32, (count, LANES), 0) * LANES
    place = place + lax.broadcasted_iota(jnp.int32, (count, LANES), 1) + begin * LANES
    if low % LANES or high % LANES:
        rows = jnp.where((place >= low) & (place < high), rows, 0.0)
    if turn == 0:
        held[at : at + count, :] += rows
        return
    rows = pltpu.roll(rows, turn, 1)
    here = jnp.where(lane >= turn, rows, 0.0)
    after = jnp.where(lane < turn, rows, 0.0)
    skip = max(-at, 0)
    if count > skip:
        held[at + skip : at + count, :] += here[skip:, :]
    held[at + 1 : at + 1 + count, :] += after


def pack_kernel(plan, tiles, chunk, region_ref, middle_ref, head_ref, rest_ref, out_ref, held):
    sources = {"region": region_ref, "middle": middle_ref, "head": head_ref, "rest": rest_ref}
    for a, pieces in enumerate(plan):
        held[...] = jnp.zeros_like(held)
        for name, low, high, start in pieces:
            if name in sources:
                add_piece(held, sources[name], low, high, start)
        for t in range(tiles):
            out_ref[t * len(plan) + a] = held[t * chunk : (t + 1) * chunk, :].astype(BF16)


def pack(plan, tiles, chunk, region, middle, head, rest):
    return pl.pallas_call(
        functools.partial(pack_kernel, plan, tiles, chunk),
        out_shape=jax.ShapeDtypeStruct((tiles * len(plan), chunk, LANES), BF16),
        in_specs=vmem(4),
        out_specs=vmem(1)[0],
        scratch_shapes=[pltpu.VMEM((tiles * chunk, LANES), F32)],
        compiler_params=params(limit=28),
        cost_estimate=work(3),
        name="pack",
    )(region, middle, head, rest)


def sum_chunk_kernel(parts_ref, out_ref, square_ref):
    total = jnp.sum(parts_ref[...].astype(F32), axis=0)
    for i in range(out_ref.shape[0]):
        out_ref[i] = total
    square_ref[...] = jnp.broadcast_to(jnp.sum(total * total), square_ref.shape)


def sum_chunk(parts, tiles):
    _, rows, lanes = parts.shape
    return pl.pallas_call(
        sum_chunk_kernel,
        out_shape=(
            jax.ShapeDtypeStruct((tiles, rows, lanes), F32),
            jax.ShapeDtypeStruct((1, lanes), F32),
        ),
        in_specs=vmem(1),
        out_specs=vmem(2),
        compiler_params=params(limit=24),
        cost_estimate=work(2),
        name="sum_chunk",
    )(parts)


def finish_kernel(
    plan, anc_ref, early_ref, late_ref, stats_ref, kernel_ref, gain_ref,
    out_ref, scalar_ref, one, norm,
):
    stats = jnp.sum(stats_ref[...], axis=0)
    kernel = kernel_ref[:, :LANES]
    mixed, mean, inv_std, count = batch_norm(stats, kernel)
    layers = late_ref.shape[1] - 1
    late = jnp.concatenate([late_ref[:, k, :] for k in range(layers)], axis=0)
    sums = late[0:8, :]
    total_shift = sums[7:8, :]
    total_gain = inv_std * (jnp.sum(kernel * sums, axis=0, keepdims=True) - mean * total_shift)
    slope = gain_ref[0:1, :LANES] * inv_std
    lane = lax.broadcasted_iota(jnp.int32, (1, LANES), 1)
    one[...] = jnp.zeros_like(one)
    norm[...] = jnp.zeros_like(norm)
    for k in range(7):
        first = stats[7:8, k : k + 1]
        pull = total_shift * first + total_gain * inv_std * (mixed[k : k + 1, :] - mean * first)
        grad = jnp.where(lane < 32, slope * (sums[k : k + 1, :] - pull / count), 0.0)
        if k % 4:
            grad = pltpu.roll(grad, 32 * (k % 4), 1)
        one[k // 4 : k // 4 + 1, :] += grad
    bias = late[72:73, :]
    top = jnp.where(lane < 32, total_gain, 0.0)
    top = top + pltpu.roll(jnp.where(lane < 32, total_shift, 0.0), 32, 1)
    norm[0:1, :] = top + jnp.where(lane < 64, 0.0, pltpu.roll(bias, 64, 1))
    norm[1:2, :] = jnp.where(lane < 64, pltpu.roll(bias, 64, 1), 0.0)
    two = late[8:72, :]
    square = jnp.sum(late_ref[:, layers, :]) / LANES
    square = square + jnp.sum(two * two) + jnp.sum(one[...] * one[...])
    square = square + jnp.sum(norm[...] * norm[...])
    size = jnp.sqrt(jnp.broadcast_to(square, (1, LANES)))
    scalar_ref[0:1, :] = late[80:81, :] / stats[1:2, 8:9]
    scalar_ref[1:2, :] = size
    scalar_ref[2:8, :] = jnp.broadcast_to(jnp.minimum(1.0, CLIP_LIMIT / (size + 1e-06)), (6, LANES))
    chunk = early_ref.shape[1]
    for i in range(early_ref.shape[0]):
        out_ref[i * chunk : (i + 1) * chunk, :] = early_ref[i]
    sources = {"one": one, "two": two, "norm": norm}
    for a, pieces in enumerate(plan):

        @pl.when(anc_ref[0] == a)
        def _():
            for name, low, high, start in pieces:
                if name in sources:
                    add_piece(out_ref, sources[name], low, high, start)


def finish(plan, anc, early, late, stats, kernel, gain):
    return pl.pallas_call(
        functools.partial(finish_kernel, plan),
        out_shape=(
            jax.ShapeDtypeStruct((early.shape[0] * early.shape[1], LANES), F32),
            jax.ShapeDtypeStruct((8, LANES), F32),
        ),
        in_specs=smem(1) + vmem(5),
        out_specs=vmem(2),
        scratch_shapes=[pltpu.VMEM((8, LANES), F32), pltpu.VMEM((8, LANES), F32)],
        compiler_params=params(limit=24),
        cost_estimate=work(3),
        name="finish",
    )(anc, early, late, stats, kernel, gain)


def everyone(values, axes):
    count = 1
    for axis in axes:
        count *= lax.axis_size(axis)
    copies = jnp.broadcast_to(values[None], (count,) + values.shape)
    return lax.all_to_all(copies, axes, 0, 0)


def swap_rows(beside, across):
    axes = ("tile", "anc")
    count = lax.axis_size("tile") * lax.axis_size("anc")
    pairs = [(i, i ^ 1) for i in range(count)]
    others = [(i, i + 1) for i in range(1, count - 1, 2)]
    others += [(j, i) for i, j in others]
    return lax.ppermute(beside, axes, pairs), lax.ppermute(across, axes, others)


def shard_windows(segments, shard, count):
    windows = []
    for a in range(count):
        begin, end = a * shard, (a + 1) * shard
        at = 0
        pieces = []
        for name, size in segments:
            low, high = max(begin, at), min(end, at + size)
            if low < high:
                pieces.append((name, low - at, high - at, low - begin))
            at += size
        windows.append(tuple(pieces))
    return tuple(windows)


def on_device(
    points,
    npoints,
    coords,
    labels,
    targets,
    w_vfe1,
    w_vfe2,
    w_mid,
    w_rpn,
    w_head,
    bn_gain,
    biases,
    master,
    moment1,
    moment2,
):
    both = ("tile", "anc")
    anc_count = lax.axis_size("anc")
    tile_count = lax.axis_size("tile")
    anc = lax.axis_index("anc")
    tile = lax.axis_index("tile")
    device_rows = labels.shape[1]
    columns = labels.shape[2]
    blocks = device_rows // BLOCK_ROWS
    tile_rows = device_rows * anc_count
    all_rows = tile_rows * tile_count
    slots = points.shape[1]
    voxels = points.shape[2]
    c_vfe = w_vfe1.shape[1]
    c_vox = w_vfe2.shape[1]
    c_mid = w_mid.shape[4]
    c_rpn = w_rpn.shape[3]
    outs = w_head.shape[1]
    shift = biases[:c_vfe]
    bias_two = biases[c_vfe : c_vfe + c_vox]
    bias_mid, bias_rpn, bias_head = jnp.split(
        biases[c_vfe + c_vox :].astype(F32), [c_mid, c_mid + c_rpn]
    )

    def joined(row):
        return (row % CROP_ROWS != CROP_ROWS // 2) & (row > 0) & (row < all_rows)

    padded = -(-voxels // CHUNK) * CHUNK
    width = -(-(points.shape[0] * slots + 1) // LANES) * LANES
    flat_points = points.reshape(-1, voxels).T
    flat_points = jnp.pad(
        flat_points, ((0, padded - voxels), (0, width - flat_points.shape[1]))
    )
    lane = lax.broadcasted_iota(jnp.int32, flat_points.shape, 1)
    flat_points = jnp.where(lane == points.shape[0] * slots, jnp.ones((), BF16), flat_points)
    spare = (0, padded - voxels)
    row = coords[:, 1] - tile * tile_rows
    lines = [coords[:, 0], row, coords[:, 2], jnp.ones_like(row), npoints]
    lines = jnp.pad(jnp.stack(lines), ((0, 3), spare))
    tile_edges = jnp.stack([joined(tile * tile_rows), joined((tile + 1) * tile_rows)])
    devices = anc_count * tile_count
    parts = everyone(w_rpn, ("anc",))
    stats, place, digits = prepare(
        tile_edges.astype(jnp.int32),
        flat_points,
        lines,
        labels.transpose(1, 0, 2),
        anc_count,
        device_rows,
        slots,
        devices,
    )
    stats, parts = lax.optimization_barrier((stats, parts))
    stats = lax.all_to_all(stats, both, 0, 0)
    region_in, region_back = region_order(parts)
    counts = digits
    count_pos = jnp.sum(stats[:, 1, 8])
    rounds = jnp.ceil(jnp.max(stats[:, 2, 8])).astype(jnp.int32)
    middle_kernel_all = w_mid.transpose(0, 1, 2, 4, 3).reshape(-1, c_mid, c_vox)

    first, second, kernel, gain_rows = encoder_weights(
        w_vfe1, w_vfe2, bias_two, bn_gain, shift, slots
    )
    feat, share, found = encode(
        flat_points, counts, stats, kernel, gain_rows, first, second, slots
    )
    feat, region_in, region_back = lax.optimization_barrier((feat, region_in, region_back))

    in_tile = lax.axis_size("tile")
    upward = [(i + 1, i) for i in range(in_tile - 1)]
    downward = [(i, i + 1) for i in range(in_tile - 1)]

    def exchange(number):
        offsets = jnp.stack([number * CAP, number * EDGE_CAP]).astype(jnp.int32)
        up, down = edge_lists(offsets, feat, digits, place, anc_count)
        from_below = lax.ppermute(up, "tile", upward)
        from_above = lax.ppermute(down, "tile", downward)
        main = gather_lists(offsets, feat, digits, place, anc_count)
        main, from_below, from_above = lax.optimization_barrier((main, from_below, from_above))
        main = lax.dynamic_update_slice(main, from_above[None], (0, CAP + 32, 0))
        main = lax.dynamic_update_slice(main, from_below[None], (anc_count - 1, CAP + 32, 0))
        return lax.all_to_all(main, "anc", 0, 0)

    def cells(got):
        words = got[:, CAP : CAP + 32].reshape(anc_count, -1).astype(jnp.int32)
        start = CAP + 32 + EDGE_CAP
        edge_words = got[:, start : start + 16].astype(jnp.int32)

        def word(k):
            gap = jnp.zeros((anc_count, 32), jnp.int32)
            parts = [words[:, k * CAP : (k + 1) * CAP], gap, edge_words[:, k], gap[:, :16]]
            return jnp.concatenate(parts, axis=1)

        high, half, mixed = word(0), word(1), word(2)
        local = mixed // 2 - anc * device_rows
        is_edge = lax.broadcasted_iota(jnp.int32, local.shape, 1) >= CAP
        local = local + jnp.where(is_edge, jnp.where(anc == 0, -tile_rows, tile_rows), 0)
        cross = half * 2 + mixed % 2
        scatter_at, own_at = [], []
        for k in range(blocks):
            line = local - k * BLOCK_ROWS
            tall = BLOCK_ROWS + 2 * HALO
            inside = (high > 0) & (line >= -HALO) & (line < BLOCK_ROWS + HALO)
            spot = ((high - 1) * tall + line + HALO) * columns + cross
            scatter_at.append(jnp.where(inside, spot, DEPTH * tall * columns).reshape(-1))
            inside = (high > 0) & (line >= 0) & (line < BLOCK_ROWS)
            spot = ((high - 1) * BLOCK_ROWS + line) * columns + cross
            spot = jnp.where(inside, spot, DEPTH * BLOCK_ROWS * columns)
            own_at.append(spot[:, :CAP].reshape(-1, LANES))
        return scatter_at, own_at

    got = exchange(0)
    first_row = tile * tile_rows + anc * device_rows
    edges = []
    even = (tile * anc_count + anc) % 2 == 0
    for k in range(blocks):
        top = first_row + k * BLOCK_ROWS
        flags = [
            joined(top),
            joined(top + BLOCK_ROWS),
            even,
            anc * device_rows + k * BLOCK_ROWS,
            jnp.where(anc == 0, -tile_rows, tile_rows),
        ]
        edges.append(jnp.stack([flag.astype(jnp.int32) for flag in flags]))

    def more(state):
        return state[0] < rounds

    def another(state):
        number, held = state
        rows = exchange(number)
        index, _ = cells(rows)
        rows = rows.reshape(-1, LANES)
        held = [scatter_rows(at, rows, old, columns) for at, old in zip(index, held)]
        return number + 1, held

    def one_round():
        made = [
            scatter_middle(
                edges[k], got.reshape(-1, LANES), middle_kernel_all, bias_mid, columns
            )
            for k in range(blocks)
        ]
        return tuple([one[i] for one in made] for i in range(3))

    def many_rounds():
        index, own = cells(got)
        held = [scatter_rows(at, got.reshape(-1, LANES), None, columns) for at in index]
        _, held = lax.while_loop(more, another, (jnp.int32(1), held))
        bevs = [
            middle_forward(edges[k], held[k], middle_kernel_all, bias_mid, columns)
            for k in range(blocks)
        ]
        return held, bevs, own

    grids, bevs, own_at = lax.cond(rounds > 1, many_rounds, one_round)

    wide_labels = jnp.repeat(labels.reshape(2, -1), outs // 2, axis=0)
    wide_targets = jnp.pad(targets, ((0, 0), (1, 0), (0, 0), (0, 0))).reshape(outs, -1)
    step = BLOCK_ROWS * columns
    scale = 1.0 / count_pos
    d_rows, head_sums, row_sums = [], 0.0, 0.0
    d_beside, d_across = [], []
    for k in range(blocks):
        here = slice(k * step, (k + 1) * step)
        d_block, near_row, far_row, heads, sums = region_forward(
            scale,
            edges[k],
            bevs[k],
            region_in,
            bias_rpn,
            w_head.T,
            bias_head,
            wide_labels[:, here],
            wide_targets[:, here],
            columns,
        )
        d_rows.append(d_block)
        d_beside.append(near_row)
        d_across.append(far_row)
        head_sums = head_sums + heads
        row_sums = row_sums + sums

    def swapped(near, far):
        if blocks == 1:
            got_near, got_far = swap_rows(near[0], far[0])
            return [got_near], [got_far]
        firsts = [jnp.where(even, f, n) for n, f in zip(near, far)]
        lasts = [jnp.where(even, n, f) for n, f in zip(near, far)]
        got_near, got_far = swap_rows(
            jnp.where(even, lasts[-1], firsts[0]), jnp.where(even, firsts[0], lasts[-1])
        )
        above = [jnp.where(even, got_far, got_near)] + lasts[:-1]
        below = firsts[1:] + [jnp.where(even, got_near, got_far)]
        return (
            [jnp.where(even, y, x) for x, y in zip(above, below)],
            [jnp.where(even, x, y) for x, y in zip(above, below)],
        )

    beside, across = swapped(d_beside, d_across)
    grad_region = sum(
        region_weight(d_rows[k], bevs[k], columns, anc_count) for k in range(blocks)
    )
    d_rows, grad_region, beside, across = lax.optimization_barrier(
        (d_rows, grad_region, beside, across)
    )
    d_mids, mid_sums = [], 0.0
    mid_beside, mid_across = [], []
    for k in range(blocks):
        d_block, near_row, far_row, sums = region_data(
            edges[k], d_rows[k], beside[k], across[k], bevs[k], region_back, columns
        )
        d_mids.append(d_block)
        mid_beside.append(near_row)
        mid_across.append(far_row)
        mid_sums = mid_sums + sums
    beside, across = swapped(mid_beside, mid_across)
    grad_mid = sum(middle_weight(grids[k], d_mids[k], columns) for k in range(blocks))
    grad_mid, beside, across = lax.optimization_barrier((grad_mid, beside, across))

    head_three = head_sums.reshape(3, outs, c_rpn)
    grad_head = (head_three[0] + head_three[1] + head_three[2]).T
    grad_bias_mid = jnp.sum(mid_sums, axis=0)[: c_mid * DEPTH // 2].reshape(-1, c_mid).sum(axis=0)
    grad_bias_rpn = jnp.sum(row_sums[:8], axis=0)
    head_rows = grad_head.reshape(-1, LANES)
    rest = jnp.concatenate([grad_bias_mid, grad_bias_rpn, row_sums[8 : 8 + outs, 0]])
    segments = (
        ("region", grad_region.size),
        ("one", w_vfe1.size),
        ("two", w_vfe2.size),
        ("middle", grad_mid.size),
        ("head", w_head.size),
        ("norm", c_vfe + c_vfe + c_vox),
        ("rest", rest.shape[0]),
    )
    rest_rows = jnp.pad(rest, (0, -rest.shape[0] % LANES)).reshape(-1, LANES)
    shard = master.shape[0]
    plan = shard_windows(segments, shard, anc_count)
    chunk_rows = -(-(shard // LANES + 2) // (8 * tile_count)) * 8
    packed = pack(
        plan, tile_count, chunk_rows, grad_region, grad_mid, head_rows, rest_rows
    )
    own_at, packed = lax.optimization_barrier((own_at, packed))
    chunk, chunk_square = sum_chunk(lax.all_to_all(packed, both, 0, 0), tile_count)

    def collect(number, own_index, chunk):
        lists = sum(
            middle_data(
                own_index[k], edges[k], d_mids[k], beside[k], across[k], middle_kernel_all, columns
            )
            for k in range(blocks)
        )
        lists, chunk = lax.optimization_barrier((lists, chunk))
        back = lax.all_to_all(lists.reshape(anc_count, CAP, LANES), "anc", 0, 0)
        mine = place[7] - number * CAP
        known = (mine >= 0) & (mine < CAP)
        index = jnp.where(known, place[6] * CAP + mine, anc_count * CAP)
        return spread_lists(index, back.reshape(-1, LANES)), chunk

    d_feat, chunk = collect(0, own_at, chunk)
    early = lax.all_to_all(chunk, "tile", 0, 0)

    def collect_more(state):
        number, held = state
        _, index = cells(exchange(number))
        return number + 1, held + collect(number, index, ())[0]

    d_feat = lax.cond(
        rounds > 1,
        lambda held: lax.while_loop(more, collect_more, (jnp.int32(1), held))[1],
        lambda held: held,
        d_feat,
    )
    layers = -(-88 // devices)
    late = decode(
        flat_points,
        counts,
        stats,
        kernel,
        gain_rows,
        first,
        second,
        feat,
        share,
        found,
        d_feat,
        row_sums[24:32],
        (devices, layers),
        slots,
    )
    late, early = lax.optimization_barrier((late, early))
    late = jnp.sum(lax.all_to_all(late, both, 0, 0), axis=0)
    late = everyone(jnp.concatenate([late, chunk_square], axis=0), both)
    reduced, scalars = finish(plan, anc.reshape(1), early, late, stats, kernel, gain_rows)
    loss = scalars[0, 0]
    norm_value = scalars[1, 0]
    reduced = reduced.reshape(-1)[:shard]
    clipped = reduced * scalars[2, 0]
    first_new = BETA_FIRST * moment1 + (1.0 - BETA_FIRST) * clipped
    second_new = BETA_SECOND * moment2 + (1.0 - BETA_SECOND) * clipped * clipped
    first_hat = first_new / (1.0 - BETA_FIRST**STEP_NUMBER)
    second_hat = second_new / (1.0 - BETA_SECOND**STEP_NUMBER)
    updated = master - LEARN_RATE * (
        first_hat / (jnp.sqrt(second_hat) + ADAM_EPSILON) + WEIGHT_DECAY * master
    )
    return (updated, first_new, second_new, loss, norm_value)


def solution(mesh):
    placed = (
        P(None, None, ("tile", "anc")),
        P(("tile", "anc")),
        P(("tile", "anc"), None),
        P(None, ("tile", "anc"), None),
        P(None, None, ("tile", "anc"), None),
        P(),
        P(),
        P(),
        P(None, None, "anc", None),
        P(),
        P(),
        P(),
        P("anc"),
        P("anc"),
        P("anc"),
    )
    return jax.shard_map(
        on_device,
        mesh=mesh,
        in_specs=placed,
        out_specs=(P("anc"), P("anc"), P("anc"), P(), P()),
        check_vma=False,
    )
```

```python
import functools
import jax
import jax.numpy as jnp
from jax import lax
from jax.experimental import pallas as pl
from jax.experimental.pallas import tpu as pltpu
from jax.sharding import PartitionSpec as P

DEPTH = 10
PAIRS = DEPTH // 4 + 1
CROP_ROWS = 192
BLOCK_ROWS = 12
HALO = 2
LANES = 128
CHUNK = 384
CAP = 768
EDGE_CAP = 128
EMPTY = -1e30
FOCAL_ALPHA = 0.25
BN_EPSILON = 0.001
CLIP_LIMIT = 0.05
LEARN_RATE = 0.03
BETA_FIRST = 0.9
BETA_SECOND = 0.999
WEIGHT_DECAY = 0.01
ADAM_EPSILON = 1e-08
STEP_NUMBER = 10
F32 = jnp.float32
BF16 = jnp.bfloat16


def vmem(count):
    return [pl.BlockSpec(memory_space=pltpu.VMEM)] * count


def smem(count):
    return [pl.BlockSpec(memory_space=pltpu.SMEM)] * count


def params(*semantics, limit=60):
    return pltpu.CompilerParams(
        vmem_limit_bytes=limit * 1024 * 1024, dimension_semantics=semantics or None
    )


def work(micros):
    return pl.CostEstimate(flops=micros, transcendentals=0, bytes_accessed=micros * 3_000_000)


def at_row(index, columns):
    if isinstance(index, int):
        return pl.ds(index * columns, columns)
    return pl.ds(pl.multiple_of(index * columns, 32), columns)


def column_edges(columns, lanes):
    place = lax.broadcasted_iota(jnp.int32, (columns, lanes), 0)
    return place == 0, place == columns - 1


def from_left(values):
    columns, lanes = values.shape
    first, _ = column_edges(columns, lanes)
    return jnp.where(first, 0.0, pltpu.roll(values, 1, 0))


def from_right(values):
    columns, lanes = values.shape
    _, last = column_edges(columns, lanes)
    return jnp.where(last, 0.0, pltpu.roll(values, columns - 1, 0))


def low_lanes(columns):
    return lax.broadcasted_iota(jnp.int32, (columns, LANES), 1) < LANES // 2


def clear(wide, cells):
    step = 512

    def begin(i, carry):
        wide[pl.ds(pl.multiple_of(i * step, step), step), :] = jnp.zeros((step, LANES), F32)
        return carry

    lax.fori_loop(0, cells // step, begin, 0)


def narrow(wide, out_ref):
    step = 512

    def finish(i, carry):
        block = pl.ds(pl.multiple_of(i * step, step), step)
        out_ref[block, :] = wide[block, :].astype(BF16)
        return carry

    lax.fori_loop(0, out_ref.shape[0] // step, finish, 0)


def place_rows(count, cells, index_ref, feat_ref, old_ref, out_ref, wide, rows):
    if old_ref is None:
        clear(wide, cells)
    else:
        wide[0:cells, :] = old_ref[...].astype(F32)
    rows[...] = feat_ref[...].astype(F32)

    def place(i, carry):
        for j in range(8):
            wide[pl.ds(index_ref[i * 8 + j], 1), :] = rows[pl.ds(i * 8 + j, 1), :]
        return carry

    lax.fori_loop(0, count // 8, place, 0)
    narrow(wide, out_ref)


def scatter_kernel(count, cells, fresh, *refs):
    if fresh:
        index_ref, feat_ref, out_ref, wide, rows = refs
        place_rows(count, cells, index_ref, feat_ref, None, out_ref, wide, rows)
    else:
        place_rows(count, cells, *refs)


def scatter_rows(index, feats, old, columns):
    cells = DEPTH * (BLOCK_ROWS + 2 * HALO) * columns
    count = index.shape[0]
    fresh = old is None
    return pl.pallas_call(
        functools.partial(scatter_kernel, count, cells, fresh),
        out_shape=jax.ShapeDtypeStruct((cells, LANES), BF16),
        in_specs=smem(1) + vmem(1 if fresh else 2),
        out_specs=vmem(1)[0],
        scratch_shapes=[pltpu.VMEM((cells + 8, LANES), F32), pltpu.VMEM((count, LANES), F32)],
        compiler_params=params(),
        cost_estimate=work(15),
        name="grid_scatter",
    )(*((index, feats) if fresh else (index, feats, old)))


TOP, BOTTOM, EVEN, FIRST_ROW, EDGE_SHIFT = range(5)


def list_cells(columns, edge_ref, feat_ref, spots, owns):
    sources = feat_ref.shape[0] // (CAP + EDGE_CAP + 48)
    main = CAP // LANES
    tall = BLOCK_ROWS + 2 * HALO
    for a in range(sources):
        base = a * (CAP + EDGE_CAP + 48)
        words = feat_ref[base + CAP : base + CAP + 32, :].astype(F32).astype(jnp.int32)
        start = base + CAP + 32 + EDGE_CAP
        edges = feat_ref[start : start + 16, :].astype(F32).astype(jnp.int32)
        for side, (high, half, mixed) in enumerate(
            (
                (words[0:main], words[main : 2 * main], words[2 * main : 3 * main]),
                (edges[0:1], edges[1:2], edges[2:3]),
            )
        ):
            line = (mixed >> 1) - edge_ref[FIRST_ROW]
            if side:
                line = line + edge_ref[EDGE_SHIFT]
            cross = half * 2 + (mixed & 1)
            inside = (high > 0) & (line >= -HALO) & (line < BLOCK_ROWS + HALO)
            spot = ((high - 1) * tall + line + HALO) * columns + cross
            spot = jnp.where(inside, spot, DEPTH * tall * columns)
            if side:
                spots[a * (main + 1) + main : (a + 1) * (main + 1), :] = spot
                continue
            spots[a * (main + 1) : a * (main + 1) + main, :] = spot
            inside = (high > 0) & (line >= 0) & (line < BLOCK_ROWS)
            spot = ((high - 1) * BLOCK_ROWS + line) * columns + cross
            owns[a * main : (a + 1) * main, :] = jnp.where(
                inside, spot, DEPTH * BLOCK_ROWS * columns
            )


def scatter_middle_kernel(
    columns, edge_ref, feat_ref, kernel_ref, bias_ref, grid_ref, out_ref, own_ref,
    wide, rows, held, weight_ref, spots, index, copied, done,
):
    list_cells(columns, edge_ref, feat_ref, spots, own_ref)
    to_scalar = pltpu.make_async_copy(spots, index, copied)
    to_scalar.start()
    clear(wide, held.shape[0])
    rows[...] = feat_ref[...].astype(F32)
    to_scalar.wait()
    blocks = CAP // LANES + 1
    length = CAP + EDGE_CAP + 48

    def place(part, carry):
        block = part % blocks
        base = part // blocks * length + block * LANES + jnp.where(block == blocks - 1, 32, 0)

        base = pl.multiple_of(base, 8)
        for j in range(LANES):
            wide[pl.ds(index[part, j], 1), :] = rows[pl.ds(base + j, 1), :]
        return carry

    lax.fori_loop(0, index.shape[0], place, 0)
    narrow(wide, held)
    copy = pltpu.make_async_copy(held, grid_ref, done)
    copy.start()
    middle_kernel(columns, edge_ref, held, kernel_ref, bias_ref, out_ref, weight_ref)
    copy.wait()


def scatter_middle(edges, feats, w_mid, bias, columns):
    cells = DEPTH * (BLOCK_ROWS + 2 * HALO) * columns
    count = feats.shape[0]
    sources = count // (CAP + EDGE_CAP + 48)
    parts = sources * (CAP // LANES + 1)
    return pl.pallas_call(
        functools.partial(scatter_middle_kernel, columns),
        out_shape=(
            jax.ShapeDtypeStruct((cells, LANES), BF16),
            jax.ShapeDtypeStruct(((BLOCK_ROWS + 2) * columns, PAIRS * LANES), BF16),
            jax.ShapeDtypeStruct((sources * CAP // LANES, LANES), jnp.int32),
        ),
        in_specs=smem(1) + vmem(3),
        out_specs=[pl.BlockSpec(memory_space=pl.ANY)] + vmem(2),
        scratch_shapes=[
            pltpu.VMEM((cells + 8, LANES), F32),
            pltpu.VMEM((count, LANES), F32),
            pltpu.VMEM((cells, LANES), BF16),
            pltpu.VMEM((2, 9 * LANES, 2 * LANES), BF16),
            pltpu.VMEM((parts, LANES), jnp.int32),
            pltpu.SMEM((parts, LANES), jnp.int32),
            pltpu.SemaphoreType.DMA,
            pltpu.SemaphoreType.DMA,
        ],
        compiler_params=params(limit=57),
        cost_estimate=work(36),
        name="scatter_middle",
    )(edges, feats, w_mid, jnp.tile(bias.reshape(1, -1), (8, 2)))


def middle_kernel(columns, edge_ref, grid_ref, kernel_ref, bias_ref, out_ref, weight_ref):
    low = low_lanes(columns)
    none = jnp.zeros((LANES, LANES // 2), BF16)
    for place in range(9):
        one, two, three = (
            kernel_ref[place * 3 + e].astype(F32).T.astype(BF16) for e in range(3)
        )
        rows = slice(place * LANES, (place + 1) * LANES)
        weight_ref[0, rows, :] = jnp.concatenate([one, two, three, none], axis=1)
        weight_ref[1, rows, :] = jnp.concatenate([two, one, none, three], axis=1)
    grid_rows = BLOCK_ROWS + 2 * HALO
    depth_out = DEPTH // 2

    def row(m, carry):
        sums = []
        for o in range(depth_out):
            taps = (1, 2) if o == 0 else (0, 1, 2)
            left = jnp.concatenate(
                [
                    grid_ref[at_row((2 * o + a - 1) * grid_rows + m + b, columns), :]
                    for a in taps
                    for b in range(3)
                ],
                axis=1,
            )
            right = weight_ref[o % 2, 3 * LANES * (3 - len(taps)) :, :]
            sums.append(jnp.dot(left, right, preferred_element_type=F32))
        inside = (m > 0) & (m < BLOCK_ROWS + 1) | (m == 0) & (edge_ref[0] > 0)
        inside = inside | (m == BLOCK_ROWS + 1) & (edge_ref[1] > 0)
        keep = jnp.where(inside, 1.0, 0.0)
        for j in range(PAIRS):
            even = sums[2 * j]
            if 2 * j + 1 < depth_out:
                odd = sums[2 * j + 1]
                first = jnp.where(low, even[:, :LANES], odd[:, :LANES])
                middle = jnp.where(low, odd[:, :LANES], even[:, :LANES])
                last = even[:, LANES:] + odd[:, LANES:]
            else:
                first = even[:, :LANES]
                middle = first
                last = even[:, LANES:]
            total = from_left(first) + pltpu.roll(middle, LANES // 2, 1) + from_right(last)
            total = jnp.maximum(total + bias_ref[0:1, :], 0.0) * keep
            if 2 * j + 1 == depth_out:
                total = jnp.where(low, total, 0.0)
            out_ref[at_row(m, columns), j * LANES : (j + 1) * LANES] = total.astype(BF16)
        return carry

    lax.fori_loop(0, BLOCK_ROWS + 2, row, 0, unroll=2)


def middle_forward(edges, grid, w_mid, bias, columns):
    return pl.pallas_call(
        functools.partial(middle_kernel, columns),
        out_shape=jax.ShapeDtypeStruct(((BLOCK_ROWS + 2) * columns, PAIRS * LANES), BF16),
        in_specs=smem(1) + vmem(3),
        out_specs=vmem(1)[0],
        scratch_shapes=[pltpu.VMEM((2, 9 * LANES, 2 * LANES), BF16)],
        compiler_params=params(),
        cost_estimate=work(26),
        name="middle_forward",
    )(edges, grid, w_mid, jnp.tile(bias.reshape(1, -1), (8, 2)))


def row_above(edge_ref, beside_ref, across_ref, lanes):
    found = jnp.where(
        edge_ref[EVEN] > 0, across_ref[:, lanes].astype(F32), beside_ref[:, lanes].astype(F32)
    )
    return jnp.where(edge_ref[TOP] > 0, found, 0.0)


def row_below(edge_ref, beside_ref, across_ref, lanes):
    found = jnp.where(
        edge_ref[EVEN] > 0, beside_ref[:, lanes].astype(F32), across_ref[:, lanes].astype(F32)
    )
    return jnp.where(edge_ref[BOTTOM] > 0, found, 0.0)


def put_edges(edge_ref, beside_ref, across_ref, first, last):
    if first is not None:

        @pl.when(edge_ref[EVEN] > 0)
        def _():
            across_ref[...] = first

        @pl.when(edge_ref[EVEN] == 0)
        def _():
            beside_ref[...] = first

    if last is not None:

        @pl.when(edge_ref[EVEN] > 0)
        def _():
            beside_ref[...] = last

        @pl.when(edge_ref[EVEN] == 0)
        def _():
            across_ref[...] = last


def column_taps(own, j):
    low = low_lanes(own.shape[0])
    other = pltpu.roll(own, LANES // 2, 1)
    both = [jnp.where(low, own, other)]
    if 2 * j + 1 < DEPTH // 2:
        both.append(jnp.where(low, other, own))
    return [(jnp.where(low, from_right(x), x), from_left(x)) for x in both]


def middle_data_kernel(
    count, columns, index_ref, edge_ref, d_ref, beside_ref, across_ref, kernel_ref, out_ref,
    near, far, wide, rows, weight_ref,
):
    padded = BLOCK_ROWS + 2
    half = LANES // 2
    cells = DEPTH * BLOCK_ROWS * columns
    span = 10 * half
    for a, first, side in ((1, 0, 0), (2, 0, 1), (0, span, 1)):
        lanes = slice(side * LANES, (side + 1) * LANES)
        for b in range(3):
            for e in range(3):
                block = (2 - b) * 2 + e if e < 2 else 6 + 2 - b
                own = kernel_ref[(a * 3 + b) * 3 + e]
                weight_ref[first + block * half : first + (block + 1) * half, lanes] = own
        weight_ref[first + span - half : first + span, lanes] = jnp.zeros((half, LANES), BF16)
    weight_ref[span:, :LANES] = jnp.zeros((span, LANES), BF16)

    def build(r, load):
        for j in range(PAIRS):
            own = load(slice(j * LANES, (j + 1) * LANES))
            for k, (pair, left) in enumerate(column_taps(own, j)):
                o = 2 * j + k
                near[o, at_row(r, columns), :] = pair.astype(BF16)
                far[o, at_row(r, columns), 0:half] = left[:, 0:half].astype(BF16)
                if not (isinstance(r, int) and r == 0):
                    far[o, at_row(r - 1, columns), half:LANES] = left[:, half:].astype(BF16)

    def build_own(r):
        build(r + 1, lambda lanes: d_ref[at_row(r, columns), lanes].astype(F32))

    build(0, lambda lanes: row_above(edge_ref, beside_ref, across_ref, lanes))
    for r in range(3):
        build_own(r)
    for o in range(DEPTH // 2):
        far[o, (padded - 1) * columns :, half:LANES] = jnp.zeros((columns, half), BF16)

    def row(r):
        def pieces(o):
            return [near[o, at_row(r + i, columns), :] for i in range(3)] + [
                far[o, at_row(r + i, columns), :] for i in (0, 2)
            ]

        for o in range(DEPTH // 2):
            left = jnp.concatenate(pieces(o) + (pieces(o + 1) if o < DEPTH // 2 - 1 else []), axis=1)
            total = jnp.dot(left, weight_ref[0 : left.shape[1], :], preferred_element_type=F32)
            wide[at_row(2 * o * BLOCK_ROWS + r, columns), :] = total[:, :LANES]
            wide[at_row((2 * o + 1) * BLOCK_ROWS + r, columns), :] = total[:, LANES:]

    def row_and_build(r, carry):
        row(r)
        build_own(r + 3)
        return carry

    lax.fori_loop(0, BLOCK_ROWS - 3, row_and_build, 0)
    row(BLOCK_ROWS - 3)
    build(BLOCK_ROWS + 1, lambda lanes: row_below(edge_ref, beside_ref, across_ref, lanes))
    row(BLOCK_ROWS - 2)
    row(BLOCK_ROWS - 1)
    wide[cells:, :] = jnp.zeros((8, LANES), F32)

    def pick(part, carry):
        base = pl.multiple_of(part * LANES, LANES)
        for j in range(LANES):
            rows[pl.ds(base + j, 1), :] = wide[pl.ds(index_ref[part, j], 1), :]
        return carry

    lax.fori_loop(0, count // LANES, pick, 0)
    out_ref[...] = rows[...].astype(BF16)


def middle_data(index, edges, d_rows, beside, across, w_mid, columns):
    count = index.size
    padded = (BLOCK_ROWS + 2) * columns
    return pl.pallas_call(
        functools.partial(middle_data_kernel, count, columns),
        out_shape=jax.ShapeDtypeStruct((count, LANES), BF16),
        in_specs=smem(2) + vmem(4),
        out_specs=vmem(1)[0],
        scratch_shapes=[
            pltpu.VMEM((DEPTH // 2, padded, LANES), BF16),
            pltpu.VMEM((DEPTH // 2, padded, LANES), BF16),
            pltpu.VMEM((DEPTH * BLOCK_ROWS * columns + 8, LANES), F32),
            pltpu.VMEM((count, LANES), F32),
            pltpu.VMEM((10 * LANES, 2 * LANES), BF16),
        ],
        compiler_params=params(limit=50),
        cost_estimate=work(30),
        name="middle_data",
    )(index, edges, d_rows, beside, across, w_mid)


def middle_weight_kernel(
    columns, grid_hbm, d_ref, out_ref, total, taps_ref, turned, grid_ref, arrived
):
    grid_rows = BLOCK_ROWS + 2 * HALO
    half = LANES // 2

    def copy(i):
        ahead = 2 if isinstance(i, int) and i == 0 else 0
        parts = []
        for d in range(DEPTH):
            begin = (d * grid_rows + 2 * i + 3 - ahead) * columns
            rows = pl.ds(begin if isinstance(i, int) else pl.multiple_of(begin, 32), (2 + ahead) * columns)
            parts.append(
                pltpu.make_async_copy(grid_hbm.at[rows, :], grid_ref.at[rows, :], arrived.at[i, d])
            )
        return parts

    for i in range(BLOCK_ROWS // 2):
        for part in copy(i):
            part.start()
    total[...] = jnp.zeros_like(total)
    for part in copy(0):
        part.wait()

    def rows(i, carry):
        @pl.when(i > 0)
        def _():
            for part in copy(i):
                part.wait()

        for k in range(2):
            for j in range(PAIRS):
                own = d_ref[at_row(i * 2 + k, columns), j * LANES : (j + 1) * LANES].astype(F32)
                for n, (pair, left) in enumerate(column_taps(own, j)):
                    place = slice(k * columns, (k + 1) * columns)
                    taps_ref[2 * j + n, place, 0:LANES] = pair.astype(BF16)
                    taps_ref[2 * j + n, place, LANES:] = left.astype(BF16)
        for o in range(DEPTH // 2):
            depth_taps = (1, 2) if o == 0 else (0, 1, 2)
            cells = jnp.concatenate(
                [
                    grid_ref[
                        pl.ds(
                            pl.multiple_of(
                                ((2 * o + a - 1) * grid_rows + i * 2 + 1 + b) * columns, 32
                            ),
                            2 * columns,
                        ),
                        :,
                    ]
                    for a in depth_taps
                    for b in range(3)
                ],
                axis=1,
            )
            part = lax.dot_general(
                taps_ref[o], cells, (((0,), (0,)), ((), ())), preferred_element_type=F32
            )
            if o == 0:
                total[:, 3 * LANES :] += part
            else:
                total[...] += part
        return carry

    lax.fori_loop(0, BLOCK_ROWS // 2, rows, 0, unroll=2)
    low = low_lanes(LANES // 2)
    for place in range(9):
        for side in range(2):
            turned[...] = total[
                side * LANES : (side + 1) * LANES, place * LANES : (place + 1) * LANES
            ].T
            even = turned[pl.ds(0, half, stride=2), :]
            odd = turned[pl.ds(1, half, stride=2), :]
            at = (place * 3 + side * 2) * half
            out_ref[at : at + half, :] = jnp.where(low, even, pltpu.roll(odd, half, 1))
            if side == 0:
                out_ref[at + half : at + 2 * half, :] = jnp.where(
                    low, pltpu.roll(even, half, 1), odd
                )


def middle_weight(grid, d_rows, columns):
    return pl.pallas_call(
        functools.partial(middle_weight_kernel, columns),
        out_shape=jax.ShapeDtypeStruct((27 * LANES // 2, LANES), F32),
        in_specs=[pl.BlockSpec(memory_space=pl.ANY)] + vmem(1),
        out_specs=vmem(1)[0],
        scratch_shapes=[
            pltpu.VMEM((2 * LANES, 9 * LANES), F32),
            pltpu.VMEM((DEPTH // 2, 2 * columns, 2 * LANES), BF16),
            pltpu.VMEM((LANES, LANES), F32),
            pltpu.VMEM(grid.shape, BF16),
            pltpu.SemaphoreType.DMA((BLOCK_ROWS // 2, DEPTH)),
        ],
        compiler_params=params(limit=32),
        cost_estimate=work(26),
        name="middle_weight",
    )(grid, d_rows)


def region_kernel(
    columns,
    scale_ref,
    edge_ref,
    bev_ref,
    weight_ref,
    bias_ref,
    head_ref,
    head_bias_ref,
    labels_ref,
    targets_ref,
    d_ref,
    beside_ref,
    across_ref,
    grad_head_ref,
    sums_ref,
    held,
):
    outs = head_ref.shape[0]
    cells = d_ref.shape[0]
    span = cells // 3
    scale = scale_ref[0, 0]
    head = head_ref[...]
    head_three = jnp.concatenate([head, head, head], axis=0)

    def row(r, carry):
        left = jnp.concatenate([bev_ref[at_row(r + b, columns), :] for b in range(3)], axis=1)
        part = jnp.dot(left, weight_ref[...], preferred_element_type=F32)
        pre = from_left(part[:, :LANES]) + part[:, LANES : 2 * LANES]
        held[at_row(r, columns), :] = pre + from_right(part[:, 2 * LANES :]) + bias_ref[0:1, :]
        return carry

    lax.fori_loop(0, cells // columns, row, 0, unroll=2)
    kind = lax.broadcasted_iota(jnp.int32, (outs, span), 0) % 8 == 0
    grad_head = jnp.zeros((3 * outs, LANES), F32)
    head_sum = jnp.zeros((outs, 1), F32)
    loss_sum = jnp.zeros((outs, 1), F32)
    row_sum = jnp.zeros((8, LANES), F32)
    for i in range(3):
        place = slice(i * span, (i + 1) * span)
        pre = held[place, :]
        act = jnp.maximum(pre, 0.0).astype(BF16)
        heads = lax.dot_general(head, act, (((1,), (1,)), ((), ())), preferred_element_type=F32)
        heads = heads + head_bias_ref[:, 0:1]
        label = labels_ref[:, place]
        positive = jnp.where(label == 1, 1.0, 0.0)
        negative = jnp.where(label == 0, 1.0, 0.0)
        tail = jnp.log1p(jnp.exp(-jnp.abs(heads)))
        soft_up = jnp.maximum(heads, 0.0) + tail
        soft_down = jnp.maximum(-heads, 0.0) + tail
        probab = jax.nn.sigmoid(heads)
        rest = 1.0 - probab
        focal = positive * FOCAL_ALPHA * rest * rest * soft_down
        focal = focal + negative * (1.0 - FOCAL_ALPHA) * probab * probab * soft_up
        d_focal = positive * FOCAL_ALPHA * rest * rest * (-2.0 * probab * soft_down - rest)
        d_focal = d_focal + negative * (1.0 - FOCAL_ALPHA) * probab * probab * (
            2.0 * rest * soft_up + probab
        )
        offset = heads - targets_ref[:, place]
        size = jnp.abs(offset)
        near = size < 1.0 / 9.0
        smooth = jnp.where(near, 4.5 * offset * offset, size - 1.0 / 18.0)
        d_smooth = jnp.where(near, 9.0 * offset, jnp.where(offset > 0.0, 1.0, -1.0))
        losses = jnp.where(kind, focal, 2.0 * positive * smooth)
        loss_sum = loss_sum + jnp.sum(losses, axis=1, keepdims=True)
        d_heads = jnp.where(kind, d_focal, 2.0 * positive * d_smooth) * scale
        head_sum = head_sum + jnp.sum(d_heads, axis=1, keepdims=True)
        high = d_heads.astype(BF16)
        rest_one = d_heads - high.astype(F32)
        mid = rest_one.astype(BF16)
        tiny = (rest_one - mid.astype(F32)).astype(BF16)
        three = jnp.concatenate([high, mid, tiny], axis=0)
        grad_head = grad_head + jnp.dot(three, act, preferred_element_type=F32)
        d_act = lax.dot_general(
            three, head_three, (((0,), (0,)), ((), ())), preferred_element_type=F32
        )
        d_pre = jnp.where(pre > 0.0, d_act, 0.0).astype(BF16)
        d_ref[place, :] = d_pre
        row_sum = row_sum + jnp.sum(d_pre.astype(F32).reshape(span // 8, 8, LANES), axis=0)
        if i == 0:
            put_edges(edge_ref, beside_ref, across_ref, d_pre[:columns, :], None)
        if i == 2:
            put_edges(edge_ref, beside_ref, across_ref, None, d_pre[span - columns :, :])
    grad_head_ref[...] = grad_head
    sums_ref[0:8, :] = row_sum
    sums_ref[8:24, :] = jnp.broadcast_to(head_sum, (outs, LANES))
    sums_ref[24:32, :] = jnp.broadcast_to(jnp.sum(loss_sum, axis=0, keepdims=True), (8, LANES))


def region_forward(scale, edges, bev, weights, bias, head, head_bias, labels, targets, columns):
    cells = labels.shape[1]
    outs = head.shape[0]
    return pl.pallas_call(
        functools.partial(region_kernel, columns),
        out_shape=(
            jax.ShapeDtypeStruct((cells, LANES), BF16),
            jax.ShapeDtypeStruct((columns, LANES), BF16),
            jax.ShapeDtypeStruct((columns, LANES), BF16),
            jax.ShapeDtypeStruct((3 * outs, LANES), F32),
            jax.ShapeDtypeStruct((32, LANES), F32),
        ),
        in_specs=smem(2) + vmem(7),
        out_specs=vmem(5),
        scratch_shapes=[pltpu.VMEM((cells, LANES), F32)],
        compiler_params=params(limit=28),
        cost_estimate=work(16),
        name="region_forward",
    )(
        scale.reshape(1, 1),
        edges,
        bev,
        weights,
        jnp.broadcast_to(bias.reshape(1, -1), (8, LANES)),
        head,
        jnp.broadcast_to(head_bias.reshape(-1, 1), (outs, LANES)),
        labels,
        targets,
    )


def region_order_kernel(part_ref, in_ref, back_ref, wide, lined):
    depth_out = DEPTH // 2
    half = LANES // 2
    width = PAIRS * LANES
    blocks = part_ref.shape[0]
    share = half // blocks
    used = depth_out * half
    for b in range(3):
        for e in range(3):
            for q in range(blocks):
                wide[...] = part_ref[q, b, e].astype(F32)
                for h in range(depth_out):
                    at = h * half + q * share
                    lined[at : at + share, :] = wide[pl.ds(h, share, stride=depth_out), :]
            lined[used:, :] = jnp.zeros((width - used, LANES), F32)
            in_ref[b * width : (b + 1) * width, e * LANES : (e + 1) * LANES] = lined[...].astype(
                BF16
            )
            at = (b * 3 + e) * LANES
            back_ref[at : at + LANES, :] = lined[...].T.astype(BF16)


def region_order(parts):
    width = PAIRS * LANES
    return pl.pallas_call(
        region_order_kernel,
        out_shape=(
            jax.ShapeDtypeStruct((3 * width, 3 * LANES), BF16),
            jax.ShapeDtypeStruct((9 * LANES, width), BF16),
        ),
        in_specs=vmem(1),
        out_specs=vmem(2),
        scratch_shapes=[
            pltpu.VMEM((parts.shape[3], LANES), F32),
            pltpu.VMEM((width, LANES), F32),
        ],
        compiler_params=params(limit=24),
        cost_estimate=work(4),
        name="region_order",
    )(parts)


def region_data_kernel(
    columns, edge_ref, d_ref, beside_in, across_in, bev_ref, weight_ref,
    out_ref, beside_ref, across_ref, sums_ref, taps_ref,
):
    rows = out_ref.shape[0] // columns
    width = PAIRS * LANES
    sums_ref[...] = jnp.zeros_like(sums_ref)

    def build(r, own):
        taps_ref[at_row(r, columns), 0:LANES] = from_right(own).astype(BF16)
        taps_ref[at_row(r, columns), LANES : 2 * LANES] = own.astype(BF16)
        taps_ref[at_row(r, columns), 2 * LANES :] = from_left(own).astype(BF16)

    def build_own(r):
        build(r + 1, d_ref[at_row(r, columns), :].astype(F32))

    build(0, row_above(edge_ref, beside_in, across_in, slice(None)))
    build_own(0)
    build_own(1)

    def row(r):
        left = jnp.concatenate([taps_ref[at_row(r + 2 - b, columns), :] for b in range(3)], axis=1)
        total = jnp.dot(left, weight_ref[...], preferred_element_type=F32)
        alive = bev_ref[at_row(r + 1, columns), :].astype(F32) > 0.0
        kept = jnp.where(alive, total, 0.0).astype(BF16)
        out_ref[at_row(r, columns), :] = kept

        sums_ref[...] += jnp.sum(kept.astype(F32).reshape(columns // 8, 8, width), axis=0)
        return kept

    def row_and_build(r, carry):
        row(r)
        build_own(r + 2)
        return carry

    put_edges(edge_ref, beside_ref, across_ref, row(0), None)
    build_own(2)
    lax.fori_loop(1, rows - 2, row_and_build, 0)
    row(rows - 2)
    build(rows + 1, row_below(edge_ref, beside_in, across_in, slice(None)))
    put_edges(edge_ref, beside_ref, across_ref, None, row(rows - 1))


def region_data(edges, d_rows, beside, across, bev, weights, columns):
    width = PAIRS * LANES
    return pl.pallas_call(
        functools.partial(region_data_kernel, columns),
        out_shape=(
            jax.ShapeDtypeStruct((d_rows.shape[0], width), BF16),
            jax.ShapeDtypeStruct((columns, width), BF16),
            jax.ShapeDtypeStruct((columns, width), BF16),
            jax.ShapeDtypeStruct((8, width), F32),
        ),
        in_specs=smem(1) + vmem(5),
        out_specs=vmem(4),
        scratch_shapes=[pltpu.VMEM((d_rows.shape[0] + 2 * columns, 3 * LANES), BF16)],
        compiler_params=params(limit=28),
        cost_estimate=work(13),
        name="region_data",
    )(edges, d_rows, beside, across, bev, weights)


def region_weight_kernel(columns, blocks, d_ref, bev_ref, out_ref, total, taps_ref):
    rows = d_ref.shape[0] // columns
    width = PAIRS * LANES
    depth_out = DEPTH // 2
    half = LANES // 2
    total[...] = jnp.zeros_like(total)

    def two(i, carry):
        for k in range(2):
            own = d_ref[at_row(i * 2 + k, columns), :].astype(F32)
            place = slice(k * columns, (k + 1) * columns)
            taps_ref[place, 0:LANES] = from_right(own).astype(BF16)
            taps_ref[place, LANES : 2 * LANES] = own.astype(BF16)
            taps_ref[place, 2 * LANES :] = from_left(own).astype(BF16)
        cells = jnp.concatenate(
            [
                bev_ref[pl.ds(pl.multiple_of((i * 2 + b) * columns, 32), 2 * columns), :]
                for b in range(3)
            ],
            axis=1,
        )
        total[...] += lax.dot_general(
            taps_ref[...], cells, (((0,), (0,)), ((), ())), preferred_element_type=F32
        )
        return carry

    lax.fori_loop(0, rows // 2, two, 0, unroll=2)
    share = half // blocks
    for b in range(3):
        for e in range(3):
            for j in range(PAIRS):
                start = b * width + j * LANES
                turned = total[e * LANES : (e + 1) * LANES, start : start + LANES].T
                for k in range(min(2, depth_out - 2 * j)):
                    for q in range(blocks):
                        begin = k * half + q * share
                        base = ((q * 3 + b) * 3 + e) * share * depth_out
                        out_ref[pl.ds(base + 2 * j + k, share, stride=depth_out), :] = turned[
                            begin : begin + share, :
                        ]


def region_weight(d_own, bev, columns, blocks):
    width = PAIRS * LANES
    return pl.pallas_call(
        functools.partial(region_weight_kernel, columns, blocks),
        out_shape=jax.ShapeDtypeStruct((9 * (DEPTH // 2) * (LANES // 2), LANES), F32),
        in_specs=vmem(2),
        out_specs=vmem(1)[0],
        scratch_shapes=[
            pltpu.VMEM((3 * LANES, 3 * width), F32),
            pltpu.VMEM((2 * columns, 3 * LANES), BF16),
        ],
        compiler_params=params(limit=28),
        cost_estimate=work(10),
        name="region_weight",
    )(d_own, bev)


def prepare_kernel(
    slots, anc_count, device_rows, edge_ref, points_ref, line_ref, labels_ref,
    stats_ref, place_ref, digit_ref,
):
    voxels, width = points_ref.shape
    features = 7
    row = line_ref[1:2, :]
    exists = line_ref[3:4, :]
    column = line_ref[2:3, :]
    digits = jnp.concatenate(
        [
            (line_ref[0:1, :] + 1) * exists,
            (column >> 1) * exists,
            (row * 2 + (column & 1)) * exists,
            line_ref[4:5, :],
        ],
        axis=0,
    ).astype(F32)
    none = jnp.zeros((LANES - 4, LANES), F32)
    for i in range(voxels // LANES):
        here = slice(i * LANES, (i + 1) * LANES)
        digit_ref[here, :] = jnp.concatenate([digits[:, here], none], axis=0).T.astype(BF16)
    lane = lax.broadcasted_iota(jnp.int32, (CHUNK, width), 1)
    ones_lane = features * slots
    slot = jnp.where(lane == ones_lane, -1, lane % slots)
    total = jnp.zeros((width, width), F32)
    for i in range(voxels // CHUNK):
        here = slice(i * CHUNK, (i + 1) * CHUNK)
        count = digit_ref[here, 3:4].astype(F32).astype(jnp.int32)
        block = jnp.where(slot < count, points_ref[here, :].astype(F32), 0.0).astype(BF16)
        total = total + lax.dot_general(
            block, block, (((0,), (0,)), ((), ())), preferred_element_type=F32
        )
    row_at = lax.broadcasted_iota(jnp.int32, (width, width), 0)
    col_at = lax.broadcasted_iota(jnp.int32, (width, width), 1)
    same = (row_at % slots == col_at % slots) | (row_at == ones_lane)
    total = jnp.where(same & (row_at <= ones_lane) & (col_at < ones_lane), total, 0.0)
    rows = [
        jnp.sum(jnp.where(row_at // slots == k, total, 0.0), axis=0, keepdims=True)
        for k in range(features + 1)
    ]
    stacked = jnp.concatenate(rows, axis=0)
    col_eight = lax.broadcasted_iota(jnp.int32, (8, width), 1)
    lane_eight = lax.broadcasted_iota(jnp.int32, (8, LANES), 1)
    row_eight = lax.broadcasted_iota(jnp.int32, (8, LANES), 0)
    stats = jnp.zeros((8, LANES), F32)
    for k in range(features):
        picked = jnp.sum(jnp.where(col_eight // slots == k, stacked, 0.0), axis=1, keepdims=True)
        stats = stats + jnp.where(lane_eight == k, picked, 0.0)
    counted = jnp.sum(digits[3:4, :], axis=1, keepdims=True)
    hits = jnp.zeros(labels_ref.shape[1:], F32)
    for r in range(labels_ref.shape[0]):
        hits = hits + jnp.where(labels_ref[r] == 1, 1.0, 0.0)
    found = jnp.sum(jnp.sum(hits, axis=1, keepdims=True), axis=0, keepdims=True)
    real = exists > 0
    lists = []
    for q in range(anc_count):
        begin = q * device_rows - HALO
        lists.append(real & (row >= begin) & (row < begin + device_rows + 2 * HALO))
    lists.append(real & (row < HALO) & (edge_ref[0] > 0))
    lists.append(real & (row >= anc_count * device_rows - HALO) & (edge_ref[1] > 0))
    lists += [real & (row < 0)] * (8 - len(lists))
    member = jnp.concatenate([jnp.where(x, 1.0, 0.0) for x in lists], axis=0)
    before = (
        lax.broadcasted_iota(jnp.int32, (LANES, LANES), 0)
        < lax.broadcasted_iota(jnp.int32, (LANES, LANES), 1)
    )
    before = jnp.where(before, 1.0, 0.0).astype(BF16)
    carry = jnp.zeros((8, 1), F32)
    eight = lax.broadcasted_iota(jnp.int32, (8, LANES), 0)
    for i in range(voxels // LANES):
        here = slice(i * LANES, (i + 1) * LANES)
        part = member[:, here]
        ahead = jnp.dot(part.astype(BF16), before, preferred_element_type=F32) + carry
        places = jnp.where(part > 0.0, ahead, -1.0).astype(jnp.int32)
        owner = jnp.zeros((1, LANES), jnp.int32)
        own = jnp.full((1, LANES), -1, jnp.int32)
        for q in range(anc_count):
            mine = (row[:, here] >= q * device_rows) & (row[:, here] < (q + 1) * device_rows)
            mine = mine & real[:, here]
            owner = jnp.where(mine, q, owner)
            own = jnp.where(mine, places[q : q + 1, :], own)
        places = jnp.where(eight == 6, owner, jnp.where(eight == 7, own, places))
        place_ref[:, here] = places
        carry = carry + jnp.sum(part, axis=1, keepdims=True)
    is_edge = lax.broadcasted_iota(jnp.int32, (8, 1), 0) >= anc_count
    need = carry / jnp.where(is_edge, float(EDGE_CAP), float(CAP))
    need = jnp.max(need, axis=0, keepdims=True)
    for k, value in enumerate((counted, found, need)):
        stats = stats + jnp.where((lane_eight == 8) & (row_eight == k), value, 0.0)
    for i in range(stats_ref.shape[0]):
        stats_ref[i] = stats


def prepare(edges, points, lines, labels, anc_count, device_rows, slots, devices):
    voxels = points.shape[0]
    return pl.pallas_call(
        functools.partial(prepare_kernel, slots, anc_count, device_rows),
        out_shape=(
            jax.ShapeDtypeStruct((devices, 8, LANES), F32),
            jax.ShapeDtypeStruct((8, voxels), jnp.int32),
            jax.ShapeDtypeStruct((voxels, LANES), BF16),
        ),
        in_specs=smem(1) + vmem(3),
        out_specs=vmem(3),
        compiler_params=params(limit=24),
        cost_estimate=work(4),
        name="prepare",
    )(edges, points, lines, labels)


def batch_norm(stats, kernel):
    lanes = kernel.shape[1]
    moments = stats[:, 0:8]
    count = stats[0:1, 8:9]
    mixed = jnp.zeros((8, lanes), F32)
    for k in range(7):
        mixed = mixed + moments[:, k : k + 1] * kernel[k : k + 1, :]
    mean = mixed[7:8, :] / count
    second = jnp.sum(mixed * kernel, axis=0, keepdims=True) / count
    inv_std = lax.rsqrt(second - mean * mean + BN_EPSILON)
    return mixed, mean, inv_std, count


def first_layer(points, first_ref, scale, offset, valid):
    hidden = jnp.dot(points, first_ref[...], preferred_element_type=F32)
    act = jnp.where(valid, jnp.maximum(hidden * scale + offset, 0.0), 0.0)
    return act


def group_fold(values, combine):
    groups = values.shape[1] // LANES
    out = values[:, :LANES]
    for g in range(1, groups):
        out = combine(out, values[:, g * LANES : (g + 1) * LANES])
    out = combine(out, pltpu.roll(out, 32, 1))
    return combine(out, pltpu.roll(out, 64, 1))


def second_tail(pooled):
    lane = lax.broadcasted_iota(jnp.int32, pooled.shape, 1)
    return jnp.where(lane < 32, pooled, jnp.where(lane == 32, 1.0, 0.0))


def group_left(low, tail, count, g):
    lane = lax.broadcasted_iota(jnp.int32, tail.shape, 1)
    marked = (lane > 32) & (lane < 37) & (lane - (33 - 4 * g) >= count)
    side = jnp.where(marked, 1.0, tail).astype(BF16)
    return jnp.concatenate([low[:, g * LANES : (g + 1) * LANES], side], axis=1)


def encode_kernel(
    slots, points_ref, count_ref, stats_ref, kernel_ref, gain_ref, first_ref, second_ref,
    feat_ref, share_ref, slot_ref, held,
):
    lanes = first_ref.shape[1]
    _, mean, inv_std, _ = batch_norm(jnp.sum(stats_ref[...], axis=0), kernel_ref[...])
    scale = gain_ref[0:1, :] * inv_std
    offset = gain_ref[1:2, :] - mean * scale
    count = count_ref[:, 3:4].astype(F32).astype(jnp.int32)
    slot = lax.broadcasted_iota(jnp.int32, (CHUNK, lanes), 1) // 32
    act = first_layer(points_ref[...], first_ref, scale, offset, slot < count)
    tail = second_tail(group_fold(act, jnp.maximum))
    low = act.astype(BF16)
    top = jnp.full((CHUNK, LANES), -jnp.inf, F32)
    for g in range(lanes // LANES):
        left = group_left(low, tail, count, g)
        part = jnp.dot(left, second_ref[...], preferred_element_type=F32)
        for s in range(min(4, slots - 4 * g)):
            p = 4 * g + s
            one = part[:, s * LANES : (s + 1) * LANES]
            held[p] = one
            top = jnp.maximum(top, one)
    code = jnp.zeros((CHUNK, LANES), F32)
    for p in range(slots):
        code = code + jnp.where(held[p] == top, 2048.0 + p, 0.0)
    ties = jnp.floor(code / 2048.0)
    feat_ref[...] = jnp.maximum(top, 0.0)
    share_ref[...] = jnp.where(top > 0.0, 1.0 / ties, 0.0)
    slot_ref[...] = jnp.minimum(code - 2048.0 * ties, 127.0).astype(BF16)


def encode(points, counts, stats, kernel, gain, first, second, slots):
    voxels, width = points.shape
    lanes = first.shape[1]
    whole = lambda *shape: pl.BlockSpec(shape, lambda i: (0,) * len(shape))
    block = lambda size: pl.BlockSpec((CHUNK, size), lambda i: (i, 0))
    return pl.pallas_call(
        functools.partial(encode_kernel, slots),
        grid=(voxels // CHUNK,),
        out_shape=(
            jax.ShapeDtypeStruct((voxels, LANES), F32),
            jax.ShapeDtypeStruct((voxels, LANES), F32),
            jax.ShapeDtypeStruct((voxels, LANES), BF16),
        ),
        in_specs=[
            block(width),
            block(LANES),
            whole(*stats.shape),
            whole(8, lanes),
            whole(8, lanes),
            whole(width, lanes),
            whole(2 * LANES, 4 * LANES),
        ],
        out_specs=[block(LANES), block(LANES), block(LANES)],
        scratch_shapes=[pltpu.VMEM((slots, CHUNK, LANES), F32)],
        compiler_params=params("arbitrary", limit=30),
        cost_estimate=work(14),
        name="encode",
    )(points, counts, stats, kernel, gain, first, second)


def decode_kernel(
    slots, points_ref, count_ref, stats_ref, kernel_ref, gain_ref, first_ref, second_ref,
    feat_ref, share_ref, slot_ref, d_feat_ref, loss_ref, out_ref,
    first_sum, second_sum, joined, tail_sum,
):
    lanes = first_ref.shape[1]
    width = points_ref.shape[1]
    step = pl.program_id(0)

    @pl.when(step == 0)
    def _():
        first_sum[...] = jnp.zeros_like(first_sum)
        second_sum[...] = jnp.zeros_like(second_sum)

    _, mean, inv_std, _ = batch_norm(jnp.sum(stats_ref[...], axis=0), kernel_ref[...])
    scale = gain_ref[0:1, :] * inv_std
    offset = gain_ref[1:2, :] - mean * scale
    count = count_ref[:, 3:4].astype(F32).astype(jnp.int32)
    points = points_ref[...]
    slot = lax.broadcasted_iota(jnp.int32, (CHUNK, lanes), 1) // 32
    act = first_layer(points, first_ref, scale, offset, slot < count)
    pooled = group_fold(act, jnp.maximum)
    tail = second_tail(pooled)
    low = act.astype(BF16)
    share = share_ref[...]
    d_feat = d_feat_ref[...] * share
    d_low = d_feat.astype(BF16)
    shared = jnp.where((share > 0.0) & (share < 1.0), 1.0, 0.0)
    shared = jnp.max(jnp.max(shared, axis=1, keepdims=True)) > 0.0

    def group_back(g, left, pieces):
        d_part = jnp.concatenate(pieces, axis=1)
        second_sum[...] += lax.dot_general(
            left, d_part, (((0,), (0,)), ((), ())), preferred_element_type=F32
        )
        d_left = lax.dot_general(
            d_part, second_ref[...], (((1,), (1,)), ((), ())), preferred_element_type=F32
        )
        joined[:, g * LANES : (g + 1) * LANES] = d_left[:, :LANES]
        return d_left[:, LANES:]

    none = jnp.zeros((CHUNK, LANES), BF16)

    @pl.when(jnp.logical_not(shared))
    def _():
        found = slot_ref[...]
        d_tail = jnp.zeros((CHUNK, LANES), F32)
        for g in range(lanes // LANES):
            left = group_left(low, tail, count, g)
            pieces = [
                jnp.where(found == jnp.asarray(4 * g + s, BF16), d_low, none)
                if 4 * g + s < slots
                else none
                for s in range(4)
            ]
            d_tail = d_tail + group_back(g, left, pieces)
        tail_sum[...] = d_tail

    @pl.when(shared)
    def _():
        top = feat_ref[...]
        d_tail = jnp.zeros((CHUNK, LANES), F32)
        for g in range(lanes // LANES):
            left = group_left(low, tail, count, g)
            part = jnp.dot(left, second_ref[...], preferred_element_type=F32)
            pieces = []
            for s in range(4):
                if 4 * g + s < slots:
                    hit = part[:, s * LANES : (s + 1) * LANES] == top
                    pieces.append(jnp.where(hit, d_feat, 0.0).astype(BF16))
                else:
                    pieces.append(none)
            d_tail = d_tail + group_back(g, left, pieces)
        tail_sum[...] = d_tail

    wide = jnp.concatenate([pooled] * (lanes // LANES), axis=1)
    reached = act == wide
    ties = group_fold(jnp.where(reached, 1.0, 0.0), jnp.add)
    lane = lax.broadcasted_iota(jnp.int32, (CHUNK, LANES), 1)
    spread = jnp.where(lane < 32, tail_sum[...], 0.0)
    spread = spread + pltpu.roll(spread, 32, 1)
    spread = (spread + pltpu.roll(spread, 64, 1)) / ties
    spread = jnp.concatenate([spread] * (lanes // LANES), axis=1)
    d_act = joined[...] + jnp.where(reached, spread, 0.0)
    d_act = jnp.where(act > 0.0, d_act, 0.0).astype(BF16)
    first_sum[...] += lax.dot_general(
        points, d_act, (((0,), (0,)), ((), ())), preferred_element_type=F32
    )

    @pl.when(step == pl.num_programs(0) - 1)
    def _():
        row_at = lax.broadcasted_iota(jnp.int32, (width, lanes), 0)
        col_at = lax.broadcasted_iota(jnp.int32, (width, lanes), 1)
        same = (row_at % slots == col_at // 32) | (row_at == 7 * slots)
        total = jnp.where(same & (col_at // 32 < slots), first_sum[...], 0.0)
        rows = [
            jnp.sum(jnp.where(row_at // slots == k, total, 0.0), axis=0, keepdims=True)
            for k in range(8)
        ]
        first = group_fold(jnp.concatenate(rows, axis=0), jnp.add)
        upper = second_sum[0:32, 0:LANES]
        lower = second_sum[LANES : LANES + 40, 0:LANES]
        for s in range(1, 4):
            cols = slice(s * LANES, (s + 1) * LANES)
            upper = upper + second_sum[s * 32 : (s + 1) * 32, cols]
            lower = lower + second_sum[LANES : LANES + 40, cols]
        devices, layers = out_ref.shape[:2]
        none = jnp.zeros((devices * layers - 88, LANES), F32)
        rows = jnp.concatenate([first, upper, lower, loss_ref[...], none], axis=0)
        for k in range(layers):
            out_ref[:, k, :] = rows[k * devices : (k + 1) * devices, :]


def decode(
    points, counts, stats, kernel, gain, first, second, feat, share, slot, d_feat, loss, shape, slots
):
    voxels, width = points.shape
    lanes = first.shape[1]
    whole = lambda *shape: pl.BlockSpec(shape, lambda i: (0,) * len(shape))
    block = lambda size: pl.BlockSpec((CHUNK, size), lambda i: (i, 0))
    return pl.pallas_call(
        functools.partial(decode_kernel, slots),
        grid=(voxels // CHUNK,),
        out_shape=jax.ShapeDtypeStruct(shape + (LANES,), F32),
        in_specs=[
            block(width),
            block(LANES),
            whole(*stats.shape),
            whole(8, lanes),
            whole(8, lanes),
            whole(width, lanes),
            whole(2 * LANES, 4 * LANES),
            block(LANES),
            block(LANES),
            block(LANES),
            block(LANES),
            whole(8, LANES),
        ],
        out_specs=whole(*shape, LANES),
        scratch_shapes=[
            pltpu.VMEM((width, lanes), F32),
            pltpu.VMEM((2 * LANES, 4 * LANES), F32),
            pltpu.VMEM((CHUNK, lanes), F32),
            pltpu.VMEM((CHUNK, LANES), F32),
        ],
        compiler_params=params("arbitrary", limit=30),
        cost_estimate=work(28),
        name="decode",
    )(points, counts, stats, kernel, gain, first, second, feat, share, slot, d_feat, loss)


def encoder_weights_kernel(
    slots, one_ref, two_ref, bias_ref, gain_ref, first_ref, second_ref, kernel_ref, rows_ref
):
    width, lanes = first_ref.shape
    features = one_ref.shape[0] - 1
    row_at = lax.broadcasted_iota(jnp.int32, (width, LANES), 0)
    slot_at = lax.broadcasted_iota(jnp.int32, (width, LANES), 1) // 32
    one = jnp.concatenate([one_ref[...]] * 4, axis=1)
    tall = jnp.zeros((width, LANES), F32)
    for k in range(features):
        tall = jnp.where(row_at // slots == k, one[k : k + 1, :], tall)
    own_slot = row_at % slots
    for g in range(lanes // LANES):
        here = slice(g * LANES, (g + 1) * LANES)
        first_ref[:, here] = jnp.where(own_slot == 4 * g + slot_at, tall, 0.0).astype(BF16)
        kernel_ref[:, here] = one
        rows_ref[:, here] = jnp.concatenate([gain_ref[...]] * 4, axis=1)
    two = two_ref[...]
    half = two.shape[0] // 2
    upper = jnp.concatenate([two[:half]] * 4, axis=0)
    row_two = lax.broadcasted_iota(jnp.int32, (LANES, LANES), 0)
    for s in range(4):
        here = slice(s * LANES, (s + 1) * LANES)
        second_ref[0:LANES, here] = jnp.where(row_two // half == s, upper, 0.0).astype(BF16)
        lower = jnp.concatenate(
            [two[half:], bias_ref[...], jnp.zeros((LANES - half - 8, LANES), F32)], axis=0
        )
        second_ref[LANES:, here] = jnp.where(row_two == half + 1 + s, EMPTY, lower).astype(BF16)


def encoder_weights(w_one, w_two, bias_two, gain, shift, slots):
    features, c_one = w_one.shape
    lanes = -(-slots // 4) * LANES
    width = -(-(features * slots + 1) // LANES) * LANES
    one = jnp.pad(w_one.astype(F32), ((0, 1), (0, 0)))
    bias = jnp.pad(bias_two.astype(F32).reshape(1, -1), ((0, 7), (0, 0)))
    rows = jnp.pad(jnp.stack([gain, shift]).astype(F32), ((0, 6), (0, 0)))
    return pl.pallas_call(
        functools.partial(encoder_weights_kernel, slots),
        out_shape=(
            jax.ShapeDtypeStruct((width, lanes), BF16),
            jax.ShapeDtypeStruct((2 * LANES, 4 * LANES), BF16),
            jax.ShapeDtypeStruct((8, lanes), F32),
            jax.ShapeDtypeStruct((8, lanes), F32),
        ),
        in_specs=vmem(4),
        out_specs=vmem(4),
        compiler_params=params(limit=24),
        cost_estimate=work(2),
        name="encoder_weights",
    )(one, w_two.astype(F32), bias, rows)


def pick_rows(source, place_ref, line, capacity, offset):
    want = place_ref[line : line + 1, :] - offset
    row_at = lax.broadcasted_iota(jnp.int32, (capacity, source.shape[0]), 0)
    chosen = jnp.where(want == row_at, 1.0, 0.0).astype(BF16)
    found = jnp.dot(chosen, source, preferred_element_type=F32)
    return found[:, :LANES].astype(BF16), found[:, LANES:].T


def edge_lists_kernel(anc_count, offset_ref, feat_ref, digit_ref, place_ref, up_ref, down_ref):
    source = jnp.concatenate([feat_ref[...].astype(BF16), digit_ref[...]], axis=1)
    for side, edge_ref in enumerate((up_ref, down_ref)):
        rows, digits = pick_rows(source, place_ref, anc_count + side, EDGE_CAP, offset_ref[1])
        edge_ref[0:EDGE_CAP, :] = rows
        digits = jnp.concatenate([digits[0:8, :], jnp.zeros((8, LANES), F32)], axis=0)
        edge_ref[EDGE_CAP : EDGE_CAP + 16, :] = digits.astype(BF16)


def edge_lists(offsets, feat, digits, place, anc_count):
    return pl.pallas_call(
        functools.partial(edge_lists_kernel, anc_count),
        out_shape=(
            jax.ShapeDtypeStruct((EDGE_CAP + 16, LANES), BF16),
            jax.ShapeDtypeStruct((EDGE_CAP + 16, LANES), BF16),
        ),
        in_specs=smem(1) + vmem(3),
        out_specs=vmem(2),
        compiler_params=params(limit=24),
        cost_estimate=work(1),
        name="edge_lists",
    )(offsets, feat, digits, place)


def gather_lists_kernel(anc_count, offset_ref, feat_ref, digit_ref, place_ref, main_ref):
    source = jnp.concatenate([feat_ref[...].astype(BF16), digit_ref[...]], axis=1)
    for q in range(anc_count):
        rows, digits = pick_rows(source, place_ref, q, CAP, offset_ref[0])
        main_ref[q, 0:CAP, :] = rows
        lines = [
            digits[k : k + 1, i * LANES : (i + 1) * LANES]
            for k in range(3)
            for i in range(CAP // LANES)
        ]
        lines.append(jnp.zeros((32 - len(lines), LANES), F32))
        main_ref[q, CAP : CAP + 32, :] = jnp.concatenate(lines, axis=0).astype(BF16)
        main_ref[q, CAP + 32 :, :] = jnp.zeros((EDGE_CAP + 16, LANES), BF16)


def gather_lists(offsets, feat, digits, place, anc_count):
    return pl.pallas_call(
        functools.partial(gather_lists_kernel, anc_count),
        out_shape=jax.ShapeDtypeStruct((anc_count, CAP + EDGE_CAP + 48, LANES), BF16),
        in_specs=smem(1) + vmem(3),
        out_specs=vmem(1)[0],
        compiler_params=params(limit=30),
        cost_estimate=work(5),
        name="gather_lists",
    )(offsets, feat, digits, place)


def spread_lists_kernel(index_ref, received_ref, out_ref, held):
    total = received_ref.shape[0]
    held[0:total, :] = received_ref[...].astype(F32)
    held[total:, :] = jnp.zeros((8, LANES), F32)

    def pick(i, carry):
        base = pl.multiple_of(i * LANES, LANES)
        for j in range(LANES):
            out_ref[pl.ds(base + j, 1), :] = held[pl.ds(index_ref[base + j], 1), :]
        return carry

    lax.fori_loop(0, out_ref.shape[0] // LANES, pick, 0)


def spread_lists(index, received):
    voxels = index.shape[0]
    total = received.shape[0]
    return pl.pallas_call(
        spread_lists_kernel,
        out_shape=jax.ShapeDtypeStruct((voxels, LANES), F32),
        in_specs=smem(1) + vmem(1),
        out_specs=vmem(1)[0],
        scratch_shapes=[pltpu.VMEM((total + 8, LANES), F32)],
        compiler_params=params(limit=24),
        cost_estimate=work(4),
        name="spread_lists",
    )(index, received)


def add_piece(held, source, low, high, start):
    lane = lax.broadcasted_iota(jnp.int32, (1, LANES), 1)
    begin, end = low // LANES, -(-high // LANES)
    gap = start - low
    turn = gap % LANES
    at = begin + gap // LANES
    rows = source[begin:end, :]
    count = end - begin
    place = lax.broadcasted_iota(jnp.int32, (count, LANES), 0) * LANES
    place = place + lax.broadcasted_iota(jnp.int32, (count, LANES), 1) + begin * LANES
    if low % LANES or high % LANES:
        rows = jnp.where((place >= low) & (place < high), rows, 0.0)
    if turn == 0:
        held[at : at + count, :] += rows
        return
    rows = pltpu.roll(rows, turn, 1)
    here = jnp.where(lane >= turn, rows, 0.0)
    after = jnp.where(lane < turn, rows, 0.0)
    skip = max(-at, 0)
    if count > skip:
        held[at + skip : at + count, :] += here[skip:, :]
    held[at + 1 : at + 1 + count, :] += after


def pack_kernel(
    plan, tiles, chunk, region_ref, middle_ref, head_ref, mid_ref, row_ref, out_ref, held, rest_ref
):
    half = LANES // 2
    lane = lax.broadcasted_iota(jnp.int32, (1, LANES), 1)
    mid = jnp.sum(mid_ref[...], axis=0, keepdims=True)
    mid = group_sum(mid)
    mid = mid + pltpu.roll(mid, half, 1)
    region_bias = pltpu.roll(jnp.sum(row_ref[0:8, :], axis=0, keepdims=True), half, 1)
    outs = row_ref.shape[0] - 16
    wide = lax.broadcasted_iota(jnp.int32, (outs, LANES), 1) - half
    own = lax.broadcasted_iota(jnp.int32, (outs, LANES), 0) == wide
    head_bias = jnp.sum(jnp.where(own, row_ref[8 : 8 + outs, :], 0.0), axis=0, keepdims=True)
    rest_ref[0:1, :] = jnp.where(lane < half, mid, region_bias)
    rest_ref[1:2, :] = jnp.where(lane < half, region_bias, head_bias)
    sources = {"region": region_ref, "middle": middle_ref, "head": head_ref, "rest": rest_ref}
    for a, pieces in enumerate(plan):
        held[...] = jnp.zeros_like(held)
        for name, low, high, start in pieces:
            if name in sources:
                add_piece(held, sources[name], low, high, start)
        for t in range(tiles):
            out_ref[t * len(plan) + a] = held[t * chunk : (t + 1) * chunk, :].astype(BF16)


def group_sum(values):
    out = values[:, :LANES]
    for g in range(1, values.shape[1] // LANES):
        out = out + values[:, g * LANES : (g + 1) * LANES]
    return out


def pack(plan, tiles, chunk, region, middle, head, mid_sums, row_sums):
    return pl.pallas_call(
        functools.partial(pack_kernel, plan, tiles, chunk),
        out_shape=jax.ShapeDtypeStruct((tiles * len(plan), chunk, LANES), BF16),
        in_specs=vmem(5),
        out_specs=vmem(1)[0],
        scratch_shapes=[pltpu.VMEM((tiles * chunk, LANES), F32), pltpu.VMEM((8, LANES), F32)],
        compiler_params=params(limit=28),
        cost_estimate=work(3),
        name="pack",
    )(region, middle, head, mid_sums, row_sums)


def sum_chunk_kernel(parts_ref, out_ref, square_ref):
    total = jnp.sum(parts_ref[...].astype(F32), axis=0)
    for i in range(out_ref.shape[0]):
        out_ref[i] = total
    square_ref[...] = jnp.broadcast_to(jnp.sum(total * total), square_ref.shape)


def sum_chunk(parts, tiles):
    _, rows, lanes = parts.shape
    return pl.pallas_call(
        sum_chunk_kernel,
        out_shape=(
            jax.ShapeDtypeStruct((tiles, rows, lanes), F32),
            jax.ShapeDtypeStruct((1, lanes), F32),
        ),
        in_specs=vmem(1),
        out_specs=vmem(2),
        compiler_params=params(limit=24),
        cost_estimate=work(2),
        name="sum_chunk",
    )(parts)


def finish_kernel(
    plan, anc_ref, early_ref, late_ref, stats_ref, kernel_ref, gain_ref,
    out_ref, scalar_ref, one, norm,
):
    stats = jnp.sum(stats_ref[...], axis=0)
    kernel = kernel_ref[:, :LANES]
    mixed, mean, inv_std, count = batch_norm(stats, kernel)
    layers = late_ref.shape[1] - 1
    late = jnp.concatenate([late_ref[:, k, :] for k in range(layers)], axis=0)
    sums = late[0:8, :]
    total_shift = sums[7:8, :]
    total_gain = inv_std * (jnp.sum(kernel * sums, axis=0, keepdims=True) - mean * total_shift)
    slope = gain_ref[0:1, :LANES] * inv_std
    lane = lax.broadcasted_iota(jnp.int32, (1, LANES), 1)
    one[...] = jnp.zeros_like(one)
    norm[...] = jnp.zeros_like(norm)
    for k in range(7):
        first = stats[7:8, k : k + 1]
        pull = total_shift * first + total_gain * inv_std * (mixed[k : k + 1, :] - mean * first)
        grad = jnp.where(lane < 32, slope * (sums[k : k + 1, :] - pull / count), 0.0)
        if k % 4:
            grad = pltpu.roll(grad, 32 * (k % 4), 1)
        one[k // 4 : k // 4 + 1, :] += grad
    bias = late[72:73, :]
    top = jnp.where(lane < 32, total_gain, 0.0)
    top = top + pltpu.roll(jnp.where(lane < 32, total_shift, 0.0), 32, 1)
    norm[0:1, :] = top + jnp.where(lane < 64, 0.0, pltpu.roll(bias, 64, 1))
    norm[1:2, :] = jnp.where(lane < 64, pltpu.roll(bias, 64, 1), 0.0)
    two = late[8:72, :]
    square = jnp.sum(late_ref[:, layers, :]) / LANES
    square = square + jnp.sum(two * two) + jnp.sum(one[...] * one[...])
    square = square + jnp.sum(norm[...] * norm[...])
    size = jnp.sqrt(jnp.broadcast_to(square, (1, LANES)))
    scalar_ref[0:1, :] = late[80:81, :] / stats[1:2, 8:9]
    scalar_ref[1:2, :] = size
    scalar_ref[2:8, :] = jnp.broadcast_to(jnp.minimum(1.0, CLIP_LIMIT / (size + 1e-06)), (6, LANES))
    chunk = early_ref.shape[1]
    for i in range(early_ref.shape[0]):
        out_ref[i * chunk : (i + 1) * chunk, :] = early_ref[i]
    sources = {"one": one, "two": two, "norm": norm}
    for a, pieces in enumerate(plan):

        @pl.when(anc_ref[0] == a)
        def _():
            for name, low, high, start in pieces:
                if name in sources:
                    add_piece(out_ref, sources[name], low, high, start)


def finish(plan, anc, early, late, stats, kernel, gain):
    return pl.pallas_call(
        functools.partial(finish_kernel, plan),
        out_shape=(
            jax.ShapeDtypeStruct((early.shape[0] * early.shape[1], LANES), F32),
            jax.ShapeDtypeStruct((8, LANES), F32),
        ),
        in_specs=smem(1) + vmem(5),
        out_specs=vmem(2),
        scratch_shapes=[pltpu.VMEM((8, LANES), F32), pltpu.VMEM((8, LANES), F32)],
        compiler_params=params(limit=24),
        cost_estimate=work(3),
        name="finish",
    )(anc, early, late, stats, kernel, gain)


def everyone(values, axes):
    count = 1
    for axis in axes:
        count *= lax.axis_size(axis)
    copies = jnp.broadcast_to(values[None], (count,) + values.shape)
    return lax.all_to_all(copies, axes, 0, 0)


def swap_rows(beside, across):
    axes = ("tile", "anc")
    count = lax.axis_size("tile") * lax.axis_size("anc")
    pairs = [(i, i ^ 1) for i in range(count)]
    others = [(i, i + 1) for i in range(1, count - 1, 2)]
    others += [(j, i) for i, j in others]
    return lax.ppermute(beside, axes, pairs), lax.ppermute(across, axes, others)


def shard_windows(segments, shard, count):
    windows = []
    for a in range(count):
        begin, end = a * shard, (a + 1) * shard
        at = 0
        pieces = []
        for name, size in segments:
            low, high = max(begin, at), min(end, at + size)
            if low < high:
                pieces.append((name, low - at, high - at, low - begin))
            at += size
        windows.append(tuple(pieces))
    return tuple(windows)


def on_device(
    points,
    npoints,
    coords,
    labels,
    targets,
    w_vfe1,
    w_vfe2,
    w_mid,
    w_rpn,
    w_head,
    bn_gain,
    biases,
    master,
    moment1,
    moment2,
):
    both = ("tile", "anc")
    anc_count = lax.axis_size("anc")
    tile_count = lax.axis_size("tile")
    anc = lax.axis_index("anc")
    tile = lax.axis_index("tile")
    device_rows = labels.shape[1]
    columns = labels.shape[2]
    blocks = device_rows // BLOCK_ROWS
    tile_rows = device_rows * anc_count
    all_rows = tile_rows * tile_count
    slots = points.shape[1]
    voxels = points.shape[2]
    c_vfe = w_vfe1.shape[1]
    c_vox = w_vfe2.shape[1]
    c_mid = w_mid.shape[4]
    c_rpn = w_rpn.shape[3]
    outs = w_head.shape[1]
    shift = biases[:c_vfe]
    bias_two = biases[c_vfe : c_vfe + c_vox]
    bias_mid, bias_rpn, bias_head = jnp.split(
        biases[c_vfe + c_vox :].astype(F32), [c_mid, c_mid + c_rpn]
    )

    def joined(row):
        return (row % CROP_ROWS != CROP_ROWS // 2) & (row > 0) & (row < all_rows)

    padded = -(-voxels // CHUNK) * CHUNK
    width = -(-(points.shape[0] * slots + 1) // LANES) * LANES
    flat_points = points.reshape(-1, voxels).T
    flat_points = jnp.pad(
        flat_points, ((0, padded - voxels), (0, width - flat_points.shape[1]))
    )
    lane = lax.broadcasted_iota(jnp.int32, flat_points.shape, 1)
    flat_points = jnp.where(lane == points.shape[0] * slots, jnp.ones((), BF16), flat_points)
    spare = (0, padded - voxels)
    row = coords[:, 1] - tile * tile_rows
    lines = [coords[:, 0], row, coords[:, 2], jnp.ones_like(row), npoints]
    lines = jnp.pad(jnp.stack(lines), ((0, 3), spare))
    tile_edges = jnp.stack([joined(tile * tile_rows), joined((tile + 1) * tile_rows)])
    devices = anc_count * tile_count
    parts = everyone(w_rpn, ("anc",))
    stats, place, digits = prepare(
        tile_edges.astype(jnp.int32),
        flat_points,
        lines,
        labels.transpose(1, 0, 2),
        anc_count,
        device_rows,
        slots,
        devices,
    )
    stats, parts = lax.optimization_barrier((stats, parts))
    stats = lax.all_to_all(stats, both, 0, 0)
    region_in, region_back = region_order(parts)
    counts = digits
    count_pos = jnp.sum(stats[:, 1, 8])
    rounds = jnp.ceil(jnp.max(stats[:, 2, 8])).astype(jnp.int32)
    middle_kernel_all = w_mid.transpose(0, 1, 2, 4, 3).reshape(-1, c_mid, c_vox)

    first, second, kernel, gain_rows = encoder_weights(
        w_vfe1, w_vfe2, bias_two, bn_gain, shift, slots
    )
    feat, share, found = encode(
        flat_points, counts, stats, kernel, gain_rows, first, second, slots
    )
    feat, region_in, region_back = lax.optimization_barrier((feat, region_in, region_back))

    in_tile = lax.axis_size("tile")
    upward = [(i + 1, i) for i in range(in_tile - 1)]
    downward = [(i, i + 1) for i in range(in_tile - 1)]

    def exchange(number):
        offsets = jnp.stack([number * CAP, number * EDGE_CAP]).astype(jnp.int32)
        up, down = edge_lists(offsets, feat, digits, place, anc_count)
        from_below = lax.ppermute(up, "tile", upward)
        from_above = lax.ppermute(down, "tile", downward)
        main = gather_lists(offsets, feat, digits, place, anc_count)
        main, from_below, from_above = lax.optimization_barrier((main, from_below, from_above))
        main = lax.dynamic_update_slice(main, from_above[None], (0, CAP + 32, 0))
        main = lax.dynamic_update_slice(main, from_below[None], (anc_count - 1, CAP + 32, 0))
        return lax.all_to_all(main, "anc", 0, 0)

    def cells(got):
        words = got[:, CAP : CAP + 32].reshape(anc_count, -1).astype(jnp.int32)
        start = CAP + 32 + EDGE_CAP
        edge_words = got[:, start : start + 16].astype(jnp.int32)

        def word(k):
            gap = jnp.zeros((anc_count, 32), jnp.int32)
            parts = [words[:, k * CAP : (k + 1) * CAP], gap, edge_words[:, k], gap[:, :16]]
            return jnp.concatenate(parts, axis=1)

        high, half, mixed = word(0), word(1), word(2)
        local = mixed // 2 - anc * device_rows
        is_edge = lax.broadcasted_iota(jnp.int32, local.shape, 1) >= CAP
        local = local + jnp.where(is_edge, jnp.where(anc == 0, -tile_rows, tile_rows), 0)
        cross = half * 2 + mixed % 2
        scatter_at, own_at = [], []
        for k in range(blocks):
            line = local - k * BLOCK_ROWS
            tall = BLOCK_ROWS + 2 * HALO
            inside = (high > 0) & (line >= -HALO) & (line < BLOCK_ROWS + HALO)
            spot = ((high - 1) * tall + line + HALO) * columns + cross
            scatter_at.append(jnp.where(inside, spot, DEPTH * tall * columns).reshape(-1))
            inside = (high > 0) & (line >= 0) & (line < BLOCK_ROWS)
            spot = ((high - 1) * BLOCK_ROWS + line) * columns + cross
            spot = jnp.where(inside, spot, DEPTH * BLOCK_ROWS * columns)
            own_at.append(spot[:, :CAP].reshape(-1, LANES))
        return scatter_at, own_at

    got = exchange(0)
    first_row = tile * tile_rows + anc * device_rows
    edges = []
    even = (tile * anc_count + anc) % 2 == 0
    for k in range(blocks):
        top = first_row + k * BLOCK_ROWS
        flags = [
            joined(top),
            joined(top + BLOCK_ROWS),
            even,
            anc * device_rows + k * BLOCK_ROWS,
            jnp.where(anc == 0, -tile_rows, tile_rows),
        ]
        edges.append(jnp.stack([flag.astype(jnp.int32) for flag in flags]))

    def more(state):
        return state[0] < rounds

    def another(state):
        number, held = state
        rows = exchange(number)
        index, _ = cells(rows)
        rows = rows.reshape(-1, LANES)
        held = [scatter_rows(at, rows, old, columns) for at, old in zip(index, held)]
        return number + 1, held

    def one_round():
        made = [
            scatter_middle(
                edges[k], got.reshape(-1, LANES), middle_kernel_all, bias_mid, columns
            )
            for k in range(blocks)
        ]
        return tuple([one[i] for one in made] for i in range(3))

    def many_rounds():
        index, own = cells(got)
        held = [scatter_rows(at, got.reshape(-1, LANES), None, columns) for at in index]
        _, held = lax.while_loop(more, another, (jnp.int32(1), held))
        bevs = [
            middle_forward(edges[k], held[k], middle_kernel_all, bias_mid, columns)
            for k in range(blocks)
        ]
        return held, bevs, own

    grids, bevs, own_at = lax.cond(rounds > 1, many_rounds, one_round)

    wide_labels = jnp.repeat(labels.reshape(2, -1), outs // 2, axis=0)
    wide_targets = jnp.pad(targets, ((0, 0), (1, 0), (0, 0), (0, 0))).reshape(outs, -1)
    step = BLOCK_ROWS * columns
    scale = 1.0 / count_pos
    d_rows, head_sums, row_sums = [], 0.0, 0.0
    d_beside, d_across = [], []
    for k in range(blocks):
        here = slice(k * step, (k + 1) * step)
        d_block, near_row, far_row, heads, sums = region_forward(
            scale,
            edges[k],
            bevs[k],
            region_in,
            bias_rpn,
            w_head.T,
            bias_head,
            wide_labels[:, here],
            wide_targets[:, here],
            columns,
        )
        d_rows.append(d_block)
        d_beside.append(near_row)
        d_across.append(far_row)
        head_sums = head_sums + heads
        row_sums = row_sums + sums

    def swapped(near, far):
        if blocks == 1:
            got_near, got_far = swap_rows(near[0], far[0])
            return [got_near], [got_far]
        firsts = [jnp.where(even, f, n) for n, f in zip(near, far)]
        lasts = [jnp.where(even, n, f) for n, f in zip(near, far)]
        got_near, got_far = swap_rows(
            jnp.where(even, lasts[-1], firsts[0]), jnp.where(even, firsts[0], lasts[-1])
        )
        above = [jnp.where(even, got_far, got_near)] + lasts[:-1]
        below = firsts[1:] + [jnp.where(even, got_near, got_far)]
        return (
            [jnp.where(even, y, x) for x, y in zip(above, below)],
            [jnp.where(even, x, y) for x, y in zip(above, below)],
        )

    beside, across = swapped(d_beside, d_across)
    grad_region = sum(
        region_weight(d_rows[k], bevs[k], columns, anc_count) for k in range(blocks)
    )
    d_rows, grad_region, beside, across = lax.optimization_barrier(
        (d_rows, grad_region, beside, across)
    )
    d_mids, mid_sums = [], 0.0
    mid_beside, mid_across = [], []
    for k in range(blocks):
        d_block, near_row, far_row, sums = region_data(
            edges[k], d_rows[k], beside[k], across[k], bevs[k], region_back, columns
        )
        d_mids.append(d_block)
        mid_beside.append(near_row)
        mid_across.append(far_row)
        mid_sums = mid_sums + sums
    beside, across = swapped(mid_beside, mid_across)
    grad_mid = sum(middle_weight(grids[k], d_mids[k], columns) for k in range(blocks))
    grad_mid, beside, across = lax.optimization_barrier((grad_mid, beside, across))

    head_three = head_sums.reshape(3, outs, c_rpn)
    grad_head = (head_three[0] + head_three[1] + head_three[2]).T
    head_rows = grad_head.reshape(-1, LANES)
    segments = (
        ("region", grad_region.size),
        ("one", w_vfe1.size),
        ("two", w_vfe2.size),
        ("middle", grad_mid.size),
        ("head", w_head.size),
        ("norm", c_vfe + c_vfe + c_vox),
        ("rest", c_mid + c_rpn + outs),
    )
    shard = master.shape[0]
    plan = shard_windows(segments, shard, anc_count)
    chunk_rows = -(-(shard // LANES + 2) // (8 * tile_count)) * 8
    packed = pack(
        plan, tile_count, chunk_rows, grad_region, grad_mid, head_rows, mid_sums, row_sums
    )
    own_at, packed = lax.optimization_barrier((own_at, packed))
    chunk, chunk_square = sum_chunk(lax.all_to_all(packed, both, 0, 0), tile_count)

    def collect(number, own_index, chunk):
        lists = sum(
            middle_data(
                own_index[k], edges[k], d_mids[k], beside[k], across[k], middle_kernel_all, columns
            )
            for k in range(blocks)
        )
        lists, chunk = lax.optimization_barrier((lists, chunk))
        back = lax.all_to_all(lists.reshape(anc_count, CAP, LANES), "anc", 0, 0)
        mine = place[7] - number * CAP
        known = (mine >= 0) & (mine < CAP)
        index = jnp.where(known, place[6] * CAP + mine, anc_count * CAP)
        return spread_lists(index, back.reshape(-1, LANES)), chunk

    d_feat, chunk = collect(0, own_at, chunk)
    early = lax.all_to_all(chunk, "tile", 0, 0)

    def collect_more(state):
        number, held = state
        _, index = cells(exchange(number))
        return number + 1, held + collect(number, index, ())[0]

    d_feat = lax.cond(
        rounds > 1,
        lambda held: lax.while_loop(more, collect_more, (jnp.int32(1), held))[1],
        lambda held: held,
        d_feat,
    )
    layers = -(-88 // devices)
    late = decode(
        flat_points,
        counts,
        stats,
        kernel,
        gain_rows,
        first,
        second,
        feat,
        share,
        found,
        d_feat,
        row_sums[24:32],
        (devices, layers),
        slots,
    )
    late, early = lax.optimization_barrier((late, early))
    late = jnp.sum(lax.all_to_all(late, both, 0, 0), axis=0)
    late = everyone(jnp.concatenate([late, chunk_square], axis=0), both)
    reduced, scalars = finish(plan, anc.reshape(1), early, late, stats, kernel, gain_rows)
    loss = scalars[0, 0]
    norm_value = scalars[1, 0]
    reduced = reduced.reshape(-1)[:shard]
    clipped = reduced * scalars[2, 0]
    first_new = BETA_FIRST * moment1 + (1.0 - BETA_FIRST) * clipped
    second_new = BETA_SECOND * moment2 + (1.0 - BETA_SECOND) * clipped * clipped
    first_hat = first_new / (1.0 - BETA_FIRST**STEP_NUMBER)
    second_hat = second_new / (1.0 - BETA_SECOND**STEP_NUMBER)
    updated = master - LEARN_RATE * (
        first_hat / (jnp.sqrt(second_hat) + ADAM_EPSILON) + WEIGHT_DECAY * master
    )
    return (updated, first_new, second_new, loss, norm_value)


def solution(mesh):
    placed = (
        P(None, None, ("tile", "anc")),
        P(("tile", "anc")),
        P(("tile", "anc"), None),
        P(None, ("tile", "anc"), None),
        P(None, None, ("tile", "anc"), None),
        P(),
        P(),
        P(),
        P(None, None, "anc", None),
        P(),
        P(),
        P(),
        P("anc"),
        P("anc"),
        P("anc"),
    )
    return jax.shard_map(
        on_device,
        mesh=mesh,
        in_specs=placed,
        out_specs=(P("anc"), P("anc"), P("anc"), P(), P()),
        check_vma=False,
    )
```

```python
import functools
import jax
import jax.numpy as jnp
from jax import lax
from jax.experimental import pallas as pl
from jax.experimental.pallas import tpu as pltpu
from jax.sharding import PartitionSpec as P

DEPTH = 10
PAIRS = DEPTH // 4 + 1
CROP_ROWS = 192
BLOCK_ROWS = 12
HALO = 2
LANES = 128
CHUNK = 384
CAP = 768
EDGE_CAP = 128
EMPTY = -1e30
FOCAL_ALPHA = 0.25
BN_EPSILON = 0.001
CLIP_LIMIT = 0.05
LEARN_RATE = 0.03
BETA_FIRST = 0.9
BETA_SECOND = 0.999
WEIGHT_DECAY = 0.01
ADAM_EPSILON = 1e-08
STEP_NUMBER = 10
F32 = jnp.float32
BF16 = jnp.bfloat16


def vmem(count):
    return [pl.BlockSpec(memory_space=pltpu.VMEM)] * count


def smem(count):
    return [pl.BlockSpec(memory_space=pltpu.SMEM)] * count


def params(*semantics, limit=60):
    return pltpu.CompilerParams(
        vmem_limit_bytes=limit * 1024 * 1024, dimension_semantics=semantics or None
    )


def work(micros):
    return pl.CostEstimate(flops=micros, transcendentals=0, bytes_accessed=micros * 3_000_000)


def at_row(index, columns):
    if isinstance(index, int):
        return pl.ds(index * columns, columns)
    return pl.ds(pl.multiple_of(index * columns, 32), columns)


def column_edges(columns, lanes):
    place = lax.broadcasted_iota(jnp.int32, (columns, lanes), 0)
    return place == 0, place == columns - 1


def from_left(values):
    columns, lanes = values.shape
    first, _ = column_edges(columns, lanes)
    return jnp.where(first, 0.0, pltpu.roll(values, 1, 0))


def from_right(values):
    columns, lanes = values.shape
    _, last = column_edges(columns, lanes)
    return jnp.where(last, 0.0, pltpu.roll(values, columns - 1, 0))


def low_lanes(columns):
    return lax.broadcasted_iota(jnp.int32, (columns, LANES), 1) < LANES // 2


def clear(wide, cells):
    step = 512

    def begin(i, carry):
        wide[pl.ds(pl.multiple_of(i * step, step), step), :] = jnp.zeros((step, LANES), F32)
        return carry

    lax.fori_loop(0, cells // step, begin, 0)


def narrow(wide, out_ref):
    step = 512

    def finish(i, carry):
        block = pl.ds(pl.multiple_of(i * step, step), step)
        out_ref[block, :] = wide[block, :].astype(BF16)
        return carry

    lax.fori_loop(0, out_ref.shape[0] // step, finish, 0)


def place_rows(count, cells, index_ref, feat_ref, old_ref, out_ref, wide, rows):
    if old_ref is None:
        clear(wide, cells)
    else:
        wide[0:cells, :] = old_ref[...].astype(F32)
    rows[...] = feat_ref[...].astype(F32)

    def place(i, carry):
        for j in range(8):
            wide[pl.ds(index_ref[i * 8 + j], 1), :] = rows[pl.ds(i * 8 + j, 1), :]
        return carry

    lax.fori_loop(0, count // 8, place, 0)
    narrow(wide, out_ref)


def scatter_kernel(count, cells, fresh, *refs):
    if fresh:
        index_ref, feat_ref, out_ref, wide, rows = refs
        place_rows(count, cells, index_ref, feat_ref, None, out_ref, wide, rows)
    else:
        place_rows(count, cells, *refs)


def scatter_rows(index, feats, old, columns):
    cells = DEPTH * (BLOCK_ROWS + 2 * HALO) * columns
    count = index.shape[0]
    fresh = old is None
    return pl.pallas_call(
        functools.partial(scatter_kernel, count, cells, fresh),
        out_shape=jax.ShapeDtypeStruct((cells, LANES), BF16),
        in_specs=smem(1) + vmem(1 if fresh else 2),
        out_specs=vmem(1)[0],
        scratch_shapes=[pltpu.VMEM((cells + 8, LANES), F32), pltpu.VMEM((count, LANES), F32)],
        compiler_params=params(),
        cost_estimate=work(15),
        name="grid_scatter",
    )(*((index, feats) if fresh else (index, feats, old)))


TOP, BOTTOM, EVEN, FIRST_ROW, EDGE_SHIFT = range(5)


def list_cells(columns, edge_ref, feat_ref, spots, owns):
    sources = feat_ref.shape[0] // (CAP + EDGE_CAP + 48)
    main = CAP // LANES
    tall = BLOCK_ROWS + 2 * HALO
    for a in range(sources):
        base = a * (CAP + EDGE_CAP + 48)
        words = feat_ref[base + CAP : base + CAP + 32, :].astype(F32).astype(jnp.int32)
        start = base + CAP + 32 + EDGE_CAP
        edges = feat_ref[start : start + 16, :].astype(F32).astype(jnp.int32)
        for side, (high, half, mixed) in enumerate(
            (
                (words[0:main], words[main : 2 * main], words[2 * main : 3 * main]),
                (edges[0:1], edges[1:2], edges[2:3]),
            )
        ):
            line = (mixed >> 1) - edge_ref[FIRST_ROW]
            if side:
                line = line + edge_ref[EDGE_SHIFT]
            cross = half * 2 + (mixed & 1)
            inside = (high > 0) & (line >= -HALO) & (line < BLOCK_ROWS + HALO)
            spot = ((high - 1) * tall + line + HALO) * columns + cross
            spot = jnp.where(inside, spot, DEPTH * tall * columns)
            if side:
                spots[a * (main + 1) + main : (a + 1) * (main + 1), :] = spot
                continue
            spots[a * (main + 1) : a * (main + 1) + main, :] = spot
            inside = (high > 0) & (line >= 0) & (line < BLOCK_ROWS)
            spot = ((high - 1) * BLOCK_ROWS + line) * columns + cross
            owns[a * main : (a + 1) * main, :] = jnp.where(
                inside, spot, DEPTH * BLOCK_ROWS * columns
            )


def scatter_middle_kernel(
    columns, edge_ref, feat_ref, kernel_ref, bias_ref, grid_ref, out_ref, own_ref,
    wide, rows, held, weight_ref, spots, index, copied, done,
):
    list_cells(columns, edge_ref, feat_ref, spots, own_ref)
    to_scalar = pltpu.make_async_copy(spots, index, copied)
    to_scalar.start()
    clear(wide, held.shape[0])
    rows[...] = feat_ref[...].astype(F32)
    to_scalar.wait()
    blocks = CAP // LANES + 1
    length = CAP + EDGE_CAP + 48

    def place(part, carry):
        block = part % blocks
        base = part // blocks * length + block * LANES + jnp.where(block == blocks - 1, 32, 0)

        base = pl.multiple_of(base, 8)
        for j in range(LANES):
            wide[pl.ds(index[part, j], 1), :] = rows[pl.ds(base + j, 1), :]
        return carry

    lax.fori_loop(0, index.shape[0], place, 0)
    narrow(wide, held)
    copy = pltpu.make_async_copy(held, grid_ref, done)
    copy.start()
    middle_kernel(columns, edge_ref, held, kernel_ref, bias_ref, out_ref, weight_ref)
    copy.wait()


def scatter_middle(edges, feats, w_mid, bias, columns):
    cells = DEPTH * (BLOCK_ROWS + 2 * HALO) * columns
    count = feats.shape[0]
    sources = count // (CAP + EDGE_CAP + 48)
    parts = sources * (CAP // LANES + 1)
    return pl.pallas_call(
        functools.partial(scatter_middle_kernel, columns),
        out_shape=(
            jax.ShapeDtypeStruct((cells, LANES), BF16),
            jax.ShapeDtypeStruct(((BLOCK_ROWS + 2) * columns, PAIRS * LANES), BF16),
            jax.ShapeDtypeStruct((sources * CAP // LANES, LANES), jnp.int32),
        ),
        in_specs=smem(1) + vmem(3),
        out_specs=[pl.BlockSpec(memory_space=pl.ANY)] + vmem(2),
        scratch_shapes=[
            pltpu.VMEM((cells + 8, LANES), F32),
            pltpu.VMEM((count, LANES), F32),
            pltpu.VMEM((cells, LANES), BF16),
            pltpu.VMEM((2, 9 * LANES, 2 * LANES), BF16),
            pltpu.VMEM((parts, LANES), jnp.int32),
            pltpu.SMEM((parts, LANES), jnp.int32),
            pltpu.SemaphoreType.DMA,
            pltpu.SemaphoreType.DMA,
        ],
        compiler_params=params(limit=57),
        cost_estimate=work(36),
        name="scatter_middle",
    )(edges, feats, w_mid, bias)


def middle_kernel(columns, edge_ref, grid_ref, kernel_ref, bias_ref, out_ref, weight_ref):
    low = low_lanes(columns)
    none = jnp.zeros((LANES, LANES // 2), BF16)
    for place in range(9):
        one, two, three = (
            kernel_ref[place * 3 + e].astype(F32).T.astype(BF16) for e in range(3)
        )
        rows = slice(place * LANES, (place + 1) * LANES)
        weight_ref[0, rows, :] = jnp.concatenate([one, two, three, none], axis=1)
        weight_ref[1, rows, :] = jnp.concatenate([two, one, none, three], axis=1)
    grid_rows = BLOCK_ROWS + 2 * HALO
    depth_out = DEPTH // 2

    def row(m, carry):
        sums = []
        for o in range(depth_out):
            taps = (1, 2) if o == 0 else (0, 1, 2)
            left = jnp.concatenate(
                [
                    grid_ref[at_row((2 * o + a - 1) * grid_rows + m + b, columns), :]
                    for a in taps
                    for b in range(3)
                ],
                axis=1,
            )
            right = weight_ref[o % 2, 3 * LANES * (3 - len(taps)) :, :]
            sums.append(jnp.dot(left, right, preferred_element_type=F32))
        inside = (m > 0) & (m < BLOCK_ROWS + 1) | (m == 0) & (edge_ref[0] > 0)
        inside = inside | (m == BLOCK_ROWS + 1) & (edge_ref[1] > 0)
        keep = jnp.where(inside, 1.0, 0.0)
        for j in range(PAIRS):
            even = sums[2 * j]
            if 2 * j + 1 < depth_out:
                odd = sums[2 * j + 1]
                first = jnp.where(low, even[:, :LANES], odd[:, :LANES])
                middle = jnp.where(low, odd[:, :LANES], even[:, :LANES])
                last = even[:, LANES:] + odd[:, LANES:]
            else:
                first = even[:, :LANES]
                middle = first
                last = even[:, LANES:]
            total = from_left(first) + pltpu.roll(middle, LANES // 2, 1) + from_right(last)
            total = jnp.maximum(total + bias_ref[0:1, :], 0.0) * keep
            if 2 * j + 1 == depth_out:
                total = jnp.where(low, total, 0.0)
            out_ref[at_row(m, columns), j * LANES : (j + 1) * LANES] = total.astype(BF16)
        return carry

    lax.fori_loop(0, BLOCK_ROWS + 2, row, 0, unroll=2)


def middle_forward(edges, grid, w_mid, bias, columns):
    return pl.pallas_call(
        functools.partial(middle_kernel, columns),
        out_shape=jax.ShapeDtypeStruct(((BLOCK_ROWS + 2) * columns, PAIRS * LANES), BF16),
        in_specs=smem(1) + vmem(3),
        out_specs=vmem(1)[0],
        scratch_shapes=[pltpu.VMEM((2, 9 * LANES, 2 * LANES), BF16)],
        compiler_params=params(),
        cost_estimate=work(26),
        name="middle_forward",
    )(edges, grid, w_mid, bias)


def row_above(edge_ref, beside_ref, across_ref, lanes):
    found = jnp.where(
        edge_ref[EVEN] > 0, across_ref[:, lanes].astype(F32), beside_ref[:, lanes].astype(F32)
    )
    return jnp.where(edge_ref[TOP] > 0, found, 0.0)


def row_below(edge_ref, beside_ref, across_ref, lanes):
    found = jnp.where(
        edge_ref[EVEN] > 0, beside_ref[:, lanes].astype(F32), across_ref[:, lanes].astype(F32)
    )
    return jnp.where(edge_ref[BOTTOM] > 0, found, 0.0)


def put_edges(edge_ref, beside_ref, across_ref, first, last):
    if first is not None:

        @pl.when(edge_ref[EVEN] > 0)
        def _():
            across_ref[...] = first

        @pl.when(edge_ref[EVEN] == 0)
        def _():
            beside_ref[...] = first

    if last is not None:

        @pl.when(edge_ref[EVEN] > 0)
        def _():
            beside_ref[...] = last

        @pl.when(edge_ref[EVEN] == 0)
        def _():
            across_ref[...] = last


def column_taps(own, j):
    low = low_lanes(own.shape[0])
    other = pltpu.roll(own, LANES // 2, 1)
    both = [jnp.where(low, own, other)]
    if 2 * j + 1 < DEPTH // 2:
        both.append(jnp.where(low, other, own))
    return [(jnp.where(low, from_right(x), x), from_left(x)) for x in both]


def middle_data_kernel(
    count, columns, index_ref, edge_ref, d_ref, beside_ref, across_ref, kernel_ref, out_ref,
    near, far, wide, rows, weight_ref,
):
    padded = BLOCK_ROWS + 2
    half = LANES // 2
    cells = DEPTH * BLOCK_ROWS * columns
    span = 10 * half
    for a, first, side in ((1, 0, 0), (2, 0, 1), (0, span, 1)):
        lanes = slice(side * LANES, (side + 1) * LANES)
        for b in range(3):
            for e in range(3):
                block = (2 - b) * 2 + e if e < 2 else 6 + 2 - b
                own = kernel_ref[(a * 3 + b) * 3 + e]
                weight_ref[first + block * half : first + (block + 1) * half, lanes] = own
        weight_ref[first + span - half : first + span, lanes] = jnp.zeros((half, LANES), BF16)
    weight_ref[span:, :LANES] = jnp.zeros((span, LANES), BF16)

    def build(r, load):
        for j in range(PAIRS):
            own = load(slice(j * LANES, (j + 1) * LANES))
            for k, (pair, left) in enumerate(column_taps(own, j)):
                o = 2 * j + k
                near[o, at_row(r, columns), :] = pair.astype(BF16)
                far[o, at_row(r, columns), 0:half] = left[:, 0:half].astype(BF16)
                if not (isinstance(r, int) and r == 0):
                    far[o, at_row(r - 1, columns), half:LANES] = left[:, half:].astype(BF16)

    def build_own(r):
        build(r + 1, lambda lanes: d_ref[at_row(r, columns), lanes].astype(F32))

    build(0, lambda lanes: row_above(edge_ref, beside_ref, across_ref, lanes))
    for r in range(3):
        build_own(r)
    for o in range(DEPTH // 2):
        far[o, (padded - 1) * columns :, half:LANES] = jnp.zeros((columns, half), BF16)

    def row(r):
        def pieces(o):
            return [near[o, at_row(r + i, columns), :] for i in range(3)] + [
                far[o, at_row(r + i, columns), :] for i in (0, 2)
            ]

        for o in range(DEPTH // 2):
            left = jnp.concatenate(pieces(o) + (pieces(o + 1) if o < DEPTH // 2 - 1 else []), axis=1)
            total = jnp.dot(left, weight_ref[0 : left.shape[1], :], preferred_element_type=F32)
            wide[at_row(2 * o * BLOCK_ROWS + r, columns), :] = total[:, :LANES]
            wide[at_row((2 * o + 1) * BLOCK_ROWS + r, columns), :] = total[:, LANES:]

    def row_and_build(r, carry):
        row(r)
        build_own(r + 3)
        return carry

    lax.fori_loop(0, BLOCK_ROWS - 3, row_and_build, 0)
    row(BLOCK_ROWS - 3)
    build(BLOCK_ROWS + 1, lambda lanes: row_below(edge_ref, beside_ref, across_ref, lanes))
    row(BLOCK_ROWS - 2)
    row(BLOCK_ROWS - 1)
    wide[cells:, :] = jnp.zeros((8, LANES), F32)

    def pick(part, carry):
        base = pl.multiple_of(part * LANES, LANES)
        for j in range(LANES):
            rows[pl.ds(base + j, 1), :] = wide[pl.ds(index_ref[part, j], 1), :]
        return carry

    lax.fori_loop(0, count // LANES, pick, 0)
    out_ref[...] = rows[...].astype(BF16)


def middle_data(index, edges, d_rows, beside, across, w_mid, columns):
    count = index.size
    padded = (BLOCK_ROWS + 2) * columns
    return pl.pallas_call(
        functools.partial(middle_data_kernel, count, columns),
        out_shape=jax.ShapeDtypeStruct((count, LANES), BF16),
        in_specs=smem(2) + vmem(4),
        out_specs=vmem(1)[0],
        scratch_shapes=[
            pltpu.VMEM((DEPTH // 2, padded, LANES), BF16),
            pltpu.VMEM((DEPTH // 2, padded, LANES), BF16),
            pltpu.VMEM((DEPTH * BLOCK_ROWS * columns + 8, LANES), F32),
            pltpu.VMEM((count, LANES), F32),
            pltpu.VMEM((10 * LANES, 2 * LANES), BF16),
        ],
        compiler_params=params(limit=50),
        cost_estimate=work(30),
        name="middle_data",
    )(index, edges, d_rows, beside, across, w_mid)


def middle_weight_kernel(
    columns, grid_hbm, d_ref, out_ref, total, taps_ref, turned, grid_ref, arrived
):
    grid_rows = BLOCK_ROWS + 2 * HALO
    half = LANES // 2

    def copy(i):
        ahead = 2 if isinstance(i, int) and i == 0 else 0
        parts = []
        for d in range(DEPTH):
            begin = (d * grid_rows + 2 * i + 3 - ahead) * columns
            rows = pl.ds(begin if isinstance(i, int) else pl.multiple_of(begin, 32), (2 + ahead) * columns)
            parts.append(
                pltpu.make_async_copy(grid_hbm.at[rows, :], grid_ref.at[rows, :], arrived.at[i, d])
            )
        return parts

    for i in range(BLOCK_ROWS // 2):
        for part in copy(i):
            part.start()
    total[...] = jnp.zeros_like(total)
    for part in copy(0):
        part.wait()

    def rows(i, carry):
        @pl.when(i > 0)
        def _():
            for part in copy(i):
                part.wait()

        for k in range(2):
            for j in range(PAIRS):
                own = d_ref[at_row(i * 2 + k, columns), j * LANES : (j + 1) * LANES].astype(F32)
                for n, (pair, left) in enumerate(column_taps(own, j)):
                    place = slice(k * columns, (k + 1) * columns)
                    taps_ref[2 * j + n, place, 0:LANES] = pair.astype(BF16)
                    taps_ref[2 * j + n, place, LANES:] = left.astype(BF16)
        for o in range(DEPTH // 2):
            depth_taps = (1, 2) if o == 0 else (0, 1, 2)
            cells = jnp.concatenate(
                [
                    grid_ref[
                        pl.ds(
                            pl.multiple_of(
                                ((2 * o + a - 1) * grid_rows + i * 2 + 1 + b) * columns, 32
                            ),
                            2 * columns,
                        ),
                        :,
                    ]
                    for a in depth_taps
                    for b in range(3)
                ],
                axis=1,
            )
            part = lax.dot_general(
                taps_ref[o], cells, (((0,), (0,)), ((), ())), preferred_element_type=F32
            )
            if o == 0:
                total[:, 3 * LANES :] += part
            else:
                total[...] += part
        return carry

    lax.fori_loop(0, BLOCK_ROWS // 2, rows, 0, unroll=2)
    low = low_lanes(LANES // 2)
    for place in range(9):
        for side in range(2):
            turned[...] = total[
                side * LANES : (side + 1) * LANES, place * LANES : (place + 1) * LANES
            ].T
            even = turned[pl.ds(0, half, stride=2), :]
            odd = turned[pl.ds(1, half, stride=2), :]
            at = (place * 3 + side * 2) * half
            out_ref[at : at + half, :] = jnp.where(low, even, pltpu.roll(odd, half, 1))
            if side == 0:
                out_ref[at + half : at + 2 * half, :] = jnp.where(
                    low, pltpu.roll(even, half, 1), odd
                )


def middle_weight(grid, d_rows, columns):
    return pl.pallas_call(
        functools.partial(middle_weight_kernel, columns),
        out_shape=jax.ShapeDtypeStruct((27 * LANES // 2, LANES), F32),
        in_specs=[pl.BlockSpec(memory_space=pl.ANY)] + vmem(1),
        out_specs=vmem(1)[0],
        scratch_shapes=[
            pltpu.VMEM((2 * LANES, 9 * LANES), F32),
            pltpu.VMEM((DEPTH // 2, 2 * columns, 2 * LANES), BF16),
            pltpu.VMEM((LANES, LANES), F32),
            pltpu.VMEM(grid.shape, BF16),
            pltpu.SemaphoreType.DMA((BLOCK_ROWS // 2, DEPTH)),
        ],
        compiler_params=params(limit=32),
        cost_estimate=work(26),
        name="middle_weight",
    )(grid, d_rows)


def region_kernel(
    columns,
    scale_ref,
    edge_ref,
    bev_ref,
    weight_ref,
    bias_ref,
    head_ref,
    labels_ref,
    targets_ref,
    d_ref,
    beside_ref,
    across_ref,
    grad_head_ref,
    sums_ref,
    held,
):
    outs = head_ref.shape[0]
    cells = d_ref.shape[0]
    span = cells // 3
    scale = scale_ref[0, 0]
    head = head_ref[...]
    head_three = jnp.concatenate([head, head, head], axis=0)
    own = lax.broadcasted_iota(jnp.int32, (outs, LANES), 0)
    own = own == lax.broadcasted_iota(jnp.int32, (outs, LANES), 1)
    head_bias = jnp.sum(jnp.where(own, bias_ref[2:3, :], 0.0), axis=1, keepdims=True)

    def row(r, carry):
        left = jnp.concatenate([bev_ref[at_row(r + b, columns), :] for b in range(3)], axis=1)
        part = jnp.dot(left, weight_ref[...], preferred_element_type=F32)
        pre = from_left(part[:, :LANES]) + part[:, LANES : 2 * LANES]
        held[at_row(r, columns), :] = pre + from_right(part[:, 2 * LANES :]) + bias_ref[1:2, :]
        return carry

    lax.fori_loop(0, cells // columns, row, 0, unroll=2)
    kind = lax.broadcasted_iota(jnp.int32, (outs, span), 0) % 8 == 0
    grad_head = jnp.zeros((3 * outs, LANES), F32)
    head_sum = jnp.zeros((outs, 1), F32)
    loss_sum = jnp.zeros((outs, 1), F32)
    row_sum = jnp.zeros((8, LANES), F32)
    for i in range(3):
        place = slice(i * span, (i + 1) * span)
        pre = held[place, :]
        act = jnp.maximum(pre, 0.0).astype(BF16)
        heads = lax.dot_general(head, act, (((1,), (1,)), ((), ())), preferred_element_type=F32)
        heads = heads + head_bias
        label = labels_ref[:, place]
        positive = jnp.where(label == 1, 1.0, 0.0)
        negative = jnp.where(label == 0, 1.0, 0.0)
        tail = jnp.log1p(jnp.exp(-jnp.abs(heads)))
        soft_up = jnp.maximum(heads, 0.0) + tail
        soft_down = jnp.maximum(-heads, 0.0) + tail
        probab = jax.nn.sigmoid(heads)
        rest = 1.0 - probab
        focal = positive * FOCAL_ALPHA * rest * rest * soft_down
        focal = focal + negative * (1.0 - FOCAL_ALPHA) * probab * probab * soft_up
        d_focal = positive * FOCAL_ALPHA * rest * rest * (-2.0 * probab * soft_down - rest)
        d_focal = d_focal + negative * (1.0 - FOCAL_ALPHA) * probab * probab * (
            2.0 * rest * soft_up + probab
        )
        offset = heads - targets_ref[:, place]
        size = jnp.abs(offset)
        near = size < 1.0 / 9.0
        smooth = jnp.where(near, 4.5 * offset * offset, size - 1.0 / 18.0)
        d_smooth = jnp.where(near, 9.0 * offset, jnp.where(offset > 0.0, 1.0, -1.0))
        losses = jnp.where(kind, focal, 2.0 * positive * smooth)
        loss_sum = loss_sum + jnp.sum(losses, axis=1, keepdims=True)
        d_heads = jnp.where(kind, d_focal, 2.0 * positive * d_smooth) * scale
        head_sum = head_sum + jnp.sum(d_heads, axis=1, keepdims=True)
        high = d_heads.astype(BF16)
        rest_one = d_heads - high.astype(F32)
        mid = rest_one.astype(BF16)
        tiny = (rest_one - mid.astype(F32)).astype(BF16)
        three = jnp.concatenate([high, mid, tiny], axis=0)
        grad_head = grad_head + jnp.dot(three, act, preferred_element_type=F32)
        d_act = lax.dot_general(
            three, head_three, (((0,), (0,)), ((), ())), preferred_element_type=F32
        )
        d_pre = jnp.where(pre > 0.0, d_act, 0.0).astype(BF16)
        d_ref[place, :] = d_pre
        row_sum = row_sum + jnp.sum(d_pre.astype(F32).reshape(span // 8, 8, LANES), axis=0)
        if i == 0:
            put_edges(edge_ref, beside_ref, across_ref, d_pre[:columns, :], None)
        if i == 2:
            put_edges(edge_ref, beside_ref, across_ref, None, d_pre[span - columns :, :])
    grad_head_ref[...] = grad_head
    sums_ref[0:8, :] = row_sum
    sums_ref[8:24, :] = jnp.broadcast_to(head_sum, (outs, LANES))
    sums_ref[24:32, :] = jnp.broadcast_to(jnp.sum(loss_sum, axis=0, keepdims=True), (8, LANES))


def region_forward(scale, edges, bev, weights, bias, head, labels, targets, columns):
    cells = labels.shape[1]
    outs = head.shape[0]
    return pl.pallas_call(
        functools.partial(region_kernel, columns),
        out_shape=(
            jax.ShapeDtypeStruct((cells, LANES), BF16),
            jax.ShapeDtypeStruct((columns, LANES), BF16),
            jax.ShapeDtypeStruct((columns, LANES), BF16),
            jax.ShapeDtypeStruct((3 * outs, LANES), F32),
            jax.ShapeDtypeStruct((32, LANES), F32),
        ),
        in_specs=smem(2) + vmem(6),
        out_specs=vmem(5),
        scratch_shapes=[pltpu.VMEM((cells, LANES), F32)],
        compiler_params=params(limit=28),
        cost_estimate=work(16),
        name="region_forward",
    )(
        scale.reshape(1, 1),
        edges,
        bev,
        weights,
        bias,
        head,
        labels,
        targets,
    )


def region_order_kernel(blocks, anc_ref, *refs):
    part_refs, (in_ref, back_ref, wide, lined) = refs[:blocks], refs[blocks:]
    depth_out = DEPTH // 2
    half = LANES // 2
    width = PAIRS * LANES
    share = half // blocks
    used = depth_out * half
    for b in range(3):
        for e in range(3):
            for k, part_ref in enumerate(part_refs):
                first = lax.rem(anc_ref[0] + k, blocks) * share
                wide[...] = part_ref[b, e].astype(F32)
                for h in range(depth_out):
                    at = pl.multiple_of(h * half + first, 8)
                    lined[pl.ds(at, share), :] = wide[pl.ds(h, share, stride=depth_out), :]
            lined[used:, :] = jnp.zeros((width - used, LANES), F32)
            in_ref[b * width : (b + 1) * width, e * LANES : (e + 1) * LANES] = lined[...].astype(
                BF16
            )
            at = (b * 3 + e) * LANES
            back_ref[at : at + LANES, :] = lined[...].T.astype(BF16)


def region_order(anc, parts):
    width = PAIRS * LANES
    return pl.pallas_call(
        functools.partial(region_order_kernel, len(parts)),
        out_shape=(
            jax.ShapeDtypeStruct((3 * width, 3 * LANES), BF16),
            jax.ShapeDtypeStruct((9 * LANES, width), BF16),
        ),
        in_specs=smem(1) + vmem(len(parts)),
        out_specs=vmem(2),
        scratch_shapes=[
            pltpu.VMEM((parts[0].shape[2], LANES), F32),
            pltpu.VMEM((width, LANES), F32),
        ],
        compiler_params=params(limit=24),
        cost_estimate=work(4),
        name="region_order",
    )(anc, *parts)


def region_data_kernel(
    columns, edge_ref, d_ref, beside_in, across_in, bev_ref, weight_ref,
    out_ref, beside_ref, across_ref, sums_ref, taps_ref,
):
    rows = out_ref.shape[0] // columns
    width = PAIRS * LANES
    sums_ref[...] = jnp.zeros_like(sums_ref)

    def build(r, own):
        taps_ref[at_row(r, columns), 0:LANES] = from_right(own).astype(BF16)
        taps_ref[at_row(r, columns), LANES : 2 * LANES] = own.astype(BF16)
        taps_ref[at_row(r, columns), 2 * LANES :] = from_left(own).astype(BF16)

    def build_own(r):
        build(r + 1, d_ref[at_row(r, columns), :].astype(F32))

    build(0, row_above(edge_ref, beside_in, across_in, slice(None)))
    build_own(0)
    build_own(1)

    def row(r):
        left = jnp.concatenate([taps_ref[at_row(r + 2 - b, columns), :] for b in range(3)], axis=1)
        total = jnp.dot(left, weight_ref[...], preferred_element_type=F32)
        alive = bev_ref[at_row(r + 1, columns), :].astype(F32) > 0.0
        kept = jnp.where(alive, total, 0.0).astype(BF16)
        out_ref[at_row(r, columns), :] = kept

        sums_ref[...] += jnp.sum(kept.astype(F32).reshape(columns // 8, 8, width), axis=0)
        return kept

    def row_and_build(r, carry):
        row(r)
        build_own(r + 2)
        return carry

    put_edges(edge_ref, beside_ref, across_ref, row(0), None)
    build_own(2)
    lax.fori_loop(1, rows - 2, row_and_build, 0)
    row(rows - 2)
    build(rows + 1, row_below(edge_ref, beside_in, across_in, slice(None)))
    put_edges(edge_ref, beside_ref, across_ref, None, row(rows - 1))


def region_data(edges, d_rows, beside, across, bev, weights, columns):
    width = PAIRS * LANES
    return pl.pallas_call(
        functools.partial(region_data_kernel, columns),
        out_shape=(
            jax.ShapeDtypeStruct((d_rows.shape[0], width), BF16),
            jax.ShapeDtypeStruct((columns, width), BF16),
            jax.ShapeDtypeStruct((columns, width), BF16),
            jax.ShapeDtypeStruct((8, width), F32),
        ),
        in_specs=smem(1) + vmem(5),
        out_specs=vmem(4),
        scratch_shapes=[pltpu.VMEM((d_rows.shape[0] + 2 * columns, 3 * LANES), BF16)],
        compiler_params=params(limit=28),
        cost_estimate=work(13),
        name="region_data",
    )(edges, d_rows, beside, across, bev, weights)


def region_weight_kernel(columns, blocks, d_ref, bev_ref, out_ref, total, taps_ref):
    rows = d_ref.shape[0] // columns
    width = PAIRS * LANES
    depth_out = DEPTH // 2
    half = LANES // 2
    total[...] = jnp.zeros_like(total)

    def two(i, carry):
        for k in range(2):
            own = d_ref[at_row(i * 2 + k, columns), :].astype(F32)
            place = slice(k * columns, (k + 1) * columns)
            taps_ref[place, 0:LANES] = from_right(own).astype(BF16)
            taps_ref[place, LANES : 2 * LANES] = own.astype(BF16)
            taps_ref[place, 2 * LANES :] = from_left(own).astype(BF16)
        cells = jnp.concatenate(
            [
                bev_ref[pl.ds(pl.multiple_of((i * 2 + b) * columns, 32), 2 * columns), :]
                for b in range(3)
            ],
            axis=1,
        )
        total[...] += lax.dot_general(
            taps_ref[...], cells, (((0,), (0,)), ((), ())), preferred_element_type=F32
        )
        return carry

    lax.fori_loop(0, rows // 2, two, 0, unroll=2)
    share = half // blocks
    for b in range(3):
        for e in range(3):
            for j in range(PAIRS):
                start = b * width + j * LANES
                turned = total[e * LANES : (e + 1) * LANES, start : start + LANES].T
                for k in range(min(2, depth_out - 2 * j)):
                    for q in range(blocks):
                        begin = k * half + q * share
                        base = ((q * 3 + b) * 3 + e) * share * depth_out
                        out_ref[pl.ds(base + 2 * j + k, share, stride=depth_out), :] = turned[
                            begin : begin + share, :
                        ]


def region_weight(d_own, bev, columns, blocks):
    width = PAIRS * LANES
    return pl.pallas_call(
        functools.partial(region_weight_kernel, columns, blocks),
        out_shape=jax.ShapeDtypeStruct((9 * (DEPTH // 2) * (LANES // 2), LANES), F32),
        in_specs=vmem(2),
        out_specs=vmem(1)[0],
        scratch_shapes=[
            pltpu.VMEM((3 * LANES, 3 * width), F32),
            pltpu.VMEM((2 * columns, 3 * LANES), BF16),
        ],
        compiler_params=params(limit=28),
        cost_estimate=work(10),
        name="region_weight",
    )(d_own, bev)


def prepare_kernel(
    slots, anc_count, device_rows, edge_ref, points_ref, line_ref, labels_ref,
    stats_ref, place_ref, digit_ref,
):
    voxels, width = points_ref.shape
    features = 7
    row = line_ref[1:2, :]
    exists = line_ref[3:4, :]
    column = line_ref[2:3, :]
    digits = jnp.concatenate(
        [
            (line_ref[0:1, :] + 1) * exists,
            (column >> 1) * exists,
            (row * 2 + (column & 1)) * exists,
            line_ref[4:5, :],
        ],
        axis=0,
    ).astype(F32)
    none = jnp.zeros((LANES - 4, LANES), F32)
    for i in range(voxels // LANES):
        here = slice(i * LANES, (i + 1) * LANES)
        digit_ref[here, :] = jnp.concatenate([digits[:, here], none], axis=0).T.astype(BF16)
    lane = lax.broadcasted_iota(jnp.int32, (CHUNK, width), 1)
    ones_lane = features * slots
    slot = jnp.where(lane == ones_lane, -1, lane % slots)
    total = jnp.zeros((width, width), F32)
    for i in range(voxels // CHUNK):
        here = slice(i * CHUNK, (i + 1) * CHUNK)
        count = digit_ref[here, 3:4].astype(F32).astype(jnp.int32)
        block = jnp.where(slot < count, points_ref[here, :].astype(F32), 0.0).astype(BF16)
        total = total + lax.dot_general(
            block, block, (((0,), (0,)), ((), ())), preferred_element_type=F32
        )
    row_at = lax.broadcasted_iota(jnp.int32, (width, width), 0)
    col_at = lax.broadcasted_iota(jnp.int32, (width, width), 1)
    same = (row_at % slots == col_at % slots) | (row_at == ones_lane)
    total = jnp.where(same & (row_at <= ones_lane) & (col_at < ones_lane), total, 0.0)
    rows = [
        jnp.sum(jnp.where(row_at // slots == k, total, 0.0), axis=0, keepdims=True)
        for k in range(features + 1)
    ]
    stacked = jnp.concatenate(rows, axis=0)
    col_eight = lax.broadcasted_iota(jnp.int32, (8, width), 1)
    lane_eight = lax.broadcasted_iota(jnp.int32, (8, LANES), 1)
    row_eight = lax.broadcasted_iota(jnp.int32, (8, LANES), 0)
    stats = jnp.zeros((8, LANES), F32)
    for k in range(features):
        picked = jnp.sum(jnp.where(col_eight // slots == k, stacked, 0.0), axis=1, keepdims=True)
        stats = stats + jnp.where(lane_eight == k, picked, 0.0)
    counted = jnp.sum(digits[3:4, :], axis=1, keepdims=True)
    hits = jnp.zeros(labels_ref.shape[1:], F32)
    for r in range(labels_ref.shape[0]):
        hits = hits + jnp.where(labels_ref[r] == 1, 1.0, 0.0)
    found = jnp.sum(jnp.sum(hits, axis=1, keepdims=True), axis=0, keepdims=True)
    real = exists > 0
    lists = []
    for q in range(anc_count):
        begin = q * device_rows - HALO
        lists.append(real & (row >= begin) & (row < begin + device_rows + 2 * HALO))
    lists.append(real & (row < HALO) & (edge_ref[0] > 0))
    lists.append(real & (row >= anc_count * device_rows - HALO) & (edge_ref[1] > 0))
    lists += [real & (row < 0)] * (8 - len(lists))
    member = jnp.concatenate([jnp.where(x, 1.0, 0.0) for x in lists], axis=0)
    before = (
        lax.broadcasted_iota(jnp.int32, (LANES, LANES), 0)
        < lax.broadcasted_iota(jnp.int32, (LANES, LANES), 1)
    )
    before = jnp.where(before, 1.0, 0.0).astype(BF16)
    carry = jnp.zeros((8, 1), F32)
    eight = lax.broadcasted_iota(jnp.int32, (8, LANES), 0)
    for i in range(voxels // LANES):
        here = slice(i * LANES, (i + 1) * LANES)
        part = member[:, here]
        ahead = jnp.dot(part.astype(BF16), before, preferred_element_type=F32) + carry
        places = jnp.where(part > 0.0, ahead, -1.0).astype(jnp.int32)
        owner = jnp.zeros((1, LANES), jnp.int32)
        own = jnp.full((1, LANES), -1, jnp.int32)
        for q in range(anc_count):
            mine = (row[:, here] >= q * device_rows) & (row[:, here] < (q + 1) * device_rows)
            mine = mine & real[:, here]
            owner = jnp.where(mine, q, owner)
            own = jnp.where(mine, places[q : q + 1, :], own)
        places = jnp.where(eight == 6, owner, jnp.where(eight == 7, own, places))
        place_ref[:, here] = places
        carry = carry + jnp.sum(part, axis=1, keepdims=True)
    is_edge = lax.broadcasted_iota(jnp.int32, (8, 1), 0) >= anc_count
    need = carry / jnp.where(is_edge, float(EDGE_CAP), float(CAP))
    need = jnp.max(need, axis=0, keepdims=True)
    for k, value in enumerate((counted, found, need)):
        stats = stats + jnp.where((lane_eight == 8) & (row_eight == k), value, 0.0)
    for i in range(stats_ref.shape[0]):
        stats_ref[i] = stats


def prepare(edges, points, lines, labels, anc_count, device_rows, slots, devices):
    voxels = points.shape[0]
    return pl.pallas_call(
        functools.partial(prepare_kernel, slots, anc_count, device_rows),
        out_shape=(
            jax.ShapeDtypeStruct((devices, 8, LANES), F32),
            jax.ShapeDtypeStruct((8, voxels), jnp.int32),
            jax.ShapeDtypeStruct((voxels, LANES), BF16),
        ),
        in_specs=smem(1) + vmem(3),
        out_specs=vmem(3),
        compiler_params=params(limit=24),
        cost_estimate=work(4),
        name="prepare",
    )(edges, points, lines, labels)


def batch_norm(stats, kernel):
    lanes = kernel.shape[1]
    moments = stats[:, 0:8]
    count = stats[0:1, 8:9]
    mixed = jnp.zeros((8, lanes), F32)
    for k in range(7):
        mixed = mixed + moments[:, k : k + 1] * kernel[k : k + 1, :]
    mean = mixed[7:8, :] / count
    second = jnp.sum(mixed * kernel, axis=0, keepdims=True) / count
    inv_std = lax.rsqrt(second - mean * mean + BN_EPSILON)
    return mixed, mean, inv_std, count


def first_layer(points, first_ref, scale, offset, valid):
    hidden = jnp.dot(points, first_ref[...], preferred_element_type=F32)
    act = jnp.where(valid, jnp.maximum(hidden * scale + offset, 0.0), 0.0)
    return act


def group_fold(values, combine):
    groups = values.shape[1] // LANES
    out = values[:, :LANES]
    for g in range(1, groups):
        out = combine(out, values[:, g * LANES : (g + 1) * LANES])
    out = combine(out, pltpu.roll(out, 32, 1))
    return combine(out, pltpu.roll(out, 64, 1))


def second_tail(pooled):
    lane = lax.broadcasted_iota(jnp.int32, pooled.shape, 1)
    return jnp.where(lane < 32, pooled, jnp.where(lane == 32, 1.0, 0.0))


def group_left(low, tail, count, g):
    lane = lax.broadcasted_iota(jnp.int32, tail.shape, 1)
    marked = (lane > 32) & (lane < 37) & (lane - (33 - 4 * g) >= count)
    side = jnp.where(marked, 1.0, tail).astype(BF16)
    return jnp.concatenate([low[:, g * LANES : (g + 1) * LANES], side], axis=1)


def encode_kernel(
    slots, points_ref, count_ref, stats_ref, kernel_ref, gain_ref, first_ref, second_ref,
    feat_ref, share_ref, slot_ref, held,
):
    lanes = first_ref.shape[1]
    _, mean, inv_std, _ = batch_norm(jnp.sum(stats_ref[...], axis=0), kernel_ref[...])
    scale = gain_ref[0:1, :] * inv_std
    offset = gain_ref[1:2, :] - mean * scale
    count = count_ref[:, 3:4].astype(F32).astype(jnp.int32)
    slot = lax.broadcasted_iota(jnp.int32, (CHUNK, lanes), 1) // 32
    act = first_layer(points_ref[...], first_ref, scale, offset, slot < count)
    tail = second_tail(group_fold(act, jnp.maximum))
    low = act.astype(BF16)
    top = jnp.full((CHUNK, LANES), -jnp.inf, F32)
    for g in range(lanes // LANES):
        left = group_left(low, tail, count, g)
        part = jnp.dot(left, second_ref[...], preferred_element_type=F32)
        for s in range(min(4, slots - 4 * g)):
            p = 4 * g + s
            one = part[:, s * LANES : (s + 1) * LANES]
            held[p] = one
            top = jnp.maximum(top, one)
    code = jnp.zeros((CHUNK, LANES), F32)
    for p in range(slots):
        code = code + jnp.where(held[p] == top, 2048.0 + p, 0.0)
    ties = jnp.floor(code / 2048.0)
    feat_ref[...] = jnp.maximum(top, 0.0)
    share_ref[...] = jnp.where(top > 0.0, 1.0 / ties, 0.0)
    slot_ref[...] = jnp.minimum(code - 2048.0 * ties, 127.0).astype(BF16)


def encode(points, counts, stats, kernel, gain, first, second, slots):
    voxels, width = points.shape
    lanes = first.shape[1]
    whole = lambda *shape: pl.BlockSpec(shape, lambda i: (0,) * len(shape))
    block = lambda size: pl.BlockSpec((CHUNK, size), lambda i: (i, 0))
    return pl.pallas_call(
        functools.partial(encode_kernel, slots),
        grid=(voxels // CHUNK,),
        out_shape=(
            jax.ShapeDtypeStruct((voxels, LANES), F32),
            jax.ShapeDtypeStruct((voxels, LANES), F32),
            jax.ShapeDtypeStruct((voxels, LANES), BF16),
        ),
        in_specs=[
            block(width),
            block(LANES),
            whole(*stats.shape),
            whole(8, lanes),
            whole(8, lanes),
            whole(width, lanes),
            whole(2 * LANES, 4 * LANES),
        ],
        out_specs=[block(LANES), block(LANES), block(LANES)],
        scratch_shapes=[pltpu.VMEM((slots, CHUNK, LANES), F32)],
        compiler_params=params("arbitrary", limit=30),
        cost_estimate=work(14),
        name="encode",
    )(points, counts, stats, kernel, gain, first, second)


def decode_kernel(
    slots, points_ref, count_ref, stats_ref, kernel_ref, gain_ref, first_ref, second_ref,
    feat_ref, share_ref, slot_ref, d_feat_ref, loss_ref, out_ref,
    first_sum, second_sum, joined, tail_sum,
):
    lanes = first_ref.shape[1]
    width = points_ref.shape[1]
    step = pl.program_id(0)

    @pl.when(step == 0)
    def _():
        first_sum[...] = jnp.zeros_like(first_sum)
        second_sum[...] = jnp.zeros_like(second_sum)

    _, mean, inv_std, _ = batch_norm(jnp.sum(stats_ref[...], axis=0), kernel_ref[...])
    scale = gain_ref[0:1, :] * inv_std
    offset = gain_ref[1:2, :] - mean * scale
    count = count_ref[:, 3:4].astype(F32).astype(jnp.int32)
    points = points_ref[...]
    slot = lax.broadcasted_iota(jnp.int32, (CHUNK, lanes), 1) // 32
    act = first_layer(points, first_ref, scale, offset, slot < count)
    pooled = group_fold(act, jnp.maximum)
    tail = second_tail(pooled)
    low = act.astype(BF16)
    share = share_ref[...]
    d_feat = d_feat_ref[...] * share
    d_low = d_feat.astype(BF16)
    shared = jnp.where((share > 0.0) & (share < 1.0), 1.0, 0.0)
    shared = jnp.max(jnp.max(shared, axis=1, keepdims=True)) > 0.0

    def group_back(g, left, pieces):
        d_part = jnp.concatenate(pieces, axis=1)
        second_sum[...] += lax.dot_general(
            left, d_part, (((0,), (0,)), ((), ())), preferred_element_type=F32
        )
        d_left = lax.dot_general(
            d_part, second_ref[...], (((1,), (1,)), ((), ())), preferred_element_type=F32
        )
        joined[:, g * LANES : (g + 1) * LANES] = d_left[:, :LANES]
        return d_left[:, LANES:]

    none = jnp.zeros((CHUNK, LANES), BF16)

    @pl.when(jnp.logical_not(shared))
    def _():
        found = slot_ref[...]
        d_tail = jnp.zeros((CHUNK, LANES), F32)
        for g in range(lanes // LANES):
            left = group_left(low, tail, count, g)
            pieces = [
                jnp.where(found == jnp.asarray(4 * g + s, BF16), d_low, none)
                if 4 * g + s < slots
                else none
                for s in range(4)
            ]
            d_tail = d_tail + group_back(g, left, pieces)
        tail_sum[...] = d_tail

    @pl.when(shared)
    def _():
        top = feat_ref[...]
        d_tail = jnp.zeros((CHUNK, LANES), F32)
        for g in range(lanes // LANES):
            left = group_left(low, tail, count, g)
            part = jnp.dot(left, second_ref[...], preferred_element_type=F32)
            pieces = []
            for s in range(4):
                if 4 * g + s < slots:
                    hit = part[:, s * LANES : (s + 1) * LANES] == top
                    pieces.append(jnp.where(hit, d_feat, 0.0).astype(BF16))
                else:
                    pieces.append(none)
            d_tail = d_tail + group_back(g, left, pieces)
        tail_sum[...] = d_tail

    wide = jnp.concatenate([pooled] * (lanes // LANES), axis=1)
    reached = act == wide
    ties = group_fold(jnp.where(reached, 1.0, 0.0), jnp.add)
    lane = lax.broadcasted_iota(jnp.int32, (CHUNK, LANES), 1)
    spread = jnp.where(lane < 32, tail_sum[...], 0.0)
    spread = spread + pltpu.roll(spread, 32, 1)
    spread = (spread + pltpu.roll(spread, 64, 1)) / ties
    spread = jnp.concatenate([spread] * (lanes // LANES), axis=1)
    d_act = joined[...] + jnp.where(reached, spread, 0.0)
    d_act = jnp.where(act > 0.0, d_act, 0.0).astype(BF16)
    first_sum[...] += lax.dot_general(
        points, d_act, (((0,), (0,)), ((), ())), preferred_element_type=F32
    )

    @pl.when(step == pl.num_programs(0) - 1)
    def _():
        row_at = lax.broadcasted_iota(jnp.int32, (width, lanes), 0)
        col_at = lax.broadcasted_iota(jnp.int32, (width, lanes), 1)
        same = (row_at % slots == col_at // 32) | (row_at == 7 * slots)
        total = jnp.where(same & (col_at // 32 < slots), first_sum[...], 0.0)
        rows = [
            jnp.sum(jnp.where(row_at // slots == k, total, 0.0), axis=0, keepdims=True)
            for k in range(8)
        ]
        first = group_fold(jnp.concatenate(rows, axis=0), jnp.add)
        upper = second_sum[0:32, 0:LANES]
        lower = second_sum[LANES : LANES + 40, 0:LANES]
        for s in range(1, 4):
            cols = slice(s * LANES, (s + 1) * LANES)
            upper = upper + second_sum[s * 32 : (s + 1) * 32, cols]
            lower = lower + second_sum[LANES : LANES + 40, cols]
        devices, layers = out_ref.shape[:2]
        none = jnp.zeros((devices * layers - 88, LANES), F32)
        rows = jnp.concatenate([first, upper, lower, loss_ref[...], none], axis=0)
        for k in range(layers):
            out_ref[:, k, :] = rows[k * devices : (k + 1) * devices, :]


def decode(
    points, counts, stats, kernel, gain, first, second, feat, share, slot, d_feat, loss, shape, slots
):
    voxels, width = points.shape
    lanes = first.shape[1]
    whole = lambda *shape: pl.BlockSpec(shape, lambda i: (0,) * len(shape))
    block = lambda size: pl.BlockSpec((CHUNK, size), lambda i: (i, 0))
    return pl.pallas_call(
        functools.partial(decode_kernel, slots),
        grid=(voxels // CHUNK,),
        out_shape=jax.ShapeDtypeStruct(shape + (LANES,), F32),
        in_specs=[
            block(width),
            block(LANES),
            whole(*stats.shape),
            whole(8, lanes),
            whole(8, lanes),
            whole(width, lanes),
            whole(2 * LANES, 4 * LANES),
            block(LANES),
            block(LANES),
            block(LANES),
            block(LANES),
            whole(8, LANES),
        ],
        out_specs=whole(*shape, LANES),
        scratch_shapes=[
            pltpu.VMEM((width, lanes), F32),
            pltpu.VMEM((2 * LANES, 4 * LANES), F32),
            pltpu.VMEM((CHUNK, lanes), F32),
            pltpu.VMEM((CHUNK, LANES), F32),
        ],
        compiler_params=params("arbitrary", limit=30),
        cost_estimate=work(28),
        name="decode",
    )(points, counts, stats, kernel, gain, first, second, feat, share, slot, d_feat, loss)


def encoder_weights_kernel(
    slots, one_ref, two_ref, bias_ref, gain_ref, first_ref, second_ref, kernel_ref, rows_ref
):
    width, lanes = first_ref.shape
    features = one_ref.shape[0] - 1
    row_at = lax.broadcasted_iota(jnp.int32, (width, LANES), 0)
    slot_at = lax.broadcasted_iota(jnp.int32, (width, LANES), 1) // 32
    one = jnp.concatenate([one_ref[...]] * 4, axis=1)
    tall = jnp.zeros((width, LANES), F32)
    for k in range(features):
        tall = jnp.where(row_at // slots == k, one[k : k + 1, :], tall)
    own_slot = row_at % slots
    for g in range(lanes // LANES):
        here = slice(g * LANES, (g + 1) * LANES)
        first_ref[:, here] = jnp.where(own_slot == 4 * g + slot_at, tall, 0.0).astype(BF16)
        kernel_ref[:, here] = one
        rows_ref[:, here] = jnp.concatenate([gain_ref[...]] * 4, axis=1)
    two = two_ref[...]
    half = two.shape[0] // 2
    upper = jnp.concatenate([two[:half]] * 4, axis=0)
    row_two = lax.broadcasted_iota(jnp.int32, (LANES, LANES), 0)
    for s in range(4):
        here = slice(s * LANES, (s + 1) * LANES)
        second_ref[0:LANES, here] = jnp.where(row_two // half == s, upper, 0.0).astype(BF16)
        lower = jnp.concatenate(
            [two[half:], bias_ref[...], jnp.zeros((LANES - half - 8, LANES), F32)], axis=0
        )
        second_ref[LANES:, here] = jnp.where(row_two == half + 1 + s, EMPTY, lower).astype(BF16)


def encoder_weights(w_one, w_two, bias_two, gain, shift, slots):
    features, c_one = w_one.shape
    lanes = -(-slots // 4) * LANES
    width = -(-(features * slots + 1) // LANES) * LANES
    one = jnp.pad(w_one.astype(F32), ((0, 1), (0, 0)))
    bias = jnp.pad(bias_two.astype(F32).reshape(1, -1), ((0, 7), (0, 0)))
    rows = jnp.pad(jnp.stack([gain, shift]).astype(F32), ((0, 6), (0, 0)))
    return pl.pallas_call(
        functools.partial(encoder_weights_kernel, slots),
        out_shape=(
            jax.ShapeDtypeStruct((width, lanes), BF16),
            jax.ShapeDtypeStruct((2 * LANES, 4 * LANES), BF16),
            jax.ShapeDtypeStruct((8, lanes), F32),
            jax.ShapeDtypeStruct((8, lanes), F32),
        ),
        in_specs=vmem(4),
        out_specs=vmem(4),
        compiler_params=params(limit=24),
        cost_estimate=work(2),
        name="encoder_weights",
    )(one, w_two.astype(F32), bias, rows)


def pick_rows(source, place_ref, line, capacity, offset):
    want = place_ref[line : line + 1, :] - offset
    row_at = lax.broadcasted_iota(jnp.int32, (capacity, source.shape[0]), 0)
    chosen = jnp.where(want == row_at, 1.0, 0.0).astype(BF16)
    found = jnp.dot(chosen, source, preferred_element_type=F32)
    return found[:, :LANES].astype(BF16), found[:, LANES:].T


def edge_lists_kernel(anc_count, offset_ref, feat_ref, digit_ref, place_ref, up_ref, down_ref):
    source = jnp.concatenate([feat_ref[...].astype(BF16), digit_ref[...]], axis=1)
    for side, edge_ref in enumerate((up_ref, down_ref)):
        rows, digits = pick_rows(source, place_ref, anc_count + side, EDGE_CAP, offset_ref[1])
        edge_ref[0:EDGE_CAP, :] = rows
        digits = jnp.concatenate([digits[0:8, :], jnp.zeros((8, LANES), F32)], axis=0)
        edge_ref[EDGE_CAP : EDGE_CAP + 16, :] = digits.astype(BF16)


def edge_lists(offsets, feat, digits, place, anc_count):
    return pl.pallas_call(
        functools.partial(edge_lists_kernel, anc_count),
        out_shape=(
            jax.ShapeDtypeStruct((EDGE_CAP + 16, LANES), BF16),
            jax.ShapeDtypeStruct((EDGE_CAP + 16, LANES), BF16),
        ),
        in_specs=smem(1) + vmem(3),
        out_specs=vmem(2),
        compiler_params=params(limit=24),
        cost_estimate=work(1),
        name="edge_lists",
    )(offsets, feat, digits, place)


def gather_lists_kernel(anc_count, offset_ref, feat_ref, digit_ref, place_ref, main_ref):
    source = jnp.concatenate([feat_ref[...].astype(BF16), digit_ref[...]], axis=1)
    for q in range(anc_count):
        rows, digits = pick_rows(source, place_ref, q, CAP, offset_ref[0])
        main_ref[q, 0:CAP, :] = rows
        lines = [
            digits[k : k + 1, i * LANES : (i + 1) * LANES]
            for k in range(3)
            for i in range(CAP // LANES)
        ]
        lines.append(jnp.zeros((32 - len(lines), LANES), F32))
        main_ref[q, CAP : CAP + 32, :] = jnp.concatenate(lines, axis=0).astype(BF16)
        main_ref[q, CAP + 32 :, :] = jnp.zeros((EDGE_CAP + 16, LANES), BF16)


def gather_lists(offsets, feat, digits, place, anc_count):
    return pl.pallas_call(
        functools.partial(gather_lists_kernel, anc_count),
        out_shape=jax.ShapeDtypeStruct((anc_count, CAP + EDGE_CAP + 48, LANES), BF16),
        in_specs=smem(1) + vmem(3),
        out_specs=vmem(1)[0],
        compiler_params=params(limit=30),
        cost_estimate=work(5),
        name="gather_lists",
    )(offsets, feat, digits, place)


def spread_lists_kernel(index_ref, received_ref, out_ref, held):
    total = received_ref.shape[0]
    held[0:total, :] = received_ref[...].astype(F32)
    held[total:, :] = jnp.zeros((8, LANES), F32)

    def pick(i, carry):
        base = pl.multiple_of(i * LANES, LANES)
        for j in range(LANES):
            out_ref[pl.ds(base + j, 1), :] = held[pl.ds(index_ref[base + j], 1), :]
        return carry

    lax.fori_loop(0, out_ref.shape[0] // LANES, pick, 0)


def spread_lists(index, received):
    voxels = index.shape[0]
    total = received.shape[0]
    return pl.pallas_call(
        spread_lists_kernel,
        out_shape=jax.ShapeDtypeStruct((voxels, LANES), F32),
        in_specs=smem(1) + vmem(1),
        out_specs=vmem(1)[0],
        scratch_shapes=[pltpu.VMEM((total + 8, LANES), F32)],
        compiler_params=params(limit=24),
        cost_estimate=work(4),
        name="spread_lists",
    )(index, received)


def add_piece(held, source, low, high, start):
    lane = lax.broadcasted_iota(jnp.int32, (1, LANES), 1)
    begin, end = low // LANES, -(-high // LANES)
    gap = start - low
    turn = gap % LANES
    at = begin + gap // LANES
    rows = source[begin:end, :]
    count = end - begin
    place = lax.broadcasted_iota(jnp.int32, (count, LANES), 0) * LANES
    place = place + lax.broadcasted_iota(jnp.int32, (count, LANES), 1) + begin * LANES
    if low % LANES or high % LANES:
        rows = jnp.where((place >= low) & (place < high), rows, 0.0)
    if turn == 0:
        held[at : at + count, :] += rows
        return
    rows = pltpu.roll(rows, turn, 1)
    here = jnp.where(lane >= turn, rows, 0.0)
    after = jnp.where(lane < turn, rows, 0.0)
    skip = max(-at, 0)
    if count > skip:
        held[at + skip : at + count, :] += here[skip:, :]
    held[at + 1 : at + 1 + count, :] += after


def pack_kernel(
    plan, tiles, chunk, region_ref, middle_ref, head_ref, mid_ref, row_ref, out_ref, held, rest_ref
):
    half = LANES // 2
    lane = lax.broadcasted_iota(jnp.int32, (1, LANES), 1)
    mid = jnp.sum(mid_ref[...], axis=0, keepdims=True)
    mid = group_sum(mid)
    mid = mid + pltpu.roll(mid, half, 1)
    region_bias = pltpu.roll(jnp.sum(row_ref[0:8, :], axis=0, keepdims=True), half, 1)
    outs = row_ref.shape[0] - 16
    wide = lax.broadcasted_iota(jnp.int32, (outs, LANES), 1) - half
    own = lax.broadcasted_iota(jnp.int32, (outs, LANES), 0) == wide
    head_bias = jnp.sum(jnp.where(own, row_ref[8 : 8 + outs, :], 0.0), axis=0, keepdims=True)
    rest_ref[0:1, :] = jnp.where(lane < half, mid, region_bias)
    rest_ref[1:2, :] = jnp.where(lane < half, region_bias, head_bias)
    sources = {"region": region_ref, "middle": middle_ref, "head": head_ref, "rest": rest_ref}
    for a, pieces in enumerate(plan):
        held[...] = jnp.zeros_like(held)
        for name, low, high, start in pieces:
            if name in sources:
                add_piece(held, sources[name], low, high, start)
        for t in range(tiles):
            out_ref[t * len(plan) + a] = held[t * chunk : (t + 1) * chunk, :].astype(BF16)


def group_sum(values):
    out = values[:, :LANES]
    for g in range(1, values.shape[1] // LANES):
        out = out + values[:, g * LANES : (g + 1) * LANES]
    return out


def pack(plan, tiles, chunk, region, middle, head, mid_sums, row_sums):
    return pl.pallas_call(
        functools.partial(pack_kernel, plan, tiles, chunk),
        out_shape=jax.ShapeDtypeStruct((tiles * len(plan), chunk, LANES), BF16),
        in_specs=vmem(5),
        out_specs=vmem(1)[0],
        scratch_shapes=[pltpu.VMEM((tiles * chunk, LANES), F32), pltpu.VMEM((8, LANES), F32)],
        compiler_params=params(limit=28),
        cost_estimate=work(3),
        name="pack",
    )(region, middle, head, mid_sums, row_sums)


def sum_chunk_kernel(parts_ref, out_ref, square_ref):
    total = jnp.sum(parts_ref[...].astype(F32), axis=0)
    for i in range(out_ref.shape[0]):
        out_ref[i] = total
    square_ref[...] = jnp.broadcast_to(jnp.sum(total * total), square_ref.shape)


def sum_chunk(parts, tiles):
    _, rows, lanes = parts.shape
    return pl.pallas_call(
        sum_chunk_kernel,
        out_shape=(
            jax.ShapeDtypeStruct((tiles, rows, lanes), F32),
            jax.ShapeDtypeStruct((1, lanes), F32),
        ),
        in_specs=vmem(1),
        out_specs=vmem(2),
        compiler_params=params(limit=24),
        cost_estimate=work(2),
        name="sum_chunk",
    )(parts)


def finish_kernel(
    plan, anc_ref, early_ref, late_ref, stats_ref, kernel_ref, gain_ref,
    out_ref, scalar_ref, one, norm,
):
    stats = jnp.sum(stats_ref[...], axis=0)
    kernel = kernel_ref[:, :LANES]
    mixed, mean, inv_std, count = batch_norm(stats, kernel)
    layers = late_ref.shape[1] - 1
    late = jnp.concatenate([late_ref[:, k, :] for k in range(layers)], axis=0)
    sums = late[0:8, :]
    total_shift = sums[7:8, :]
    total_gain = inv_std * (jnp.sum(kernel * sums, axis=0, keepdims=True) - mean * total_shift)
    slope = gain_ref[0:1, :LANES] * inv_std
    lane = lax.broadcasted_iota(jnp.int32, (1, LANES), 1)
    one[...] = jnp.zeros_like(one)
    norm[...] = jnp.zeros_like(norm)
    for k in range(7):
        first = stats[7:8, k : k + 1]
        pull = total_shift * first + total_gain * inv_std * (mixed[k : k + 1, :] - mean * first)
        grad = jnp.where(lane < 32, slope * (sums[k : k + 1, :] - pull / count), 0.0)
        if k % 4:
            grad = pltpu.roll(grad, 32 * (k % 4), 1)
        one[k // 4 : k // 4 + 1, :] += grad
    bias = late[72:73, :]
    top = jnp.where(lane < 32, total_gain, 0.0)
    top = top + pltpu.roll(jnp.where(lane < 32, total_shift, 0.0), 32, 1)
    norm[0:1, :] = top + jnp.where(lane < 64, 0.0, pltpu.roll(bias, 64, 1))
    norm[1:2, :] = jnp.where(lane < 64, pltpu.roll(bias, 64, 1), 0.0)
    two = late[8:72, :]
    square = jnp.sum(late_ref[:, layers, :]) / LANES
    square = square + jnp.sum(two * two) + jnp.sum(one[...] * one[...])
    square = square + jnp.sum(norm[...] * norm[...])
    size = jnp.sqrt(jnp.broadcast_to(square, (1, LANES)))
    scalar_ref[0:1, :] = late[80:81, :] / stats[1:2, 8:9]
    scalar_ref[1:2, :] = size
    scalar_ref[2:8, :] = jnp.broadcast_to(jnp.minimum(1.0, CLIP_LIMIT / (size + 1e-06)), (6, LANES))
    chunk = early_ref.shape[1]
    for i in range(early_ref.shape[0]):
        out_ref[i * chunk : (i + 1) * chunk, :] = early_ref[i]
    sources = {"one": one, "two": two, "norm": norm}
    for a, pieces in enumerate(plan):

        @pl.when(anc_ref[0] == a)
        def _():
            for name, low, high, start in pieces:
                if name in sources:
                    add_piece(out_ref, sources[name], low, high, start)


def finish(plan, anc, early, late, stats, kernel, gain):
    return pl.pallas_call(
        functools.partial(finish_kernel, plan),
        out_shape=(
            jax.ShapeDtypeStruct((early.shape[0] * early.shape[1], LANES), F32),
            jax.ShapeDtypeStruct((8, LANES), F32),
        ),
        in_specs=smem(1) + vmem(5),
        out_specs=vmem(2),
        scratch_shapes=[pltpu.VMEM((8, LANES), F32), pltpu.VMEM((8, LANES), F32)],
        compiler_params=params(limit=24),
        cost_estimate=work(3),
        name="finish",
    )(anc, early, late, stats, kernel, gain)


def everyone(values, axes):
    count = 1
    for axis in axes:
        count *= lax.axis_size(axis)
    copies = jnp.broadcast_to(values[None], (count,) + values.shape)
    return lax.all_to_all(copies, axes, 0, 0)


def swap_rows(beside, across):
    axes = ("tile", "anc")
    count = lax.axis_size("tile") * lax.axis_size("anc")
    pairs = [(i, i ^ 1) for i in range(count)]
    others = [(i, i + 1) for i in range(1, count - 1, 2)]
    others += [(j, i) for i, j in others]
    return lax.ppermute(beside, axes, pairs), lax.ppermute(across, axes, others)


def shard_windows(segments, shard, count):
    windows = []
    for a in range(count):
        begin, end = a * shard, (a + 1) * shard
        at = 0
        pieces = []
        for name, size in segments:
            low, high = max(begin, at), min(end, at + size)
            if low < high:
                pieces.append((name, low - at, high - at, low - begin))
            at += size
        windows.append(tuple(pieces))
    return tuple(windows)


def on_device(
    points,
    npoints,
    coords,
    labels,
    targets,
    w_vfe1,
    w_vfe2,
    w_mid,
    w_rpn,
    w_head,
    bn_gain,
    biases,
    master,
    moment1,
    moment2,
):
    both = ("tile", "anc")
    anc_count = lax.axis_size("anc")
    tile_count = lax.axis_size("tile")
    anc = lax.axis_index("anc")
    tile = lax.axis_index("tile")
    device_rows = labels.shape[1]
    columns = labels.shape[2]
    blocks = device_rows // BLOCK_ROWS
    tile_rows = device_rows * anc_count
    all_rows = tile_rows * tile_count
    slots = points.shape[1]
    voxels = points.shape[2]
    c_vfe = w_vfe1.shape[1]
    c_vox = w_vfe2.shape[1]
    c_mid = w_mid.shape[4]
    c_rpn = w_rpn.shape[3]
    outs = w_head.shape[1]
    shift = biases[:c_vfe]
    bias_two = biases[c_vfe : c_vfe + c_vox]
    rest = biases[c_vfe + c_vox :].astype(F32)
    bias_rows = jnp.concatenate(
        [rest[:c_mid], rest, jnp.zeros((LANES - outs,), F32)]
    ).reshape(3, LANES)

    def joined(row):
        return (row % CROP_ROWS != CROP_ROWS // 2) & (row > 0) & (row < all_rows)

    padded = -(-voxels // CHUNK) * CHUNK
    width = -(-(points.shape[0] * slots + 1) // LANES) * LANES
    flat_points = points.reshape(-1, voxels).T
    flat_points = jnp.pad(
        flat_points, ((0, padded - voxels), (0, width - flat_points.shape[1]))
    )
    lane = lax.broadcasted_iota(jnp.int32, flat_points.shape, 1)
    flat_points = jnp.where(lane == points.shape[0] * slots, jnp.ones((), BF16), flat_points)
    spare = (0, padded - voxels)
    row = coords[:, 1] - tile * tile_rows
    lines = [coords[:, 0], row, coords[:, 2], jnp.ones_like(row), npoints]
    lines = jnp.pad(jnp.stack(lines), ((0, 3), spare))
    tile_edges = jnp.stack([joined(tile * tile_rows), joined((tile + 1) * tile_rows)])
    devices = anc_count * tile_count
    parts = [w_rpn]
    for k in range(1, anc_count):
        around = [((i + k) % anc_count, i) for i in range(anc_count)]
        parts.append(lax.ppermute(w_rpn, "anc", around))
    stats, place, digits = prepare(
        tile_edges.astype(jnp.int32),
        flat_points,
        lines,
        labels.transpose(1, 0, 2),
        anc_count,
        device_rows,
        slots,
        devices,
    )
    stats, parts = lax.optimization_barrier((stats, parts))
    stats = lax.all_to_all(stats, both, 0, 0)
    region_in, region_back = region_order(anc.reshape(1), parts)
    counts = digits
    count_pos = jnp.sum(stats[:, 1, 8])
    rounds = jnp.ceil(jnp.max(stats[:, 2, 8])).astype(jnp.int32)
    middle_kernel_all = w_mid.transpose(0, 1, 2, 4, 3).reshape(-1, c_mid, c_vox)

    first, second, kernel, gain_rows = encoder_weights(
        w_vfe1, w_vfe2, bias_two, bn_gain, shift, slots
    )
    feat, share, found = encode(
        flat_points, counts, stats, kernel, gain_rows, first, second, slots
    )
    feat, region_in, region_back = lax.optimization_barrier((feat, region_in, region_back))

    in_tile = lax.axis_size("tile")
    upward = [(i + 1, i) for i in range(in_tile - 1)]
    downward = [(i, i + 1) for i in range(in_tile - 1)]

    def exchange(number):
        offsets = jnp.stack([number * CAP, number * EDGE_CAP]).astype(jnp.int32)
        up, down = edge_lists(offsets, feat, digits, place, anc_count)
        from_below = lax.ppermute(up, "tile", upward)
        from_above = lax.ppermute(down, "tile", downward)
        main = gather_lists(offsets, feat, digits, place, anc_count)
        main, from_below, from_above = lax.optimization_barrier((main, from_below, from_above))
        main = lax.dynamic_update_slice(main, from_above[None], (0, CAP + 32, 0))
        main = lax.dynamic_update_slice(main, from_below[None], (anc_count - 1, CAP + 32, 0))
        return lax.all_to_all(main, "anc", 0, 0), main

    def cells(got):
        words = got[:, CAP : CAP + 32].reshape(anc_count, -1).astype(jnp.int32)
        start = CAP + 32 + EDGE_CAP
        edge_words = got[:, start : start + 16].astype(jnp.int32)

        def word(k):
            gap = jnp.zeros((anc_count, 32), jnp.int32)
            parts = [words[:, k * CAP : (k + 1) * CAP], gap, edge_words[:, k], gap[:, :16]]
            return jnp.concatenate(parts, axis=1)

        high, half, mixed = word(0), word(1), word(2)
        local = mixed // 2 - anc * device_rows
        is_edge = lax.broadcasted_iota(jnp.int32, local.shape, 1) >= CAP
        local = local + jnp.where(is_edge, jnp.where(anc == 0, -tile_rows, tile_rows), 0)
        cross = half * 2 + mixed % 2
        scatter_at, own_at = [], []
        for k in range(blocks):
            line = local - k * BLOCK_ROWS
            tall = BLOCK_ROWS + 2 * HALO
            inside = (high > 0) & (line >= -HALO) & (line < BLOCK_ROWS + HALO)
            spot = ((high - 1) * tall + line + HALO) * columns + cross
            scatter_at.append(jnp.where(inside, spot, DEPTH * tall * columns).reshape(-1))
            inside = (high > 0) & (line >= 0) & (line < BLOCK_ROWS)
            spot = ((high - 1) * BLOCK_ROWS + line) * columns + cross
            spot = jnp.where(inside, spot, DEPTH * BLOCK_ROWS * columns)
            own_at.append(spot[:, :CAP].reshape(-1, LANES))
        return scatter_at, own_at

    got, sent = exchange(0)
    labels, targets, _ = lax.optimization_barrier((labels, targets, sent[0, 0, 0]))
    first_row = tile * tile_rows + anc * device_rows
    edges = []
    even = (tile * anc_count + anc) % 2 == 0
    for k in range(blocks):
        top = first_row + k * BLOCK_ROWS
        flags = [
            joined(top),
            joined(top + BLOCK_ROWS),
            even,
            anc * device_rows + k * BLOCK_ROWS,
            jnp.where(anc == 0, -tile_rows, tile_rows),
        ]
        edges.append(jnp.stack([flag.astype(jnp.int32) for flag in flags]))

    def more(state):
        return state[0] < rounds

    def another(state):
        number, held = state
        rows, _ = exchange(number)
        index, _ = cells(rows)
        rows = rows.reshape(-1, LANES)
        held = [scatter_rows(at, rows, old, columns) for at, old in zip(index, held)]
        return number + 1, held

    def one_round():
        made = [
            scatter_middle(
                edges[k], got.reshape(-1, LANES), middle_kernel_all, bias_rows, columns
            )
            for k in range(blocks)
        ]
        return tuple([one[i] for one in made] for i in range(3))

    def many_rounds():
        index, own = cells(got)
        held = [scatter_rows(at, got.reshape(-1, LANES), None, columns) for at in index]
        _, held = lax.while_loop(more, another, (jnp.int32(1), held))
        bevs = [
            middle_forward(edges[k], held[k], middle_kernel_all, bias_rows, columns)
            for k in range(blocks)
        ]
        return held, bevs, own

    grids, bevs, own_at = lax.cond(rounds > 1, many_rounds, one_round)

    wide_labels = jnp.repeat(labels.reshape(2, -1), outs // 2, axis=0)
    wide_targets = jnp.pad(targets, ((0, 0), (1, 0), (0, 0), (0, 0))).reshape(outs, -1)
    step = BLOCK_ROWS * columns
    scale = 1.0 / count_pos
    d_rows, head_sums, row_sums = [], 0.0, 0.0
    d_beside, d_across = [], []
    for k in range(blocks):
        here = slice(k * step, (k + 1) * step)
        d_block, near_row, far_row, heads, sums = region_forward(
            scale,
            edges[k],
            bevs[k],
            region_in,
            bias_rows,
            w_head.T,
            wide_labels[:, here],
            wide_targets[:, here],
            columns,
        )
        d_rows.append(d_block)
        d_beside.append(near_row)
        d_across.append(far_row)
        head_sums = head_sums + heads
        row_sums = row_sums + sums

    def swapped(near, far):
        if blocks == 1:
            got_near, got_far = swap_rows(near[0], far[0])
            return [got_near], [got_far]
        firsts = [jnp.where(even, f, n) for n, f in zip(near, far)]
        lasts = [jnp.where(even, n, f) for n, f in zip(near, far)]
        got_near, got_far = swap_rows(
            jnp.where(even, lasts[-1], firsts[0]), jnp.where(even, firsts[0], lasts[-1])
        )
        above = [jnp.where(even, got_far, got_near)] + lasts[:-1]
        below = firsts[1:] + [jnp.where(even, got_near, got_far)]
        return (
            [jnp.where(even, y, x) for x, y in zip(above, below)],
            [jnp.where(even, x, y) for x, y in zip(above, below)],
        )

    beside, across = swapped(d_beside, d_across)
    grad_region = sum(
        region_weight(d_rows[k], bevs[k], columns, anc_count) for k in range(blocks)
    )
    d_rows, grad_region, beside, across = lax.optimization_barrier(
        (d_rows, grad_region, beside, across)
    )
    d_mids, mid_sums = [], 0.0
    mid_beside, mid_across = [], []
    for k in range(blocks):
        d_block, near_row, far_row, sums = region_data(
            edges[k], d_rows[k], beside[k], across[k], bevs[k], region_back, columns
        )
        d_mids.append(d_block)
        mid_beside.append(near_row)
        mid_across.append(far_row)
        mid_sums = mid_sums + sums
    beside, across = swapped(mid_beside, mid_across)
    grad_mid = sum(middle_weight(grids[k], d_mids[k], columns) for k in range(blocks))
    grad_mid, beside, across = lax.optimization_barrier((grad_mid, beside, across))

    head_three = head_sums.reshape(3, outs, c_rpn)
    grad_head = (head_three[0] + head_three[1] + head_three[2]).T
    head_rows = grad_head.reshape(-1, LANES)
    segments = (
        ("region", grad_region.size),
        ("one", w_vfe1.size),
        ("two", w_vfe2.size),
        ("middle", grad_mid.size),
        ("head", w_head.size),
        ("norm", c_vfe + c_vfe + c_vox),
        ("rest", c_mid + c_rpn + outs),
    )
    shard = master.shape[0]
    plan = shard_windows(segments, shard, anc_count)
    chunk_rows = -(-(shard // LANES + 2) // (8 * tile_count)) * 8
    packed = pack(
        plan, tile_count, chunk_rows, grad_region, grad_mid, head_rows, mid_sums, row_sums
    )
    own_at, packed = lax.optimization_barrier((own_at, packed))
    chunk, chunk_square = sum_chunk(lax.all_to_all(packed, both, 0, 0), tile_count)

    def collect(number, own_index, chunk):
        lists = sum(
            middle_data(
                own_index[k], edges[k], d_mids[k], beside[k], across[k], middle_kernel_all, columns
            )
            for k in range(blocks)
        )
        lists, chunk = lax.optimization_barrier((lists, chunk))
        back = lax.all_to_all(lists.reshape(anc_count, CAP, LANES), "anc", 0, 0)
        mine = place[7] - number * CAP
        known = (mine >= 0) & (mine < CAP)
        index = jnp.where(known, place[6] * CAP + mine, anc_count * CAP)
        return spread_lists(index, back.reshape(-1, LANES)), chunk

    d_feat, chunk = collect(0, own_at, chunk)
    early = lax.all_to_all(chunk, "tile", 0, 0)

    def collect_more(state):
        number, held = state
        _, index = cells(exchange(number)[0])
        return number + 1, held + collect(number, index, ())[0]

    d_feat = lax.cond(
        rounds > 1,
        lambda held: lax.while_loop(more, collect_more, (jnp.int32(1), held))[1],
        lambda held: held,
        d_feat,
    )
    layers = -(-88 // devices)
    late = decode(
        flat_points,
        counts,
        stats,
        kernel,
        gain_rows,
        first,
        second,
        feat,
        share,
        found,
        d_feat,
        row_sums[24:32],
        (devices, layers),
        slots,
    )
    late, early = lax.optimization_barrier((late, early))
    late = jnp.sum(lax.all_to_all(late, both, 0, 0), axis=0)
    late = everyone(jnp.concatenate([late, chunk_square], axis=0), both)
    reduced, scalars = finish(plan, anc.reshape(1), early, late, stats, kernel, gain_rows)
    loss = scalars[0, 0]
    norm_value = scalars[1, 0]
    reduced = reduced.reshape(-1)[:shard]
    clipped = reduced * scalars[2, 0]
    first_new = BETA_FIRST * moment1 + (1.0 - BETA_FIRST) * clipped
    second_new = BETA_SECOND * moment2 + (1.0 - BETA_SECOND) * clipped * clipped
    first_hat = first_new / (1.0 - BETA_FIRST**STEP_NUMBER)
    second_hat = second_new / (1.0 - BETA_SECOND**STEP_NUMBER)
    updated = master - LEARN_RATE * (
        first_hat / (jnp.sqrt(second_hat) + ADAM_EPSILON) + WEIGHT_DECAY * master
    )
    return (updated, first_new, second_new, loss, norm_value)


def solution(mesh):
    placed = (
        P(None, None, ("tile", "anc")),
        P(("tile", "anc")),
        P(("tile", "anc"), None),
        P(None, ("tile", "anc"), None),
        P(None, None, ("tile", "anc"), None),
        P(),
        P(),
        P(),
        P(None, None, "anc", None),
        P(),
        P(),
        P(),
        P("anc"),
        P("anc"),
        P("anc"),
    )
    return jax.shard_map(
        on_device,
        mesh=mesh,
        in_specs=placed,
        out_specs=(P("anc"), P("anc"), P("anc"), P(), P()),
        check_vma=False,
    )
```

```python
import functools
import jax
import jax.numpy as jnp
from jax import lax
from jax.experimental import pallas as pl
from jax.experimental.pallas import tpu as pltpu
from jax.sharding import PartitionSpec as P

DEPTH = 10
PAIRS = DEPTH // 4 + 1
CROP_ROWS = 192
BLOCK_ROWS = 12
HALO = 2
LANES = 128
CHUNK = 384
CAP = 768
EDGE_CAP = 128
EMPTY = -1e30
FOCAL_ALPHA = 0.25
BN_EPSILON = 0.001
CLIP_LIMIT = 0.05
LEARN_RATE = 0.03
BETA_FIRST = 0.9
BETA_SECOND = 0.999
WEIGHT_DECAY = 0.01
ADAM_EPSILON = 1e-08
STEP_NUMBER = 10
F32 = jnp.float32
BF16 = jnp.bfloat16


def vmem(count):
    return [pl.BlockSpec(memory_space=pltpu.VMEM)] * count


def smem(count):
    return [pl.BlockSpec(memory_space=pltpu.SMEM)] * count


def params(*semantics, limit=60):
    return pltpu.CompilerParams(
        vmem_limit_bytes=limit * 1024 * 1024, dimension_semantics=semantics or None
    )


def work(micros):
    return pl.CostEstimate(flops=micros, transcendentals=0, bytes_accessed=micros * 3_000_000)


def at_row(index, columns):
    if isinstance(index, int):
        return pl.ds(index * columns, columns)
    return pl.ds(pl.multiple_of(index * columns, 32), columns)


def column_edges(columns, lanes):
    place = lax.broadcasted_iota(jnp.int32, (columns, lanes), 0)
    return place == 0, place == columns - 1


def from_left(values):
    columns, lanes = values.shape
    first, _ = column_edges(columns, lanes)
    return jnp.where(first, 0.0, pltpu.roll(values, 1, 0))


def from_right(values):
    columns, lanes = values.shape
    _, last = column_edges(columns, lanes)
    return jnp.where(last, 0.0, pltpu.roll(values, columns - 1, 0))


def low_lanes(columns):
    return lax.broadcasted_iota(jnp.int32, (columns, LANES), 1) < LANES // 2


def clear(wide, cells):
    step = 512

    def begin(i, carry):
        wide[pl.ds(pl.multiple_of(i * step, step), step), :] = jnp.zeros((step, LANES), F32)
        return carry

    lax.fori_loop(0, cells // step, begin, 0)


def narrow(wide, out_ref):
    step = 512

    def finish(i, carry):
        block = pl.ds(pl.multiple_of(i * step, step), step)
        out_ref[block, :] = wide[block, :].astype(BF16)
        return carry

    lax.fori_loop(0, out_ref.shape[0] // step, finish, 0)


def place_rows(count, cells, index_ref, feat_ref, old_ref, out_ref, wide, rows):
    if old_ref is None:
        clear(wide, cells)
    else:
        wide[0:cells, :] = old_ref[...].astype(F32)
    rows[...] = feat_ref[...].astype(F32)

    def place(i, carry):
        for j in range(8):
            wide[pl.ds(index_ref[i * 8 + j], 1), :] = rows[pl.ds(i * 8 + j, 1), :]
        return carry

    lax.fori_loop(0, count // 8, place, 0)
    narrow(wide, out_ref)


def scatter_kernel(count, cells, fresh, *refs):
    if fresh:
        index_ref, feat_ref, out_ref, wide, rows = refs
        place_rows(count, cells, index_ref, feat_ref, None, out_ref, wide, rows)
    else:
        place_rows(count, cells, *refs)


def scatter_rows(index, feats, old, columns):
    cells = DEPTH * (BLOCK_ROWS + 2 * HALO) * columns
    count = index.shape[0]
    fresh = old is None
    return pl.pallas_call(
        functools.partial(scatter_kernel, count, cells, fresh),
        out_shape=jax.ShapeDtypeStruct((cells, LANES), BF16),
        in_specs=smem(1) + vmem(1 if fresh else 2),
        out_specs=vmem(1)[0],
        scratch_shapes=[pltpu.VMEM((cells + 8, LANES), F32), pltpu.VMEM((count, LANES), F32)],
        compiler_params=params(),
        cost_estimate=work(15),
        name="grid_scatter",
    )(*((index, feats) if fresh else (index, feats, old)))


TOP, BOTTOM, EVEN, FIRST_ROW, EDGE_SHIFT, PLACE = range(6)


def list_cells(columns, edge_ref, feat_ref, spots, owns):
    sources = feat_ref.shape[0] // (CAP + EDGE_CAP + 48)
    main = CAP // LANES
    tall = BLOCK_ROWS + 2 * HALO
    for a in range(sources):
        base = a * (CAP + EDGE_CAP + 48)
        words = feat_ref[base + CAP : base + CAP + 32, :].astype(F32).astype(jnp.int32)
        start = base + CAP + 32 + EDGE_CAP
        edges = feat_ref[start : start + 16, :].astype(F32).astype(jnp.int32)
        for side, (high, half, mixed) in enumerate(
            (
                (words[0:main], words[main : 2 * main], words[2 * main : 3 * main]),
                (edges[0:1], edges[1:2], edges[2:3]),
            )
        ):
            line = (mixed >> 1) - edge_ref[FIRST_ROW]
            if side:
                line = line + edge_ref[EDGE_SHIFT]
            cross = half * 2 + (mixed & 1)
            inside = (high > 0) & (line >= -HALO) & (line < BLOCK_ROWS + HALO)
            spot = ((high - 1) * tall + line + HALO) * columns + cross
            spot = jnp.where(inside, spot, DEPTH * tall * columns)
            if side:
                spots[a * (main + 1) + main : (a + 1) * (main + 1), :] = spot
                continue
            spots[a * (main + 1) : a * (main + 1) + main, :] = spot
            inside = (high > 0) & (line >= 0) & (line < BLOCK_ROWS)
            spot = ((high - 1) * BLOCK_ROWS + line) * columns + cross
            owns[a * main : (a + 1) * main, :] = jnp.where(
                inside, spot, DEPTH * BLOCK_ROWS * columns
            )


def scatter_middle_kernel(
    columns, edge_ref, feat_ref, kernel_ref, bias_ref, grid_ref, out_ref, own_ref,
    wide, rows, held, weight_ref, spots, index, copied, done,
):
    list_cells(columns, edge_ref, feat_ref, spots, own_ref)
    to_scalar = pltpu.make_async_copy(spots, index, copied)
    to_scalar.start()
    clear(wide, held.shape[0])
    rows[...] = feat_ref[...].astype(F32)
    to_scalar.wait()
    blocks = CAP // LANES + 1
    length = CAP + EDGE_CAP + 48

    def place(part, carry):
        block = part % blocks
        base = part // blocks * length + block * LANES + jnp.where(block == blocks - 1, 32, 0)

        base = pl.multiple_of(base, 8)
        for j in range(LANES):
            wide[pl.ds(index[part, j], 1), :] = rows[pl.ds(base + j, 1), :]
        return carry

    lax.fori_loop(0, index.shape[0], place, 0)
    narrow(wide, held)
    copy = pltpu.make_async_copy(held, grid_ref, done)
    copy.start()
    middle_kernel(columns, edge_ref, held, kernel_ref, bias_ref, out_ref, weight_ref)
    copy.wait()


def scatter_middle(edges, feats, w_mid, bias, columns):
    cells = DEPTH * (BLOCK_ROWS + 2 * HALO) * columns
    count = feats.shape[0]
    sources = count // (CAP + EDGE_CAP + 48)
    parts = sources * (CAP // LANES + 1)
    return pl.pallas_call(
        functools.partial(scatter_middle_kernel, columns),
        out_shape=(
            jax.ShapeDtypeStruct((cells, LANES), BF16),
            jax.ShapeDtypeStruct(((BLOCK_ROWS + 2) * columns, PAIRS * LANES), BF16),
            jax.ShapeDtypeStruct((sources * CAP // LANES, LANES), jnp.int32),
        ),
        in_specs=smem(1) + vmem(3),
        out_specs=[pl.BlockSpec(memory_space=pl.ANY)] + vmem(2),
        scratch_shapes=[
            pltpu.VMEM((cells + 8, LANES), F32),
            pltpu.VMEM((count, LANES), F32),
            pltpu.VMEM((cells, LANES), BF16),
            pltpu.VMEM((2, 9 * LANES, 2 * LANES), BF16),
            pltpu.VMEM((parts, LANES), jnp.int32),
            pltpu.SMEM((parts, LANES), jnp.int32),
            pltpu.SemaphoreType.DMA,
            pltpu.SemaphoreType.DMA,
        ],
        compiler_params=params(limit=57),
        cost_estimate=work(36),
        name="scatter_middle",
    )(edges, feats, w_mid, bias)


def middle_kernel(columns, edge_ref, grid_ref, kernel_ref, bias_ref, out_ref, weight_ref):
    low = low_lanes(columns)
    none = jnp.zeros((LANES, LANES // 2), BF16)
    for place in range(9):
        one, two, three = (
            kernel_ref[place * 3 + e].astype(F32).T.astype(BF16) for e in range(3)
        )
        rows = slice(place * LANES, (place + 1) * LANES)
        weight_ref[0, rows, :] = jnp.concatenate([one, two, three, none], axis=1)
        weight_ref[1, rows, :] = jnp.concatenate([two, one, none, three], axis=1)
    grid_rows = BLOCK_ROWS + 2 * HALO
    depth_out = DEPTH // 2

    def row(m, carry):
        sums = []
        for o in range(depth_out):
            taps = (1, 2) if o == 0 else (0, 1, 2)
            left = jnp.concatenate(
                [
                    grid_ref[at_row((2 * o + a - 1) * grid_rows + m + b, columns), :]
                    for a in taps
                    for b in range(3)
                ],
                axis=1,
            )
            right = weight_ref[o % 2, 3 * LANES * (3 - len(taps)) :, :]
            sums.append(jnp.dot(left, right, preferred_element_type=F32))
        inside = (m > 0) & (m < BLOCK_ROWS + 1) | (m == 0) & (edge_ref[0] > 0)
        inside = inside | (m == BLOCK_ROWS + 1) & (edge_ref[1] > 0)
        keep = jnp.where(inside, 1.0, 0.0)
        for j in range(PAIRS):
            even = sums[2 * j]
            if 2 * j + 1 < depth_out:
                odd = sums[2 * j + 1]
                first = jnp.where(low, even[:, :LANES], odd[:, :LANES])
                middle = jnp.where(low, odd[:, :LANES], even[:, :LANES])
                last = even[:, LANES:] + odd[:, LANES:]
            else:
                first = even[:, :LANES]
                middle = first
                last = even[:, LANES:]
            total = from_left(first) + pltpu.roll(middle, LANES // 2, 1) + from_right(last)
            total = jnp.maximum(total + bias_ref[0:1, :], 0.0) * keep
            if 2 * j + 1 == depth_out:
                total = jnp.where(low, total, 0.0)
            out_ref[at_row(m, columns), j * LANES : (j + 1) * LANES] = total.astype(BF16)
        return carry

    lax.fori_loop(0, BLOCK_ROWS + 2, row, 0, unroll=2)


def middle_forward(edges, grid, w_mid, bias, columns):
    return pl.pallas_call(
        functools.partial(middle_kernel, columns),
        out_shape=jax.ShapeDtypeStruct(((BLOCK_ROWS + 2) * columns, PAIRS * LANES), BF16),
        in_specs=smem(1) + vmem(3),
        out_specs=vmem(1)[0],
        scratch_shapes=[pltpu.VMEM((2, 9 * LANES, 2 * LANES), BF16)],
        compiler_params=params(),
        cost_estimate=work(26),
        name="middle_forward",
    )(edges, grid, w_mid, bias)


def row_above(edge_ref, beside_ref, across_ref, lanes):
    found = jnp.where(
        edge_ref[EVEN] > 0, across_ref[:, lanes].astype(F32), beside_ref[:, lanes].astype(F32)
    )
    return jnp.where(edge_ref[TOP] > 0, found, 0.0)


def row_below(edge_ref, beside_ref, across_ref, lanes):
    found = jnp.where(
        edge_ref[EVEN] > 0, beside_ref[:, lanes].astype(F32), across_ref[:, lanes].astype(F32)
    )
    return jnp.where(edge_ref[BOTTOM] > 0, found, 0.0)


def put_edges(edge_ref, beside_ref, across_ref, first, last):
    if first is not None:

        @pl.when(edge_ref[EVEN] > 0)
        def _():
            across_ref[...] = first

        @pl.when(edge_ref[EVEN] == 0)
        def _():
            beside_ref[...] = first

    if last is not None:

        @pl.when(edge_ref[EVEN] > 0)
        def _():
            beside_ref[...] = last

        @pl.when(edge_ref[EVEN] == 0)
        def _():
            across_ref[...] = last


def column_taps(own, j):
    low = low_lanes(own.shape[0])
    other = pltpu.roll(own, LANES // 2, 1)
    both = [jnp.where(low, own, other)]
    if 2 * j + 1 < DEPTH // 2:
        both.append(jnp.where(low, other, own))
    return [(jnp.where(low, from_right(x), x), from_left(x)) for x in both]


def middle_data_kernel(
    count, columns, sources, index_ref, edge_ref, d_ref, beside_ref, across_ref, kernel_ref, *refs
):
    out_refs, (near, far, wide, rows, weight_ref) = refs[:sources], refs[sources:]
    padded = BLOCK_ROWS + 2
    half = LANES // 2
    cells = DEPTH * BLOCK_ROWS * columns
    span = 10 * half
    for a, first, side in ((1, 0, 0), (2, 0, 1), (0, span, 1)):
        lanes = slice(side * LANES, (side + 1) * LANES)
        for b in range(3):
            for e in range(3):
                block = (2 - b) * 2 + e if e < 2 else 6 + 2 - b
                own = kernel_ref[(a * 3 + b) * 3 + e]
                weight_ref[first + block * half : first + (block + 1) * half, lanes] = own
        weight_ref[first + span - half : first + span, lanes] = jnp.zeros((half, LANES), BF16)
    weight_ref[span:, :LANES] = jnp.zeros((span, LANES), BF16)

    def build(r, load):
        for j in range(PAIRS):
            own = load(slice(j * LANES, (j + 1) * LANES))
            for k, (pair, left) in enumerate(column_taps(own, j)):
                o = 2 * j + k
                near[o, at_row(r, columns), :] = pair.astype(BF16)
                far[o, at_row(r, columns), 0:half] = left[:, 0:half].astype(BF16)
                if not (isinstance(r, int) and r == 0):
                    far[o, at_row(r - 1, columns), half:LANES] = left[:, half:].astype(BF16)

    def build_own(r):
        build(r + 1, lambda lanes: d_ref[at_row(r, columns), lanes].astype(F32))

    build(0, lambda lanes: row_above(edge_ref, beside_ref, across_ref, lanes))
    for r in range(3):
        build_own(r)
    for o in range(DEPTH // 2):
        far[o, (padded - 1) * columns :, half:LANES] = jnp.zeros((columns, half), BF16)

    def row(r):
        def pieces(o):
            return [near[o, at_row(r + i, columns), :] for i in range(3)] + [
                far[o, at_row(r + i, columns), :] for i in (0, 2)
            ]

        for o in range(DEPTH // 2):
            left = jnp.concatenate(pieces(o) + (pieces(o + 1) if o < DEPTH // 2 - 1 else []), axis=1)
            total = jnp.dot(left, weight_ref[0 : left.shape[1], :], preferred_element_type=F32)
            wide[at_row(2 * o * BLOCK_ROWS + r, columns), :] = total[:, :LANES]
            wide[at_row((2 * o + 1) * BLOCK_ROWS + r, columns), :] = total[:, LANES:]

    def row_and_build(r, carry):
        row(r)
        build_own(r + 3)
        return carry

    lax.fori_loop(0, BLOCK_ROWS - 3, row_and_build, 0)
    row(BLOCK_ROWS - 3)
    build(BLOCK_ROWS + 1, lambda lanes: row_below(edge_ref, beside_ref, across_ref, lanes))
    row(BLOCK_ROWS - 2)
    row(BLOCK_ROWS - 1)
    wide[cells:, :] = jnp.zeros((8, LANES), F32)

    length = count // sources
    lines = length // LANES

    def pick(part, carry):
        source = lax.rem(edge_ref[PLACE] + part // lines, sources) * lines + part % lines
        base = pl.multiple_of(part * LANES, LANES)
        for j in range(LANES):
            rows[pl.ds(base + j, 1), :] = wide[pl.ds(index_ref[source, j], 1), :]
        return carry

    lax.fori_loop(0, count // LANES, pick, 0)
    for k, out_ref in enumerate(out_refs):
        out_ref[...] = rows[k * length : (k + 1) * length, :].astype(BF16)


def middle_data(index, edges, d_rows, beside, across, w_mid, columns):
    count = index.size
    sources = count // CAP
    padded = (BLOCK_ROWS + 2) * columns
    return pl.pallas_call(
        functools.partial(middle_data_kernel, count, columns, sources),
        out_shape=[jax.ShapeDtypeStruct((CAP, LANES), BF16)] * sources,
        in_specs=smem(2) + vmem(4),
        out_specs=vmem(sources),
        scratch_shapes=[
            pltpu.VMEM((DEPTH // 2, padded, LANES), BF16),
            pltpu.VMEM((DEPTH // 2, padded, LANES), BF16),
            pltpu.VMEM((DEPTH * BLOCK_ROWS * columns + 8, LANES), F32),
            pltpu.VMEM((count, LANES), F32),
            pltpu.VMEM((10 * LANES, 2 * LANES), BF16),
        ],
        compiler_params=params(limit=50),
        cost_estimate=work(30),
        name="middle_data",
    )(index, edges, d_rows, beside, across, w_mid)


def middle_weight_kernel(
    columns, grid_hbm, d_ref, out_ref, total, taps_ref, turned, grid_ref, arrived
):
    grid_rows = BLOCK_ROWS + 2 * HALO
    half = LANES // 2

    def copy(i):
        ahead = 2 if isinstance(i, int) and i == 0 else 0
        parts = []
        for d in range(DEPTH):
            begin = (d * grid_rows + 2 * i + 3 - ahead) * columns
            rows = pl.ds(begin if isinstance(i, int) else pl.multiple_of(begin, 32), (2 + ahead) * columns)
            parts.append(
                pltpu.make_async_copy(grid_hbm.at[rows, :], grid_ref.at[rows, :], arrived.at[i, d])
            )
        return parts

    for i in range(BLOCK_ROWS // 2):
        for part in copy(i):
            part.start()
    total[...] = jnp.zeros_like(total)
    for part in copy(0):
        part.wait()

    def rows(i, carry):
        @pl.when(i > 0)
        def _():
            for part in copy(i):
                part.wait()

        for k in range(2):
            for j in range(PAIRS):
                own = d_ref[at_row(i * 2 + k, columns), j * LANES : (j + 1) * LANES].astype(F32)
                for n, (pair, left) in enumerate(column_taps(own, j)):
                    place = slice(k * columns, (k + 1) * columns)
                    taps_ref[2 * j + n, place, 0:LANES] = pair.astype(BF16)
                    taps_ref[2 * j + n, place, LANES:] = left.astype(BF16)
        for o in range(DEPTH // 2):
            depth_taps = (1, 2) if o == 0 else (0, 1, 2)
            cells = jnp.concatenate(
                [
                    grid_ref[
                        pl.ds(
                            pl.multiple_of(
                                ((2 * o + a - 1) * grid_rows + i * 2 + 1 + b) * columns, 32
                            ),
                            2 * columns,
                        ),
                        :,
                    ]
                    for a in depth_taps
                    for b in range(3)
                ],
                axis=1,
            )
            part = lax.dot_general(
                taps_ref[o], cells, (((0,), (0,)), ((), ())), preferred_element_type=F32
            )
            if o == 0:
                total[:, 3 * LANES :] += part
            else:
                total[...] += part
        return carry

    lax.fori_loop(0, BLOCK_ROWS // 2, rows, 0, unroll=2)
    low = low_lanes(LANES // 2)
    for place in range(9):
        for side in range(2):
            turned[...] = total[
                side * LANES : (side + 1) * LANES, place * LANES : (place + 1) * LANES
            ].T
            even = turned[pl.ds(0, half, stride=2), :]
            odd = turned[pl.ds(1, half, stride=2), :]
            at = (place * 3 + side * 2) * half
            out_ref[at : at + half, :] = jnp.where(low, even, pltpu.roll(odd, half, 1))
            if side == 0:
                out_ref[at + half : at + 2 * half, :] = jnp.where(
                    low, pltpu.roll(even, half, 1), odd
                )


def middle_weight(grid, d_rows, columns):
    return pl.pallas_call(
        functools.partial(middle_weight_kernel, columns),
        out_shape=jax.ShapeDtypeStruct((27 * LANES // 2, LANES), F32),
        in_specs=[pl.BlockSpec(memory_space=pl.ANY)] + vmem(1),
        out_specs=vmem(1)[0],
        scratch_shapes=[
            pltpu.VMEM((2 * LANES, 9 * LANES), F32),
            pltpu.VMEM((DEPTH // 2, 2 * columns, 2 * LANES), BF16),
            pltpu.VMEM((LANES, LANES), F32),
            pltpu.VMEM(grid.shape, BF16),
            pltpu.SemaphoreType.DMA((BLOCK_ROWS // 2, DEPTH)),
        ],
        compiler_params=params(limit=32),
        cost_estimate=work(26),
        name="middle_weight",
    )(grid, d_rows)


def region_kernel(
    columns,
    scale_ref,
    edge_ref,
    bev_ref,
    weight_ref,
    bias_ref,
    head_ref,
    labels_ref,
    targets_ref,
    d_ref,
    beside_ref,
    across_ref,
    grad_head_ref,
    sums_ref,
    held,
):
    outs = head_ref.shape[0]
    cells = d_ref.shape[0]
    span = cells // 3
    scale = scale_ref[0, 0]
    head = head_ref[...]
    head_three = jnp.concatenate([head, head, head], axis=0)
    own = lax.broadcasted_iota(jnp.int32, (outs, LANES), 0)
    own = own == lax.broadcasted_iota(jnp.int32, (outs, LANES), 1)
    head_bias = jnp.sum(jnp.where(own, bias_ref[2:3, :], 0.0), axis=1, keepdims=True)

    def row(r, carry):
        left = jnp.concatenate([bev_ref[at_row(r + b, columns), :] for b in range(3)], axis=1)
        part = jnp.dot(left, weight_ref[...], preferred_element_type=F32)
        pre = from_left(part[:, :LANES]) + part[:, LANES : 2 * LANES]
        held[at_row(r, columns), :] = pre + from_right(part[:, 2 * LANES :]) + bias_ref[1:2, :]
        return carry

    lax.fori_loop(0, cells // columns, row, 0, unroll=2)
    kind = lax.broadcasted_iota(jnp.int32, (outs, span), 0) % 8 == 0
    grad_head = jnp.zeros((3 * outs, LANES), F32)
    head_sum = jnp.zeros((outs, 1), F32)
    loss_sum = jnp.zeros((outs, 1), F32)
    row_sum = jnp.zeros((8, LANES), F32)
    for i in range(3):
        place = slice(i * span, (i + 1) * span)
        pre = held[place, :]
        act = jnp.maximum(pre, 0.0).astype(BF16)
        heads = lax.dot_general(head, act, (((1,), (1,)), ((), ())), preferred_element_type=F32)
        heads = heads + head_bias
        label = labels_ref[:, place]
        positive = jnp.where(label == 1, 1.0, 0.0)
        negative = jnp.where(label == 0, 1.0, 0.0)
        tail = jnp.log1p(jnp.exp(-jnp.abs(heads)))
        soft_up = jnp.maximum(heads, 0.0) + tail
        soft_down = jnp.maximum(-heads, 0.0) + tail
        probab = jax.nn.sigmoid(heads)
        rest = 1.0 - probab
        focal = positive * FOCAL_ALPHA * rest * rest * soft_down
        focal = focal + negative * (1.0 - FOCAL_ALPHA) * probab * probab * soft_up
        d_focal = positive * FOCAL_ALPHA * rest * rest * (-2.0 * probab * soft_down - rest)
        d_focal = d_focal + negative * (1.0 - FOCAL_ALPHA) * probab * probab * (
            2.0 * rest * soft_up + probab
        )
        offset = heads - targets_ref[:, place]
        size = jnp.abs(offset)
        near = size < 1.0 / 9.0
        smooth = jnp.where(near, 4.5 * offset * offset, size - 1.0 / 18.0)
        d_smooth = jnp.where(near, 9.0 * offset, jnp.where(offset > 0.0, 1.0, -1.0))
        losses = jnp.where(kind, focal, 2.0 * positive * smooth)
        loss_sum = loss_sum + jnp.sum(losses, axis=1, keepdims=True)
        d_heads = jnp.where(kind, d_focal, 2.0 * positive * d_smooth) * scale
        head_sum = head_sum + jnp.sum(d_heads, axis=1, keepdims=True)
        high = d_heads.astype(BF16)
        rest_one = d_heads - high.astype(F32)
        mid = rest_one.astype(BF16)
        tiny = (rest_one - mid.astype(F32)).astype(BF16)
        three = jnp.concatenate([high, mid, tiny], axis=0)
        grad_head = grad_head + jnp.dot(three, act, preferred_element_type=F32)
        d_act = lax.dot_general(
            three, head_three, (((0,), (0,)), ((), ())), preferred_element_type=F32
        )
        d_pre = jnp.where(pre > 0.0, d_act, 0.0).astype(BF16)
        d_ref[place, :] = d_pre
        row_sum = row_sum + jnp.sum(d_pre.astype(F32).reshape(span // 8, 8, LANES), axis=0)
        if i == 0:
            put_edges(edge_ref, beside_ref, across_ref, d_pre[:columns, :], None)
        if i == 2:
            put_edges(edge_ref, beside_ref, across_ref, None, d_pre[span - columns :, :])
    grad_head_ref[...] = grad_head
    sums_ref[0:8, :] = row_sum
    sums_ref[8:24, :] = jnp.broadcast_to(head_sum, (outs, LANES))
    sums_ref[24:32, :] = jnp.broadcast_to(jnp.sum(loss_sum, axis=0, keepdims=True), (8, LANES))


def region_forward(scale, edges, bev, weights, bias, head, labels, targets, columns):
    cells = labels.shape[1]
    outs = head.shape[0]
    return pl.pallas_call(
        functools.partial(region_kernel, columns),
        out_shape=(
            jax.ShapeDtypeStruct((cells, LANES), BF16),
            jax.ShapeDtypeStruct((columns, LANES), BF16),
            jax.ShapeDtypeStruct((columns, LANES), BF16),
            jax.ShapeDtypeStruct((3 * outs, LANES), F32),
            jax.ShapeDtypeStruct((32, LANES), F32),
        ),
        in_specs=smem(2) + vmem(6),
        out_specs=vmem(5),
        scratch_shapes=[pltpu.VMEM((cells, LANES), F32)],
        compiler_params=params(limit=28),
        cost_estimate=work(16),
        name="region_forward",
    )(
        scale.reshape(1, 1),
        edges,
        bev,
        weights,
        bias,
        head,
        labels,
        targets,
    )


def region_order_kernel(blocks, anc_ref, *refs):
    part_refs, (in_ref, back_ref, wide, lined) = refs[:blocks], refs[blocks:]
    depth_out = DEPTH // 2
    half = LANES // 2
    width = PAIRS * LANES
    share = half // blocks
    used = depth_out * half
    for b in range(3):
        for e in range(3):
            for k, part_ref in enumerate(part_refs):
                first = lax.rem(anc_ref[0] + k, blocks) * share
                wide[...] = part_ref[b, e].astype(F32)
                for h in range(depth_out):
                    at = pl.multiple_of(h * half + first, 8)
                    lined[pl.ds(at, share), :] = wide[pl.ds(h, share, stride=depth_out), :]
            lined[used:, :] = jnp.zeros((width - used, LANES), F32)
            in_ref[b * width : (b + 1) * width, e * LANES : (e + 1) * LANES] = lined[...].astype(
                BF16
            )
            at = (b * 3 + e) * LANES
            back_ref[at : at + LANES, :] = lined[...].T.astype(BF16)


def region_order(anc, parts):
    width = PAIRS * LANES
    return pl.pallas_call(
        functools.partial(region_order_kernel, len(parts)),
        out_shape=(
            jax.ShapeDtypeStruct((3 * width, 3 * LANES), BF16),
            jax.ShapeDtypeStruct((9 * LANES, width), BF16),
        ),
        in_specs=smem(1) + vmem(len(parts)),
        out_specs=vmem(2),
        scratch_shapes=[
            pltpu.VMEM((parts[0].shape[2], LANES), F32),
            pltpu.VMEM((width, LANES), F32),
        ],
        compiler_params=params(limit=24),
        cost_estimate=work(4),
        name="region_order",
    )(anc, *parts)


def region_data_kernel(
    columns, edge_ref, d_ref, beside_in, across_in, bev_ref, weight_ref,
    out_ref, beside_ref, across_ref, sums_ref, taps_ref,
):
    rows = out_ref.shape[0] // columns
    width = PAIRS * LANES
    sums_ref[...] = jnp.zeros_like(sums_ref)

    def build(r, own):
        taps_ref[at_row(r, columns), 0:LANES] = from_right(own).astype(BF16)
        taps_ref[at_row(r, columns), LANES : 2 * LANES] = own.astype(BF16)
        taps_ref[at_row(r, columns), 2 * LANES :] = from_left(own).astype(BF16)

    def build_own(r):
        build(r + 1, d_ref[at_row(r, columns), :].astype(F32))

    build(0, row_above(edge_ref, beside_in, across_in, slice(None)))
    build_own(0)
    build_own(1)

    def row(r):
        left = jnp.concatenate([taps_ref[at_row(r + 2 - b, columns), :] for b in range(3)], axis=1)
        total = jnp.dot(left, weight_ref[...], preferred_element_type=F32)
        alive = bev_ref[at_row(r + 1, columns), :].astype(F32) > 0.0
        kept = jnp.where(alive, total, 0.0).astype(BF16)
        out_ref[at_row(r, columns), :] = kept

        sums_ref[...] += jnp.sum(kept.astype(F32).reshape(columns // 8, 8, width), axis=0)
        return kept

    def row_and_build(r, carry):
        row(r)
        build_own(r + 2)
        return carry

    put_edges(edge_ref, beside_ref, across_ref, row(0), None)
    build_own(2)
    lax.fori_loop(1, rows - 2, row_and_build, 0)
    row(rows - 2)
    build(rows + 1, row_below(edge_ref, beside_in, across_in, slice(None)))
    put_edges(edge_ref, beside_ref, across_ref, None, row(rows - 1))


def region_data(edges, d_rows, beside, across, bev, weights, columns):
    width = PAIRS * LANES
    return pl.pallas_call(
        functools.partial(region_data_kernel, columns),
        out_shape=(
            jax.ShapeDtypeStruct((d_rows.shape[0], width), BF16),
            jax.ShapeDtypeStruct((columns, width), BF16),
            jax.ShapeDtypeStruct((columns, width), BF16),
            jax.ShapeDtypeStruct((8, width), F32),
        ),
        in_specs=smem(1) + vmem(5),
        out_specs=vmem(4),
        scratch_shapes=[pltpu.VMEM((d_rows.shape[0] + 2 * columns, 3 * LANES), BF16)],
        compiler_params=params(limit=28),
        cost_estimate=work(13),
        name="region_data",
    )(edges, d_rows, beside, across, bev, weights)


def region_weight_kernel(columns, blocks, d_ref, bev_ref, out_ref, total, taps_ref):
    rows = d_ref.shape[0] // columns
    width = PAIRS * LANES
    depth_out = DEPTH // 2
    half = LANES // 2
    total[...] = jnp.zeros_like(total)

    def two(i, carry):
        for k in range(2):
            own = d_ref[at_row(i * 2 + k, columns), :].astype(F32)
            place = slice(k * columns, (k + 1) * columns)
            taps_ref[place, 0:LANES] = from_right(own).astype(BF16)
            taps_ref[place, LANES : 2 * LANES] = own.astype(BF16)
            taps_ref[place, 2 * LANES :] = from_left(own).astype(BF16)
        cells = jnp.concatenate(
            [
                bev_ref[pl.ds(pl.multiple_of((i * 2 + b) * columns, 32), 2 * columns), :]
                for b in range(3)
            ],
            axis=1,
        )
        total[...] += lax.dot_general(
            taps_ref[...], cells, (((0,), (0,)), ((), ())), preferred_element_type=F32
        )
        return carry

    lax.fori_loop(0, rows // 2, two, 0, unroll=2)
    share = half // blocks
    for b in range(3):
        for e in range(3):
            for j in range(PAIRS):
                start = b * width + j * LANES
                turned = total[e * LANES : (e + 1) * LANES, start : start + LANES].T
                for k in range(min(2, depth_out - 2 * j)):
                    for q in range(blocks):
                        begin = k * half + q * share
                        base = ((q * 3 + b) * 3 + e) * share * depth_out
                        out_ref[pl.ds(base + 2 * j + k, share, stride=depth_out), :] = turned[
                            begin : begin + share, :
                        ]


def region_weight(d_own, bev, columns, blocks):
    width = PAIRS * LANES
    return pl.pallas_call(
        functools.partial(region_weight_kernel, columns, blocks),
        out_shape=jax.ShapeDtypeStruct((9 * (DEPTH // 2) * (LANES // 2), LANES), F32),
        in_specs=vmem(2),
        out_specs=vmem(1)[0],
        scratch_shapes=[
            pltpu.VMEM((3 * LANES, 3 * width), F32),
            pltpu.VMEM((2 * columns, 3 * LANES), BF16),
        ],
        compiler_params=params(limit=28),
        cost_estimate=work(10),
        name="region_weight",
    )(d_own, bev)


def prepare_kernel(
    slots, anc_count, device_rows, edge_ref, points_ref, line_ref, labels_ref,
    stats_ref, place_ref, digit_ref,
):
    voxels, width = points_ref.shape
    features = 7
    row = line_ref[1:2, :]
    exists = line_ref[3:4, :]
    column = line_ref[2:3, :]
    digits = jnp.concatenate(
        [
            (line_ref[0:1, :] + 1) * exists,
            (column >> 1) * exists,
            (row * 2 + (column & 1)) * exists,
            line_ref[4:5, :],
        ],
        axis=0,
    ).astype(F32)
    none = jnp.zeros((LANES - 4, LANES), F32)
    for i in range(voxels // LANES):
        here = slice(i * LANES, (i + 1) * LANES)
        digit_ref[here, :] = jnp.concatenate([digits[:, here], none], axis=0).T.astype(BF16)
    lane = lax.broadcasted_iota(jnp.int32, (CHUNK, width), 1)
    ones_lane = features * slots
    slot = jnp.where(lane == ones_lane, -1, lane % slots)
    total = jnp.zeros((width, width), F32)
    for i in range(voxels // CHUNK):
        here = slice(i * CHUNK, (i + 1) * CHUNK)
        count = digit_ref[here, 3:4].astype(F32).astype(jnp.int32)
        block = jnp.where(slot < count, points_ref[here, :].astype(F32), 0.0).astype(BF16)
        total = total + lax.dot_general(
            block, block, (((0,), (0,)), ((), ())), preferred_element_type=F32
        )
    row_at = lax.broadcasted_iota(jnp.int32, (width, width), 0)
    col_at = lax.broadcasted_iota(jnp.int32, (width, width), 1)
    same = (row_at % slots == col_at % slots) | (row_at == ones_lane)
    total = jnp.where(same & (row_at <= ones_lane) & (col_at < ones_lane), total, 0.0)
    rows = [
        jnp.sum(jnp.where(row_at // slots == k, total, 0.0), axis=0, keepdims=True)
        for k in range(features + 1)
    ]
    stacked = jnp.concatenate(rows, axis=0)
    col_eight = lax.broadcasted_iota(jnp.int32, (8, width), 1)
    lane_eight = lax.broadcasted_iota(jnp.int32, (8, LANES), 1)
    row_eight = lax.broadcasted_iota(jnp.int32, (8, LANES), 0)
    stats = jnp.zeros((8, LANES), F32)
    for k in range(features):
        picked = jnp.sum(jnp.where(col_eight // slots == k, stacked, 0.0), axis=1, keepdims=True)
        stats = stats + jnp.where(lane_eight == k, picked, 0.0)
    counted = jnp.sum(digits[3:4, :], axis=1, keepdims=True)
    hits = jnp.zeros(labels_ref.shape[1:], F32)
    for r in range(labels_ref.shape[0]):
        hits = hits + jnp.where(labels_ref[r] == 1, 1.0, 0.0)
    found = jnp.sum(jnp.sum(hits, axis=1, keepdims=True), axis=0, keepdims=True)
    real = exists > 0
    lists = []
    for q in range(anc_count):
        begin = q * device_rows - HALO
        lists.append(real & (row >= begin) & (row < begin + device_rows + 2 * HALO))
    lists.append(real & (row < HALO) & (edge_ref[0] > 0))
    lists.append(real & (row >= anc_count * device_rows - HALO) & (edge_ref[1] > 0))
    lists += [real & (row < 0)] * (8 - len(lists))
    member = jnp.concatenate([jnp.where(x, 1.0, 0.0) for x in lists], axis=0)
    before = (
        lax.broadcasted_iota(jnp.int32, (LANES, LANES), 0)
        < lax.broadcasted_iota(jnp.int32, (LANES, LANES), 1)
    )
    before = jnp.where(before, 1.0, 0.0).astype(BF16)
    carry = jnp.zeros((8, 1), F32)
    eight = lax.broadcasted_iota(jnp.int32, (8, LANES), 0)
    for i in range(voxels // LANES):
        here = slice(i * LANES, (i + 1) * LANES)
        part = member[:, here]
        ahead = jnp.dot(part.astype(BF16), before, preferred_element_type=F32) + carry
        places = jnp.where(part > 0.0, ahead, -1.0).astype(jnp.int32)
        owner = jnp.zeros((1, LANES), jnp.int32)
        own = jnp.full((1, LANES), -1, jnp.int32)
        for q in range(anc_count):
            mine = (row[:, here] >= q * device_rows) & (row[:, here] < (q + 1) * device_rows)
            mine = mine & real[:, here]
            owner = jnp.where(mine, q, owner)
            own = jnp.where(mine, places[q : q + 1, :], own)
        places = jnp.where(eight == 6, owner, jnp.where(eight == 7, own, places))
        place_ref[:, here] = places
        carry = carry + jnp.sum(part, axis=1, keepdims=True)
    is_edge = lax.broadcasted_iota(jnp.int32, (8, 1), 0) >= anc_count
    need = carry / jnp.where(is_edge, float(EDGE_CAP), float(CAP))
    need = jnp.max(need, axis=0, keepdims=True)
    for k, value in enumerate((counted, found, need)):
        stats = stats + jnp.where((lane_eight == 8) & (row_eight == k), value, 0.0)
    for i in range(stats_ref.shape[0]):
        stats_ref[i] = stats


def prepare(edges, points, lines, labels, anc_count, device_rows, slots, devices):
    voxels = points.shape[0]
    return pl.pallas_call(
        functools.partial(prepare_kernel, slots, anc_count, device_rows),
        out_shape=(
            jax.ShapeDtypeStruct((devices, 8, LANES), F32),
            jax.ShapeDtypeStruct((8, voxels), jnp.int32),
            jax.ShapeDtypeStruct((voxels, LANES), BF16),
        ),
        in_specs=smem(1) + vmem(3),
        out_specs=vmem(3),
        compiler_params=params(limit=24),
        cost_estimate=work(4),
        name="prepare",
    )(edges, points, lines, labels)


def batch_norm(stats, kernel):
    lanes = kernel.shape[1]
    moments = stats[:, 0:8]
    count = stats[0:1, 8:9]
    mixed = jnp.zeros((8, lanes), F32)
    for k in range(7):
        mixed = mixed + moments[:, k : k + 1] * kernel[k : k + 1, :]
    mean = mixed[7:8, :] / count
    second = jnp.sum(mixed * kernel, axis=0, keepdims=True) / count
    inv_std = lax.rsqrt(second - mean * mean + BN_EPSILON)
    return mixed, mean, inv_std, count


def first_layer(points, first_ref, scale, offset, valid):
    hidden = jnp.dot(points, first_ref[...], preferred_element_type=F32)
    act = jnp.where(valid, jnp.maximum(hidden * scale + offset, 0.0), 0.0)
    return act


def group_fold(values, combine):
    groups = values.shape[1] // LANES
    out = values[:, :LANES]
    for g in range(1, groups):
        out = combine(out, values[:, g * LANES : (g + 1) * LANES])
    out = combine(out, pltpu.roll(out, 32, 1))
    return combine(out, pltpu.roll(out, 64, 1))


def second_tail(pooled):
    lane = lax.broadcasted_iota(jnp.int32, pooled.shape, 1)
    return jnp.where(lane < 32, pooled, jnp.where(lane == 32, 1.0, 0.0))


def group_left(low, tail, count, g):
    lane = lax.broadcasted_iota(jnp.int32, tail.shape, 1)
    marked = (lane > 32) & (lane < 37) & (lane - (33 - 4 * g) >= count)
    side = jnp.where(marked, 1.0, tail).astype(BF16)
    return jnp.concatenate([low[:, g * LANES : (g + 1) * LANES], side], axis=1)


def encode_kernel(
    slots, points_ref, count_ref, stats_ref, kernel_ref, gain_ref, first_ref, second_ref,
    feat_ref, share_ref, slot_ref, held,
):
    lanes = first_ref.shape[1]
    _, mean, inv_std, _ = batch_norm(jnp.sum(stats_ref[...], axis=0), kernel_ref[...])
    scale = gain_ref[0:1, :] * inv_std
    offset = gain_ref[1:2, :] - mean * scale
    count = count_ref[:, 3:4].astype(F32).astype(jnp.int32)
    slot = lax.broadcasted_iota(jnp.int32, (CHUNK, lanes), 1) // 32
    act = first_layer(points_ref[...], first_ref, scale, offset, slot < count)
    tail = second_tail(group_fold(act, jnp.maximum))
    low = act.astype(BF16)
    top = jnp.full((CHUNK, LANES), -jnp.inf, F32)
    for g in range(lanes // LANES):
        left = group_left(low, tail, count, g)
        part = jnp.dot(left, second_ref[...], preferred_element_type=F32)
        for s in range(min(4, slots - 4 * g)):
            p = 4 * g + s
            one = part[:, s * LANES : (s + 1) * LANES]
            held[p] = one
            top = jnp.maximum(top, one)
    code = jnp.zeros((CHUNK, LANES), F32)
    for p in range(slots):
        code = code + jnp.where(held[p] == top, 2048.0 + p, 0.0)
    ties = jnp.floor(code / 2048.0)
    feat_ref[...] = jnp.maximum(top, 0.0)
    share_ref[...] = jnp.where(top > 0.0, 1.0 / ties, 0.0)
    slot_ref[...] = jnp.minimum(code - 2048.0 * ties, 127.0).astype(BF16)


def encode(points, counts, stats, kernel, gain, first, second, slots):
    voxels, width = points.shape
    lanes = first.shape[1]
    whole = lambda *shape: pl.BlockSpec(shape, lambda i: (0,) * len(shape))
    block = lambda size: pl.BlockSpec((CHUNK, size), lambda i: (i, 0))
    return pl.pallas_call(
        functools.partial(encode_kernel, slots),
        grid=(voxels // CHUNK,),
        out_shape=(
            jax.ShapeDtypeStruct((voxels, LANES), F32),
            jax.ShapeDtypeStruct((voxels, LANES), F32),
            jax.ShapeDtypeStruct((voxels, LANES), BF16),
        ),
        in_specs=[
            block(width),
            block(LANES),
            whole(*stats.shape),
            whole(8, lanes),
            whole(8, lanes),
            whole(width, lanes),
            whole(2 * LANES, 4 * LANES),
        ],
        out_specs=[block(LANES), block(LANES), block(LANES)],
        scratch_shapes=[pltpu.VMEM((slots, CHUNK, LANES), F32)],
        compiler_params=params("arbitrary", limit=30),
        cost_estimate=work(14),
        name="encode",
    )(points, counts, stats, kernel, gain, first, second)


def decode_kernel(
    slots, points_ref, count_ref, stats_ref, kernel_ref, gain_ref, first_ref, second_ref,
    feat_ref, share_ref, slot_ref, d_feat_ref, loss_ref, out_ref,
    first_sum, second_sum, joined, tail_sum,
):
    lanes = first_ref.shape[1]
    width = points_ref.shape[1]
    step = pl.program_id(0)

    @pl.when(step == 0)
    def _():
        first_sum[...] = jnp.zeros_like(first_sum)
        second_sum[...] = jnp.zeros_like(second_sum)

    _, mean, inv_std, _ = batch_norm(jnp.sum(stats_ref[...], axis=0), kernel_ref[...])
    scale = gain_ref[0:1, :] * inv_std
    offset = gain_ref[1:2, :] - mean * scale
    count = count_ref[:, 3:4].astype(F32).astype(jnp.int32)
    points = points_ref[...]
    slot = lax.broadcasted_iota(jnp.int32, (CHUNK, lanes), 1) // 32
    act = first_layer(points, first_ref, scale, offset, slot < count)
    pooled = group_fold(act, jnp.maximum)
    tail = second_tail(pooled)
    low = act.astype(BF16)
    share = share_ref[...]
    d_feat = d_feat_ref[...] * share
    d_low = d_feat.astype(BF16)
    shared = jnp.where((share > 0.0) & (share < 1.0), 1.0, 0.0)
    shared = jnp.max(jnp.max(shared, axis=1, keepdims=True)) > 0.0

    def group_back(g, left, pieces):
        d_part = jnp.concatenate(pieces, axis=1)
        second_sum[...] += lax.dot_general(
            left, d_part, (((0,), (0,)), ((), ())), preferred_element_type=F32
        )
        d_left = lax.dot_general(
            d_part, second_ref[...], (((1,), (1,)), ((), ())), preferred_element_type=F32
        )
        joined[:, g * LANES : (g + 1) * LANES] = d_left[:, :LANES]
        return d_left[:, LANES:]

    none = jnp.zeros((CHUNK, LANES), BF16)

    @pl.when(jnp.logical_not(shared))
    def _():
        found = slot_ref[...]
        d_tail = jnp.zeros((CHUNK, LANES), F32)
        for g in range(lanes // LANES):
            left = group_left(low, tail, count, g)
            pieces = [
                jnp.where(found == jnp.asarray(4 * g + s, BF16), d_low, none)
                if 4 * g + s < slots
                else none
                for s in range(4)
            ]
            d_tail = d_tail + group_back(g, left, pieces)
        tail_sum[...] = d_tail

    @pl.when(shared)
    def _():
        top = feat_ref[...]
        d_tail = jnp.zeros((CHUNK, LANES), F32)
        for g in range(lanes // LANES):
            left = group_left(low, tail, count, g)
            part = jnp.dot(left, second_ref[...], preferred_element_type=F32)
            pieces = []
            for s in range(4):
                if 4 * g + s < slots:
                    hit = part[:, s * LANES : (s + 1) * LANES] == top
                    pieces.append(jnp.where(hit, d_feat, 0.0).astype(BF16))
                else:
                    pieces.append(none)
            d_tail = d_tail + group_back(g, left, pieces)
        tail_sum[...] = d_tail

    wide = jnp.concatenate([pooled] * (lanes // LANES), axis=1)
    reached = act == wide
    ties = group_fold(jnp.where(reached, 1.0, 0.0), jnp.add)
    lane = lax.broadcasted_iota(jnp.int32, (CHUNK, LANES), 1)
    spread = jnp.where(lane < 32, tail_sum[...], 0.0)
    spread = spread + pltpu.roll(spread, 32, 1)
    spread = (spread + pltpu.roll(spread, 64, 1)) / ties
    spread = jnp.concatenate([spread] * (lanes // LANES), axis=1)
    d_act = joined[...] + jnp.where(reached, spread, 0.0)
    d_act = jnp.where(act > 0.0, d_act, 0.0).astype(BF16)
    first_sum[...] += lax.dot_general(
        points, d_act, (((0,), (0,)), ((), ())), preferred_element_type=F32
    )

    @pl.when(step == pl.num_programs(0) - 1)
    def _():
        row_at = lax.broadcasted_iota(jnp.int32, (width, lanes), 0)
        col_at = lax.broadcasted_iota(jnp.int32, (width, lanes), 1)
        same = (row_at % slots == col_at // 32) | (row_at == 7 * slots)
        total = jnp.where(same & (col_at // 32 < slots), first_sum[...], 0.0)
        rows = [
            jnp.sum(jnp.where(row_at // slots == k, total, 0.0), axis=0, keepdims=True)
            for k in range(8)
        ]
        first = group_fold(jnp.concatenate(rows, axis=0), jnp.add)
        upper = second_sum[0:32, 0:LANES]
        lower = second_sum[LANES : LANES + 40, 0:LANES]
        for s in range(1, 4):
            cols = slice(s * LANES, (s + 1) * LANES)
            upper = upper + second_sum[s * 32 : (s + 1) * 32, cols]
            lower = lower + second_sum[LANES : LANES + 40, cols]
        devices, layers = out_ref.shape[:2]
        none = jnp.zeros((devices * layers - 88, LANES), F32)
        rows = jnp.concatenate([first, upper, lower, loss_ref[...], none], axis=0)
        for k in range(layers):
            out_ref[:, k, :] = rows[k * devices : (k + 1) * devices, :]


def decode(
    points, counts, stats, kernel, gain, first, second, feat, share, slot, d_feat, loss, shape, slots
):
    voxels, width = points.shape
    lanes = first.shape[1]
    whole = lambda *shape: pl.BlockSpec(shape, lambda i: (0,) * len(shape))
    block = lambda size: pl.BlockSpec((CHUNK, size), lambda i: (i, 0))
    return pl.pallas_call(
        functools.partial(decode_kernel, slots),
        grid=(voxels // CHUNK,),
        out_shape=jax.ShapeDtypeStruct(shape + (LANES,), F32),
        in_specs=[
            block(width),
            block(LANES),
            whole(*stats.shape),
            whole(8, lanes),
            whole(8, lanes),
            whole(width, lanes),
            whole(2 * LANES, 4 * LANES),
            block(LANES),
            block(LANES),
            block(LANES),
            block(LANES),
            whole(8, LANES),
        ],
        out_specs=whole(*shape, LANES),
        scratch_shapes=[
            pltpu.VMEM((width, lanes), F32),
            pltpu.VMEM((2 * LANES, 4 * LANES), F32),
            pltpu.VMEM((CHUNK, lanes), F32),
            pltpu.VMEM((CHUNK, LANES), F32),
        ],
        compiler_params=params("arbitrary", limit=30),
        cost_estimate=work(28),
        name="decode",
    )(points, counts, stats, kernel, gain, first, second, feat, share, slot, d_feat, loss)


def encoder_weights_kernel(
    slots, one_ref, two_ref, bias_ref, gain_ref, first_ref, second_ref, kernel_ref, rows_ref
):
    width, lanes = first_ref.shape
    features = one_ref.shape[0] - 1
    row_at = lax.broadcasted_iota(jnp.int32, (width, LANES), 0)
    slot_at = lax.broadcasted_iota(jnp.int32, (width, LANES), 1) // 32
    one = jnp.concatenate([one_ref[...]] * 4, axis=1)
    tall = jnp.zeros((width, LANES), F32)
    for k in range(features):
        tall = jnp.where(row_at // slots == k, one[k : k + 1, :], tall)
    own_slot = row_at % slots
    for g in range(lanes // LANES):
        here = slice(g * LANES, (g + 1) * LANES)
        first_ref[:, here] = jnp.where(own_slot == 4 * g + slot_at, tall, 0.0).astype(BF16)
        kernel_ref[:, here] = one
        rows_ref[:, here] = jnp.concatenate([gain_ref[...]] * 4, axis=1)
    two = two_ref[...]
    half = two.shape[0] // 2
    upper = jnp.concatenate([two[:half]] * 4, axis=0)
    row_two = lax.broadcasted_iota(jnp.int32, (LANES, LANES), 0)
    for s in range(4):
        here = slice(s * LANES, (s + 1) * LANES)
        second_ref[0:LANES, here] = jnp.where(row_two // half == s, upper, 0.0).astype(BF16)
        lower = jnp.concatenate(
            [two[half:], bias_ref[...], jnp.zeros((LANES - half - 8, LANES), F32)], axis=0
        )
        second_ref[LANES:, here] = jnp.where(row_two == half + 1 + s, EMPTY, lower).astype(BF16)


def encoder_weights(w_one, w_two, bias_two, gain, shift, slots):
    features, c_one = w_one.shape
    lanes = -(-slots // 4) * LANES
    width = -(-(features * slots + 1) // LANES) * LANES
    one = jnp.pad(w_one.astype(F32), ((0, 1), (0, 0)))
    bias = jnp.pad(bias_two.astype(F32).reshape(1, -1), ((0, 7), (0, 0)))
    rows = jnp.pad(jnp.stack([gain, shift]).astype(F32), ((0, 6), (0, 0)))
    return pl.pallas_call(
        functools.partial(encoder_weights_kernel, slots),
        out_shape=(
            jax.ShapeDtypeStruct((width, lanes), BF16),
            jax.ShapeDtypeStruct((2 * LANES, 4 * LANES), BF16),
            jax.ShapeDtypeStruct((8, lanes), F32),
            jax.ShapeDtypeStruct((8, lanes), F32),
        ),
        in_specs=vmem(4),
        out_specs=vmem(4),
        compiler_params=params(limit=24),
        cost_estimate=work(2),
        name="encoder_weights",
    )(one, w_two.astype(F32), bias, rows)


def pick_rows(source, place_ref, line, capacity, offset):
    want = place_ref[line : line + 1, :] - offset
    row_at = lax.broadcasted_iota(jnp.int32, (capacity, source.shape[0]), 0)
    chosen = jnp.where(want == row_at, 1.0, 0.0).astype(BF16)
    found = jnp.dot(chosen, source, preferred_element_type=F32)
    return found[:, :LANES].astype(BF16), found[:, LANES:].T


def edge_lists_kernel(anc_count, offset_ref, feat_ref, digit_ref, place_ref, up_ref, down_ref):
    source = jnp.concatenate([feat_ref[...].astype(BF16), digit_ref[...]], axis=1)
    for side, edge_ref in enumerate((up_ref, down_ref)):
        rows, digits = pick_rows(source, place_ref, anc_count + side, EDGE_CAP, offset_ref[1])
        edge_ref[0:EDGE_CAP, :] = rows
        digits = jnp.concatenate([digits[0:8, :], jnp.zeros((8, LANES), F32)], axis=0)
        edge_ref[EDGE_CAP : EDGE_CAP + 16, :] = digits.astype(BF16)


def edge_lists(offsets, feat, digits, place, anc_count):
    return pl.pallas_call(
        functools.partial(edge_lists_kernel, anc_count),
        out_shape=(
            jax.ShapeDtypeStruct((EDGE_CAP + 16, LANES), BF16),
            jax.ShapeDtypeStruct((EDGE_CAP + 16, LANES), BF16),
        ),
        in_specs=smem(1) + vmem(3),
        out_specs=vmem(2),
        compiler_params=params(limit=24),
        cost_estimate=work(1),
        name="edge_lists",
    )(offsets, feat, digits, place)


def gather_lists_kernel(anc_count, offset_ref, feat_ref, digit_ref, place_ref, main_ref):
    source = jnp.concatenate([feat_ref[...].astype(BF16), digit_ref[...]], axis=1)
    for q in range(anc_count):
        rows, digits = pick_rows(source, place_ref, q, CAP, offset_ref[0])
        main_ref[q, 0:CAP, :] = rows
        lines = [
            digits[k : k + 1, i * LANES : (i + 1) * LANES]
            for k in range(3)
            for i in range(CAP // LANES)
        ]
        lines.append(jnp.zeros((32 - len(lines), LANES), F32))
        main_ref[q, CAP : CAP + 32, :] = jnp.concatenate(lines, axis=0).astype(BF16)
        main_ref[q, CAP + 32 :, :] = jnp.zeros((EDGE_CAP + 16, LANES), BF16)


def gather_lists(offsets, feat, digits, place, anc_count):
    return pl.pallas_call(
        functools.partial(gather_lists_kernel, anc_count),
        out_shape=jax.ShapeDtypeStruct((anc_count, CAP + EDGE_CAP + 48, LANES), BF16),
        in_specs=smem(1) + vmem(3),
        out_specs=vmem(1)[0],
        compiler_params=params(limit=30),
        cost_estimate=work(5),
        name="gather_lists",
    )(offsets, feat, digits, place)


def spread_lists_kernel(index_ref, *refs):
    received, (out_ref, held) = refs[:-2], refs[-2:]
    length = received[0].shape[0]
    for k, received_ref in enumerate(received):
        held[k * length : (k + 1) * length, :] = received_ref[...].astype(F32)
    held[len(received) * length :, :] = jnp.zeros((8, LANES), F32)

    def pick(i, carry):
        base = pl.multiple_of(i * LANES, LANES)
        for j in range(LANES):
            out_ref[pl.ds(base + j, 1), :] = held[pl.ds(index_ref[base + j], 1), :]
        return carry

    lax.fori_loop(0, out_ref.shape[0] // LANES, pick, 0)


def spread_lists(index, received):
    voxels = index.shape[0]
    total = sum(rows.shape[0] for rows in received)
    return pl.pallas_call(
        spread_lists_kernel,
        out_shape=jax.ShapeDtypeStruct((voxels, LANES), F32),
        in_specs=smem(1) + vmem(len(received)),
        out_specs=vmem(1)[0],
        scratch_shapes=[pltpu.VMEM((total + 8, LANES), F32)],
        compiler_params=params(limit=24),
        cost_estimate=work(4),
        name="spread_lists",
    )(index, *received)


def add_piece(held, source, low, high, start):
    lane = lax.broadcasted_iota(jnp.int32, (1, LANES), 1)
    begin, end = low // LANES, -(-high // LANES)
    gap = start - low
    turn = gap % LANES
    at = begin + gap // LANES
    rows = source[begin:end, :]
    count = end - begin
    place = lax.broadcasted_iota(jnp.int32, (count, LANES), 0) * LANES
    place = place + lax.broadcasted_iota(jnp.int32, (count, LANES), 1) + begin * LANES
    if low % LANES or high % LANES:
        rows = jnp.where((place >= low) & (place < high), rows, 0.0)
    if turn == 0:
        held[at : at + count, :] += rows
        return
    rows = pltpu.roll(rows, turn, 1)
    here = jnp.where(lane >= turn, rows, 0.0)
    after = jnp.where(lane < turn, rows, 0.0)
    skip = max(-at, 0)
    if count > skip:
        held[at + skip : at + count, :] += here[skip:, :]
    held[at + 1 : at + 1 + count, :] += after


def pack_kernel(
    plan, tiles, chunk, region_ref, middle_ref, head_ref, mid_ref, row_ref, out_ref, held, rest_ref
):
    half = LANES // 2
    lane = lax.broadcasted_iota(jnp.int32, (1, LANES), 1)
    mid = jnp.sum(mid_ref[...], axis=0, keepdims=True)
    mid = group_sum(mid)
    mid = mid + pltpu.roll(mid, half, 1)
    region_bias = pltpu.roll(jnp.sum(row_ref[0:8, :], axis=0, keepdims=True), half, 1)
    outs = row_ref.shape[0] - 16
    wide = lax.broadcasted_iota(jnp.int32, (outs, LANES), 1) - half
    own = lax.broadcasted_iota(jnp.int32, (outs, LANES), 0) == wide
    head_bias = jnp.sum(jnp.where(own, row_ref[8 : 8 + outs, :], 0.0), axis=0, keepdims=True)
    rest_ref[0:1, :] = jnp.where(lane < half, mid, region_bias)
    rest_ref[1:2, :] = jnp.where(lane < half, region_bias, head_bias)
    sources = {"region": region_ref, "middle": middle_ref, "head": head_ref, "rest": rest_ref}
    for a, pieces in enumerate(plan):
        held[...] = jnp.zeros_like(held)
        for name, low, high, start in pieces:
            if name in sources:
                add_piece(held, sources[name], low, high, start)
        for t in range(tiles):
            out_ref[t * len(plan) + a] = held[t * chunk : (t + 1) * chunk, :].astype(BF16)


def group_sum(values):
    out = values[:, :LANES]
    for g in range(1, values.shape[1] // LANES):
        out = out + values[:, g * LANES : (g + 1) * LANES]
    return out


def pack(plan, tiles, chunk, region, middle, head, mid_sums, row_sums):
    return pl.pallas_call(
        functools.partial(pack_kernel, plan, tiles, chunk),
        out_shape=jax.ShapeDtypeStruct((tiles * len(plan), chunk, LANES), BF16),
        in_specs=vmem(5),
        out_specs=vmem(1)[0],
        scratch_shapes=[pltpu.VMEM((tiles * chunk, LANES), F32), pltpu.VMEM((8, LANES), F32)],
        compiler_params=params(limit=28),
        cost_estimate=work(3),
        name="pack",
    )(region, middle, head, mid_sums, row_sums)


def sum_chunk_kernel(parts_ref, out_ref, square_ref):
    total = jnp.sum(parts_ref[...].astype(F32), axis=0)
    for i in range(out_ref.shape[0]):
        out_ref[i] = total
    square_ref[...] = jnp.broadcast_to(jnp.sum(total * total), square_ref.shape)


def sum_chunk(parts, tiles):
    _, rows, lanes = parts.shape
    return pl.pallas_call(
        sum_chunk_kernel,
        out_shape=(
            jax.ShapeDtypeStruct((tiles, rows, lanes), F32),
            jax.ShapeDtypeStruct((1, lanes), F32),
        ),
        in_specs=vmem(1),
        out_specs=vmem(2),
        compiler_params=params(limit=24),
        cost_estimate=work(2),
        name="sum_chunk",
    )(parts)


def finish_kernel(
    plan, anc_ref, early_ref, late_ref, stats_ref, kernel_ref, gain_ref,
    out_ref, scalar_ref, one, norm,
):
    stats = jnp.sum(stats_ref[...], axis=0)
    kernel = kernel_ref[:, :LANES]
    mixed, mean, inv_std, count = batch_norm(stats, kernel)
    layers = late_ref.shape[1] - 1
    late = jnp.concatenate([late_ref[:, k, :] for k in range(layers)], axis=0)
    sums = late[0:8, :]
    total_shift = sums[7:8, :]
    total_gain = inv_std * (jnp.sum(kernel * sums, axis=0, keepdims=True) - mean * total_shift)
    slope = gain_ref[0:1, :LANES] * inv_std
    lane = lax.broadcasted_iota(jnp.int32, (1, LANES), 1)
    one[...] = jnp.zeros_like(one)
    norm[...] = jnp.zeros_like(norm)
    for k in range(7):
        first = stats[7:8, k : k + 1]
        pull = total_shift * first + total_gain * inv_std * (mixed[k : k + 1, :] - mean * first)
        grad = jnp.where(lane < 32, slope * (sums[k : k + 1, :] - pull / count), 0.0)
        if k % 4:
            grad = pltpu.roll(grad, 32 * (k % 4), 1)
        one[k // 4 : k // 4 + 1, :] += grad
    bias = late[72:73, :]
    top = jnp.where(lane < 32, total_gain, 0.0)
    top = top + pltpu.roll(jnp.where(lane < 32, total_shift, 0.0), 32, 1)
    norm[0:1, :] = top + jnp.where(lane < 64, 0.0, pltpu.roll(bias, 64, 1))
    norm[1:2, :] = jnp.where(lane < 64, pltpu.roll(bias, 64, 1), 0.0)
    two = late[8:72, :]
    square = jnp.sum(late_ref[:, layers, :]) / LANES
    square = square + jnp.sum(two * two) + jnp.sum(one[...] * one[...])
    square = square + jnp.sum(norm[...] * norm[...])
    size = jnp.sqrt(jnp.broadcast_to(square, (1, LANES)))
    scalar_ref[0:1, :] = late[80:81, :] / stats[1:2, 8:9]
    scalar_ref[1:2, :] = size
    scalar_ref[2:8, :] = jnp.broadcast_to(jnp.minimum(1.0, CLIP_LIMIT / (size + 1e-06)), (6, LANES))
    chunk = early_ref.shape[1]
    for i in range(early_ref.shape[0]):
        out_ref[i * chunk : (i + 1) * chunk, :] = early_ref[i]
    sources = {"one": one, "two": two, "norm": norm}
    for a, pieces in enumerate(plan):

        @pl.when(anc_ref[0] == a)
        def _():
            for name, low, high, start in pieces:
                if name in sources:
                    add_piece(out_ref, sources[name], low, high, start)


def finish(plan, anc, early, late, stats, kernel, gain):
    return pl.pallas_call(
        functools.partial(finish_kernel, plan),
        out_shape=(
            jax.ShapeDtypeStruct((early.shape[0] * early.shape[1], LANES), F32),
            jax.ShapeDtypeStruct((8, LANES), F32),
        ),
        in_specs=smem(1) + vmem(5),
        out_specs=vmem(2),
        scratch_shapes=[pltpu.VMEM((8, LANES), F32), pltpu.VMEM((8, LANES), F32)],
        compiler_params=params(limit=24),
        cost_estimate=work(3),
        name="finish",
    )(anc, early, late, stats, kernel, gain)


def everyone(values, axes):
    count = 1
    for axis in axes:
        count *= lax.axis_size(axis)
    copies = jnp.broadcast_to(values[None], (count,) + values.shape)
    return lax.all_to_all(copies, axes, 0, 0)


def swap_rows(beside, across):
    axes = ("tile", "anc")
    count = lax.axis_size("tile") * lax.axis_size("anc")
    pairs = [(i, i ^ 1) for i in range(count)]
    others = [(i, i + 1) for i in range(1, count - 1, 2)]
    others += [(j, i) for i, j in others]
    return lax.ppermute(beside, axes, pairs), lax.ppermute(across, axes, others)


def shard_windows(segments, shard, count):
    windows = []
    for a in range(count):
        begin, end = a * shard, (a + 1) * shard
        at = 0
        pieces = []
        for name, size in segments:
            low, high = max(begin, at), min(end, at + size)
            if low < high:
                pieces.append((name, low - at, high - at, low - begin))
            at += size
        windows.append(tuple(pieces))
    return tuple(windows)


def on_device(
    points,
    npoints,
    coords,
    labels,
    targets,
    w_vfe1,
    w_vfe2,
    w_mid,
    w_rpn,
    w_head,
    bn_gain,
    biases,
    master,
    moment1,
    moment2,
):
    both = ("tile", "anc")
    anc_count = lax.axis_size("anc")
    tile_count = lax.axis_size("tile")
    anc = lax.axis_index("anc")
    tile = lax.axis_index("tile")
    device_rows = labels.shape[1]
    columns = labels.shape[2]
    blocks = device_rows // BLOCK_ROWS
    tile_rows = device_rows * anc_count
    all_rows = tile_rows * tile_count
    slots = points.shape[1]
    voxels = points.shape[2]
    c_vfe = w_vfe1.shape[1]
    c_vox = w_vfe2.shape[1]
    c_mid = w_mid.shape[4]
    c_rpn = w_rpn.shape[3]
    outs = w_head.shape[1]
    shift = biases[:c_vfe]
    bias_two = biases[c_vfe : c_vfe + c_vox]
    rest = biases[c_vfe + c_vox :].astype(F32)
    bias_rows = jnp.concatenate(
        [rest[:c_mid], rest, jnp.zeros((LANES - outs,), F32)]
    ).reshape(3, LANES)

    def joined(row):
        return (row % CROP_ROWS != CROP_ROWS // 2) & (row > 0) & (row < all_rows)

    padded = -(-voxels // CHUNK) * CHUNK
    width = -(-(points.shape[0] * slots + 1) // LANES) * LANES
    flat_points = points.reshape(-1, voxels).T
    flat_points = jnp.pad(
        flat_points, ((0, padded - voxels), (0, width - flat_points.shape[1]))
    )
    lane = lax.broadcasted_iota(jnp.int32, flat_points.shape, 1)
    flat_points = jnp.where(lane == points.shape[0] * slots, jnp.ones((), BF16), flat_points)
    spare = (0, padded - voxels)
    row = coords[:, 1] - tile * tile_rows
    lines = [coords[:, 0], row, coords[:, 2], jnp.ones_like(row), npoints]
    lines = jnp.pad(jnp.stack(lines), ((0, 3), spare))
    tile_edges = jnp.stack([joined(tile * tile_rows), joined((tile + 1) * tile_rows)])
    devices = anc_count * tile_count
    parts = [w_rpn]
    for k in range(1, anc_count):
        around = [((i + k) % anc_count, i) for i in range(anc_count)]
        parts.append(lax.ppermute(w_rpn, "anc", around))
    stats, place, digits = prepare(
        tile_edges.astype(jnp.int32),
        flat_points,
        lines,
        labels.transpose(1, 0, 2),
        anc_count,
        device_rows,
        slots,
        devices,
    )
    stats, parts = lax.optimization_barrier((stats, parts))
    stats = lax.all_to_all(stats, both, 0, 0)
    region_in, region_back = region_order(anc.reshape(1), parts)
    counts = digits
    count_pos = jnp.sum(stats[:, 1, 8])
    rounds = jnp.ceil(jnp.max(stats[:, 2, 8])).astype(jnp.int32)
    middle_kernel_all = w_mid.transpose(0, 1, 2, 4, 3).reshape(-1, c_mid, c_vox)

    first, second, kernel, gain_rows = encoder_weights(
        w_vfe1, w_vfe2, bias_two, bn_gain, shift, slots
    )
    feat, share, found = encode(
        flat_points, counts, stats, kernel, gain_rows, first, second, slots
    )
    feat, region_in, region_back = lax.optimization_barrier((feat, region_in, region_back))

    in_tile = lax.axis_size("tile")
    upward = [(i + 1, i) for i in range(in_tile - 1)]
    downward = [(i, i + 1) for i in range(in_tile - 1)]

    def exchange(number):
        offsets = jnp.stack([number * CAP, number * EDGE_CAP]).astype(jnp.int32)
        up, down = edge_lists(offsets, feat, digits, place, anc_count)
        from_below = lax.ppermute(up, "tile", upward)
        from_above = lax.ppermute(down, "tile", downward)
        main = gather_lists(offsets, feat, digits, place, anc_count)
        main, from_below, from_above = lax.optimization_barrier((main, from_below, from_above))
        main = lax.dynamic_update_slice(main, from_above[None], (0, CAP + 32, 0))
        main = lax.dynamic_update_slice(main, from_below[None], (anc_count - 1, CAP + 32, 0))
        return lax.all_to_all(main, "anc", 0, 0), main

    def cells(got):
        words = got[:, CAP : CAP + 32].reshape(anc_count, -1).astype(jnp.int32)
        start = CAP + 32 + EDGE_CAP
        edge_words = got[:, start : start + 16].astype(jnp.int32)

        def word(k):
            gap = jnp.zeros((anc_count, 32), jnp.int32)
            parts = [words[:, k * CAP : (k + 1) * CAP], gap, edge_words[:, k], gap[:, :16]]
            return jnp.concatenate(parts, axis=1)

        high, half, mixed = word(0), word(1), word(2)
        local = mixed // 2 - anc * device_rows
        is_edge = lax.broadcasted_iota(jnp.int32, local.shape, 1) >= CAP
        local = local + jnp.where(is_edge, jnp.where(anc == 0, -tile_rows, tile_rows), 0)
        cross = half * 2 + mixed % 2
        scatter_at, own_at = [], []
        for k in range(blocks):
            line = local - k * BLOCK_ROWS
            tall = BLOCK_ROWS + 2 * HALO
            inside = (high > 0) & (line >= -HALO) & (line < BLOCK_ROWS + HALO)
            spot = ((high - 1) * tall + line + HALO) * columns + cross
            scatter_at.append(jnp.where(inside, spot, DEPTH * tall * columns).reshape(-1))
            inside = (high > 0) & (line >= 0) & (line < BLOCK_ROWS)
            spot = ((high - 1) * BLOCK_ROWS + line) * columns + cross
            spot = jnp.where(inside, spot, DEPTH * BLOCK_ROWS * columns)
            own_at.append(spot[:, :CAP].reshape(-1, LANES))
        return scatter_at, own_at

    got, sent = exchange(0)
    labels, targets, _ = lax.optimization_barrier((labels, targets, sent[0, 0, 0]))
    first_row = tile * tile_rows + anc * device_rows
    edges = []
    even = (tile * anc_count + anc) % 2 == 0
    for k in range(blocks):
        top = first_row + k * BLOCK_ROWS
        flags = [
            joined(top),
            joined(top + BLOCK_ROWS),
            even,
            anc * device_rows + k * BLOCK_ROWS,
            jnp.where(anc == 0, -tile_rows, tile_rows),
            anc,
        ]
        edges.append(jnp.stack([flag.astype(jnp.int32) for flag in flags]))

    def more(state):
        return state[0] < rounds

    def another(state):
        number, held = state
        rows, _ = exchange(number)
        index, _ = cells(rows)
        rows = rows.reshape(-1, LANES)
        held = [scatter_rows(at, rows, old, columns) for at, old in zip(index, held)]
        return number + 1, held

    def one_round():
        made = [
            scatter_middle(
                edges[k], got.reshape(-1, LANES), middle_kernel_all, bias_rows, columns
            )
            for k in range(blocks)
        ]
        return tuple([one[i] for one in made] for i in range(3))

    def many_rounds():
        index, own = cells(got)
        held = [scatter_rows(at, got.reshape(-1, LANES), None, columns) for at in index]
        _, held = lax.while_loop(more, another, (jnp.int32(1), held))
        bevs = [
            middle_forward(edges[k], held[k], middle_kernel_all, bias_rows, columns)
            for k in range(blocks)
        ]
        return held, bevs, own

    grids, bevs, own_at = lax.cond(rounds > 1, many_rounds, one_round)

    wide_labels = jnp.repeat(labels.reshape(2, -1), outs // 2, axis=0)
    wide_targets = jnp.pad(targets, ((0, 0), (1, 0), (0, 0), (0, 0))).reshape(outs, -1)
    step = BLOCK_ROWS * columns
    scale = 1.0 / count_pos
    d_rows, head_sums, row_sums = [], 0.0, 0.0
    d_beside, d_across = [], []
    for k in range(blocks):
        here = slice(k * step, (k + 1) * step)
        d_block, near_row, far_row, heads, sums = region_forward(
            scale,
            edges[k],
            bevs[k],
            region_in,
            bias_rows,
            w_head.T,
            wide_labels[:, here],
            wide_targets[:, here],
            columns,
        )
        d_rows.append(d_block)
        d_beside.append(near_row)
        d_across.append(far_row)
        head_sums = head_sums + heads
        row_sums = row_sums + sums

    def swapped(near, far):
        if blocks == 1:
            got_near, got_far = swap_rows(near[0], far[0])
            return [got_near], [got_far]
        firsts = [jnp.where(even, f, n) for n, f in zip(near, far)]
        lasts = [jnp.where(even, n, f) for n, f in zip(near, far)]
        got_near, got_far = swap_rows(
            jnp.where(even, lasts[-1], firsts[0]), jnp.where(even, firsts[0], lasts[-1])
        )
        above = [jnp.where(even, got_far, got_near)] + lasts[:-1]
        below = firsts[1:] + [jnp.where(even, got_near, got_far)]
        return (
            [jnp.where(even, y, x) for x, y in zip(above, below)],
            [jnp.where(even, x, y) for x, y in zip(above, below)],
        )

    beside, across = swapped(d_beside, d_across)
    grad_region = sum(
        region_weight(d_rows[k], bevs[k], columns, anc_count) for k in range(blocks)
    )
    d_rows, grad_region, beside, across = lax.optimization_barrier(
        (d_rows, grad_region, beside, across)
    )
    d_mids, mid_sums = [], 0.0
    mid_beside, mid_across = [], []
    for k in range(blocks):
        d_block, near_row, far_row, sums = region_data(
            edges[k], d_rows[k], beside[k], across[k], bevs[k], region_back, columns
        )
        d_mids.append(d_block)
        mid_beside.append(near_row)
        mid_across.append(far_row)
        mid_sums = mid_sums + sums
    beside, across = swapped(mid_beside, mid_across)
    grad_mid = sum(middle_weight(grids[k], d_mids[k], columns) for k in range(blocks))
    grad_mid, beside, across = lax.optimization_barrier((grad_mid, beside, across))

    head_three = head_sums.reshape(3, outs, c_rpn)
    grad_head = (head_three[0] + head_three[1] + head_three[2]).T
    head_rows = grad_head.reshape(-1, LANES)
    segments = (
        ("region", grad_region.size),
        ("one", w_vfe1.size),
        ("two", w_vfe2.size),
        ("middle", grad_mid.size),
        ("head", w_head.size),
        ("norm", c_vfe + c_vfe + c_vox),
        ("rest", c_mid + c_rpn + outs),
    )
    shard = master.shape[0]
    plan = shard_windows(segments, shard, anc_count)
    chunk_rows = -(-(shard // LANES + 2) // (8 * tile_count)) * 8
    packed = pack(
        plan, tile_count, chunk_rows, grad_region, grad_mid, head_rows, mid_sums, row_sums
    )
    own_at, packed = lax.optimization_barrier((own_at, packed))
    chunk, chunk_square = sum_chunk(lax.all_to_all(packed, both, 0, 0), tile_count)

    def collect(number, own_index):
        lists = [
            middle_data(
                own_index[k], edges[k], d_mids[k], beside[k], across[k], middle_kernel_all, columns
            )
            for k in range(blocks)
        ]
        lists = [sum(parts) for parts in zip(*lists)]
        back = lists[:1]
        for k in range(1, anc_count):
            onward = [(i, (i + k) % anc_count) for i in range(anc_count)]
            back.append(lax.ppermute(lists[k], "anc", onward))
        mine = place[7] - number * CAP
        known = (mine >= 0) & (mine < CAP)
        index = (anc - place[6] + anc_count) % anc_count * CAP + mine
        return spread_lists(jnp.where(known, index, anc_count * CAP), back)

    d_feat = collect(0, own_at)
    d_feat, chunk = lax.optimization_barrier((d_feat, chunk))
    early = lax.all_to_all(chunk, "tile", 0, 0)

    def collect_more(state):
        number, held = state
        _, index = cells(exchange(number)[0])
        return number + 1, held + collect(number, index)

    d_feat = lax.cond(
        rounds > 1,
        lambda held: lax.while_loop(more, collect_more, (jnp.int32(1), held))[1],
        lambda held: held,
        d_feat,
    )
    layers = -(-88 // devices)
    late = decode(
        flat_points,
        counts,
        stats,
        kernel,
        gain_rows,
        first,
        second,
        feat,
        share,
        found,
        d_feat,
        row_sums[24:32],
        (devices, layers),
        slots,
    )
    late, early = lax.optimization_barrier((late, early))
    late = jnp.sum(lax.all_to_all(late, both, 0, 0), axis=0)
    late = everyone(jnp.concatenate([late, chunk_square], axis=0), both)
    reduced, scalars = finish(plan, anc.reshape(1), early, late, stats, kernel, gain_rows)
    loss = scalars[0, 0]
    norm_value = scalars[1, 0]
    reduced = reduced.reshape(-1)[:shard]
    clipped = reduced * scalars[2, 0]
    first_new = BETA_FIRST * moment1 + (1.0 - BETA_FIRST) * clipped
    second_new = BETA_SECOND * moment2 + (1.0 - BETA_SECOND) * clipped * clipped
    first_hat = first_new / (1.0 - BETA_FIRST**STEP_NUMBER)
    second_hat = second_new / (1.0 - BETA_SECOND**STEP_NUMBER)
    updated = master - LEARN_RATE * (
        first_hat / (jnp.sqrt(second_hat) + ADAM_EPSILON) + WEIGHT_DECAY * master
    )
    return (updated, first_new, second_new, loss, norm_value)


def solution(mesh):
    placed = (
        P(None, None, ("tile", "anc")),
        P(("tile", "anc")),
        P(("tile", "anc"), None),
        P(None, ("tile", "anc"), None),
        P(None, None, ("tile", "anc"), None),
        P(),
        P(),
        P(),
        P(None, None, "anc", None),
        P(),
        P(),
        P(),
        P("anc"),
        P("anc"),
        P("anc"),
    )
    return jax.shard_map(
        on_device,
        mesh=mesh,
        in_specs=placed,
        out_specs=(P("anc"), P("anc"), P("anc"), P(), P()),
        check_vma=False,
    )
```

```python
import functools
import jax
import jax.numpy as jnp
from jax import lax
from jax.experimental import pallas as pl
from jax.experimental.pallas import tpu as pltpu
from jax.sharding import PartitionSpec as P

DEPTH = 10
PAIRS = DEPTH // 4 + 1
CROP_ROWS = 192
BLOCK_ROWS = 12
HALO = 2
LANES = 128
CHUNK = 384
LINE = 1024
CAP = 768
EDGE_CAP = 128
EMPTY = -1e30
FOCAL_ALPHA = 0.25
BN_EPSILON = 0.001
CLIP_LIMIT = 0.05
LEARN_RATE = 0.03
BETA_FIRST = 0.9
BETA_SECOND = 0.999
WEIGHT_DECAY = 0.01
ADAM_EPSILON = 1e-08
STEP_NUMBER = 10
F32 = jnp.float32
BF16 = jnp.bfloat16


def vmem(count):
    return [pl.BlockSpec(memory_space=pltpu.VMEM)] * count


def smem(count):
    return [pl.BlockSpec(memory_space=pltpu.SMEM)] * count


def params(*semantics, limit=60):
    return pltpu.CompilerParams(
        vmem_limit_bytes=limit * 1024 * 1024, dimension_semantics=semantics or None
    )


def work(micros):
    return pl.CostEstimate(flops=micros, transcendentals=0, bytes_accessed=micros * 3_000_000)


def at_row(index, columns):
    if isinstance(index, int):
        return pl.ds(index * columns, columns)
    return pl.ds(pl.multiple_of(index * columns, 32), columns)


def column_edges(columns, lanes):
    place = lax.broadcasted_iota(jnp.int32, (columns, lanes), 0)
    return place == 0, place == columns - 1


def from_left(values):
    columns, lanes = values.shape
    first, _ = column_edges(columns, lanes)
    return jnp.where(first, 0.0, pltpu.roll(values, 1, 0))


def from_right(values):
    columns, lanes = values.shape
    _, last = column_edges(columns, lanes)
    return jnp.where(last, 0.0, pltpu.roll(values, columns - 1, 0))


def low_lanes(columns):
    return lax.broadcasted_iota(jnp.int32, (columns, LANES), 1) < LANES // 2


def clear(wide, cells):
    step = 512

    def begin(i, carry):
        wide[pl.ds(pl.multiple_of(i * step, step), step), :] = jnp.zeros((step, LANES), F32)
        return carry

    lax.fori_loop(0, cells // step, begin, 0)


def narrow(wide, out_ref):
    step = 512

    def finish(i, carry):
        block = pl.ds(pl.multiple_of(i * step, step), step)
        out_ref[block, :] = wide[block, :].astype(BF16)
        return carry

    lax.fori_loop(0, out_ref.shape[0] // step, finish, 0)


def place_rows(count, cells, index_ref, feat_ref, old_ref, out_ref, wide, rows):
    if old_ref is None:
        clear(wide, cells)
    else:
        wide[0:cells, :] = old_ref[...].astype(F32)
    rows[...] = feat_ref[...].astype(F32)

    def place(i, carry):
        for j in range(8):
            wide[pl.ds(index_ref[i * 8 + j], 1), :] = rows[pl.ds(i * 8 + j, 1), :]
        return carry

    lax.fori_loop(0, count // 8, place, 0)
    narrow(wide, out_ref)


def scatter_kernel(count, cells, fresh, *refs):
    if fresh:
        index_ref, feat_ref, out_ref, wide, rows = refs
        place_rows(count, cells, index_ref, feat_ref, None, out_ref, wide, rows)
    else:
        place_rows(count, cells, *refs)


def scatter_rows(index, feats, old, columns):
    cells = DEPTH * (BLOCK_ROWS + 2 * HALO) * columns
    count = index.shape[0]
    fresh = old is None
    return pl.pallas_call(
        functools.partial(scatter_kernel, count, cells, fresh),
        out_shape=jax.ShapeDtypeStruct((cells, LANES), BF16),
        in_specs=smem(1) + vmem(1 if fresh else 2),
        out_specs=vmem(1)[0],
        scratch_shapes=[pltpu.VMEM((cells + 8, LANES), F32), pltpu.VMEM((count, LANES), F32)],
        compiler_params=params(),
        cost_estimate=work(15),
        name="grid_scatter",
    )(*((index, feats) if fresh else (index, feats, old)))


TOP, BOTTOM, EVEN, FIRST_ROW, EDGE_SHIFT, PLACE = range(6)


def list_cells(columns, edge_ref, feat_ref, spots, owns):
    sources = feat_ref.shape[0] // (CAP + EDGE_CAP + 48)
    main = CAP // LANES
    tall = BLOCK_ROWS + 2 * HALO
    for a in range(sources):
        base = a * (CAP + EDGE_CAP + 48)
        words = feat_ref[base + CAP : base + CAP + 32, :].astype(F32).astype(jnp.int32)
        start = base + CAP + 32 + EDGE_CAP
        edges = feat_ref[start : start + 16, :].astype(F32).astype(jnp.int32)
        for side, (high, half, mixed) in enumerate(
            (
                (words[0:main], words[main : 2 * main], words[2 * main : 3 * main]),
                (edges[0:1], edges[1:2], edges[2:3]),
            )
        ):
            line = (mixed >> 1) - edge_ref[FIRST_ROW]
            if side:
                line = line + edge_ref[EDGE_SHIFT]
            cross = half * 2 + (mixed & 1)
            inside = (high > 0) & (line >= -HALO) & (line < BLOCK_ROWS + HALO)
            spot = ((high - 1) * tall + line + HALO) * columns + cross
            spot = jnp.where(inside, spot, DEPTH * tall * columns)
            if side:
                spots[a * (main + 1) + main : (a + 1) * (main + 1), :] = spot
                continue
            spots[a * (main + 1) : a * (main + 1) + main, :] = spot
            inside = (high > 0) & (line >= 0) & (line < BLOCK_ROWS)
            spot = ((high - 1) * BLOCK_ROWS + line) * columns + cross
            owns[a * main : (a + 1) * main, :] = jnp.where(
                inside, spot, DEPTH * BLOCK_ROWS * columns
            )


def scatter_middle_kernel(
    columns, edge_ref, feat_ref, kernel_ref, bias_ref, grid_ref, out_ref, own_ref,
    wide, rows, held, weight_ref, spots, index, copied, done,
):
    list_cells(columns, edge_ref, feat_ref, spots, own_ref)
    to_scalar = pltpu.make_async_copy(spots, index, copied)
    to_scalar.start()
    clear(wide, held.shape[0])
    rows[...] = feat_ref[...].astype(F32)
    to_scalar.wait()
    blocks = CAP // LANES + 1
    length = CAP + EDGE_CAP + 48

    def place(part, carry):
        block = part % blocks
        base = part // blocks * length + block * LANES + jnp.where(block == blocks - 1, 32, 0)

        base = pl.multiple_of(base, 8)
        for j in range(LANES):
            wide[pl.ds(index[part, j], 1), :] = rows[pl.ds(base + j, 1), :]
        return carry

    lax.fori_loop(0, index.shape[0], place, 0)
    narrow(wide, held)
    copy = pltpu.make_async_copy(held, grid_ref, done)
    copy.start()
    middle_kernel(columns, edge_ref, held, kernel_ref, bias_ref, out_ref, weight_ref)
    copy.wait()


def scatter_middle(edges, feats, w_mid, bias, columns):
    cells = DEPTH * (BLOCK_ROWS + 2 * HALO) * columns
    count = feats.shape[0]
    sources = count // (CAP + EDGE_CAP + 48)
    parts = sources * (CAP // LANES + 1)
    return pl.pallas_call(
        functools.partial(scatter_middle_kernel, columns),
        out_shape=(
            jax.ShapeDtypeStruct((cells, LANES), BF16),
            jax.ShapeDtypeStruct(((BLOCK_ROWS + 2) * columns, PAIRS * LANES), BF16),
            jax.ShapeDtypeStruct((sources * CAP // LANES, LANES), jnp.int32),
        ),
        in_specs=smem(1) + vmem(3),
        out_specs=[pl.BlockSpec(memory_space=pl.ANY)] + vmem(2),
        scratch_shapes=[
            pltpu.VMEM((cells + 8, LANES), F32),
            pltpu.VMEM((count, LANES), F32),
            pltpu.VMEM((cells, LANES), BF16),
            pltpu.VMEM((2, 9 * LANES, 2 * LANES), BF16),
            pltpu.VMEM((parts, LANES), jnp.int32),
            pltpu.SMEM((parts, LANES), jnp.int32),
            pltpu.SemaphoreType.DMA,
            pltpu.SemaphoreType.DMA,
        ],
        compiler_params=params(limit=57),
        cost_estimate=work(36),
        name="scatter_middle",
    )(edges, feats, w_mid, bias)


def middle_kernel(columns, edge_ref, grid_ref, kernel_ref, bias_ref, out_ref, weight_ref):
    low = low_lanes(columns)
    none = jnp.zeros((LANES, LANES // 2), BF16)
    for place in range(9):
        one, two, three = (
            kernel_ref[place * 3 + e].astype(F32).T.astype(BF16) for e in range(3)
        )
        rows = slice(place * LANES, (place + 1) * LANES)
        weight_ref[0, rows, :] = jnp.concatenate([one, two, three, none], axis=1)
        weight_ref[1, rows, :] = jnp.concatenate([two, one, none, three], axis=1)
    grid_rows = BLOCK_ROWS + 2 * HALO
    depth_out = DEPTH // 2

    def row(m, carry):
        sums = []
        for o in range(depth_out):
            taps = (1, 2) if o == 0 else (0, 1, 2)
            left = jnp.concatenate(
                [
                    grid_ref[at_row((2 * o + a - 1) * grid_rows + m + b, columns), :]
                    for a in taps
                    for b in range(3)
                ],
                axis=1,
            )
            right = weight_ref[o % 2, 3 * LANES * (3 - len(taps)) :, :]
            sums.append(jnp.dot(left, right, preferred_element_type=F32))
        inside = (m > 0) & (m < BLOCK_ROWS + 1) | (m == 0) & (edge_ref[0] > 0)
        inside = inside | (m == BLOCK_ROWS + 1) & (edge_ref[1] > 0)
        keep = jnp.where(inside, 1.0, 0.0)
        for j in range(PAIRS):
            even = sums[2 * j]
            if 2 * j + 1 < depth_out:
                odd = sums[2 * j + 1]
                first = jnp.where(low, even[:, :LANES], odd[:, :LANES])
                middle = jnp.where(low, odd[:, :LANES], even[:, :LANES])
                last = even[:, LANES:] + odd[:, LANES:]
            else:
                first = even[:, :LANES]
                middle = first
                last = even[:, LANES:]
            total = from_left(first) + pltpu.roll(middle, LANES // 2, 1) + from_right(last)
            total = jnp.maximum(total + bias_ref[0:1, :], 0.0) * keep
            if 2 * j + 1 == depth_out:
                total = jnp.where(low, total, 0.0)
            out_ref[at_row(m, columns), j * LANES : (j + 1) * LANES] = total.astype(BF16)
        return carry

    lax.fori_loop(0, BLOCK_ROWS + 2, row, 0, unroll=2)


def middle_forward(edges, grid, w_mid, bias, columns):
    return pl.pallas_call(
        functools.partial(middle_kernel, columns),
        out_shape=jax.ShapeDtypeStruct(((BLOCK_ROWS + 2) * columns, PAIRS * LANES), BF16),
        in_specs=smem(1) + vmem(3),
        out_specs=vmem(1)[0],
        scratch_shapes=[pltpu.VMEM((2, 9 * LANES, 2 * LANES), BF16)],
        compiler_params=params(),
        cost_estimate=work(26),
        name="middle_forward",
    )(edges, grid, w_mid, bias)


def row_above(edge_ref, beside_ref, across_ref, lanes):
    found = jnp.where(
        edge_ref[EVEN] > 0, across_ref[:, lanes].astype(F32), beside_ref[:, lanes].astype(F32)
    )
    return jnp.where(edge_ref[TOP] > 0, found, 0.0)


def row_below(edge_ref, beside_ref, across_ref, lanes):
    found = jnp.where(
        edge_ref[EVEN] > 0, beside_ref[:, lanes].astype(F32), across_ref[:, lanes].astype(F32)
    )
    return jnp.where(edge_ref[BOTTOM] > 0, found, 0.0)


def put_edges(edge_ref, beside_ref, across_ref, first, last):
    if first is not None:

        @pl.when(edge_ref[EVEN] > 0)
        def _():
            across_ref[...] = first

        @pl.when(edge_ref[EVEN] == 0)
        def _():
            beside_ref[...] = first

    if last is not None:

        @pl.when(edge_ref[EVEN] > 0)
        def _():
            beside_ref[...] = last

        @pl.when(edge_ref[EVEN] == 0)
        def _():
            across_ref[...] = last


def column_taps(own, j):
    low = low_lanes(own.shape[0])
    other = pltpu.roll(own, LANES // 2, 1)
    both = [jnp.where(low, own, other)]
    if 2 * j + 1 < DEPTH // 2:
        both.append(jnp.where(low, other, own))
    return [(jnp.where(low, from_right(x), x), from_left(x)) for x in both]


def middle_data_kernel(
    count, columns, sources, index_ref, edge_ref, d_ref, beside_ref, across_ref, kernel_ref, *refs
):
    out_refs, (near, far, wide, rows, weight_ref) = refs[:sources], refs[sources:]
    padded = BLOCK_ROWS + 2
    half = LANES // 2
    cells = DEPTH * BLOCK_ROWS * columns
    span = 10 * half
    for a, first, side in ((1, 0, 0), (2, 0, 1), (0, span, 1)):
        lanes = slice(side * LANES, (side + 1) * LANES)
        for b in range(3):
            for e in range(3):
                block = (2 - b) * 2 + e if e < 2 else 6 + 2 - b
                own = kernel_ref[(a * 3 + b) * 3 + e]
                weight_ref[first + block * half : first + (block + 1) * half, lanes] = own
        weight_ref[first + span - half : first + span, lanes] = jnp.zeros((half, LANES), BF16)
    weight_ref[span:, :LANES] = jnp.zeros((span, LANES), BF16)

    def build(r, load):
        for j in range(PAIRS):
            own = load(slice(j * LANES, (j + 1) * LANES))
            for k, (pair, left) in enumerate(column_taps(own, j)):
                o = 2 * j + k
                near[o, at_row(r, columns), :] = pair.astype(BF16)
                far[o, at_row(r, columns), 0:half] = left[:, 0:half].astype(BF16)
                if not (isinstance(r, int) and r == 0):
                    far[o, at_row(r - 1, columns), half:LANES] = left[:, half:].astype(BF16)

    def build_own(r):
        build(r + 1, lambda lanes: d_ref[at_row(r, columns), lanes].astype(F32))

    build(0, lambda lanes: row_above(edge_ref, beside_ref, across_ref, lanes))
    for r in range(3):
        build_own(r)
    for o in range(DEPTH // 2):
        far[o, (padded - 1) * columns :, half:LANES] = jnp.zeros((columns, half), BF16)

    def row(r):
        def pieces(o):
            return [near[o, at_row(r + i, columns), :] for i in range(3)] + [
                far[o, at_row(r + i, columns), :] for i in (0, 2)
            ]

        for o in range(DEPTH // 2):
            left = jnp.concatenate(pieces(o) + (pieces(o + 1) if o < DEPTH // 2 - 1 else []), axis=1)
            total = jnp.dot(left, weight_ref[0 : left.shape[1], :], preferred_element_type=F32)
            wide[at_row(2 * o * BLOCK_ROWS + r, columns), :] = total[:, :LANES]
            wide[at_row((2 * o + 1) * BLOCK_ROWS + r, columns), :] = total[:, LANES:]

    def row_and_build(r, carry):
        row(r)
        build_own(r + 3)
        return carry

    lax.fori_loop(0, BLOCK_ROWS - 3, row_and_build, 0)
    row(BLOCK_ROWS - 3)
    build(BLOCK_ROWS + 1, lambda lanes: row_below(edge_ref, beside_ref, across_ref, lanes))
    row(BLOCK_ROWS - 2)
    row(BLOCK_ROWS - 1)
    wide[cells:, :] = jnp.zeros((8, LANES), F32)

    length = count // sources
    lines = length // LANES

    def pick(part, carry):
        source = lax.rem(edge_ref[PLACE] + part // lines, sources) * lines + part % lines
        base = pl.multiple_of(part * LANES, LANES)
        for j in range(LANES):
            rows[pl.ds(base + j, 1), :] = wide[pl.ds(index_ref[source, j], 1), :]
        return carry

    lax.fori_loop(0, count // LANES, pick, 0)
    for k, out_ref in enumerate(out_refs):
        out_ref[...] = rows[k * length : (k + 1) * length, :].astype(BF16)


def middle_data(index, edges, d_rows, beside, across, w_mid, columns):
    count = index.size
    sources = count // CAP
    padded = (BLOCK_ROWS + 2) * columns
    return pl.pallas_call(
        functools.partial(middle_data_kernel, count, columns, sources),
        out_shape=[jax.ShapeDtypeStruct((CAP, LANES), BF16)] * sources,
        in_specs=smem(2) + vmem(4),
        out_specs=vmem(sources),
        scratch_shapes=[
            pltpu.VMEM((DEPTH // 2, padded, LANES), BF16),
            pltpu.VMEM((DEPTH // 2, padded, LANES), BF16),
            pltpu.VMEM((DEPTH * BLOCK_ROWS * columns + 8, LANES), F32),
            pltpu.VMEM((count, LANES), F32),
            pltpu.VMEM((10 * LANES, 2 * LANES), BF16),
        ],
        compiler_params=params(limit=50),
        cost_estimate=work(30),
        name="middle_data",
    )(index, edges, d_rows, beside, across, w_mid)


def middle_weight_kernel(
    columns, grid_hbm, d_ref, out_ref, total, taps_ref, turned, grid_ref, arrived
):
    grid_rows = BLOCK_ROWS + 2 * HALO
    half = LANES // 2

    def copy(i):
        ahead = 2 if isinstance(i, int) and i == 0 else 0
        parts = []
        for d in range(DEPTH):
            begin = (d * grid_rows + 2 * i + 3 - ahead) * columns
            rows = pl.ds(begin if isinstance(i, int) else pl.multiple_of(begin, 32), (2 + ahead) * columns)
            parts.append(
                pltpu.make_async_copy(grid_hbm.at[rows, :], grid_ref.at[rows, :], arrived.at[i, d])
            )
        return parts

    for i in range(BLOCK_ROWS // 2):
        for part in copy(i):
            part.start()
    total[...] = jnp.zeros_like(total)
    for part in copy(0):
        part.wait()

    def rows(i, carry):
        @pl.when(i > 0)
        def _():
            for part in copy(i):
                part.wait()

        for k in range(2):
            for j in range(PAIRS):
                own = d_ref[at_row(i * 2 + k, columns), j * LANES : (j + 1) * LANES].astype(F32)
                for n, (pair, left) in enumerate(column_taps(own, j)):
                    place = slice(k * columns, (k + 1) * columns)
                    taps_ref[2 * j + n, place, 0:LANES] = pair.astype(BF16)
                    taps_ref[2 * j + n, place, LANES:] = left.astype(BF16)
        for o in range(DEPTH // 2):
            depth_taps = (1, 2) if o == 0 else (0, 1, 2)
            cells = jnp.concatenate(
                [
                    grid_ref[
                        pl.ds(
                            pl.multiple_of(
                                ((2 * o + a - 1) * grid_rows + i * 2 + 1 + b) * columns, 32
                            ),
                            2 * columns,
                        ),
                        :,
                    ]
                    for a in depth_taps
                    for b in range(3)
                ],
                axis=1,
            )
            part = lax.dot_general(
                taps_ref[o], cells, (((0,), (0,)), ((), ())), preferred_element_type=F32
            )
            if o == 0:
                total[:, 3 * LANES :] += part
            else:
                total[...] += part
        return carry

    lax.fori_loop(0, BLOCK_ROWS // 2, rows, 0, unroll=2)
    low = low_lanes(LANES // 2)
    for place in range(9):
        for side in range(2):
            turned[...] = total[
                side * LANES : (side + 1) * LANES, place * LANES : (place + 1) * LANES
            ].T
            even = turned[pl.ds(0, half, stride=2), :]
            odd = turned[pl.ds(1, half, stride=2), :]
            at = (place * 3 + side * 2) * half
            out_ref[at : at + half, :] = jnp.where(low, even, pltpu.roll(odd, half, 1))
            if side == 0:
                out_ref[at + half : at + 2 * half, :] = jnp.where(
                    low, pltpu.roll(even, half, 1), odd
                )


def middle_weight(grid, d_rows, columns):
    return pl.pallas_call(
        functools.partial(middle_weight_kernel, columns),
        out_shape=jax.ShapeDtypeStruct((27 * LANES // 2, LANES), F32),
        in_specs=[pl.BlockSpec(memory_space=pl.ANY)] + vmem(1),
        out_specs=vmem(1)[0],
        scratch_shapes=[
            pltpu.VMEM((2 * LANES, 9 * LANES), F32),
            pltpu.VMEM((DEPTH // 2, 2 * columns, 2 * LANES), BF16),
            pltpu.VMEM((LANES, LANES), F32),
            pltpu.VMEM(grid.shape, BF16),
            pltpu.SemaphoreType.DMA((BLOCK_ROWS // 2, DEPTH)),
        ],
        compiler_params=params(limit=32),
        cost_estimate=work(26),
        name="middle_weight",
    )(grid, d_rows)


def region_kernel(
    columns,
    scale_ref,
    edge_ref,
    bev_ref,
    weight_ref,
    bias_ref,
    head_ref,
    labels_ref,
    targets_ref,
    d_ref,
    beside_ref,
    across_ref,
    grad_head_ref,
    sums_ref,
    held,
):
    outs = head_ref.shape[0]
    cells = d_ref.shape[0]
    span = cells // 3
    scale = scale_ref[0, 0]
    head = head_ref[...]
    head_three = jnp.concatenate([head, head, head], axis=0)
    own = lax.broadcasted_iota(jnp.int32, (outs, LANES), 0)
    own = own == lax.broadcasted_iota(jnp.int32, (outs, LANES), 1)
    head_bias = jnp.sum(jnp.where(own, bias_ref[2:3, :], 0.0), axis=1, keepdims=True)

    def row(r, carry):
        left = jnp.concatenate([bev_ref[at_row(r + b, columns), :] for b in range(3)], axis=1)
        part = jnp.dot(left, weight_ref[...], preferred_element_type=F32)
        pre = from_left(part[:, :LANES]) + part[:, LANES : 2 * LANES]
        held[at_row(r, columns), :] = pre + from_right(part[:, 2 * LANES :]) + bias_ref[1:2, :]
        return carry

    lax.fori_loop(0, cells // columns, row, 0, unroll=2)
    kind = lax.broadcasted_iota(jnp.int32, (outs, span), 0) % 8 == 0
    grad_head = jnp.zeros((3 * outs, LANES), F32)
    head_sum = jnp.zeros((outs, 1), F32)
    loss_sum = jnp.zeros((outs, 1), F32)
    row_sum = jnp.zeros((8, LANES), F32)
    for i in range(3):
        place = slice(i * span, (i + 1) * span)
        pre = held[place, :]
        act = jnp.maximum(pre, 0.0).astype(BF16)
        heads = lax.dot_general(head, act, (((1,), (1,)), ((), ())), preferred_element_type=F32)
        heads = heads + head_bias
        label = labels_ref[:, place]
        positive = jnp.where(label == 1, 1.0, 0.0)
        negative = jnp.where(label == 0, 1.0, 0.0)
        tail = jnp.log1p(jnp.exp(-jnp.abs(heads)))
        soft_up = jnp.maximum(heads, 0.0) + tail
        soft_down = jnp.maximum(-heads, 0.0) + tail
        probab = jax.nn.sigmoid(heads)
        rest = 1.0 - probab
        focal = positive * FOCAL_ALPHA * rest * rest * soft_down
        focal = focal + negative * (1.0 - FOCAL_ALPHA) * probab * probab * soft_up
        d_focal = positive * FOCAL_ALPHA * rest * rest * (-2.0 * probab * soft_down - rest)
        d_focal = d_focal + negative * (1.0 - FOCAL_ALPHA) * probab * probab * (
            2.0 * rest * soft_up + probab
        )
        offset = heads - targets_ref[:, place]
        size = jnp.abs(offset)
        near = size < 1.0 / 9.0
        smooth = jnp.where(near, 4.5 * offset * offset, size - 1.0 / 18.0)
        d_smooth = jnp.where(near, 9.0 * offset, jnp.where(offset > 0.0, 1.0, -1.0))
        losses = jnp.where(kind, focal, 2.0 * positive * smooth)
        loss_sum = loss_sum + jnp.sum(losses, axis=1, keepdims=True)
        d_heads = jnp.where(kind, d_focal, 2.0 * positive * d_smooth) * scale
        head_sum = head_sum + jnp.sum(d_heads, axis=1, keepdims=True)
        high = d_heads.astype(BF16)
        rest_one = d_heads - high.astype(F32)
        mid = rest_one.astype(BF16)
        tiny = (rest_one - mid.astype(F32)).astype(BF16)
        three = jnp.concatenate([high, mid, tiny], axis=0)
        grad_head = grad_head + jnp.dot(three, act, preferred_element_type=F32)
        d_act = lax.dot_general(
            three, head_three, (((0,), (0,)), ((), ())), preferred_element_type=F32
        )
        d_pre = jnp.where(pre > 0.0, d_act, 0.0).astype(BF16)
        d_ref[place, :] = d_pre
        row_sum = row_sum + jnp.sum(d_pre.astype(F32).reshape(span // 8, 8, LANES), axis=0)
        if i == 0:
            put_edges(edge_ref, beside_ref, across_ref, d_pre[:columns, :], None)
        if i == 2:
            put_edges(edge_ref, beside_ref, across_ref, None, d_pre[span - columns :, :])
    grad_head_ref[...] = grad_head
    sums_ref[0:8, :] = row_sum
    sums_ref[8:24, :] = jnp.broadcast_to(head_sum, (outs, LANES))
    sums_ref[24:32, :] = jnp.broadcast_to(jnp.sum(loss_sum, axis=0, keepdims=True), (8, LANES))


def region_forward(scale, edges, bev, weights, bias, head, labels, targets, columns):
    cells = labels.shape[1]
    outs = head.shape[0]
    return pl.pallas_call(
        functools.partial(region_kernel, columns),
        out_shape=(
            jax.ShapeDtypeStruct((cells, LANES), BF16),
            jax.ShapeDtypeStruct((columns, LANES), BF16),
            jax.ShapeDtypeStruct((columns, LANES), BF16),
            jax.ShapeDtypeStruct((3 * outs, LANES), F32),
            jax.ShapeDtypeStruct((32, LANES), F32),
        ),
        in_specs=smem(2) + vmem(6),
        out_specs=vmem(5),
        scratch_shapes=[pltpu.VMEM((cells, LANES), F32)],
        compiler_params=params(limit=28),
        cost_estimate=work(16),
        name="region_forward",
    )(
        scale.reshape(1, 1),
        edges,
        bev,
        weights,
        bias,
        head,
        labels,
        targets,
    )


def region_order_kernel(blocks, anc_ref, *refs):
    part_refs, (in_ref, back_ref, wide, lined) = refs[:blocks], refs[blocks:]
    depth_out = DEPTH // 2
    half = LANES // 2
    width = PAIRS * LANES
    share = half // blocks
    used = depth_out * half
    for b in range(3):
        for e in range(3):
            for k, part_ref in enumerate(part_refs):
                first = lax.rem(anc_ref[0] + k, blocks) * share
                wide[...] = part_ref[b, e].astype(F32)
                for h in range(depth_out):
                    at = pl.multiple_of(h * half + first, 8)
                    lined[pl.ds(at, share), :] = wide[pl.ds(h, share, stride=depth_out), :]
            lined[used:, :] = jnp.zeros((width - used, LANES), F32)
            in_ref[b * width : (b + 1) * width, e * LANES : (e + 1) * LANES] = lined[...].astype(
                BF16
            )
            at = (b * 3 + e) * LANES
            back_ref[at : at + LANES, :] = lined[...].T.astype(BF16)


def region_order(anc, parts):
    width = PAIRS * LANES
    return pl.pallas_call(
        functools.partial(region_order_kernel, len(parts)),
        out_shape=(
            jax.ShapeDtypeStruct((3 * width, 3 * LANES), BF16),
            jax.ShapeDtypeStruct((9 * LANES, width), BF16),
        ),
        in_specs=smem(1) + vmem(len(parts)),
        out_specs=vmem(2),
        scratch_shapes=[
            pltpu.VMEM((parts[0].shape[2], LANES), F32),
            pltpu.VMEM((width, LANES), F32),
        ],
        compiler_params=params(limit=24),
        cost_estimate=work(4),
        name="region_order",
    )(anc, *parts)


def region_data_kernel(
    columns, edge_ref, d_ref, beside_in, across_in, bev_ref, weight_ref,
    out_ref, beside_ref, across_ref, sums_ref, taps_ref,
):
    rows = out_ref.shape[0] // columns
    width = PAIRS * LANES
    sums_ref[...] = jnp.zeros_like(sums_ref)

    def build(r, own):
        taps_ref[at_row(r, columns), 0:LANES] = from_right(own).astype(BF16)
        taps_ref[at_row(r, columns), LANES : 2 * LANES] = own.astype(BF16)
        taps_ref[at_row(r, columns), 2 * LANES :] = from_left(own).astype(BF16)

    def build_own(r):
        build(r + 1, d_ref[at_row(r, columns), :].astype(F32))

    build(0, row_above(edge_ref, beside_in, across_in, slice(None)))
    build_own(0)
    build_own(1)

    def row(r):
        left = jnp.concatenate([taps_ref[at_row(r + 2 - b, columns), :] for b in range(3)], axis=1)
        total = jnp.dot(left, weight_ref[...], preferred_element_type=F32)
        alive = bev_ref[at_row(r + 1, columns), :].astype(F32) > 0.0
        kept = jnp.where(alive, total, 0.0).astype(BF16)
        out_ref[at_row(r, columns), :] = kept

        sums_ref[...] += jnp.sum(kept.astype(F32).reshape(columns // 8, 8, width), axis=0)
        return kept

    def row_and_build(r, carry):
        row(r)
        build_own(r + 2)
        return carry

    put_edges(edge_ref, beside_ref, across_ref, row(0), None)
    build_own(2)
    lax.fori_loop(1, rows - 2, row_and_build, 0)
    row(rows - 2)
    build(rows + 1, row_below(edge_ref, beside_in, across_in, slice(None)))
    put_edges(edge_ref, beside_ref, across_ref, None, row(rows - 1))


def region_data(edges, d_rows, beside, across, bev, weights, columns):
    width = PAIRS * LANES
    return pl.pallas_call(
        functools.partial(region_data_kernel, columns),
        out_shape=(
            jax.ShapeDtypeStruct((d_rows.shape[0], width), BF16),
            jax.ShapeDtypeStruct((columns, width), BF16),
            jax.ShapeDtypeStruct((columns, width), BF16),
            jax.ShapeDtypeStruct((8, width), F32),
        ),
        in_specs=smem(1) + vmem(5),
        out_specs=vmem(4),
        scratch_shapes=[pltpu.VMEM((d_rows.shape[0] + 2 * columns, 3 * LANES), BF16)],
        compiler_params=params(limit=28),
        cost_estimate=work(13),
        name="region_data",
    )(edges, d_rows, beside, across, bev, weights)


def region_weight_kernel(columns, blocks, d_ref, bev_ref, out_ref, total, taps_ref):
    rows = d_ref.shape[0] // columns
    width = PAIRS * LANES
    depth_out = DEPTH // 2
    half = LANES // 2
    total[...] = jnp.zeros_like(total)

    def two(i, carry):
        for k in range(2):
            own = d_ref[at_row(i * 2 + k, columns), :].astype(F32)
            place = slice(k * columns, (k + 1) * columns)
            taps_ref[place, 0:LANES] = from_right(own).astype(BF16)
            taps_ref[place, LANES : 2 * LANES] = own.astype(BF16)
            taps_ref[place, 2 * LANES :] = from_left(own).astype(BF16)
        cells = jnp.concatenate(
            [
                bev_ref[pl.ds(pl.multiple_of((i * 2 + b) * columns, 32), 2 * columns), :]
                for b in range(3)
            ],
            axis=1,
        )
        total[...] += lax.dot_general(
            taps_ref[...], cells, (((0,), (0,)), ((), ())), preferred_element_type=F32
        )
        return carry

    lax.fori_loop(0, rows // 2, two, 0, unroll=2)
    share = half // blocks
    for b in range(3):
        for e in range(3):
            for j in range(PAIRS):
                start = b * width + j * LANES
                turned = total[e * LANES : (e + 1) * LANES, start : start + LANES].T
                for k in range(min(2, depth_out - 2 * j)):
                    for q in range(blocks):
                        begin = k * half + q * share
                        base = ((q * 3 + b) * 3 + e) * share * depth_out
                        out_ref[pl.ds(base + 2 * j + k, share, stride=depth_out), :] = turned[
                            begin : begin + share, :
                        ]


def region_weight(d_own, bev, columns, blocks):
    width = PAIRS * LANES
    return pl.pallas_call(
        functools.partial(region_weight_kernel, columns, blocks),
        out_shape=jax.ShapeDtypeStruct((9 * (DEPTH // 2) * (LANES // 2), LANES), F32),
        in_specs=vmem(2),
        out_specs=vmem(1)[0],
        scratch_shapes=[
            pltpu.VMEM((3 * LANES, 3 * width), F32),
            pltpu.VMEM((2 * columns, 3 * LANES), BF16),
        ],
        compiler_params=params(limit=28),
        cost_estimate=work(10),
        name="region_weight",
    )(d_own, bev)


def prepare_kernel(
    slots, anc_count, device_rows, edge_ref, points_ref, line_ref, labels_ref,
    stats_ref, place_ref, digit_ref,
):
    voxels, width = points_ref.shape
    features = 7
    row = line_ref[1:2, :]
    exists = line_ref[3:4, :]
    column = line_ref[2:3, :]
    digits = jnp.concatenate(
        [
            (line_ref[0:1, :] + 1) * exists,
            (column >> 1) * exists,
            (row * 2 + (column & 1)) * exists,
            line_ref[4:5, :],
        ],
        axis=0,
    ).astype(F32)
    none = jnp.zeros((LANES - 4, LANES), F32)
    for i in range(voxels // LANES):
        here = slice(i * LANES, (i + 1) * LANES)
        digit_ref[here, :] = jnp.concatenate([digits[:, here], none], axis=0).T.astype(BF16)
    lane = lax.broadcasted_iota(jnp.int32, (CHUNK, width), 1)
    ones_lane = features * slots
    slot = jnp.where(lane == ones_lane, -1, lane % slots)
    total = jnp.zeros((width, width), F32)
    for i in range(voxels // CHUNK):
        here = slice(i * CHUNK, (i + 1) * CHUNK)
        count = digit_ref[here, 3:4].astype(F32).astype(jnp.int32)
        block = jnp.where(slot < count, points_ref[here, :].astype(F32), 0.0).astype(BF16)
        total = total + lax.dot_general(
            block, block, (((0,), (0,)), ((), ())), preferred_element_type=F32
        )
    row_at = lax.broadcasted_iota(jnp.int32, (width, width), 0)
    col_at = lax.broadcasted_iota(jnp.int32, (width, width), 1)
    same = (row_at % slots == col_at % slots) | (row_at == ones_lane)
    total = jnp.where(same & (row_at <= ones_lane) & (col_at < ones_lane), total, 0.0)
    rows = [
        jnp.sum(jnp.where(row_at // slots == k, total, 0.0), axis=0, keepdims=True)
        for k in range(features + 1)
    ]
    stacked = jnp.concatenate(rows, axis=0)
    col_eight = lax.broadcasted_iota(jnp.int32, (8, width), 1)
    lane_eight = lax.broadcasted_iota(jnp.int32, (8, LANES), 1)
    row_eight = lax.broadcasted_iota(jnp.int32, (8, LANES), 0)
    stats = jnp.zeros((8, LANES), F32)
    for k in range(features):
        picked = jnp.sum(jnp.where(col_eight // slots == k, stacked, 0.0), axis=1, keepdims=True)
        stats = stats + jnp.where(lane_eight == k, picked, 0.0)
    counted = jnp.sum(digits[3:4, :], axis=1, keepdims=True)
    hits = jnp.zeros(labels_ref.shape[1:], F32)
    for r in range(labels_ref.shape[0]):
        hits = hits + jnp.where(labels_ref[r] == 1, 1.0, 0.0)
    found = jnp.sum(jnp.sum(hits, axis=1, keepdims=True), axis=0, keepdims=True)
    real = exists > 0
    lists = []
    for q in range(anc_count):
        begin = q * device_rows - HALO
        lists.append(real & (row >= begin) & (row < begin + device_rows + 2 * HALO))
    lists.append(real & (row < HALO) & (edge_ref[0] > 0))
    lists.append(real & (row >= anc_count * device_rows - HALO) & (edge_ref[1] > 0))
    lists += [real & (row < 0)] * (8 - len(lists))
    member = jnp.concatenate([jnp.where(x, 1.0, 0.0) for x in lists], axis=0)
    before = (
        lax.broadcasted_iota(jnp.int32, (LANES, LANES), 0)
        < lax.broadcasted_iota(jnp.int32, (LANES, LANES), 1)
    )
    before = jnp.where(before, 1.0, 0.0).astype(BF16)
    carry = jnp.zeros((8, 1), F32)
    eight = lax.broadcasted_iota(jnp.int32, (8, LANES), 0)
    for i in range(place_ref.shape[1] // LANES):
        here = slice(i * LANES, (i + 1) * LANES)
        part = member[:, here]
        ahead = jnp.dot(part.astype(BF16), before, preferred_element_type=F32) + carry
        places = jnp.where(part > 0.0, ahead, -1.0).astype(jnp.int32)
        owner = jnp.zeros((1, LANES), jnp.int32)
        own = jnp.full((1, LANES), -1, jnp.int32)
        for q in range(anc_count):
            mine = (row[:, here] >= q * device_rows) & (row[:, here] < (q + 1) * device_rows)
            mine = mine & real[:, here]
            owner = jnp.where(mine, q, owner)
            own = jnp.where(mine, places[q : q + 1, :], own)
        places = jnp.where(eight == 6, owner, jnp.where(eight == 7, own, places))
        place_ref[:, here] = places
        carry = carry + jnp.sum(part, axis=1, keepdims=True)
    is_edge = lax.broadcasted_iota(jnp.int32, (8, 1), 0) >= anc_count
    need = carry / jnp.where(is_edge, float(EDGE_CAP), float(CAP))
    need = jnp.max(need, axis=0, keepdims=True)
    for k, value in enumerate((counted, found, need)):
        stats = stats + jnp.where((lane_eight == 8) & (row_eight == k), value, 0.0)
    for i in range(stats_ref.shape[0]):
        stats_ref[i] = stats


def prepare(edges, points, lines, labels, anc_count, device_rows, slots, devices):
    voxels = points.shape[0]
    return pl.pallas_call(
        functools.partial(prepare_kernel, slots, anc_count, device_rows),
        out_shape=(
            jax.ShapeDtypeStruct((devices, 8, LANES), F32),
            jax.ShapeDtypeStruct(lines.shape, jnp.int32),
            jax.ShapeDtypeStruct((voxels, LANES), BF16),
        ),
        in_specs=smem(1) + vmem(3),
        out_specs=vmem(3),
        compiler_params=params(limit=24),
        cost_estimate=work(4),
        name="prepare",
    )(edges, points, lines, labels)


def batch_norm(stats, kernel):
    lanes = kernel.shape[1]
    moments = stats[:, 0:8]
    count = stats[0:1, 8:9]
    mixed = jnp.zeros((8, lanes), F32)
    for k in range(7):
        mixed = mixed + moments[:, k : k + 1] * kernel[k : k + 1, :]
    mean = mixed[7:8, :] / count
    second = jnp.sum(mixed * kernel, axis=0, keepdims=True) / count
    inv_std = lax.rsqrt(second - mean * mean + BN_EPSILON)
    return mixed, mean, inv_std, count


def first_layer(points, first_ref, scale, offset, valid):
    hidden = jnp.dot(points, first_ref[...], preferred_element_type=F32)
    act = jnp.where(valid, jnp.maximum(hidden * scale + offset, 0.0), 0.0)
    return act


def group_fold(values, combine):
    groups = values.shape[1] // LANES
    out = values[:, :LANES]
    for g in range(1, groups):
        out = combine(out, values[:, g * LANES : (g + 1) * LANES])
    out = combine(out, pltpu.roll(out, 32, 1))
    return combine(out, pltpu.roll(out, 64, 1))


def second_tail(pooled):
    lane = lax.broadcasted_iota(jnp.int32, pooled.shape, 1)
    return jnp.where(lane < 32, pooled, jnp.where(lane == 32, 1.0, 0.0))


def group_left(low, tail, count, g):
    lane = lax.broadcasted_iota(jnp.int32, tail.shape, 1)
    marked = (lane > 32) & (lane < 37) & (lane - (33 - 4 * g) >= count)
    side = jnp.where(marked, 1.0, tail).astype(BF16)
    return jnp.concatenate([low[:, g * LANES : (g + 1) * LANES], side], axis=1)


def encode_kernel(
    slots, points_ref, count_ref, stats_ref, kernel_ref, gain_ref, first_ref, second_ref,
    feat_ref, share_ref, slot_ref, held,
):
    lanes = first_ref.shape[1]
    _, mean, inv_std, _ = batch_norm(jnp.sum(stats_ref[...], axis=0), kernel_ref[...])
    scale = gain_ref[0:1, :] * inv_std
    offset = gain_ref[1:2, :] - mean * scale
    count = count_ref[:, 3:4].astype(F32).astype(jnp.int32)
    slot = lax.broadcasted_iota(jnp.int32, (CHUNK, lanes), 1) // 32
    act = first_layer(points_ref[...], first_ref, scale, offset, slot < count)
    tail = second_tail(group_fold(act, jnp.maximum))
    low = act.astype(BF16)
    top = jnp.full((CHUNK, LANES), -jnp.inf, F32)
    for g in range(lanes // LANES):
        left = group_left(low, tail, count, g)
        part = jnp.dot(left, second_ref[...], preferred_element_type=F32)
        for s in range(min(4, slots - 4 * g)):
            p = 4 * g + s
            one = part[:, s * LANES : (s + 1) * LANES]
            held[p] = one
            top = jnp.maximum(top, one)
    code = jnp.zeros((CHUNK, LANES), F32)
    for p in range(slots):
        code = code + jnp.where(held[p] == top, 2048.0 + p, 0.0)
    ties = jnp.floor(code / 2048.0)
    feat_ref[...] = jnp.maximum(top, 0.0)
    share_ref[...] = jnp.where(top > 0.0, 1.0 / ties, 0.0)
    slot_ref[...] = jnp.minimum(code - 2048.0 * ties, 127.0).astype(BF16)


def encode(points, counts, stats, kernel, gain, first, second, slots):
    voxels, width = points.shape
    lanes = first.shape[1]
    whole = lambda *shape: pl.BlockSpec(shape, lambda i: (0,) * len(shape))
    block = lambda size: pl.BlockSpec((CHUNK, size), lambda i: (i, 0))
    return pl.pallas_call(
        functools.partial(encode_kernel, slots),
        grid=(voxels // CHUNK,),
        out_shape=(
            jax.ShapeDtypeStruct((voxels, LANES), F32),
            jax.ShapeDtypeStruct((voxels, LANES), F32),
            jax.ShapeDtypeStruct((voxels, LANES), BF16),
        ),
        in_specs=[
            block(width),
            block(LANES),
            whole(*stats.shape),
            whole(8, lanes),
            whole(8, lanes),
            whole(width, lanes),
            whole(2 * LANES, 4 * LANES),
        ],
        out_specs=[block(LANES), block(LANES), block(LANES)],
        scratch_shapes=[pltpu.VMEM((slots, CHUNK, LANES), F32)],
        compiler_params=params("arbitrary", limit=30),
        cost_estimate=work(14),
        name="encode",
    )(points, counts, stats, kernel, gain, first, second)


def decode_kernel(
    slots, points_ref, count_ref, stats_ref, kernel_ref, gain_ref, first_ref, second_ref,
    feat_ref, share_ref, slot_ref, d_feat_ref, loss_ref, out_ref,
    first_sum, second_sum, joined, tail_sum,
):
    lanes = first_ref.shape[1]
    width = points_ref.shape[1]
    step = pl.program_id(0)

    @pl.when(step == 0)
    def _():
        first_sum[...] = jnp.zeros_like(first_sum)
        second_sum[...] = jnp.zeros_like(second_sum)

    _, mean, inv_std, _ = batch_norm(jnp.sum(stats_ref[...], axis=0), kernel_ref[...])
    scale = gain_ref[0:1, :] * inv_std
    offset = gain_ref[1:2, :] - mean * scale
    count = count_ref[:, 3:4].astype(F32).astype(jnp.int32)
    points = points_ref[...]
    slot = lax.broadcasted_iota(jnp.int32, (CHUNK, lanes), 1) // 32
    act = first_layer(points, first_ref, scale, offset, slot < count)
    pooled = group_fold(act, jnp.maximum)
    tail = second_tail(pooled)
    low = act.astype(BF16)
    share = share_ref[...]
    d_feat = d_feat_ref[...] * share
    d_low = d_feat.astype(BF16)
    shared = jnp.where((share > 0.0) & (share < 1.0), 1.0, 0.0)
    shared = jnp.max(jnp.max(shared, axis=1, keepdims=True)) > 0.0

    def group_back(g, left, pieces):
        d_part = jnp.concatenate(pieces, axis=1)
        second_sum[...] += lax.dot_general(
            left, d_part, (((0,), (0,)), ((), ())), preferred_element_type=F32
        )
        d_left = lax.dot_general(
            d_part, second_ref[...], (((1,), (1,)), ((), ())), preferred_element_type=F32
        )
        joined[:, g * LANES : (g + 1) * LANES] = d_left[:, :LANES]
        return d_left[:, LANES:]

    none = jnp.zeros((CHUNK, LANES), BF16)

    @pl.when(jnp.logical_not(shared))
    def _():
        found = slot_ref[...]
        d_tail = jnp.zeros((CHUNK, LANES), F32)
        for g in range(lanes // LANES):
            left = group_left(low, tail, count, g)
            pieces = [
                jnp.where(found == jnp.asarray(4 * g + s, BF16), d_low, none)
                if 4 * g + s < slots
                else none
                for s in range(4)
            ]
            d_tail = d_tail + group_back(g, left, pieces)
        tail_sum[...] = d_tail

    @pl.when(shared)
    def _():
        top = feat_ref[...]
        d_tail = jnp.zeros((CHUNK, LANES), F32)
        for g in range(lanes // LANES):
            left = group_left(low, tail, count, g)
            part = jnp.dot(left, second_ref[...], preferred_element_type=F32)
            pieces = []
            for s in range(4):
                if 4 * g + s < slots:
                    hit = part[:, s * LANES : (s + 1) * LANES] == top
                    pieces.append(jnp.where(hit, d_feat, 0.0).astype(BF16))
                else:
                    pieces.append(none)
            d_tail = d_tail + group_back(g, left, pieces)
        tail_sum[...] = d_tail

    wide = jnp.concatenate([pooled] * (lanes // LANES), axis=1)
    reached = act == wide
    ties = group_fold(jnp.where(reached, 1.0, 0.0), jnp.add)
    lane = lax.broadcasted_iota(jnp.int32, (CHUNK, LANES), 1)
    spread = jnp.where(lane < 32, tail_sum[...], 0.0)
    spread = spread + pltpu.roll(spread, 32, 1)
    spread = (spread + pltpu.roll(spread, 64, 1)) / ties
    spread = jnp.concatenate([spread] * (lanes // LANES), axis=1)
    d_act = joined[...] + jnp.where(reached, spread, 0.0)
    d_act = jnp.where(act > 0.0, d_act, 0.0).astype(BF16)
    first_sum[...] += lax.dot_general(
        points, d_act, (((0,), (0,)), ((), ())), preferred_element_type=F32
    )

    @pl.when(step == pl.num_programs(0) - 1)
    def _():
        row_at = lax.broadcasted_iota(jnp.int32, (width, lanes), 0)
        col_at = lax.broadcasted_iota(jnp.int32, (width, lanes), 1)
        same = (row_at % slots == col_at // 32) | (row_at == 7 * slots)
        total = jnp.where(same & (col_at // 32 < slots), first_sum[...], 0.0)
        rows = [
            jnp.sum(jnp.where(row_at // slots == k, total, 0.0), axis=0, keepdims=True)
            for k in range(8)
        ]
        first = group_fold(jnp.concatenate(rows, axis=0), jnp.add)
        upper = second_sum[0:32, 0:LANES]
        lower = second_sum[LANES : LANES + 40, 0:LANES]
        for s in range(1, 4):
            cols = slice(s * LANES, (s + 1) * LANES)
            upper = upper + second_sum[s * 32 : (s + 1) * 32, cols]
            lower = lower + second_sum[LANES : LANES + 40, cols]
        devices, layers = out_ref.shape[:2]
        none = jnp.zeros((devices * layers - 88, LANES), F32)
        rows = jnp.concatenate([first, upper, lower, loss_ref[...], none], axis=0)
        for k in range(layers):
            out_ref[:, k, :] = rows[k * devices : (k + 1) * devices, :]


def decode(
    points, counts, stats, kernel, gain, first, second, feat, share, slot, d_feat, loss, shape, slots
):
    voxels, width = points.shape
    lanes = first.shape[1]
    whole = lambda *shape: pl.BlockSpec(shape, lambda i: (0,) * len(shape))
    block = lambda size: pl.BlockSpec((CHUNK, size), lambda i: (i, 0))
    return pl.pallas_call(
        functools.partial(decode_kernel, slots),
        grid=(voxels // CHUNK,),
        out_shape=jax.ShapeDtypeStruct(shape + (LANES,), F32),
        in_specs=[
            block(width),
            block(LANES),
            whole(*stats.shape),
            whole(8, lanes),
            whole(8, lanes),
            whole(width, lanes),
            whole(2 * LANES, 4 * LANES),
            block(LANES),
            block(LANES),
            block(LANES),
            block(LANES),
            whole(8, LANES),
        ],
        out_specs=whole(*shape, LANES),
        scratch_shapes=[
            pltpu.VMEM((width, lanes), F32),
            pltpu.VMEM((2 * LANES, 4 * LANES), F32),
            pltpu.VMEM((CHUNK, lanes), F32),
            pltpu.VMEM((CHUNK, LANES), F32),
        ],
        compiler_params=params("arbitrary", limit=30),
        cost_estimate=work(28),
        name="decode",
    )(points, counts, stats, kernel, gain, first, second, feat, share, slot, d_feat, loss)


def encoder_weights_kernel(
    slots, one_ref, two_ref, bias_ref, gain_ref, first_ref, second_ref, kernel_ref, rows_ref
):
    width, lanes = first_ref.shape
    features = one_ref.shape[0] - 1
    row_at = lax.broadcasted_iota(jnp.int32, (width, LANES), 0)
    slot_at = lax.broadcasted_iota(jnp.int32, (width, LANES), 1) // 32
    one = jnp.concatenate([one_ref[...]] * 4, axis=1)
    tall = jnp.zeros((width, LANES), F32)
    for k in range(features):
        tall = jnp.where(row_at // slots == k, one[k : k + 1, :], tall)
    own_slot = row_at % slots
    for g in range(lanes // LANES):
        here = slice(g * LANES, (g + 1) * LANES)
        first_ref[:, here] = jnp.where(own_slot == 4 * g + slot_at, tall, 0.0).astype(BF16)
        kernel_ref[:, here] = one
        rows_ref[:, here] = jnp.concatenate([gain_ref[...]] * 4, axis=1)
    two = two_ref[...]
    half = two.shape[0] // 2
    upper = jnp.concatenate([two[:half]] * 4, axis=0)
    row_two = lax.broadcasted_iota(jnp.int32, (LANES, LANES), 0)
    for s in range(4):
        here = slice(s * LANES, (s + 1) * LANES)
        second_ref[0:LANES, here] = jnp.where(row_two // half == s, upper, 0.0).astype(BF16)
        lower = jnp.concatenate(
            [two[half:], bias_ref[...], jnp.zeros((LANES - half - 8, LANES), F32)], axis=0
        )
        second_ref[LANES:, here] = jnp.where(row_two == half + 1 + s, EMPTY, lower).astype(BF16)


def encoder_weights(w_one, w_two, bias_two, gain, shift, slots):
    features, c_one = w_one.shape
    lanes = -(-slots // 4) * LANES
    width = -(-(features * slots + 1) // LANES) * LANES
    one = jnp.pad(w_one.astype(F32), ((0, 1), (0, 0)))
    bias = jnp.pad(bias_two.astype(F32).reshape(1, -1), ((0, 7), (0, 0)))
    rows = jnp.pad(jnp.stack([gain, shift]).astype(F32), ((0, 6), (0, 0)))
    return pl.pallas_call(
        functools.partial(encoder_weights_kernel, slots),
        out_shape=(
            jax.ShapeDtypeStruct((width, lanes), BF16),
            jax.ShapeDtypeStruct((2 * LANES, 4 * LANES), BF16),
            jax.ShapeDtypeStruct((8, lanes), F32),
            jax.ShapeDtypeStruct((8, lanes), F32),
        ),
        in_specs=vmem(4),
        out_specs=vmem(4),
        compiler_params=params(limit=24),
        cost_estimate=work(2),
        name="encoder_weights",
    )(one, w_two.astype(F32), bias, rows)


def pick_rows(source, place_ref, line, capacity, offset):
    want = place_ref[line : line + 1, :][:, : source.shape[0]] - offset
    row_at = lax.broadcasted_iota(jnp.int32, (capacity, source.shape[0]), 0)
    chosen = jnp.where(want == row_at, 1.0, 0.0).astype(BF16)
    found = jnp.dot(chosen, source, preferred_element_type=F32)
    return found[:, :LANES].astype(BF16), found[:, LANES:].T


def edge_lists_kernel(anc_count, offset_ref, feat_ref, digit_ref, place_ref, up_ref, down_ref):
    source = jnp.concatenate([feat_ref[...].astype(BF16), digit_ref[...]], axis=1)
    for side, edge_ref in enumerate((up_ref, down_ref)):
        rows, digits = pick_rows(source, place_ref, anc_count + side, EDGE_CAP, offset_ref[1])
        edge_ref[0:EDGE_CAP, :] = rows
        digits = jnp.concatenate([digits[0:8, :], jnp.zeros((8, LANES), F32)], axis=0)
        edge_ref[EDGE_CAP : EDGE_CAP + 16, :] = digits.astype(BF16)


def edge_lists(offsets, feat, digits, place, anc_count):
    return pl.pallas_call(
        functools.partial(edge_lists_kernel, anc_count),
        out_shape=(
            jax.ShapeDtypeStruct((EDGE_CAP + 16, LANES), BF16),
            jax.ShapeDtypeStruct((EDGE_CAP + 16, LANES), BF16),
        ),
        in_specs=smem(1) + vmem(3),
        out_specs=vmem(2),
        compiler_params=params(limit=24),
        cost_estimate=work(1),
        name="edge_lists",
    )(offsets, feat, digits, place)


def gather_lists_kernel(anc_count, offset_ref, feat_ref, digit_ref, place_ref, main_ref):
    source = jnp.concatenate([feat_ref[...].astype(BF16), digit_ref[...]], axis=1)
    for q in range(anc_count):
        rows, digits = pick_rows(source, place_ref, q, CAP, offset_ref[0])
        main_ref[q, 0:CAP, :] = rows
        lines = [
            digits[k : k + 1, i * LANES : (i + 1) * LANES]
            for k in range(3)
            for i in range(CAP // LANES)
        ]
        lines.append(jnp.zeros((32 - len(lines), LANES), F32))
        main_ref[q, CAP : CAP + 32, :] = jnp.concatenate(lines, axis=0).astype(BF16)
        main_ref[q, CAP + 32 :, :] = jnp.zeros((EDGE_CAP + 16, LANES), BF16)


def gather_lists(offsets, feat, digits, place, anc_count):
    return pl.pallas_call(
        functools.partial(gather_lists_kernel, anc_count),
        out_shape=jax.ShapeDtypeStruct((anc_count, CAP + EDGE_CAP + 48, LANES), BF16),
        in_specs=smem(1) + vmem(3),
        out_specs=vmem(1)[0],
        compiler_params=params(limit=30),
        cost_estimate=work(5),
        name="gather_lists",
    )(offsets, feat, digits, place)


def spread_lists_kernel(index_ref, *refs):
    received, (out_ref, held) = refs[:-2], refs[-2:]
    length = received[0].shape[0]
    for k, received_ref in enumerate(received):
        held[k * length : (k + 1) * length, :] = received_ref[...].astype(F32)
    held[len(received) * length :, :] = jnp.zeros((8, LANES), F32)

    def pick(i, carry):
        base = pl.multiple_of(i * LANES, LANES)
        for j in range(LANES):
            out_ref[pl.ds(base + j, 1), :] = held[pl.ds(index_ref[base + j], 1), :]
        return carry

    lax.fori_loop(0, out_ref.shape[0] // LANES, pick, 0)


def spread_lists(index, received):
    voxels = index.shape[0]
    total = sum(rows.shape[0] for rows in received)
    return pl.pallas_call(
        spread_lists_kernel,
        out_shape=jax.ShapeDtypeStruct((voxels, LANES), F32),
        in_specs=smem(1) + vmem(len(received)),
        out_specs=vmem(1)[0],
        scratch_shapes=[pltpu.VMEM((total + 8, LANES), F32)],
        compiler_params=params(limit=24),
        cost_estimate=work(4),
        name="spread_lists",
    )(index, *received)


def add_piece(held, source, low, high, start):
    lane = lax.broadcasted_iota(jnp.int32, (1, LANES), 1)
    begin, end = low // LANES, -(-high // LANES)
    gap = start - low
    turn = gap % LANES
    at = begin + gap // LANES
    rows = source[begin:end, :]
    count = end - begin
    place = lax.broadcasted_iota(jnp.int32, (count, LANES), 0) * LANES
    place = place + lax.broadcasted_iota(jnp.int32, (count, LANES), 1) + begin * LANES
    if low % LANES or high % LANES:
        rows = jnp.where((place >= low) & (place < high), rows, 0.0)
    if turn == 0:
        held[at : at + count, :] += rows
        return
    rows = pltpu.roll(rows, turn, 1)
    here = jnp.where(lane >= turn, rows, 0.0)
    after = jnp.where(lane < turn, rows, 0.0)
    skip = max(-at, 0)
    if count > skip:
        held[at + skip : at + count, :] += here[skip:, :]
    held[at + 1 : at + 1 + count, :] += after


def pack_kernel(
    plan, tiles, chunk, region_ref, middle_ref, head_ref, mid_ref, row_ref, out_ref, held, rest_ref
):
    half = LANES // 2
    lane = lax.broadcasted_iota(jnp.int32, (1, LANES), 1)
    mid = jnp.sum(mid_ref[...], axis=0, keepdims=True)
    mid = group_sum(mid)
    mid = mid + pltpu.roll(mid, half, 1)
    region_bias = pltpu.roll(jnp.sum(row_ref[0:8, :], axis=0, keepdims=True), half, 1)
    outs = row_ref.shape[0] - 16
    wide = lax.broadcasted_iota(jnp.int32, (outs, LANES), 1) - half
    own = lax.broadcasted_iota(jnp.int32, (outs, LANES), 0) == wide
    head_bias = jnp.sum(jnp.where(own, row_ref[8 : 8 + outs, :], 0.0), axis=0, keepdims=True)
    rest_ref[0:1, :] = jnp.where(lane < half, mid, region_bias)
    rest_ref[1:2, :] = jnp.where(lane < half, region_bias, head_bias)
    sources = {"region": region_ref, "middle": middle_ref, "head": head_ref, "rest": rest_ref}
    for a, pieces in enumerate(plan):
        held[...] = jnp.zeros_like(held)
        for name, low, high, start in pieces:
            if name in sources:
                add_piece(held, sources[name], low, high, start)
        for t in range(tiles):
            out_ref[t * len(plan) + a] = held[t * chunk : (t + 1) * chunk, :].astype(BF16)


def group_sum(values):
    out = values[:, :LANES]
    for g in range(1, values.shape[1] // LANES):
        out = out + values[:, g * LANES : (g + 1) * LANES]
    return out


def pack(plan, tiles, chunk, region, middle, head, mid_sums, row_sums):
    return pl.pallas_call(
        functools.partial(pack_kernel, plan, tiles, chunk),
        out_shape=jax.ShapeDtypeStruct((tiles * len(plan), chunk, LANES), BF16),
        in_specs=vmem(5),
        out_specs=vmem(1)[0],
        scratch_shapes=[pltpu.VMEM((tiles * chunk, LANES), F32), pltpu.VMEM((8, LANES), F32)],
        compiler_params=params(limit=28),
        cost_estimate=work(3),
        name="pack",
    )(region, middle, head, mid_sums, row_sums)


def sum_chunk_kernel(parts_ref, out_ref, square_ref):
    total = jnp.sum(parts_ref[...].astype(F32), axis=0)
    for i in range(out_ref.shape[0]):
        out_ref[i] = total
    square_ref[...] = jnp.broadcast_to(jnp.sum(total * total), square_ref.shape)


def sum_chunk(parts, tiles):
    _, rows, lanes = parts.shape
    return pl.pallas_call(
        sum_chunk_kernel,
        out_shape=(
            jax.ShapeDtypeStruct((tiles, rows, lanes), F32),
            jax.ShapeDtypeStruct((1, lanes), F32),
        ),
        in_specs=vmem(1),
        out_specs=vmem(2),
        compiler_params=params(limit=24),
        cost_estimate=work(2),
        name="sum_chunk",
    )(parts)


def finish_kernel(
    plan, anc_ref, early_ref, late_ref, stats_ref, kernel_ref, gain_ref,
    out_ref, scalar_ref, one, norm,
):
    stats = jnp.sum(stats_ref[...], axis=0)
    kernel = kernel_ref[:, :LANES]
    mixed, mean, inv_std, count = batch_norm(stats, kernel)
    layers = late_ref.shape[1] - 1
    late = jnp.concatenate([late_ref[:, k, :] for k in range(layers)], axis=0)
    sums = late[0:8, :]
    total_shift = sums[7:8, :]
    total_gain = inv_std * (jnp.sum(kernel * sums, axis=0, keepdims=True) - mean * total_shift)
    slope = gain_ref[0:1, :LANES] * inv_std
    lane = lax.broadcasted_iota(jnp.int32, (1, LANES), 1)
    one[...] = jnp.zeros_like(one)
    norm[...] = jnp.zeros_like(norm)
    for k in range(7):
        first = stats[7:8, k : k + 1]
        pull = total_shift * first + total_gain * inv_std * (mixed[k : k + 1, :] - mean * first)
        grad = jnp.where(lane < 32, slope * (sums[k : k + 1, :] - pull / count), 0.0)
        if k % 4:
            grad = pltpu.roll(grad, 32 * (k % 4), 1)
        one[k // 4 : k // 4 + 1, :] += grad
    bias = late[72:73, :]
    top = jnp.where(lane < 32, total_gain, 0.0)
    top = top + pltpu.roll(jnp.where(lane < 32, total_shift, 0.0), 32, 1)
    norm[0:1, :] = top + jnp.where(lane < 64, 0.0, pltpu.roll(bias, 64, 1))
    norm[1:2, :] = jnp.where(lane < 64, pltpu.roll(bias, 64, 1), 0.0)
    two = late[8:72, :]
    square = jnp.sum(late_ref[:, layers, :]) / LANES
    square = square + jnp.sum(two * two) + jnp.sum(one[...] * one[...])
    square = square + jnp.sum(norm[...] * norm[...])
    size = jnp.sqrt(jnp.broadcast_to(square, (1, LANES)))
    scalar_ref[0:1, :] = late[80:81, :] / stats[1:2, 8:9]
    scalar_ref[1:2, :] = size
    scalar_ref[2:8, :] = jnp.broadcast_to(jnp.minimum(1.0, CLIP_LIMIT / (size + 1e-06)), (6, LANES))
    chunk = early_ref.shape[1]
    for i in range(early_ref.shape[0]):
        out_ref[i * chunk : (i + 1) * chunk, :] = early_ref[i]
    sources = {"one": one, "two": two, "norm": norm}
    for a, pieces in enumerate(plan):

        @pl.when(anc_ref[0] == a)
        def _():
            for name, low, high, start in pieces:
                if name in sources:
                    add_piece(out_ref, sources[name], low, high, start)


def finish(plan, anc, early, late, stats, kernel, gain):
    return pl.pallas_call(
        functools.partial(finish_kernel, plan),
        out_shape=(
            jax.ShapeDtypeStruct((early.shape[0] * early.shape[1], LANES), F32),
            jax.ShapeDtypeStruct((8, LANES), F32),
        ),
        in_specs=smem(1) + vmem(5),
        out_specs=vmem(2),
        scratch_shapes=[pltpu.VMEM((8, LANES), F32), pltpu.VMEM((8, LANES), F32)],
        compiler_params=params(limit=24),
        cost_estimate=work(3),
        name="finish",
    )(anc, early, late, stats, kernel, gain)


def everyone(values, axes):
    count = 1
    for axis in axes:
        count *= lax.axis_size(axis)
    copies = jnp.broadcast_to(values[None], (count,) + values.shape)
    return lax.all_to_all(copies, axes, 0, 0)


def swap_rows(beside, across):
    axes = ("tile", "anc")
    count = lax.axis_size("tile") * lax.axis_size("anc")
    pairs = [(i, i ^ 1) for i in range(count)]
    others = [(i, i + 1) for i in range(1, count - 1, 2)]
    others += [(j, i) for i, j in others]
    return lax.ppermute(beside, axes, pairs), lax.ppermute(across, axes, others)


def shard_windows(segments, shard, count):
    windows = []
    for a in range(count):
        begin, end = a * shard, (a + 1) * shard
        at = 0
        pieces = []
        for name, size in segments:
            low, high = max(begin, at), min(end, at + size)
            if low < high:
                pieces.append((name, low - at, high - at, low - begin))
            at += size
        windows.append(tuple(pieces))
    return tuple(windows)


def on_device(
    points,
    npoints,
    coords,
    labels,
    targets,
    w_vfe1,
    w_vfe2,
    w_mid,
    w_rpn,
    w_head,
    bn_gain,
    biases,
    master,
    moment1,
    moment2,
):
    both = ("tile", "anc")
    anc_count = lax.axis_size("anc")
    tile_count = lax.axis_size("tile")
    anc = lax.axis_index("anc")
    tile = lax.axis_index("tile")
    device_rows = labels.shape[1]
    columns = labels.shape[2]
    blocks = device_rows // BLOCK_ROWS
    tile_rows = device_rows * anc_count
    all_rows = tile_rows * tile_count
    slots = points.shape[1]
    voxels = points.shape[2]
    c_vfe = w_vfe1.shape[1]
    c_vox = w_vfe2.shape[1]
    c_mid = w_mid.shape[4]
    c_rpn = w_rpn.shape[3]
    outs = w_head.shape[1]
    shift = biases[:c_vfe]
    bias_two = biases[c_vfe : c_vfe + c_vox]
    rest = biases[c_vfe + c_vox :].astype(F32)
    bias_rows = jnp.concatenate(
        [rest[:c_mid], rest, jnp.zeros((LANES - outs,), F32)]
    ).reshape(3, LANES)

    def joined(row):
        return (row % CROP_ROWS != CROP_ROWS // 2) & (row > 0) & (row < all_rows)

    padded = -(-voxels // CHUNK) * CHUNK
    width = -(-(points.shape[0] * slots + 1) // LANES) * LANES
    flat_points = points.reshape(-1, voxels).T
    flat_points = jnp.pad(
        flat_points, ((0, padded - voxels), (0, width - flat_points.shape[1]))
    )
    lane = lax.broadcasted_iota(jnp.int32, flat_points.shape, 1)
    flat_points = jnp.where(lane == points.shape[0] * slots, jnp.ones((), BF16), flat_points)
    spare = (0, -(-padded // LINE) * LINE - voxels)
    row = coords[:, 1] - tile * tile_rows
    lines = [coords[:, 0], row, coords[:, 2], jnp.ones_like(row), npoints]
    lines = jnp.pad(jnp.stack(lines), ((0, 3), spare))
    tile_edges = jnp.stack([joined(tile * tile_rows), joined((tile + 1) * tile_rows)])
    devices = anc_count * tile_count
    parts = [w_rpn]
    for k in range(1, anc_count):
        around = [((i + k) % anc_count, i) for i in range(anc_count)]
        parts.append(lax.ppermute(w_rpn, "anc", around))
    stats, place, digits = prepare(
        tile_edges.astype(jnp.int32),
        flat_points,
        lines,
        labels.transpose(1, 0, 2),
        anc_count,
        device_rows,
        slots,
        devices,
    )
    stats, parts = lax.optimization_barrier((stats, parts))
    stats = lax.all_to_all(stats, both, 0, 0)
    region_in, region_back = region_order(anc.reshape(1), parts)
    counts = digits
    count_pos = jnp.sum(stats[:, 1, 8])
    rounds = jnp.ceil(jnp.max(stats[:, 2, 8])).astype(jnp.int32)
    middle_kernel_all = w_mid.transpose(0, 1, 2, 4, 3).reshape(-1, c_mid, c_vox)

    first, second, kernel, gain_rows = encoder_weights(
        w_vfe1, w_vfe2, bias_two, bn_gain, shift, slots
    )
    feat, share, found = encode(
        flat_points, counts, stats, kernel, gain_rows, first, second, slots
    )
    feat, region_in, region_back = lax.optimization_barrier((feat, region_in, region_back))

    in_tile = lax.axis_size("tile")
    upward = [(i + 1, i) for i in range(in_tile - 1)]
    downward = [(i, i + 1) for i in range(in_tile - 1)]

    def exchange(number):
        offsets = jnp.stack([number * CAP, number * EDGE_CAP]).astype(jnp.int32)
        up, down = edge_lists(offsets, feat, digits, place, anc_count)
        from_below = lax.ppermute(up, "tile", upward)
        from_above = lax.ppermute(down, "tile", downward)
        main = gather_lists(offsets, feat, digits, place, anc_count)
        main, from_below, from_above = lax.optimization_barrier((main, from_below, from_above))
        main = lax.dynamic_update_slice(main, from_above[None], (0, CAP + 32, 0))
        main = lax.dynamic_update_slice(main, from_below[None], (anc_count - 1, CAP + 32, 0))
        return lax.all_to_all(main, "anc", 0, 0), main

    def cells(got):
        words = got[:, CAP : CAP + 32].reshape(anc_count, -1).astype(jnp.int32)
        start = CAP + 32 + EDGE_CAP
        edge_words = got[:, start : start + 16].astype(jnp.int32)

        def word(k):
            gap = jnp.zeros((anc_count, 32), jnp.int32)
            parts = [words[:, k * CAP : (k + 1) * CAP], gap, edge_words[:, k], gap[:, :16]]
            return jnp.concatenate(parts, axis=1)

        high, half, mixed = word(0), word(1), word(2)
        local = mixed // 2 - anc * device_rows
        is_edge = lax.broadcasted_iota(jnp.int32, local.shape, 1) >= CAP
        local = local + jnp.where(is_edge, jnp.where(anc == 0, -tile_rows, tile_rows), 0)
        cross = half * 2 + mixed % 2
        scatter_at, own_at = [], []
        for k in range(blocks):
            line = local - k * BLOCK_ROWS
            tall = BLOCK_ROWS + 2 * HALO
            inside = (high > 0) & (line >= -HALO) & (line < BLOCK_ROWS + HALO)
            spot = ((high - 1) * tall + line + HALO) * columns + cross
            scatter_at.append(jnp.where(inside, spot, DEPTH * tall * columns).reshape(-1))
            inside = (high > 0) & (line >= 0) & (line < BLOCK_ROWS)
            spot = ((high - 1) * BLOCK_ROWS + line) * columns + cross
            spot = jnp.where(inside, spot, DEPTH * BLOCK_ROWS * columns)
            own_at.append(spot[:, :CAP].reshape(-1, LANES))
        return scatter_at, own_at

    got, sent = exchange(0)
    labels, targets, _ = lax.optimization_barrier((labels, targets, sent[0, 0, 0]))
    first_row = tile * tile_rows + anc * device_rows
    edges = []
    even = (tile * anc_count + anc) % 2 == 0
    for k in range(blocks):
        top = first_row + k * BLOCK_ROWS
        flags = [
            joined(top),
            joined(top + BLOCK_ROWS),
            even,
            anc * device_rows + k * BLOCK_ROWS,
            jnp.where(anc == 0, -tile_rows, tile_rows),
            anc,
        ]
        edges.append(jnp.stack([flag.astype(jnp.int32) for flag in flags]))

    def more(state):
        return state[0] < rounds

    def another(state):
        number, held = state
        rows, _ = exchange(number)
        index, _ = cells(rows)
        rows = rows.reshape(-1, LANES)
        held = [scatter_rows(at, rows, old, columns) for at, old in zip(index, held)]
        return number + 1, held

    def one_round():
        made = [
            scatter_middle(
                edges[k], got.reshape(-1, LANES), middle_kernel_all, bias_rows, columns
            )
            for k in range(blocks)
        ]
        return tuple([one[i] for one in made] for i in range(3))

    def many_rounds():
        index, own = cells(got)
        held = [scatter_rows(at, got.reshape(-1, LANES), None, columns) for at in index]
        _, held = lax.while_loop(more, another, (jnp.int32(1), held))
        bevs = [
            middle_forward(edges[k], held[k], middle_kernel_all, bias_rows, columns)
            for k in range(blocks)
        ]
        return held, bevs, own

    grids, bevs, own_at = lax.cond(rounds > 1, many_rounds, one_round)

    wide_labels = jnp.repeat(labels.reshape(2, -1), outs // 2, axis=0)
    wide_targets = jnp.pad(targets, ((0, 0), (1, 0), (0, 0), (0, 0))).reshape(outs, -1)
    step = BLOCK_ROWS * columns
    scale = 1.0 / count_pos
    d_rows, head_sums, row_sums = [], 0.0, 0.0
    d_beside, d_across = [], []
    for k in range(blocks):
        here = slice(k * step, (k + 1) * step)
        d_block, near_row, far_row, heads, sums = region_forward(
            scale,
            edges[k],
            bevs[k],
            region_in,
            bias_rows,
            w_head.T,
            wide_labels[:, here],
            wide_targets[:, here],
            columns,
        )
        d_rows.append(d_block)
        d_beside.append(near_row)
        d_across.append(far_row)
        head_sums = head_sums + heads
        row_sums = row_sums + sums

    def swapped(near, far):
        if blocks == 1:
            got_near, got_far = swap_rows(near[0], far[0])
            return [got_near], [got_far]
        firsts = [jnp.where(even, f, n) for n, f in zip(near, far)]
        lasts = [jnp.where(even, n, f) for n, f in zip(near, far)]
        got_near, got_far = swap_rows(
            jnp.where(even, lasts[-1], firsts[0]), jnp.where(even, firsts[0], lasts[-1])
        )
        above = [jnp.where(even, got_far, got_near)] + lasts[:-1]
        below = firsts[1:] + [jnp.where(even, got_near, got_far)]
        return (
            [jnp.where(even, y, x) for x, y in zip(above, below)],
            [jnp.where(even, x, y) for x, y in zip(above, below)],
        )

    beside, across = swapped(d_beside, d_across)
    grad_region = sum(
        region_weight(d_rows[k], bevs[k], columns, anc_count) for k in range(blocks)
    )
    d_rows, grad_region, beside, across = lax.optimization_barrier(
        (d_rows, grad_region, beside, across)
    )
    d_mids, mid_sums = [], 0.0
    mid_beside, mid_across = [], []
    for k in range(blocks):
        d_block, near_row, far_row, sums = region_data(
            edges[k], d_rows[k], beside[k], across[k], bevs[k], region_back, columns
        )
        d_mids.append(d_block)
        mid_beside.append(near_row)
        mid_across.append(far_row)
        mid_sums = mid_sums + sums
    beside, across = swapped(mid_beside, mid_across)
    grad_mid = sum(middle_weight(grids[k], d_mids[k], columns) for k in range(blocks))
    grad_mid, beside, across = lax.optimization_barrier((grad_mid, beside, across))

    head_three = head_sums.reshape(3, outs, c_rpn)
    grad_head = (head_three[0] + head_three[1] + head_three[2]).T
    head_rows = grad_head.reshape(-1, LANES)
    segments = (
        ("region", grad_region.size),
        ("one", w_vfe1.size),
        ("two", w_vfe2.size),
        ("middle", grad_mid.size),
        ("head", w_head.size),
        ("norm", c_vfe + c_vfe + c_vox),
        ("rest", c_mid + c_rpn + outs),
    )
    shard = master.shape[0]
    plan = shard_windows(segments, shard, anc_count)
    chunk_rows = -(-(shard // LANES + 2) // (8 * tile_count)) * 8
    packed = pack(
        plan, tile_count, chunk_rows, grad_region, grad_mid, head_rows, mid_sums, row_sums
    )
    own_at, packed = lax.optimization_barrier((own_at, packed))
    chunk, chunk_square = sum_chunk(lax.all_to_all(packed, both, 0, 0), tile_count)

    def collect(number, own_index):
        lists = [
            middle_data(
                own_index[k], edges[k], d_mids[k], beside[k], across[k], middle_kernel_all, columns
            )
            for k in range(blocks)
        ]
        lists = [sum(parts) for parts in zip(*lists)]
        back = lists[:1]
        for k in range(1, anc_count):
            onward = [(i, (i + k) % anc_count) for i in range(anc_count)]
            back.append(lax.ppermute(lists[k], "anc", onward))
        mine = place[7, :padded] - number * CAP
        known = (mine >= 0) & (mine < CAP)
        index = (anc - place[6, :padded] + anc_count) % anc_count * CAP + mine
        return spread_lists(jnp.where(known, index, anc_count * CAP), back)

    d_feat = collect(0, own_at)
    d_feat, chunk = lax.optimization_barrier((d_feat, chunk))
    early = lax.all_to_all(chunk, "tile", 0, 0)

    def collect_more(state):
        number, held = state
        _, index = cells(exchange(number)[0])
        return number + 1, held + collect(number, index)

    d_feat = lax.cond(
        rounds > 1,
        lambda held: lax.while_loop(more, collect_more, (jnp.int32(1), held))[1],
        lambda held: held,
        d_feat,
    )
    layers = -(-88 // devices)
    late = decode(
        flat_points,
        counts,
        stats,
        kernel,
        gain_rows,
        first,
        second,
        feat,
        share,
        found,
        d_feat,
        row_sums[24:32],
        (devices, layers),
        slots,
    )
    late, early = lax.optimization_barrier((late, early))
    late = jnp.sum(lax.all_to_all(late, both, 0, 0), axis=0)
    late = everyone(jnp.concatenate([late, chunk_square], axis=0), both)
    reduced, scalars = finish(plan, anc.reshape(1), early, late, stats, kernel, gain_rows)
    loss = scalars[0, 0]
    norm_value = scalars[1, 0]
    reduced = reduced.reshape(-1)[:shard]
    clipped = reduced * scalars[2, 0]
    first_new = BETA_FIRST * moment1 + (1.0 - BETA_FIRST) * clipped
    second_new = BETA_SECOND * moment2 + (1.0 - BETA_SECOND) * clipped * clipped
    first_hat = first_new / (1.0 - BETA_FIRST**STEP_NUMBER)
    second_hat = second_new / (1.0 - BETA_SECOND**STEP_NUMBER)
    updated = master - LEARN_RATE * (
        first_hat / (jnp.sqrt(second_hat) + ADAM_EPSILON) + WEIGHT_DECAY * master
    )
    return (updated, first_new, second_new, loss, norm_value)


def solution(mesh):
    placed = (
        P(None, None, ("tile", "anc")),
        P(("tile", "anc")),
        P(("tile", "anc"), None),
        P(None, ("tile", "anc"), None),
        P(None, None, ("tile", "anc"), None),
        P(),
        P(),
        P(),
        P(None, None, "anc", None),
        P(),
        P(),
        P(),
        P("anc"),
        P("anc"),
        P("anc"),
    )
    return jax.shard_map(
        on_device,
        mesh=mesh,
        in_specs=placed,
        out_specs=(P("anc"), P("anc"), P("anc"), P(), P()),
        check_vma=False,
    )
```

```python
import functools
import jax
import jax.numpy as jnp
from jax import lax
from jax.experimental import pallas as pl
from jax.experimental.pallas import tpu as pltpu
from jax.sharding import PartitionSpec as P

DEPTH = 10
PAIRS = DEPTH // 4 + 1
CROP_ROWS = 192
BLOCK_ROWS = 12
HALO = 2
LANES = 128
CHUNK = 640
LINE = 1024
CAP = 768
EDGE_CAP = 128
EMPTY = -1e30
FOCAL_ALPHA = 0.25
BN_EPSILON = 0.001
CLIP_LIMIT = 0.05
LEARN_RATE = 0.03
BETA_FIRST = 0.9
BETA_SECOND = 0.999
WEIGHT_DECAY = 0.01
ADAM_EPSILON = 1e-08
STEP_NUMBER = 10
F32 = jnp.float32
BF16 = jnp.bfloat16


def vmem(count):
    return [pl.BlockSpec(memory_space=pltpu.VMEM)] * count


def smem(count):
    return [pl.BlockSpec(memory_space=pltpu.SMEM)] * count


def params(*semantics, limit=60):
    return pltpu.CompilerParams(
        vmem_limit_bytes=limit * 1024 * 1024, dimension_semantics=semantics or None
    )


def work(micros):
    return pl.CostEstimate(flops=micros, transcendentals=0, bytes_accessed=micros * 3_000_000)


def at_row(index, columns):
    if isinstance(index, int):
        return pl.ds(index * columns, columns)
    return pl.ds(pl.multiple_of(index * columns, 32), columns)


def column_edges(columns, lanes):
    place = lax.broadcasted_iota(jnp.int32, (columns, lanes), 0)
    return place == 0, place == columns - 1


def from_left(values):
    columns, lanes = values.shape
    first, _ = column_edges(columns, lanes)
    return jnp.where(first, 0.0, pltpu.roll(values, 1, 0))


def from_right(values):
    columns, lanes = values.shape
    _, last = column_edges(columns, lanes)
    return jnp.where(last, 0.0, pltpu.roll(values, columns - 1, 0))


def low_lanes(columns):
    return lax.broadcasted_iota(jnp.int32, (columns, LANES), 1) < LANES // 2


def clear(wide, cells):
    step = 512

    def begin(i, carry):
        wide[pl.ds(pl.multiple_of(i * step, step), step), :] = jnp.zeros((step, LANES), F32)
        return carry

    lax.fori_loop(0, cells // step, begin, 0)


def narrow(wide, out_ref):
    step = 512

    def finish(i, carry):
        block = pl.ds(pl.multiple_of(i * step, step), step)
        out_ref[block, :] = wide[block, :].astype(BF16)
        return carry

    lax.fori_loop(0, out_ref.shape[0] // step, finish, 0)


def place_rows(count, cells, index_ref, feat_ref, old_ref, out_ref, wide, rows):
    if old_ref is None:
        clear(wide, cells)
    else:
        wide[0:cells, :] = old_ref[...].astype(F32)
    rows[...] = feat_ref[...].astype(F32)

    def place(i, carry):
        for j in range(8):
            wide[pl.ds(index_ref[i * 8 + j], 1), :] = rows[pl.ds(i * 8 + j, 1), :]
        return carry

    lax.fori_loop(0, count // 8, place, 0)
    narrow(wide, out_ref)


def scatter_kernel(count, cells, fresh, *refs):
    if fresh:
        index_ref, feat_ref, out_ref, wide, rows = refs
        place_rows(count, cells, index_ref, feat_ref, None, out_ref, wide, rows)
    else:
        place_rows(count, cells, *refs)


def scatter_rows(index, feats, old, columns):
    cells = DEPTH * (BLOCK_ROWS + 2 * HALO) * columns
    count = index.shape[0]
    fresh = old is None
    return pl.pallas_call(
        functools.partial(scatter_kernel, count, cells, fresh),
        out_shape=jax.ShapeDtypeStruct((cells, LANES), BF16),
        in_specs=smem(1) + vmem(1 if fresh else 2),
        out_specs=vmem(1)[0],
        scratch_shapes=[pltpu.VMEM((cells + 8, LANES), F32), pltpu.VMEM((count, LANES), F32)],
        compiler_params=params(),
        cost_estimate=work(15),
        name="grid_scatter",
    )(*((index, feats) if fresh else (index, feats, old)))


TOP, BOTTOM, EVEN, FIRST_ROW, EDGE_SHIFT, PLACE = range(6)


def list_cells(columns, edge_ref, feat_ref, spots, owns):
    sources = feat_ref.shape[0] // (CAP + EDGE_CAP + 48)
    main = CAP // LANES
    tall = BLOCK_ROWS + 2 * HALO
    for a in range(sources):
        base = a * (CAP + EDGE_CAP + 48)
        words = feat_ref[base + CAP : base + CAP + 32, :].astype(F32).astype(jnp.int32)
        start = base + CAP + 32 + EDGE_CAP
        edges = feat_ref[start : start + 16, :].astype(F32).astype(jnp.int32)
        for side, (high, half, mixed) in enumerate(
            (
                (words[0:main], words[main : 2 * main], words[2 * main : 3 * main]),
                (edges[0:1], edges[1:2], edges[2:3]),
            )
        ):
            line = (mixed >> 1) - edge_ref[FIRST_ROW]
            if side:
                line = line + edge_ref[EDGE_SHIFT]
            cross = half * 2 + (mixed & 1)
            inside = (high > 0) & (line >= -HALO) & (line < BLOCK_ROWS + HALO)
            spot = ((high - 1) * tall + line + HALO) * columns + cross
            spot = jnp.where(inside, spot, DEPTH * tall * columns)
            if side:
                spots[a * (main + 1) + main : (a + 1) * (main + 1), :] = spot
                continue
            spots[a * (main + 1) : a * (main + 1) + main, :] = spot
            inside = (high > 0) & (line >= 0) & (line < BLOCK_ROWS)
            spot = ((high - 1) * BLOCK_ROWS + line) * columns + cross
            owns[a * main : (a + 1) * main, :] = jnp.where(
                inside, spot, DEPTH * BLOCK_ROWS * columns
            )


def scatter_middle_kernel(
    columns, edge_ref, feat_ref, kernel_ref, bias_ref, grid_ref, out_ref, own_ref,
    wide, rows, held, weight_ref, spots, index, copied, done,
):
    list_cells(columns, edge_ref, feat_ref, spots, own_ref)
    to_scalar = pltpu.make_async_copy(spots, index, copied)
    to_scalar.start()
    clear(wide, held.shape[0])
    rows[...] = feat_ref[...].astype(F32)
    to_scalar.wait()
    blocks = CAP // LANES + 1
    length = CAP + EDGE_CAP + 48

    def place(part, carry):
        block = part % blocks
        base = part // blocks * length + block * LANES + jnp.where(block == blocks - 1, 32, 0)

        base = pl.multiple_of(base, 8)
        for j in range(LANES):
            wide[pl.ds(index[part, j], 1), :] = rows[pl.ds(base + j, 1), :]
        return carry

    lax.fori_loop(0, index.shape[0], place, 0)
    narrow(wide, held)
    copy = pltpu.make_async_copy(held, grid_ref, done)
    copy.start()
    middle_kernel(columns, edge_ref, held, kernel_ref, bias_ref, out_ref, weight_ref)
    copy.wait()


def scatter_middle(edges, feats, w_mid, bias, columns):
    cells = DEPTH * (BLOCK_ROWS + 2 * HALO) * columns
    count = feats.shape[0]
    sources = count // (CAP + EDGE_CAP + 48)
    parts = sources * (CAP // LANES + 1)
    return pl.pallas_call(
        functools.partial(scatter_middle_kernel, columns),
        out_shape=(
            jax.ShapeDtypeStruct((cells, LANES), BF16),
            jax.ShapeDtypeStruct(((BLOCK_ROWS + 2) * columns, PAIRS * LANES), BF16),
            jax.ShapeDtypeStruct((sources * CAP // LANES, LANES), jnp.int32),
        ),
        in_specs=smem(1) + vmem(3),
        out_specs=[pl.BlockSpec(memory_space=pl.ANY)] + vmem(2),
        scratch_shapes=[
            pltpu.VMEM((cells + 8, LANES), F32),
            pltpu.VMEM((count, LANES), F32),
            pltpu.VMEM((cells, LANES), BF16),
            pltpu.VMEM((2, 9 * LANES, 2 * LANES), BF16),
            pltpu.VMEM((parts, LANES), jnp.int32),
            pltpu.SMEM((parts, LANES), jnp.int32),
            pltpu.SemaphoreType.DMA,
            pltpu.SemaphoreType.DMA,
        ],
        compiler_params=params(limit=57),
        cost_estimate=work(36),
        name="scatter_middle",
    )(edges, feats, w_mid, bias)


def middle_kernel(columns, edge_ref, grid_ref, kernel_ref, bias_ref, out_ref, weight_ref):
    low = low_lanes(columns)
    none = jnp.zeros((LANES, LANES // 2), BF16)
    for place in range(9):
        one, two, three = (
            kernel_ref[place * 3 + e].astype(F32).T.astype(BF16) for e in range(3)
        )
        rows = slice(place * LANES, (place + 1) * LANES)
        weight_ref[0, rows, :] = jnp.concatenate([one, two, three, none], axis=1)
        weight_ref[1, rows, :] = jnp.concatenate([two, one, none, three], axis=1)
    grid_rows = BLOCK_ROWS + 2 * HALO
    depth_out = DEPTH // 2

    def row(m, carry):
        sums = []
        for o in range(depth_out):
            taps = (1, 2) if o == 0 else (0, 1, 2)
            left = jnp.concatenate(
                [
                    grid_ref[at_row((2 * o + a - 1) * grid_rows + m + b, columns), :]
                    for a in taps
                    for b in range(3)
                ],
                axis=1,
            )
            right = weight_ref[o % 2, 3 * LANES * (3 - len(taps)) :, :]
            sums.append(jnp.dot(left, right, preferred_element_type=F32))
        inside = (m > 0) & (m < BLOCK_ROWS + 1) | (m == 0) & (edge_ref[0] > 0)
        inside = inside | (m == BLOCK_ROWS + 1) & (edge_ref[1] > 0)
        keep = jnp.where(inside, 1.0, 0.0)
        for j in range(PAIRS):
            even = sums[2 * j]
            if 2 * j + 1 < depth_out:
                odd = sums[2 * j + 1]
                first = jnp.where(low, even[:, :LANES], odd[:, :LANES])
                middle = jnp.where(low, odd[:, :LANES], even[:, :LANES])
                last = even[:, LANES:] + odd[:, LANES:]
            else:
                first = even[:, :LANES]
                middle = first
                last = even[:, LANES:]
            total = from_left(first) + pltpu.roll(middle, LANES // 2, 1) + from_right(last)
            total = jnp.maximum(total + bias_ref[0:1, :], 0.0) * keep
            if 2 * j + 1 == depth_out:
                total = jnp.where(low, total, 0.0)
            out_ref[at_row(m, columns), j * LANES : (j + 1) * LANES] = total.astype(BF16)
        return carry

    lax.fori_loop(0, BLOCK_ROWS + 2, row, 0, unroll=2)


def middle_forward(edges, grid, w_mid, bias, columns):
    return pl.pallas_call(
        functools.partial(middle_kernel, columns),
        out_shape=jax.ShapeDtypeStruct(((BLOCK_ROWS + 2) * columns, PAIRS * LANES), BF16),
        in_specs=smem(1) + vmem(3),
        out_specs=vmem(1)[0],
        scratch_shapes=[pltpu.VMEM((2, 9 * LANES, 2 * LANES), BF16)],
        compiler_params=params(),
        cost_estimate=work(26),
        name="middle_forward",
    )(edges, grid, w_mid, bias)


def row_above(edge_ref, beside_ref, across_ref, lanes):
    found = jnp.where(
        edge_ref[EVEN] > 0, across_ref[:, lanes].astype(F32), beside_ref[:, lanes].astype(F32)
    )
    return jnp.where(edge_ref[TOP] > 0, found, 0.0)


def row_below(edge_ref, beside_ref, across_ref, lanes):
    found = jnp.where(
        edge_ref[EVEN] > 0, beside_ref[:, lanes].astype(F32), across_ref[:, lanes].astype(F32)
    )
    return jnp.where(edge_ref[BOTTOM] > 0, found, 0.0)


def put_edges(edge_ref, beside_ref, across_ref, first, last):
    if first is not None:

        @pl.when(edge_ref[EVEN] > 0)
        def _():
            across_ref[...] = first

        @pl.when(edge_ref[EVEN] == 0)
        def _():
            beside_ref[...] = first

    if last is not None:

        @pl.when(edge_ref[EVEN] > 0)
        def _():
            beside_ref[...] = last

        @pl.when(edge_ref[EVEN] == 0)
        def _():
            across_ref[...] = last


def column_taps(own, j):
    low = low_lanes(own.shape[0])
    other = pltpu.roll(own, LANES // 2, 1)
    both = [jnp.where(low, own, other)]
    if 2 * j + 1 < DEPTH // 2:
        both.append(jnp.where(low, other, own))
    return [(jnp.where(low, from_right(x), x), from_left(x)) for x in both]


def middle_data_kernel(
    count, columns, sources, index_ref, edge_ref, d_ref, beside_ref, across_ref, kernel_ref, *refs
):
    out_refs, (near, far, wide, rows, weight_ref) = refs[:sources], refs[sources:]
    padded = BLOCK_ROWS + 2
    half = LANES // 2
    cells = DEPTH * BLOCK_ROWS * columns
    span = 10 * half
    for a, first, side in ((1, 0, 0), (2, 0, 1), (0, span, 1)):
        lanes = slice(side * LANES, (side + 1) * LANES)
        for b in range(3):
            for e in range(3):
                block = (2 - b) * 2 + e if e < 2 else 6 + 2 - b
                own = kernel_ref[(a * 3 + b) * 3 + e]
                weight_ref[first + block * half : first + (block + 1) * half, lanes] = own
        weight_ref[first + span - half : first + span, lanes] = jnp.zeros((half, LANES), BF16)
    weight_ref[span:, :LANES] = jnp.zeros((span, LANES), BF16)

    def build(r, load):
        for j in range(PAIRS):
            own = load(slice(j * LANES, (j + 1) * LANES))
            for k, (pair, left) in enumerate(column_taps(own, j)):
                o = 2 * j + k
                near[o, at_row(r, columns), :] = pair.astype(BF16)
                far[o, at_row(r, columns), 0:half] = left[:, 0:half].astype(BF16)
                if not (isinstance(r, int) and r == 0):
                    far[o, at_row(r - 1, columns), half:LANES] = left[:, half:].astype(BF16)

    def build_own(r):
        build(r + 1, lambda lanes: d_ref[at_row(r, columns), lanes].astype(F32))

    build(0, lambda lanes: row_above(edge_ref, beside_ref, across_ref, lanes))
    for r in range(3):
        build_own(r)
    for o in range(DEPTH // 2):
        far[o, (padded - 1) * columns :, half:LANES] = jnp.zeros((columns, half), BF16)

    def row(r):
        def pieces(o):
            return [near[o, at_row(r + i, columns), :] for i in range(3)] + [
                far[o, at_row(r + i, columns), :] for i in (0, 2)
            ]

        for o in range(DEPTH // 2):
            left = jnp.concatenate(pieces(o) + (pieces(o + 1) if o < DEPTH // 2 - 1 else []), axis=1)
            total = jnp.dot(left, weight_ref[0 : left.shape[1], :], preferred_element_type=F32)
            wide[at_row(2 * o * BLOCK_ROWS + r, columns), :] = total[:, :LANES]
            wide[at_row((2 * o + 1) * BLOCK_ROWS + r, columns), :] = total[:, LANES:]

    def row_and_build(r, carry):
        row(r)
        build_own(r + 3)
        return carry

    lax.fori_loop(0, BLOCK_ROWS - 3, row_and_build, 0)
    row(BLOCK_ROWS - 3)
    build(BLOCK_ROWS + 1, lambda lanes: row_below(edge_ref, beside_ref, across_ref, lanes))
    row(BLOCK_ROWS - 2)
    row(BLOCK_ROWS - 1)
    wide[cells:, :] = jnp.zeros((8, LANES), F32)

    length = count // sources
    lines = length // LANES

    def pick(part, carry):
        source = lax.rem(edge_ref[PLACE] + part // lines, sources) * lines + part % lines
        base = pl.multiple_of(part * LANES, LANES)
        for j in range(LANES):
            rows[pl.ds(base + j, 1), :] = wide[pl.ds(index_ref[source, j], 1), :]
        return carry

    lax.fori_loop(0, count // LANES, pick, 0)
    for k, out_ref in enumerate(out_refs):
        out_ref[...] = rows[k * length : (k + 1) * length, :].astype(BF16)


def middle_data(index, edges, d_rows, beside, across, w_mid, columns):
    count = index.size
    sources = count // CAP
    padded = (BLOCK_ROWS + 2) * columns
    return pl.pallas_call(
        functools.partial(middle_data_kernel, count, columns, sources),
        out_shape=[jax.ShapeDtypeStruct((CAP, LANES), BF16)] * sources,
        in_specs=smem(2) + vmem(4),
        out_specs=vmem(sources),
        scratch_shapes=[
            pltpu.VMEM((DEPTH // 2, padded, LANES), BF16),
            pltpu.VMEM((DEPTH // 2, padded, LANES), BF16),
            pltpu.VMEM((DEPTH * BLOCK_ROWS * columns + 8, LANES), F32),
            pltpu.VMEM((count, LANES), F32),
            pltpu.VMEM((10 * LANES, 2 * LANES), BF16),
        ],
        compiler_params=params(limit=50),
        cost_estimate=work(30),
        name="middle_data",
    )(index, edges, d_rows, beside, across, w_mid)


def middle_weight_kernel(
    columns, grid_hbm, d_ref, out_ref, total, taps_ref, turned, grid_ref, arrived
):
    grid_rows = BLOCK_ROWS + 2 * HALO
    half = LANES // 2

    def copy(i):
        ahead = 2 if isinstance(i, int) and i == 0 else 0
        parts = []
        for d in range(DEPTH):
            begin = (d * grid_rows + 2 * i + 3 - ahead) * columns
            rows = pl.ds(begin if isinstance(i, int) else pl.multiple_of(begin, 32), (2 + ahead) * columns)
            parts.append(
                pltpu.make_async_copy(grid_hbm.at[rows, :], grid_ref.at[rows, :], arrived.at[i, d])
            )
        return parts

    for i in range(BLOCK_ROWS // 2):
        for part in copy(i):
            part.start()
    total[...] = jnp.zeros_like(total)
    for part in copy(0):
        part.wait()

    def rows(i, carry):
        @pl.when(i > 0)
        def _():
            for part in copy(i):
                part.wait()

        for k in range(2):
            for j in range(PAIRS):
                own = d_ref[at_row(i * 2 + k, columns), j * LANES : (j + 1) * LANES].astype(F32)
                for n, (pair, left) in enumerate(column_taps(own, j)):
                    place = slice(k * columns, (k + 1) * columns)
                    taps_ref[2 * j + n, place, 0:LANES] = pair.astype(BF16)
                    taps_ref[2 * j + n, place, LANES:] = left.astype(BF16)
        for o in range(DEPTH // 2):
            depth_taps = (1, 2) if o == 0 else (0, 1, 2)
            cells = jnp.concatenate(
                [
                    grid_ref[
                        pl.ds(
                            pl.multiple_of(
                                ((2 * o + a - 1) * grid_rows + i * 2 + 1 + b) * columns, 32
                            ),
                            2 * columns,
                        ),
                        :,
                    ]
                    for a in depth_taps
                    for b in range(3)
                ],
                axis=1,
            )
            part = lax.dot_general(
                taps_ref[o], cells, (((0,), (0,)), ((), ())), preferred_element_type=F32
            )
            if o == 0:
                total[:, 3 * LANES :] += part
            else:
                total[...] += part
        return carry

    lax.fori_loop(0, BLOCK_ROWS // 2, rows, 0, unroll=2)
    low = low_lanes(LANES // 2)
    for place in range(9):
        for side in range(2):
            turned[...] = total[
                side * LANES : (side + 1) * LANES, place * LANES : (place + 1) * LANES
            ].T
            even = turned[pl.ds(0, half, stride=2), :]
            odd = turned[pl.ds(1, half, stride=2), :]
            at = (place * 3 + side * 2) * half
            out_ref[at : at + half, :] = jnp.where(low, even, pltpu.roll(odd, half, 1))
            if side == 0:
                out_ref[at + half : at + 2 * half, :] = jnp.where(
                    low, pltpu.roll(even, half, 1), odd
                )


def middle_weight(grid, d_rows, columns):
    return pl.pallas_call(
        functools.partial(middle_weight_kernel, columns),
        out_shape=jax.ShapeDtypeStruct((27 * LANES // 2, LANES), F32),
        in_specs=[pl.BlockSpec(memory_space=pl.ANY)] + vmem(1),
        out_specs=vmem(1)[0],
        scratch_shapes=[
            pltpu.VMEM((2 * LANES, 9 * LANES), F32),
            pltpu.VMEM((DEPTH // 2, 2 * columns, 2 * LANES), BF16),
            pltpu.VMEM((LANES, LANES), F32),
            pltpu.VMEM(grid.shape, BF16),
            pltpu.SemaphoreType.DMA((BLOCK_ROWS // 2, DEPTH)),
        ],
        compiler_params=params(limit=32),
        cost_estimate=work(26),
        name="middle_weight",
    )(grid, d_rows)


def region_kernel(
    columns,
    scale_ref,
    edge_ref,
    bev_ref,
    weight_ref,
    bias_ref,
    head_ref,
    labels_ref,
    targets_ref,
    d_ref,
    beside_ref,
    across_ref,
    grad_head_ref,
    sums_ref,
    held,
):
    outs = head_ref.shape[0]
    cells = d_ref.shape[0]
    span = cells // 3
    scale = scale_ref[0, 0]
    head = head_ref[...]
    head_three = jnp.concatenate([head, head, head], axis=0)
    own = lax.broadcasted_iota(jnp.int32, (outs, LANES), 0)
    own = own == lax.broadcasted_iota(jnp.int32, (outs, LANES), 1)
    head_bias = jnp.sum(jnp.where(own, bias_ref[2:3, :], 0.0), axis=1, keepdims=True)

    def row(r, carry):
        left = jnp.concatenate([bev_ref[at_row(r + b, columns), :] for b in range(3)], axis=1)
        part = jnp.dot(left, weight_ref[...], preferred_element_type=F32)
        pre = from_left(part[:, :LANES]) + part[:, LANES : 2 * LANES]
        held[at_row(r, columns), :] = pre + from_right(part[:, 2 * LANES :]) + bias_ref[1:2, :]
        return carry

    lax.fori_loop(0, cells // columns, row, 0, unroll=2)
    kind = lax.broadcasted_iota(jnp.int32, (outs, span), 0) % 8 == 0
    grad_head = jnp.zeros((3 * outs, LANES), F32)
    head_sum = jnp.zeros((outs, 1), F32)
    loss_sum = jnp.zeros((outs, 1), F32)
    row_sum = jnp.zeros((8, LANES), F32)
    for i in range(3):
        place = slice(i * span, (i + 1) * span)
        pre = held[place, :]
        act = jnp.maximum(pre, 0.0).astype(BF16)
        heads = lax.dot_general(head, act, (((1,), (1,)), ((), ())), preferred_element_type=F32)
        heads = heads + head_bias
        label = labels_ref[:, place]
        positive = jnp.where(label == 1, 1.0, 0.0)
        negative = jnp.where(label == 0, 1.0, 0.0)
        tail = jnp.log1p(jnp.exp(-jnp.abs(heads)))
        soft_up = jnp.maximum(heads, 0.0) + tail
        soft_down = jnp.maximum(-heads, 0.0) + tail
        probab = jax.nn.sigmoid(heads)
        rest = 1.0 - probab
        focal = positive * FOCAL_ALPHA * rest * rest * soft_down
        focal = focal + negative * (1.0 - FOCAL_ALPHA) * probab * probab * soft_up
        d_focal = positive * FOCAL_ALPHA * rest * rest * (-2.0 * probab * soft_down - rest)
        d_focal = d_focal + negative * (1.0 - FOCAL_ALPHA) * probab * probab * (
            2.0 * rest * soft_up + probab
        )
        offset = heads - targets_ref[:, place]
        size = jnp.abs(offset)
        near = size < 1.0 / 9.0
        smooth = jnp.where(near, 4.5 * offset * offset, size - 1.0 / 18.0)
        d_smooth = jnp.where(near, 9.0 * offset, jnp.where(offset > 0.0, 1.0, -1.0))
        losses = jnp.where(kind, focal, 2.0 * positive * smooth)
        loss_sum = loss_sum + jnp.sum(losses, axis=1, keepdims=True)
        d_heads = jnp.where(kind, d_focal, 2.0 * positive * d_smooth) * scale
        head_sum = head_sum + jnp.sum(d_heads, axis=1, keepdims=True)
        high = d_heads.astype(BF16)
        rest_one = d_heads - high.astype(F32)
        mid = rest_one.astype(BF16)
        tiny = (rest_one - mid.astype(F32)).astype(BF16)
        three = jnp.concatenate([high, mid, tiny], axis=0)
        grad_head = grad_head + jnp.dot(three, act, preferred_element_type=F32)
        d_act = lax.dot_general(
            three, head_three, (((0,), (0,)), ((), ())), preferred_element_type=F32
        )
        d_pre = jnp.where(pre > 0.0, d_act, 0.0).astype(BF16)
        d_ref[place, :] = d_pre
        row_sum = row_sum + jnp.sum(d_pre.astype(F32).reshape(span // 8, 8, LANES), axis=0)
        if i == 0:
            put_edges(edge_ref, beside_ref, across_ref, d_pre[:columns, :], None)
        if i == 2:
            put_edges(edge_ref, beside_ref, across_ref, None, d_pre[span - columns :, :])
    grad_head_ref[...] = grad_head
    sums_ref[0:8, :] = row_sum
    sums_ref[8:24, :] = jnp.broadcast_to(head_sum, (outs, LANES))
    sums_ref[24:32, :] = jnp.broadcast_to(jnp.sum(loss_sum, axis=0, keepdims=True), (8, LANES))


def region_forward(scale, edges, bev, weights, bias, head, labels, targets, columns):
    cells = labels.shape[1]
    outs = head.shape[0]
    return pl.pallas_call(
        functools.partial(region_kernel, columns),
        out_shape=(
            jax.ShapeDtypeStruct((cells, LANES), BF16),
            jax.ShapeDtypeStruct((columns, LANES), BF16),
            jax.ShapeDtypeStruct((columns, LANES), BF16),
            jax.ShapeDtypeStruct((3 * outs, LANES), F32),
            jax.ShapeDtypeStruct((32, LANES), F32),
        ),
        in_specs=smem(2) + vmem(6),
        out_specs=vmem(5),
        scratch_shapes=[pltpu.VMEM((cells, LANES), F32)],
        compiler_params=params(limit=28),
        cost_estimate=work(16),
        name="region_forward",
    )(
        scale.reshape(1, 1),
        edges,
        bev,
        weights,
        bias,
        head,
        labels,
        targets,
    )


def region_order_kernel(blocks, anc_ref, *refs):
    part_refs, (in_ref, back_ref, wide, lined) = refs[:blocks], refs[blocks:]
    depth_out = DEPTH // 2
    half = LANES // 2
    width = PAIRS * LANES
    share = half // blocks
    used = depth_out * half
    for b in range(3):
        for e in range(3):
            for k, part_ref in enumerate(part_refs):
                first = lax.rem(anc_ref[0] + k, blocks) * share
                wide[...] = part_ref[b, e].astype(F32)
                for h in range(depth_out):
                    at = pl.multiple_of(h * half + first, 8)
                    lined[pl.ds(at, share), :] = wide[pl.ds(h, share, stride=depth_out), :]
            lined[used:, :] = jnp.zeros((width - used, LANES), F32)
            in_ref[b * width : (b + 1) * width, e * LANES : (e + 1) * LANES] = lined[...].astype(
                BF16
            )
            at = (b * 3 + e) * LANES
            back_ref[at : at + LANES, :] = lined[...].T.astype(BF16)


def region_order(anc, parts):
    width = PAIRS * LANES
    return pl.pallas_call(
        functools.partial(region_order_kernel, len(parts)),
        out_shape=(
            jax.ShapeDtypeStruct((3 * width, 3 * LANES), BF16),
            jax.ShapeDtypeStruct((9 * LANES, width), BF16),
        ),
        in_specs=smem(1) + vmem(len(parts)),
        out_specs=vmem(2),
        scratch_shapes=[
            pltpu.VMEM((parts[0].shape[2], LANES), F32),
            pltpu.VMEM((width, LANES), F32),
        ],
        compiler_params=params(limit=24),
        cost_estimate=work(4),
        name="region_order",
    )(anc, *parts)


def region_data_kernel(
    columns, edge_ref, d_ref, beside_in, across_in, bev_ref, weight_ref,
    out_ref, beside_ref, across_ref, sums_ref, taps_ref,
):
    rows = out_ref.shape[0] // columns
    width = PAIRS * LANES
    sums_ref[...] = jnp.zeros_like(sums_ref)

    def build(r, own):
        taps_ref[at_row(r, columns), 0:LANES] = from_right(own).astype(BF16)
        taps_ref[at_row(r, columns), LANES : 2 * LANES] = own.astype(BF16)
        taps_ref[at_row(r, columns), 2 * LANES :] = from_left(own).astype(BF16)

    def build_own(r):
        build(r + 1, d_ref[at_row(r, columns), :].astype(F32))

    build(0, row_above(edge_ref, beside_in, across_in, slice(None)))
    build_own(0)
    build_own(1)

    def row(r):
        left = jnp.concatenate([taps_ref[at_row(r + 2 - b, columns), :] for b in range(3)], axis=1)
        total = jnp.dot(left, weight_ref[...], preferred_element_type=F32)
        alive = bev_ref[at_row(r + 1, columns), :].astype(F32) > 0.0
        kept = jnp.where(alive, total, 0.0).astype(BF16)
        out_ref[at_row(r, columns), :] = kept

        sums_ref[...] += jnp.sum(kept.astype(F32).reshape(columns // 8, 8, width), axis=0)
        return kept

    def row_and_build(r, carry):
        row(r)
        build_own(r + 2)
        return carry

    put_edges(edge_ref, beside_ref, across_ref, row(0), None)
    build_own(2)
    lax.fori_loop(1, rows - 2, row_and_build, 0)
    row(rows - 2)
    build(rows + 1, row_below(edge_ref, beside_in, across_in, slice(None)))
    put_edges(edge_ref, beside_ref, across_ref, None, row(rows - 1))


def region_data(edges, d_rows, beside, across, bev, weights, columns):
    width = PAIRS * LANES
    return pl.pallas_call(
        functools.partial(region_data_kernel, columns),
        out_shape=(
            jax.ShapeDtypeStruct((d_rows.shape[0], width), BF16),
            jax.ShapeDtypeStruct((columns, width), BF16),
            jax.ShapeDtypeStruct((columns, width), BF16),
            jax.ShapeDtypeStruct((8, width), F32),
        ),
        in_specs=smem(1) + vmem(5),
        out_specs=vmem(4),
        scratch_shapes=[pltpu.VMEM((d_rows.shape[0] + 2 * columns, 3 * LANES), BF16)],
        compiler_params=params(limit=28),
        cost_estimate=work(13),
        name="region_data",
    )(edges, d_rows, beside, across, bev, weights)


def region_weight_kernel(columns, blocks, d_ref, bev_ref, out_ref, total, taps_ref):
    rows = d_ref.shape[0] // columns
    width = PAIRS * LANES
    depth_out = DEPTH // 2
    half = LANES // 2
    total[...] = jnp.zeros_like(total)

    def two(i, carry):
        for k in range(2):
            own = d_ref[at_row(i * 2 + k, columns), :].astype(F32)
            place = slice(k * columns, (k + 1) * columns)
            taps_ref[place, 0:LANES] = from_right(own).astype(BF16)
            taps_ref[place, LANES : 2 * LANES] = own.astype(BF16)
            taps_ref[place, 2 * LANES :] = from_left(own).astype(BF16)
        cells = jnp.concatenate(
            [
                bev_ref[pl.ds(pl.multiple_of((i * 2 + b) * columns, 32), 2 * columns), :]
                for b in range(3)
            ],
            axis=1,
        )
        total[...] += lax.dot_general(
            taps_ref[...], cells, (((0,), (0,)), ((), ())), preferred_element_type=F32
        )
        return carry

    lax.fori_loop(0, rows // 2, two, 0, unroll=2)
    share = half // blocks
    for b in range(3):
        for e in range(3):
            for j in range(PAIRS):
                start = b * width + j * LANES
                turned = total[e * LANES : (e + 1) * LANES, start : start + LANES].T
                for k in range(min(2, depth_out - 2 * j)):
                    for q in range(blocks):
                        begin = k * half + q * share
                        base = ((q * 3 + b) * 3 + e) * share * depth_out
                        out_ref[pl.ds(base + 2 * j + k, share, stride=depth_out), :] = turned[
                            begin : begin + share, :
                        ]


def region_weight(d_own, bev, columns, blocks):
    width = PAIRS * LANES
    return pl.pallas_call(
        functools.partial(region_weight_kernel, columns, blocks),
        out_shape=jax.ShapeDtypeStruct((9 * (DEPTH // 2) * (LANES // 2), LANES), F32),
        in_specs=vmem(2),
        out_specs=vmem(1)[0],
        scratch_shapes=[
            pltpu.VMEM((3 * LANES, 3 * width), F32),
            pltpu.VMEM((2 * columns, 3 * LANES), BF16),
        ],
        compiler_params=params(limit=28),
        cost_estimate=work(10),
        name="region_weight",
    )(d_own, bev)


def prepare_kernel(
    slots, anc_count, device_rows, edge_ref, points_ref, line_ref, labels_ref,
    stats_ref, place_ref, digit_ref,
):
    voxels, width = points_ref.shape
    features = 7
    row = line_ref[1:2, :]
    exists = line_ref[3:4, :]
    column = line_ref[2:3, :]
    digits = jnp.concatenate(
        [
            (line_ref[0:1, :] + 1) * exists,
            (column >> 1) * exists,
            (row * 2 + (column & 1)) * exists,
            line_ref[4:5, :],
        ],
        axis=0,
    ).astype(F32)
    none = jnp.zeros((LANES - 4, LANES), F32)
    for i in range(voxels // LANES):
        here = slice(i * LANES, (i + 1) * LANES)
        digit_ref[here, :] = jnp.concatenate([digits[:, here], none], axis=0).T.astype(BF16)
    lane = lax.broadcasted_iota(jnp.int32, (CHUNK, width), 1)
    ones_lane = features * slots
    slot = jnp.where(lane == ones_lane, -1, lane % slots)
    total = jnp.zeros((width, width), F32)
    for i in range(voxels // CHUNK):
        here = slice(i * CHUNK, (i + 1) * CHUNK)
        count = digit_ref[here, 3:4].astype(F32).astype(jnp.int32)
        block = jnp.where(slot < count, points_ref[here, :].astype(F32), 0.0).astype(BF16)
        total = total + lax.dot_general(
            block, block, (((0,), (0,)), ((), ())), preferred_element_type=F32
        )
    row_at = lax.broadcasted_iota(jnp.int32, (width, width), 0)
    col_at = lax.broadcasted_iota(jnp.int32, (width, width), 1)
    same = (row_at % slots == col_at % slots) | (row_at == ones_lane)
    total = jnp.where(same & (row_at <= ones_lane) & (col_at < ones_lane), total, 0.0)
    rows = [
        jnp.sum(jnp.where(row_at // slots == k, total, 0.0), axis=0, keepdims=True)
        for k in range(features + 1)
    ]
    stacked = jnp.concatenate(rows, axis=0)
    col_eight = lax.broadcasted_iota(jnp.int32, (8, width), 1)
    lane_eight = lax.broadcasted_iota(jnp.int32, (8, LANES), 1)
    row_eight = lax.broadcasted_iota(jnp.int32, (8, LANES), 0)
    stats = jnp.zeros((8, LANES), F32)
    for k in range(features):
        picked = jnp.sum(jnp.where(col_eight // slots == k, stacked, 0.0), axis=1, keepdims=True)
        stats = stats + jnp.where(lane_eight == k, picked, 0.0)
    counted = jnp.sum(digits[3:4, :], axis=1, keepdims=True)
    hits = jnp.zeros(labels_ref.shape[1:], F32)
    for r in range(labels_ref.shape[0]):
        hits = hits + jnp.where(labels_ref[r] == 1, 1.0, 0.0)
    found = jnp.sum(jnp.sum(hits, axis=1, keepdims=True), axis=0, keepdims=True)
    real = exists > 0
    lists = []
    for q in range(anc_count):
        begin = q * device_rows - HALO
        lists.append(real & (row >= begin) & (row < begin + device_rows + 2 * HALO))
    lists.append(real & (row < HALO) & (edge_ref[0] > 0))
    lists.append(real & (row >= anc_count * device_rows - HALO) & (edge_ref[1] > 0))
    lists += [real & (row < 0)] * (8 - len(lists))
    member = jnp.concatenate([jnp.where(x, 1.0, 0.0) for x in lists], axis=0)
    before = (
        lax.broadcasted_iota(jnp.int32, (LANES, LANES), 0)
        < lax.broadcasted_iota(jnp.int32, (LANES, LANES), 1)
    )
    before = jnp.where(before, 1.0, 0.0).astype(BF16)
    carry = jnp.zeros((8, 1), F32)
    eight = lax.broadcasted_iota(jnp.int32, (8, LANES), 0)
    for i in range(place_ref.shape[1] // LANES):
        here = slice(i * LANES, (i + 1) * LANES)
        part = member[:, here]
        ahead = jnp.dot(part.astype(BF16), before, preferred_element_type=F32) + carry
        places = jnp.where(part > 0.0, ahead, -1.0).astype(jnp.int32)
        owner = jnp.zeros((1, LANES), jnp.int32)
        own = jnp.full((1, LANES), -1, jnp.int32)
        for q in range(anc_count):
            mine = (row[:, here] >= q * device_rows) & (row[:, here] < (q + 1) * device_rows)
            mine = mine & real[:, here]
            owner = jnp.where(mine, q, owner)
            own = jnp.where(mine, places[q : q + 1, :], own)
        places = jnp.where(eight == 6, owner, jnp.where(eight == 7, own, places))
        place_ref[:, here] = places
        carry = carry + jnp.sum(part, axis=1, keepdims=True)
    is_edge = lax.broadcasted_iota(jnp.int32, (8, 1), 0) >= anc_count
    need = carry / jnp.where(is_edge, float(EDGE_CAP), float(CAP))
    need = jnp.max(need, axis=0, keepdims=True)
    for k, value in enumerate((counted, found, need)):
        stats = stats + jnp.where((lane_eight == 8) & (row_eight == k), value, 0.0)
    for i in range(stats_ref.shape[0]):
        stats_ref[i] = stats


def prepare(edges, points, lines, labels, anc_count, device_rows, slots, devices):
    voxels = points.shape[0]
    return pl.pallas_call(
        functools.partial(prepare_kernel, slots, anc_count, device_rows),
        out_shape=(
            jax.ShapeDtypeStruct((devices, 8, LANES), F32),
            jax.ShapeDtypeStruct(lines.shape, jnp.int32),
            jax.ShapeDtypeStruct((voxels, LANES), BF16),
        ),
        in_specs=smem(1) + vmem(3),
        out_specs=vmem(3),
        compiler_params=params(limit=24),
        cost_estimate=work(4),
        name="prepare",
    )(edges, points, lines, labels)


def batch_norm(stats, kernel):
    lanes = kernel.shape[1]
    moments = stats[:, 0:8]
    count = stats[0:1, 8:9]
    mixed = jnp.zeros((8, lanes), F32)
    for k in range(7):
        mixed = mixed + moments[:, k : k + 1] * kernel[k : k + 1, :]
    mean = mixed[7:8, :] / count
    second = jnp.sum(mixed * kernel, axis=0, keepdims=True) / count
    inv_std = lax.rsqrt(second - mean * mean + BN_EPSILON)
    return mixed, mean, inv_std, count


def first_layer(points, first_ref, scale, offset, valid):
    hidden = jnp.dot(points, first_ref[...], preferred_element_type=F32)
    act = jnp.where(valid, jnp.maximum(hidden * scale + offset, 0.0), 0.0)
    return act


def group_fold(values, combine):
    groups = values.shape[1] // LANES
    out = values[:, :LANES]
    for g in range(1, groups):
        out = combine(out, values[:, g * LANES : (g + 1) * LANES])
    out = combine(out, pltpu.roll(out, 32, 1))
    return combine(out, pltpu.roll(out, 64, 1))


def second_tail(pooled):
    lane = lax.broadcasted_iota(jnp.int32, pooled.shape, 1)
    return jnp.where(lane < 32, pooled, jnp.where(lane == 32, 1.0, 0.0))


def group_left(low, tail, count, g):
    lane = lax.broadcasted_iota(jnp.int32, tail.shape, 1)
    marked = (lane > 32) & (lane < 37) & (lane - (33 - 4 * g) >= count)
    side = jnp.where(marked, 1.0, tail).astype(BF16)
    return jnp.concatenate([low[:, g * LANES : (g + 1) * LANES], side], axis=1)


def encode_kernel(
    slots, points_ref, count_ref, stats_ref, kernel_ref, gain_ref, first_ref, second_ref,
    feat_ref, share_ref, slot_ref, held,
):
    lanes = first_ref.shape[1]
    _, mean, inv_std, _ = batch_norm(jnp.sum(stats_ref[...], axis=0), kernel_ref[...])
    scale = gain_ref[0:1, :] * inv_std
    offset = gain_ref[1:2, :] - mean * scale
    count = count_ref[:, 3:4].astype(F32).astype(jnp.int32)
    slot = lax.broadcasted_iota(jnp.int32, (CHUNK, lanes), 1) // 32
    act = first_layer(points_ref[...], first_ref, scale, offset, slot < count)
    tail = second_tail(group_fold(act, jnp.maximum))
    low = act.astype(BF16)
    top = jnp.full((CHUNK, LANES), -jnp.inf, F32)
    for g in range(lanes // LANES):
        left = group_left(low, tail, count, g)
        part = jnp.dot(left, second_ref[...], preferred_element_type=F32)
        for s in range(min(4, slots - 4 * g)):
            p = 4 * g + s
            one = part[:, s * LANES : (s + 1) * LANES]
            held[p] = one
            top = jnp.maximum(top, one)
    code = jnp.zeros((CHUNK, LANES), F32)
    for p in range(slots):
        code = code + jnp.where(held[p] == top, 2048.0 + p, 0.0)
    ties = jnp.floor(code / 2048.0)
    feat_ref[...] = jnp.maximum(top, 0.0)
    share_ref[...] = jnp.where(top > 0.0, 1.0 / ties, 0.0)
    slot_ref[...] = jnp.minimum(code - 2048.0 * ties, 127.0).astype(BF16)


def encode(points, counts, stats, kernel, gain, first, second, slots):
    voxels, width = points.shape
    lanes = first.shape[1]
    whole = lambda *shape: pl.BlockSpec(shape, lambda i: (0,) * len(shape))
    block = lambda size: pl.BlockSpec((CHUNK, size), lambda i: (i, 0))
    return pl.pallas_call(
        functools.partial(encode_kernel, slots),
        grid=(voxels // CHUNK,),
        out_shape=(
            jax.ShapeDtypeStruct((voxels, LANES), F32),
            jax.ShapeDtypeStruct((voxels, LANES), F32),
            jax.ShapeDtypeStruct((voxels, LANES), BF16),
        ),
        in_specs=[
            block(width),
            block(LANES),
            whole(*stats.shape),
            whole(8, lanes),
            whole(8, lanes),
            whole(width, lanes),
            whole(2 * LANES, 4 * LANES),
        ],
        out_specs=[block(LANES), block(LANES), block(LANES)],
        scratch_shapes=[pltpu.VMEM((slots, CHUNK, LANES), F32)],
        compiler_params=params("arbitrary", limit=30),
        cost_estimate=work(14),
        name="encode",
    )(points, counts, stats, kernel, gain, first, second)


def decode_kernel(
    slots, points_ref, count_ref, stats_ref, kernel_ref, gain_ref, first_ref, second_ref,
    feat_ref, share_ref, slot_ref, d_feat_ref, loss_ref, out_ref,
    first_sum, second_sum, joined, tail_sum,
):
    lanes = first_ref.shape[1]
    width = points_ref.shape[1]
    step = pl.program_id(0)

    @pl.when(step == 0)
    def _():
        first_sum[...] = jnp.zeros_like(first_sum)
        second_sum[...] = jnp.zeros_like(second_sum)

    _, mean, inv_std, _ = batch_norm(jnp.sum(stats_ref[...], axis=0), kernel_ref[...])
    scale = gain_ref[0:1, :] * inv_std
    offset = gain_ref[1:2, :] - mean * scale
    count = count_ref[:, 3:4].astype(F32).astype(jnp.int32)
    points = points_ref[...]
    slot = lax.broadcasted_iota(jnp.int32, (CHUNK, lanes), 1) // 32
    act = first_layer(points, first_ref, scale, offset, slot < count)
    pooled = group_fold(act, jnp.maximum)
    tail = second_tail(pooled)
    low = act.astype(BF16)
    share = share_ref[...]
    d_feat = d_feat_ref[...] * share
    d_low = d_feat.astype(BF16)
    shared = jnp.where((share > 0.0) & (share < 1.0), 1.0, 0.0)
    shared = jnp.max(jnp.max(shared, axis=1, keepdims=True)) > 0.0

    def group_back(g, left, pieces):
        d_part = jnp.concatenate(pieces, axis=1)
        second_sum[...] += lax.dot_general(
            left, d_part, (((0,), (0,)), ((), ())), preferred_element_type=F32
        )
        d_left = lax.dot_general(
            d_part, second_ref[...], (((1,), (1,)), ((), ())), preferred_element_type=F32
        )
        joined[:, g * LANES : (g + 1) * LANES] = d_left[:, :LANES]
        return d_left[:, LANES:]

    none = jnp.zeros((CHUNK, LANES), BF16)

    @pl.when(jnp.logical_not(shared))
    def _():
        found = slot_ref[...]
        d_tail = jnp.zeros((CHUNK, LANES), F32)
        for g in range(lanes // LANES):
            left = group_left(low, tail, count, g)
            pieces = [
                jnp.where(found == jnp.asarray(4 * g + s, BF16), d_low, none)
                if 4 * g + s < slots
                else none
                for s in range(4)
            ]
            d_tail = d_tail + group_back(g, left, pieces)
        tail_sum[...] = d_tail

    @pl.when(shared)
    def _():
        top = feat_ref[...]
        d_tail = jnp.zeros((CHUNK, LANES), F32)
        for g in range(lanes // LANES):
            left = group_left(low, tail, count, g)
            part = jnp.dot(left, second_ref[...], preferred_element_type=F32)
            pieces = []
            for s in range(4):
                if 4 * g + s < slots:
                    hit = part[:, s * LANES : (s + 1) * LANES] == top
                    pieces.append(jnp.where(hit, d_feat, 0.0).astype(BF16))
                else:
                    pieces.append(none)
            d_tail = d_tail + group_back(g, left, pieces)
        tail_sum[...] = d_tail

    wide = jnp.concatenate([pooled] * (lanes // LANES), axis=1)
    reached = act == wide
    ties = group_fold(jnp.where(reached, 1.0, 0.0), jnp.add)
    lane = lax.broadcasted_iota(jnp.int32, (CHUNK, LANES), 1)
    spread = jnp.where(lane < 32, tail_sum[...], 0.0)
    spread = spread + pltpu.roll(spread, 32, 1)
    spread = (spread + pltpu.roll(spread, 64, 1)) / ties
    spread = jnp.concatenate([spread] * (lanes // LANES), axis=1)
    d_act = joined[...] + jnp.where(reached, spread, 0.0)
    d_act = jnp.where(act > 0.0, d_act, 0.0).astype(BF16)
    first_sum[...] += lax.dot_general(
        points, d_act, (((0,), (0,)), ((), ())), preferred_element_type=F32
    )

    @pl.when(step == pl.num_programs(0) - 1)
    def _():
        row_at = lax.broadcasted_iota(jnp.int32, (width, lanes), 0)
        col_at = lax.broadcasted_iota(jnp.int32, (width, lanes), 1)
        same = (row_at % slots == col_at // 32) | (row_at == 7 * slots)
        total = jnp.where(same & (col_at // 32 < slots), first_sum[...], 0.0)
        rows = [
            jnp.sum(jnp.where(row_at // slots == k, total, 0.0), axis=0, keepdims=True)
            for k in range(8)
        ]
        first = group_fold(jnp.concatenate(rows, axis=0), jnp.add)
        upper = second_sum[0:32, 0:LANES]
        lower = second_sum[LANES : LANES + 40, 0:LANES]
        for s in range(1, 4):
            cols = slice(s * LANES, (s + 1) * LANES)
            upper = upper + second_sum[s * 32 : (s + 1) * 32, cols]
            lower = lower + second_sum[LANES : LANES + 40, cols]
        devices, layers = out_ref.shape[:2]
        none = jnp.zeros((devices * layers - 88, LANES), F32)
        rows = jnp.concatenate([first, upper, lower, loss_ref[...], none], axis=0)
        for k in range(layers):
            out_ref[:, k, :] = rows[k * devices : (k + 1) * devices, :]


def decode(
    points, counts, stats, kernel, gain, first, second, feat, share, slot, d_feat, loss, shape, slots
):
    voxels, width = points.shape
    lanes = first.shape[1]
    whole = lambda *shape: pl.BlockSpec(shape, lambda i: (0,) * len(shape))
    block = lambda size: pl.BlockSpec((CHUNK, size), lambda i: (i, 0))
    return pl.pallas_call(
        functools.partial(decode_kernel, slots),
        grid=(voxels // CHUNK,),
        out_shape=jax.ShapeDtypeStruct(shape + (LANES,), F32),
        in_specs=[
            block(width),
            block(LANES),
            whole(*stats.shape),
            whole(8, lanes),
            whole(8, lanes),
            whole(width, lanes),
            whole(2 * LANES, 4 * LANES),
            block(LANES),
            block(LANES),
            block(LANES),
            block(LANES),
            whole(8, LANES),
        ],
        out_specs=whole(*shape, LANES),
        scratch_shapes=[
            pltpu.VMEM((width, lanes), F32),
            pltpu.VMEM((2 * LANES, 4 * LANES), F32),
            pltpu.VMEM((CHUNK, lanes), F32),
            pltpu.VMEM((CHUNK, LANES), F32),
        ],
        compiler_params=params("arbitrary", limit=30),
        cost_estimate=work(28),
        name="decode",
    )(points, counts, stats, kernel, gain, first, second, feat, share, slot, d_feat, loss)


def encoder_weights_kernel(
    slots, one_ref, two_ref, bias_ref, gain_ref, first_ref, second_ref, kernel_ref, rows_ref
):
    width, lanes = first_ref.shape
    features = one_ref.shape[0] - 1
    row_at = lax.broadcasted_iota(jnp.int32, (width, LANES), 0)
    slot_at = lax.broadcasted_iota(jnp.int32, (width, LANES), 1) // 32
    one = jnp.concatenate([one_ref[...]] * 4, axis=1)
    tall = jnp.zeros((width, LANES), F32)
    for k in range(features):
        tall = jnp.where(row_at // slots == k, one[k : k + 1, :], tall)
    own_slot = row_at % slots
    for g in range(lanes // LANES):
        here = slice(g * LANES, (g + 1) * LANES)
        first_ref[:, here] = jnp.where(own_slot == 4 * g + slot_at, tall, 0.0).astype(BF16)
        kernel_ref[:, here] = one
        rows_ref[:, here] = jnp.concatenate([gain_ref[...]] * 4, axis=1)
    two = two_ref[...]
    half = two.shape[0] // 2
    upper = jnp.concatenate([two[:half]] * 4, axis=0)
    row_two = lax.broadcasted_iota(jnp.int32, (LANES, LANES), 0)
    for s in range(4):
        here = slice(s * LANES, (s + 1) * LANES)
        second_ref[0:LANES, here] = jnp.where(row_two // half == s, upper, 0.0).astype(BF16)
        lower = jnp.concatenate(
            [two[half:], bias_ref[...], jnp.zeros((LANES - half - 8, LANES), F32)], axis=0
        )
        second_ref[LANES:, here] = jnp.where(row_two == half + 1 + s, EMPTY, lower).astype(BF16)


def encoder_weights(w_one, w_two, bias_two, gain, shift, slots):
    features, c_one = w_one.shape
    lanes = -(-slots // 4) * LANES
    width = -(-(features * slots + 1) // LANES) * LANES
    one = jnp.pad(w_one.astype(F32), ((0, 1), (0, 0)))
    bias = jnp.pad(bias_two.astype(F32).reshape(1, -1), ((0, 7), (0, 0)))
    rows = jnp.pad(jnp.stack([gain, shift]).astype(F32), ((0, 6), (0, 0)))
    return pl.pallas_call(
        functools.partial(encoder_weights_kernel, slots),
        out_shape=(
            jax.ShapeDtypeStruct((width, lanes), BF16),
            jax.ShapeDtypeStruct((2 * LANES, 4 * LANES), BF16),
            jax.ShapeDtypeStruct((8, lanes), F32),
            jax.ShapeDtypeStruct((8, lanes), F32),
        ),
        in_specs=vmem(4),
        out_specs=vmem(4),
        compiler_params=params(limit=24),
        cost_estimate=work(2),
        name="encoder_weights",
    )(one, w_two.astype(F32), bias, rows)


def pick_rows(source, place_ref, line, capacity, offset):
    want = place_ref[line : line + 1, :][:, : source.shape[0]] - offset
    row_at = lax.broadcasted_iota(jnp.int32, (capacity, source.shape[0]), 0)
    chosen = jnp.where(want == row_at, 1.0, 0.0).astype(BF16)
    found = jnp.dot(chosen, source, preferred_element_type=F32)
    return found[:, :LANES].astype(BF16), found[:, LANES:].T


def edge_lists_kernel(anc_count, offset_ref, feat_ref, digit_ref, place_ref, up_ref, down_ref):
    source = jnp.concatenate([feat_ref[...].astype(BF16), digit_ref[...]], axis=1)
    for side, edge_ref in enumerate((up_ref, down_ref)):
        rows, digits = pick_rows(source, place_ref, anc_count + side, EDGE_CAP, offset_ref[1])
        edge_ref[0:EDGE_CAP, :] = rows
        digits = jnp.concatenate([digits[0:8, :], jnp.zeros((8, LANES), F32)], axis=0)
        edge_ref[EDGE_CAP : EDGE_CAP + 16, :] = digits.astype(BF16)


def edge_lists(offsets, feat, digits, place, anc_count):
    return pl.pallas_call(
        functools.partial(edge_lists_kernel, anc_count),
        out_shape=(
            jax.ShapeDtypeStruct((EDGE_CAP + 16, LANES), BF16),
            jax.ShapeDtypeStruct((EDGE_CAP + 16, LANES), BF16),
        ),
        in_specs=smem(1) + vmem(3),
        out_specs=vmem(2),
        compiler_params=params(limit=24),
        cost_estimate=work(1),
        name="edge_lists",
    )(offsets, feat, digits, place)


def gather_lists_kernel(anc_count, offset_ref, feat_ref, digit_ref, place_ref, main_ref):
    source = jnp.concatenate([feat_ref[...].astype(BF16), digit_ref[...]], axis=1)
    for q in range(anc_count):
        rows, digits = pick_rows(source, place_ref, q, CAP, offset_ref[0])
        main_ref[q, 0:CAP, :] = rows
        lines = [
            digits[k : k + 1, i * LANES : (i + 1) * LANES]
            for k in range(3)
            for i in range(CAP // LANES)
        ]
        lines.append(jnp.zeros((32 - len(lines), LANES), F32))
        main_ref[q, CAP : CAP + 32, :] = jnp.concatenate(lines, axis=0).astype(BF16)
        main_ref[q, CAP + 32 :, :] = jnp.zeros((EDGE_CAP + 16, LANES), BF16)


def gather_lists(offsets, feat, digits, place, anc_count):
    return pl.pallas_call(
        functools.partial(gather_lists_kernel, anc_count),
        out_shape=jax.ShapeDtypeStruct((anc_count, CAP + EDGE_CAP + 48, LANES), BF16),
        in_specs=smem(1) + vmem(3),
        out_specs=vmem(1)[0],
        compiler_params=params(limit=30),
        cost_estimate=work(5),
        name="gather_lists",
    )(offsets, feat, digits, place)


def spread_lists_kernel(index_ref, *refs):
    received, (out_ref, held) = refs[:-2], refs[-2:]
    length = received[0].shape[0]
    for k, received_ref in enumerate(received):
        held[k * length : (k + 1) * length, :] = received_ref[...].astype(F32)
    held[len(received) * length :, :] = jnp.zeros((8, LANES), F32)

    def pick(i, carry):
        base = pl.multiple_of(i * LANES, LANES)
        for j in range(LANES):
            out_ref[pl.ds(base + j, 1), :] = held[pl.ds(index_ref[base + j], 1), :]
        return carry

    lax.fori_loop(0, out_ref.shape[0] // LANES, pick, 0)


def spread_lists(index, received):
    voxels = index.shape[0]
    total = sum(rows.shape[0] for rows in received)
    return pl.pallas_call(
        spread_lists_kernel,
        out_shape=jax.ShapeDtypeStruct((voxels, LANES), F32),
        in_specs=smem(1) + vmem(len(received)),
        out_specs=vmem(1)[0],
        scratch_shapes=[pltpu.VMEM((total + 8, LANES), F32)],
        compiler_params=params(limit=24),
        cost_estimate=work(4),
        name="spread_lists",
    )(index, *received)


def add_piece(held, source, low, high, start):
    lane = lax.broadcasted_iota(jnp.int32, (1, LANES), 1)
    begin, end = low // LANES, -(-high // LANES)
    gap = start - low
    turn = gap % LANES
    at = begin + gap // LANES
    rows = source[begin:end, :]
    count = end - begin
    place = lax.broadcasted_iota(jnp.int32, (count, LANES), 0) * LANES
    place = place + lax.broadcasted_iota(jnp.int32, (count, LANES), 1) + begin * LANES
    if low % LANES or high % LANES:
        rows = jnp.where((place >= low) & (place < high), rows, 0.0)
    if turn == 0:
        held[at : at + count, :] += rows
        return
    rows = pltpu.roll(rows, turn, 1)
    here = jnp.where(lane >= turn, rows, 0.0)
    after = jnp.where(lane < turn, rows, 0.0)
    skip = max(-at, 0)
    if count > skip:
        held[at + skip : at + count, :] += here[skip:, :]
    held[at + 1 : at + 1 + count, :] += after


def pack_kernel(
    plan, tiles, chunk, region_ref, middle_ref, head_ref, mid_ref, row_ref, out_ref, held, rest_ref
):
    half = LANES // 2
    lane = lax.broadcasted_iota(jnp.int32, (1, LANES), 1)
    mid = jnp.sum(mid_ref[...], axis=0, keepdims=True)
    mid = group_sum(mid)
    mid = mid + pltpu.roll(mid, half, 1)
    region_bias = pltpu.roll(jnp.sum(row_ref[0:8, :], axis=0, keepdims=True), half, 1)
    outs = row_ref.shape[0] - 16
    wide = lax.broadcasted_iota(jnp.int32, (outs, LANES), 1) - half
    own = lax.broadcasted_iota(jnp.int32, (outs, LANES), 0) == wide
    head_bias = jnp.sum(jnp.where(own, row_ref[8 : 8 + outs, :], 0.0), axis=0, keepdims=True)
    rest_ref[0:1, :] = jnp.where(lane < half, mid, region_bias)
    rest_ref[1:2, :] = jnp.where(lane < half, region_bias, head_bias)
    sources = {"region": region_ref, "middle": middle_ref, "head": head_ref, "rest": rest_ref}
    for a, pieces in enumerate(plan):
        held[...] = jnp.zeros_like(held)
        for name, low, high, start in pieces:
            if name in sources:
                add_piece(held, sources[name], low, high, start)
        for t in range(tiles):
            out_ref[t * len(plan) + a] = held[t * chunk : (t + 1) * chunk, :].astype(BF16)


def group_sum(values):
    out = values[:, :LANES]
    for g in range(1, values.shape[1] // LANES):
        out = out + values[:, g * LANES : (g + 1) * LANES]
    return out


def pack(plan, tiles, chunk, region, middle, head, mid_sums, row_sums):
    return pl.pallas_call(
        functools.partial(pack_kernel, plan, tiles, chunk),
        out_shape=jax.ShapeDtypeStruct((tiles * len(plan), chunk, LANES), BF16),
        in_specs=vmem(5),
        out_specs=vmem(1)[0],
        scratch_shapes=[pltpu.VMEM((tiles * chunk, LANES), F32), pltpu.VMEM((8, LANES), F32)],
        compiler_params=params(limit=28),
        cost_estimate=work(3),
        name="pack",
    )(region, middle, head, mid_sums, row_sums)


def sum_chunk_kernel(parts_ref, out_ref, square_ref):
    total = jnp.sum(parts_ref[...].astype(F32), axis=0)
    for i in range(out_ref.shape[0]):
        out_ref[i] = total
    square_ref[...] = jnp.broadcast_to(jnp.sum(total * total), square_ref.shape)


def sum_chunk(parts, tiles):
    _, rows, lanes = parts.shape
    return pl.pallas_call(
        sum_chunk_kernel,
        out_shape=(
            jax.ShapeDtypeStruct((tiles, rows, lanes), F32),
            jax.ShapeDtypeStruct((1, lanes), F32),
        ),
        in_specs=vmem(1),
        out_specs=vmem(2),
        compiler_params=params(limit=24),
        cost_estimate=work(2),
        name="sum_chunk",
    )(parts)


def finish_kernel(
    plan, anc_ref, early_ref, late_ref, stats_ref, kernel_ref, gain_ref,
    out_ref, scalar_ref, one, norm,
):
    stats = jnp.sum(stats_ref[...], axis=0)
    kernel = kernel_ref[:, :LANES]
    mixed, mean, inv_std, count = batch_norm(stats, kernel)
    layers = late_ref.shape[1] - 1
    late = jnp.concatenate([late_ref[:, k, :] for k in range(layers)], axis=0)
    sums = late[0:8, :]
    total_shift = sums[7:8, :]
    total_gain = inv_std * (jnp.sum(kernel * sums, axis=0, keepdims=True) - mean * total_shift)
    slope = gain_ref[0:1, :LANES] * inv_std
    lane = lax.broadcasted_iota(jnp.int32, (1, LANES), 1)
    one[...] = jnp.zeros_like(one)
    norm[...] = jnp.zeros_like(norm)
    for k in range(7):
        first = stats[7:8, k : k + 1]
        pull = total_shift * first + total_gain * inv_std * (mixed[k : k + 1, :] - mean * first)
        grad = jnp.where(lane < 32, slope * (sums[k : k + 1, :] - pull / count), 0.0)
        if k % 4:
            grad = pltpu.roll(grad, 32 * (k % 4), 1)
        one[k // 4 : k // 4 + 1, :] += grad
    bias = late[72:73, :]
    top = jnp.where(lane < 32, total_gain, 0.0)
    top = top + pltpu.roll(jnp.where(lane < 32, total_shift, 0.0), 32, 1)
    norm[0:1, :] = top + jnp.where(lane < 64, 0.0, pltpu.roll(bias, 64, 1))
    norm[1:2, :] = jnp.where(lane < 64, pltpu.roll(bias, 64, 1), 0.0)
    two = late[8:72, :]
    square = jnp.sum(late_ref[:, layers, :]) / LANES
    square = square + jnp.sum(two * two) + jnp.sum(one[...] * one[...])
    square = square + jnp.sum(norm[...] * norm[...])
    size = jnp.sqrt(jnp.broadcast_to(square, (1, LANES)))
    scalar_ref[0:1, :] = late[80:81, :] / stats[1:2, 8:9]
    scalar_ref[1:2, :] = size
    scalar_ref[2:8, :] = jnp.broadcast_to(jnp.minimum(1.0, CLIP_LIMIT / (size + 1e-06)), (6, LANES))
    chunk = early_ref.shape[1]
    for i in range(early_ref.shape[0]):
        out_ref[i * chunk : (i + 1) * chunk, :] = early_ref[i]
    sources = {"one": one, "two": two, "norm": norm}
    for a, pieces in enumerate(plan):

        @pl.when(anc_ref[0] == a)
        def _():
            for name, low, high, start in pieces:
                if name in sources:
                    add_piece(out_ref, sources[name], low, high, start)


def finish(plan, anc, early, late, stats, kernel, gain):
    return pl.pallas_call(
        functools.partial(finish_kernel, plan),
        out_shape=(
            jax.ShapeDtypeStruct((early.shape[0] * early.shape[1], LANES), F32),
            jax.ShapeDtypeStruct((8, LANES), F32),
        ),
        in_specs=smem(1) + vmem(5),
        out_specs=vmem(2),
        scratch_shapes=[pltpu.VMEM((8, LANES), F32), pltpu.VMEM((8, LANES), F32)],
        compiler_params=params(limit=24),
        cost_estimate=work(3),
        name="finish",
    )(anc, early, late, stats, kernel, gain)


def everyone(values, axes):
    count = 1
    for axis in axes:
        count *= lax.axis_size(axis)
    copies = jnp.broadcast_to(values[None], (count,) + values.shape)
    return lax.all_to_all(copies, axes, 0, 0)


def swap_rows(beside, across):
    axes = ("tile", "anc")
    count = lax.axis_size("tile") * lax.axis_size("anc")
    pairs = [(i, i ^ 1) for i in range(count)]
    others = [(i, i + 1) for i in range(1, count - 1, 2)]
    others += [(j, i) for i, j in others]
    return lax.ppermute(beside, axes, pairs), lax.ppermute(across, axes, others)


def shard_windows(segments, shard, count):
    windows = []
    for a in range(count):
        begin, end = a * shard, (a + 1) * shard
        at = 0
        pieces = []
        for name, size in segments:
            low, high = max(begin, at), min(end, at + size)
            if low < high:
                pieces.append((name, low - at, high - at, low - begin))
            at += size
        windows.append(tuple(pieces))
    return tuple(windows)


def on_device(
    points,
    npoints,
    coords,
    labels,
    targets,
    w_vfe1,
    w_vfe2,
    w_mid,
    w_rpn,
    w_head,
    bn_gain,
    biases,
    master,
    moment1,
    moment2,
):
    both = ("tile", "anc")
    anc_count = lax.axis_size("anc")
    tile_count = lax.axis_size("tile")
    anc = lax.axis_index("anc")
    tile = lax.axis_index("tile")
    device_rows = labels.shape[1]
    columns = labels.shape[2]
    blocks = device_rows // BLOCK_ROWS
    tile_rows = device_rows * anc_count
    all_rows = tile_rows * tile_count
    slots = points.shape[1]
    voxels = points.shape[2]
    c_vfe = w_vfe1.shape[1]
    c_vox = w_vfe2.shape[1]
    c_mid = w_mid.shape[4]
    c_rpn = w_rpn.shape[3]
    outs = w_head.shape[1]
    shift = biases[:c_vfe]
    bias_two = biases[c_vfe : c_vfe + c_vox]
    rest = biases[c_vfe + c_vox :].astype(F32)
    bias_rows = jnp.concatenate(
        [rest[:c_mid], rest, jnp.zeros((LANES - outs,), F32)]
    ).reshape(3, LANES)

    def joined(row):
        return (row % CROP_ROWS != CROP_ROWS // 2) & (row > 0) & (row < all_rows)

    padded = -(-voxels // CHUNK) * CHUNK
    width = -(-(points.shape[0] * slots + 1) // LANES) * LANES
    flat_points = points.reshape(-1, voxels).T
    flat_points = jnp.pad(
        flat_points, ((0, padded - voxels), (0, width - flat_points.shape[1]))
    )
    lane = lax.broadcasted_iota(jnp.int32, flat_points.shape, 1)
    flat_points = jnp.where(lane == points.shape[0] * slots, jnp.ones((), BF16), flat_points)
    spare = (0, -(-padded // LINE) * LINE - voxels)
    row = coords[:, 1] - tile * tile_rows
    lines = [coords[:, 0], row, coords[:, 2], jnp.ones_like(row), npoints]
    lines = jnp.pad(jnp.stack(lines), ((0, 3), spare))
    tile_edges = jnp.stack([joined(tile * tile_rows), joined((tile + 1) * tile_rows)])
    devices = anc_count * tile_count
    parts = [w_rpn]
    for k in range(1, anc_count):
        around = [((i + k) % anc_count, i) for i in range(anc_count)]
        parts.append(lax.ppermute(w_rpn, "anc", around))
    stats, place, digits = prepare(
        tile_edges.astype(jnp.int32),
        flat_points,
        lines,
        labels.transpose(1, 0, 2),
        anc_count,
        device_rows,
        slots,
        devices,
    )
    stats, parts = lax.optimization_barrier((stats, parts))
    stats = lax.all_to_all(stats, both, 0, 0)
    region_in, region_back = region_order(anc.reshape(1), parts)
    counts = digits
    count_pos = jnp.sum(stats[:, 1, 8])
    rounds = jnp.ceil(jnp.max(stats[:, 2, 8])).astype(jnp.int32)
    middle_kernel_all = w_mid.transpose(0, 1, 2, 4, 3).reshape(-1, c_mid, c_vox)

    first, second, kernel, gain_rows = encoder_weights(
        w_vfe1, w_vfe2, bias_two, bn_gain, shift, slots
    )
    feat, share, found = encode(
        flat_points, counts, stats, kernel, gain_rows, first, second, slots
    )
    feat, region_in, region_back = lax.optimization_barrier((feat, region_in, region_back))

    in_tile = lax.axis_size("tile")
    upward = [(i + 1, i) for i in range(in_tile - 1)]
    downward = [(i, i + 1) for i in range(in_tile - 1)]

    def exchange(number):
        offsets = jnp.stack([number * CAP, number * EDGE_CAP]).astype(jnp.int32)
        up, down = edge_lists(offsets, feat, digits, place, anc_count)
        from_below = lax.ppermute(up, "tile", upward)
        from_above = lax.ppermute(down, "tile", downward)
        main = gather_lists(offsets, feat, digits, place, anc_count)
        main, from_below, from_above = lax.optimization_barrier((main, from_below, from_above))
        main = lax.dynamic_update_slice(main, from_above[None], (0, CAP + 32, 0))
        main = lax.dynamic_update_slice(main, from_below[None], (anc_count - 1, CAP + 32, 0))
        return lax.all_to_all(main, "anc", 0, 0), main

    def cells(got):
        words = got[:, CAP : CAP + 32].reshape(anc_count, -1).astype(jnp.int32)
        start = CAP + 32 + EDGE_CAP
        edge_words = got[:, start : start + 16].astype(jnp.int32)

        def word(k):
            gap = jnp.zeros((anc_count, 32), jnp.int32)
            parts = [words[:, k * CAP : (k + 1) * CAP], gap, edge_words[:, k], gap[:, :16]]
            return jnp.concatenate(parts, axis=1)

        high, half, mixed = word(0), word(1), word(2)
        local = mixed // 2 - anc * device_rows
        is_edge = lax.broadcasted_iota(jnp.int32, local.shape, 1) >= CAP
        local = local + jnp.where(is_edge, jnp.where(anc == 0, -tile_rows, tile_rows), 0)
        cross = half * 2 + mixed % 2
        scatter_at, own_at = [], []
        for k in range(blocks):
            line = local - k * BLOCK_ROWS
            tall = BLOCK_ROWS + 2 * HALO
            inside = (high > 0) & (line >= -HALO) & (line < BLOCK_ROWS + HALO)
            spot = ((high - 1) * tall + line + HALO) * columns + cross
            scatter_at.append(jnp.where(inside, spot, DEPTH * tall * columns).reshape(-1))
            inside = (high > 0) & (line >= 0) & (line < BLOCK_ROWS)
            spot = ((high - 1) * BLOCK_ROWS + line) * columns + cross
            spot = jnp.where(inside, spot, DEPTH * BLOCK_ROWS * columns)
            own_at.append(spot[:, :CAP].reshape(-1, LANES))
        return scatter_at, own_at

    got, sent = exchange(0)
    labels, targets, _ = lax.optimization_barrier((labels, targets, sent[0, 0, 0]))
    first_row = tile * tile_rows + anc * device_rows
    edges = []
    even = (tile * anc_count + anc) % 2 == 0
    for k in range(blocks):
        top = first_row + k * BLOCK_ROWS
        flags = [
            joined(top),
            joined(top + BLOCK_ROWS),
            even,
            anc * device_rows + k * BLOCK_ROWS,
            jnp.where(anc == 0, -tile_rows, tile_rows),
            anc,
        ]
        edges.append(jnp.stack([flag.astype(jnp.int32) for flag in flags]))

    def more(state):
        return state[0] < rounds

    def another(state):
        number, held = state
        rows, _ = exchange(number)
        index, _ = cells(rows)
        rows = rows.reshape(-1, LANES)
        held = [scatter_rows(at, rows, old, columns) for at, old in zip(index, held)]
        return number + 1, held

    def one_round():
        made = [
            scatter_middle(
                edges[k], got.reshape(-1, LANES), middle_kernel_all, bias_rows, columns
            )
            for k in range(blocks)
        ]
        return tuple([one[i] for one in made] for i in range(3))

    def many_rounds():
        index, own = cells(got)
        held = [scatter_rows(at, got.reshape(-1, LANES), None, columns) for at in index]
        _, held = lax.while_loop(more, another, (jnp.int32(1), held))
        bevs = [
            middle_forward(edges[k], held[k], middle_kernel_all, bias_rows, columns)
            for k in range(blocks)
        ]
        return held, bevs, own

    grids, bevs, own_at = lax.cond(rounds > 1, many_rounds, one_round)

    wide_labels = jnp.repeat(labels.reshape(2, -1), outs // 2, axis=0)
    wide_targets = jnp.pad(targets, ((0, 0), (1, 0), (0, 0), (0, 0))).reshape(outs, -1)
    step = BLOCK_ROWS * columns
    scale = 1.0 / count_pos
    d_rows, head_sums, row_sums = [], 0.0, 0.0
    d_beside, d_across = [], []
    for k in range(blocks):
        here = slice(k * step, (k + 1) * step)
        d_block, near_row, far_row, heads, sums = region_forward(
            scale,
            edges[k],
            bevs[k],
            region_in,
            bias_rows,
            w_head.T,
            wide_labels[:, here],
            wide_targets[:, here],
            columns,
        )
        d_rows.append(d_block)
        d_beside.append(near_row)
        d_across.append(far_row)
        head_sums = head_sums + heads
        row_sums = row_sums + sums

    def swapped(near, far):
        if blocks == 1:
            got_near, got_far = swap_rows(near[0], far[0])
            return [got_near], [got_far]
        firsts = [jnp.where(even, f, n) for n, f in zip(near, far)]
        lasts = [jnp.where(even, n, f) for n, f in zip(near, far)]
        got_near, got_far = swap_rows(
            jnp.where(even, lasts[-1], firsts[0]), jnp.where(even, firsts[0], lasts[-1])
        )
        above = [jnp.where(even, got_far, got_near)] + lasts[:-1]
        below = firsts[1:] + [jnp.where(even, got_near, got_far)]
        return (
            [jnp.where(even, y, x) for x, y in zip(above, below)],
            [jnp.where(even, x, y) for x, y in zip(above, below)],
        )

    beside, across = swapped(d_beside, d_across)
    grad_region = sum(
        region_weight(d_rows[k], bevs[k], columns, anc_count) for k in range(blocks)
    )
    d_rows, grad_region, beside, across = lax.optimization_barrier(
        (d_rows, grad_region, beside, across)
    )
    d_mids, mid_sums = [], 0.0
    mid_beside, mid_across = [], []
    for k in range(blocks):
        d_block, near_row, far_row, sums = region_data(
            edges[k], d_rows[k], beside[k], across[k], bevs[k], region_back, columns
        )
        d_mids.append(d_block)
        mid_beside.append(near_row)
        mid_across.append(far_row)
        mid_sums = mid_sums + sums
    beside, across = swapped(mid_beside, mid_across)
    grad_mid = sum(middle_weight(grids[k], d_mids[k], columns) for k in range(blocks))
    grad_mid, beside, across = lax.optimization_barrier((grad_mid, beside, across))

    head_three = head_sums.reshape(3, outs, c_rpn)
    grad_head = (head_three[0] + head_three[1] + head_three[2]).T
    head_rows = grad_head.reshape(-1, LANES)
    segments = (
        ("region", grad_region.size),
        ("one", w_vfe1.size),
        ("two", w_vfe2.size),
        ("middle", grad_mid.size),
        ("head", w_head.size),
        ("norm", c_vfe + c_vfe + c_vox),
        ("rest", c_mid + c_rpn + outs),
    )
    shard = master.shape[0]
    plan = shard_windows(segments, shard, anc_count)
    chunk_rows = -(-(shard // LANES + 2) // (8 * tile_count)) * 8
    packed = pack(
        plan, tile_count, chunk_rows, grad_region, grad_mid, head_rows, mid_sums, row_sums
    )
    own_at, packed = lax.optimization_barrier((own_at, packed))
    chunk, chunk_square = sum_chunk(lax.all_to_all(packed, both, 0, 0), tile_count)

    def collect(number, own_index):
        lists = [
            middle_data(
                own_index[k], edges[k], d_mids[k], beside[k], across[k], middle_kernel_all, columns
            )
            for k in range(blocks)
        ]
        lists = [sum(parts) for parts in zip(*lists)]
        back = lists[:1]
        for k in range(1, anc_count):
            onward = [(i, (i + k) % anc_count) for i in range(anc_count)]
            back.append(lax.ppermute(lists[k], "anc", onward))
        mine = place[7, :padded] - number * CAP
        known = (mine >= 0) & (mine < CAP)
        index = (anc - place[6, :padded] + anc_count) % anc_count * CAP + mine
        return spread_lists(jnp.where(known, index, anc_count * CAP), back)

    d_feat = collect(0, own_at)
    d_feat, chunk = lax.optimization_barrier((d_feat, chunk))
    early = lax.all_to_all(chunk, "tile", 0, 0)

    def collect_more(state):
        number, held = state
        _, index = cells(exchange(number)[0])
        return number + 1, held + collect(number, index)

    d_feat = lax.cond(
        rounds > 1,
        lambda held: lax.while_loop(more, collect_more, (jnp.int32(1), held))[1],
        lambda held: held,
        d_feat,
    )
    layers = -(-88 // devices)
    late = decode(
        flat_points,
        counts,
        stats,
        kernel,
        gain_rows,
        first,
        second,
        feat,
        share,
        found,
        d_feat,
        row_sums[24:32],
        (devices, layers),
        slots,
    )
    late, early = lax.optimization_barrier((late, early))
    late = jnp.sum(lax.all_to_all(late, both, 0, 0), axis=0)
    late = everyone(jnp.concatenate([late, chunk_square], axis=0), both)
    reduced, scalars = finish(plan, anc.reshape(1), early, late, stats, kernel, gain_rows)
    loss = scalars[0, 0]
    norm_value = scalars[1, 0]
    reduced = reduced.reshape(-1)[:shard]
    clipped = reduced * scalars[2, 0]
    first_new = BETA_FIRST * moment1 + (1.0 - BETA_FIRST) * clipped
    second_new = BETA_SECOND * moment2 + (1.0 - BETA_SECOND) * clipped * clipped
    first_hat = first_new / (1.0 - BETA_FIRST**STEP_NUMBER)
    second_hat = second_new / (1.0 - BETA_SECOND**STEP_NUMBER)
    updated = master - LEARN_RATE * (
        first_hat / (jnp.sqrt(second_hat) + ADAM_EPSILON) + WEIGHT_DECAY * master
    )
    return (updated, first_new, second_new, loss, norm_value)


def solution(mesh):
    placed = (
        P(None, None, ("tile", "anc")),
        P(("tile", "anc")),
        P(("tile", "anc"), None),
        P(None, ("tile", "anc"), None),
        P(None, None, ("tile", "anc"), None),
        P(),
        P(),
        P(),
        P(None, None, "anc", None),
        P(),
        P(),
        P(),
        P("anc"),
        P("anc"),
        P("anc"),
    )
    return jax.shard_map(
        on_device,
        mesh=mesh,
        in_specs=placed,
        out_specs=(P("anc"), P("anc"), P("anc"), P(), P()),
        check_vma=False,
    )
```
